32 devices in a mesh: batch: 4 (over y, core), seq: 8 (over z, x).
Axes of the slice: x: 2, y: 2, z: 4, core: 2. Of those that a mesh axis runs over, the one named last changes fastest.
Arguments:
- tokens: float32 [4, 2048, 1024], P('batch', 'seq'), may hold values from -6 to 6
- cotangent: float32 [4, 2048, 1024], P('batch', 'seq'), may hold values from -6 to 6
- norm_gain: bfloat16 [1024], P(('batch', 'seq')), may hold values from 0.5 to 1.5
- in_weight: bfloat16 [1024, 4096], P(('batch', 'seq')), may hold values from -0.1875 to 0.1875
- conv_weight: bfloat16 [4, 2048], P(None, ('batch', 'seq')), may hold values from -3 to 3
- conv_bias: bfloat16 [2048], P(('batch', 'seq')), may hold values from -3 to 3
- select_weight: bfloat16 [2048, 96], P(('batch', 'seq')), may hold values from -0.125 to 0.125
- delta_weight: bfloat16 [64, 2048], P(None, ('batch', 'seq')), may hold values from -0.75 to 0.75
- delta_bias: bfloat16 [2048], P(('batch', 'seq')), may hold values from -5 to -2
- a_log: bfloat16 [16, 2048], P(None, ('batch', 'seq')), may hold values from -10 to 1
- skip_gain: bfloat16 [2048], P(('batch', 'seq')), may hold values from 0.5 to 1.5
- out_weight: bfloat16 [2048, 1024], P(('batch', 'seq')), may hold values from -0.125 to 0.125
Outputs:
- block_out: float32 [4, 2048, 1024], P('batch', 'seq')
- tokens_grad: float32 [4, 2048, 1024], P('batch', 'seq')
- gain_grad: float32 [1024], P(('batch', 'seq'))
- in_grad: float32 [1024, 4096], P(('batch', 'seq'))
- conv_grad: float32 [4, 2048], P(None, ('batch', 'seq'))
- conv_bias_grad: float32 [2048], P(('batch', 'seq'))
- select_grad: float32 [2048, 96], P(('batch', 'seq'))
- delta_grad: float32 [64, 2048], P(None, ('batch', 'seq'))
- delta_bias_grad: float32 [2048], P(('batch', 'seq'))
- a_log_grad: float32 [16, 2048], P(None, ('batch', 'seq'))
- skip_grad: float32 [2048], P(('batch', 'seq'))
- out_grad: float32 [2048, 1024], P(('batch', 'seq'))
The draws below stay inside these ranges and needn't reach their ends.
All inputs are finite; a program needn't handle non-finite values.
Results may differ from the reference program's by a relative error of at most 0.012.
Values may be sent and summed in bfloat16 or wider, within the bound.
A program may use at most 192 MiB of HBM per device.

```python
import jax
import jax.numpy as jnp
from jax import lax

D = 1024
DI = 2048
DS = 16
KW = 4
DTR = 64
SEQ_LEN = 2048
SEQS = 4


def block_scale(rng, shape, cuts, low, largest):
    def one(position, blocks):
        heights = jax.random.uniform(jax.random.fold_in(jax.random.fold_in(rng, 6), position), (blocks,), jnp.float32, low / len(cuts), largest / len(cuts))
        return jnp.repeat(jnp.exp(heights), shape[position] // blocks).reshape((-1,) + (1,) * (len(shape) - position - 1))

    loudness = one(*cuts[0])
    for cut in cuts[1:]:
        loudness = loudness * one(*cut)
    return loudness


def noise(stream_key, extent, deviation, reach, pieces=(), dtype=jnp.bfloat16):
    drawn = jax.random.normal(stream_key, extent, jnp.float32) * deviation
    if len(pieces) > 0:
        drawn = block_scale(stream_key, extent, pieces, -0.22, 0.18) * drawn
    return jnp.clip(drawn, min=-reach, max=reach).astype(dtype)


def setup_inputs(seed: int = 0) -> dict:
    splits = jax.random.split(jax.random.key(seed), 13)
    return {
        "tokens": noise(splits[0], (SEQS, SEQ_LEN, D), 1.0, 6.0, ((0, 4), (1, 8)), jnp.float32),
        "cotangent": noise(splits[1], (SEQS, SEQ_LEN, D), 1.0, 6.0, ((0, 4), (1, 8)), jnp.float32),
        "norm_gain": jnp.clip(1.0 + 0.1 * jax.random.normal(splits[2], (D,), jnp.float32), 0.5, 1.5).astype(jnp.bfloat16),
        "in_weight": noise(splits[3], (D, 2 * DI), D ** -0.5, 0.1875, ((0, 32),)),
        "conv_weight": noise(splits[4], (KW, DI), KW ** -0.5, 3.0, ((1, 32),)),
        "conv_bias": noise(splits[5], (DI,), 0.5, 3.0, ((0, 32),)),
        "select_weight": noise(splits[6], (DI, DTR + 2 * DS), DI ** -0.5, 0.125, ((0, 32),)),
        "delta_weight": noise(splits[7], (DTR, DI), DTR ** -0.5, 0.75, ((1, 32),)),
        "delta_bias": jnp.clip(-5.0 + 3.0 * jax.random.uniform(splits[8], (DI,), jnp.float32) ** block_scale(splits[8], (DI,), ((0, 32),), -0.2, 0.2), -5.0, -2.0).astype(jnp.bfloat16),
        "a_log": jnp.clip(-10.0 + 11.0 * jax.random.uniform(splits[9], (DS, DI), jnp.float32) ** block_scale(splits[9], (DS, DI), ((1, 32),), -0.2, 0.2), -10.0, 1.0).astype(jnp.bfloat16),
        "skip_gain": jnp.clip(0.5 + 1.0 * jax.random.uniform(splits[10], (DI,), jnp.float32) ** block_scale(splits[10], (DI,), ((0, 32),), -0.2, 0.2), 0.5, 1.5).astype(jnp.bfloat16),
        "out_weight": noise(splits[11], (DI, D), DI ** -0.5, 0.125, ((0, 32),)),
    }


EPS = 1e-05

@jax.custom_vjp
def low(v):
    return lax.optimization_barrier(v.astype(jnp.bfloat16)).astype(jnp.float32)

@jax.custom_vjp
def low_back(v):
    return v

def low_keep(v):
    return (low(v), None)

def low_pass(kept, grad):
    return (grad,)

def back_keep(v):
    return (v, None)

def back_low(kept, grad):
    return (low(grad),)
low.defvjp(low_keep, low_pass)
low_back.defvjp(back_keep, back_low)

def matmul(left, right):
    return jnp.dot(left, right, precision=lax.Precision.HIGHEST, preferred_element_type=jnp.float32)

def block_scan(state, delta_blk, x_blk, b_blk, c_blk, a_matrix):

    def advance(state_now, inputs):
        delta_row, x_row, b_row, c_row = inputs
        state_now = jnp.exp(delta_row[None, :] * a_matrix) * state_now + (delta_row * x_row)[None, :] * b_row[:, None]
        return (state_now, lax.optimization_barrier(jnp.sum(state_now * c_row[:, None], axis=0)))
    return lax.scan(advance, state, (delta_blk, x_blk, b_blk, c_blk))

def selective(delta, x_silu, b_input, c_output, a_matrix):
    length = delta.shape[0]
    block_len = 64 if length % 64 == 0 else length
    num_blocks = length // block_len
    checked = jax.checkpoint(block_scan)

    def outer_step(state, inputs):
        return checked(state, inputs[0], inputs[1], inputs[2], inputs[3], a_matrix)
    state_zero = jnp.zeros((DS, DI), jnp.float32)
    _, outputs = lax.scan(outer_step, state_zero, (delta.reshape(num_blocks, block_len, DI), x_silu.reshape(num_blocks, block_len, DI), b_input.reshape(num_blocks, block_len, DS), c_output.reshape(num_blocks, block_len, DS)))
    return outputs.reshape(length, DI)

def forward(residual, gain, w_in, w_conv, b_conv, w_select, w_delta, b_delta, a_log, skip, w_out):
    length = residual.shape[0]
    norm_scale = lax.rsqrt(lax.optimization_barrier(jnp.mean(residual * residual, axis=-1, keepdims=True)) + EPS)
    normed = low(residual * norm_scale * gain)
    mixed = low_back(matmul(normed, w_in))
    x_in = low(mixed[:, :DI])
    z_gate = mixed[:, DI:]
    padded = jnp.concatenate([jnp.zeros((KW - 1, DI), jnp.float32), x_in], axis=0)
    filtered = b_conv + sum((w_conv[tap] * padded[tap:tap + length] for tap in range(KW)))
    x_silu = low(jax.nn.silu(filtered))
    projected = low_back(matmul(x_silu, w_select))
    delta_low = low(projected[:, :DTR])
    b_input = projected[:, DTR:DTR + DS]
    c_output = projected[:, DTR + DS:]
    delta = jax.nn.softplus(low_back(matmul(delta_low, w_delta)) + b_delta)
    a_matrix = -jnp.exp(a_log)
    y_scan = selective(delta, x_silu, b_input, c_output, a_matrix) + skip * x_silu
    gated = low(y_scan * jax.nn.silu(z_gate))
    return residual + low_back(matmul(gated, w_out))

def reference(tokens, cotangent, norm_gain, in_weight, conv_weight, conv_bias, select_weight, delta_weight, delta_bias, a_log, skip_gain, out_weight):
    weights = tuple((w.astype(jnp.float32) for w in (norm_gain, in_weight, conv_weight, conv_bias, select_weight, delta_weight, delta_bias, a_log, skip_gain, out_weight)))

    def one_sequence(totals, inputs):
        residual, upstream = inputs
        result, pull = jax.vjp(forward, residual, *weights)
        grads = pull(upstream)
        return (tuple((a + b for a, b in zip(totals, grads[1:]))), (result, grads[0]))
    start = tuple((jnp.zeros(w.shape, jnp.float32) for w in weights))
    sums, (block_out, tokens_grad) = lax.scan(one_sequence, start, (tokens, cotangent))
    return (block_out, tokens_grad, sums[0], sums[1], sums[2], sums[3], sums[4], sums[5], sums[6], sums[7], sums[8], sums[9])
```

```python
import functools

import jax
import jax.numpy as jnp
from jax import lax
from jax.experimental import pallas as pl
from jax.experimental.pallas import tpu as pltpu
from jax.sharding import PartitionSpec as P

DS = 16
KW = 4
DTR = 64
EPS = 1e-05
LOG2E = 1.4426950408889634
LN2 = 0.6931471805599453
F32 = jnp.float32
BF16 = jnp.bfloat16
MESH = pl.DeviceIdType.MESH
VM = pl.BlockSpec(memory_space=pltpu.VMEM)
ANY = pl.BlockSpec(memory_space=pl.ANY)
GRANT = 60 << 20
ALOG0, DELTA0, PACK0, PACK = 8, 24, 96, 128


def sds(shape, dtype):
    return jax.ShapeDtypeStruct(shape, dtype)


def kernel_call(body, outs, n_in, scratch=(), flops=1e9, **params):
    return pl.pallas_call(
        body,
        out_shape=outs,
        in_specs=[VM] * n_in,
        out_specs=jax.tree.map(lambda _: VM, outs),
        scratch_shapes=list(scratch),
        cost_estimate=pl.CostEstimate(flops=int(flops), bytes_accessed=8 << 20, transcendentals=0),
        compiler_params=pltpu.CompilerParams(vmem_limit_bytes=GRANT, **params),
    )


def sigmoid(v):
    return 1.0 / (1.0 + jnp.exp(-v))


def dot(a, b):
    return jnp.dot(a, b, preferred_element_type=F32)


def dot_nt(a, b):
    return lax.dot_general(a, b, (((1,), (1,)), ((), ())), preferred_element_type=F32)


def dot_tn(a, b):
    return lax.dot_general(a, b, (((0,), (0,)), ((), ())), preferred_element_type=F32)


def lanes(k, width=128):
    return pl.ds(pl.multiple_of(k * width, width), width)


def inproj_body(tok_ref, gain_ref, inx_ref, normed_ref, xin_ref):
    rows = tok_ref.shape[0]

    def norm(i, _):
        r = pl.ds(pl.multiple_of(i * 16, 16), 16)
        u = tok_ref[r, :]
        scale = lax.rsqrt(jnp.mean(u * u, axis=-1, keepdims=True) + EPS)
        normed_ref[r, :] = (u * scale * gain_ref[...]).astype(BF16)
        return 0

    lax.fori_loop(0, rows // 16, norm, 0)
    width = 512

    def mm(j, _):
        c = lanes(j, width)
        xin_ref[:, c] = dot(normed_ref[...], inx_ref[:, c]).astype(BF16)
        return 0

    lax.fori_loop(0, inx_ref.shape[1] // width, mm, 0)


def conv_body(xin_ref, halo_ref, w0_ref, selt_ref, filt_ref, xs_ref, xt_ref, draw_ref, dt_ref, bb_ref, cb_ref, proj, xp):
    rows, di = xin_ref.shape
    tiles = di // 128
    xp_rows = 16 + rows

    def conv(k, _):
        c = lanes(k)
        xp[0:16, :] = halo_ref[:, c].astype(F32)
        xp[16:xp_rows, :] = xin_ref[:, c].astype(F32)
        for q in range(2):
            r0 = q * (rows // 2)
            f = w0_ref[4:5, c]
            for tap in range(KW):
                lo = 16 - (KW - 1) + tap + r0
                f = f + w0_ref[tap : tap + 1, c] * xp[lo : lo + rows // 2, :]
            s = (f * sigmoid(f)).astype(BF16)
            filt_ref[r0 : r0 + rows // 2, c] = f
            xs_ref[r0 : r0 + rows // 2, c] = s
            xt_ref[pl.ds(r0 * tiles + k, rows // 2, stride=tiles), :] = s.astype(F32)
        return 0

    lax.fori_loop(0, tiles, conv, 0)
    proj[:, 0:96] = dot_nt(xs_ref[...], selt_ref[...])
    low = proj[:, 0:DTR].astype(BF16)

    def delta(k, _):
        c = lanes(k)
        raw = dot(low, w0_ref[DELTA0 : DELTA0 + DTR, c].astype(BF16)) + w0_ref[5:6, c]
        draw_ref[:, c] = raw
        dt_ref[pl.ds(k, rows, stride=tiles), :] = jnp.maximum(raw, 0.0) + jnp.log1p(jnp.exp(-jnp.abs(raw)))
        return 0

    lax.fori_loop(0, tiles, delta, 0)
    row_ids = lax.broadcasted_iota(jnp.int32, (128, 128), 0) % DS
    lane_ids = lax.broadcasted_iota(jnp.int32, (128, 128), 1)
    ones = jnp.ones((128, 128), BF16)

    def spread(i, _):
        r = pl.ds(pl.multiple_of(i * 8, 8), 8)
        p = proj[r, :]
        tall = jnp.broadcast_to(p[:, None, :], (8, DS, 128)).reshape(128, 128)
        o = pl.ds(pl.multiple_of(i * 128, 128), 128)
        for first, ref in ((DTR, bb_ref), (DTR + DS, cb_ref)):
            v = jnp.where(lane_ids == row_ids + first, tall, 0.0)
            hi = v.astype(BF16)
            v = v - hi.astype(F32)
            mid = v.astype(BF16)
            lo = (v - mid.astype(F32)).astype(BF16)
            ref[o, :] = (dot(hi, ones) + dot(mid, ones)) + dot(lo, ones)
        return 0

    lax.fori_loop(0, rows // 8, spread, 0)


def row_of(ref, index):
    return ref[pl.ds(index, 8, stride=0), :]


def tile_at(ref, t, h):
    return ref[pl.ds(pl.multiple_of(t * 16 + h * 8, 8), 8), :]


def light_forward(dt_ref, xt_ref, bb_ref, a2_ref, total_ref, end_ref, rows):
    for h in range(2):
        hs = pl.ds(h * 8, 8)
        a = [a2_ref[n, hs, :] for n in range(DS)]

        def step(t, carry):
            state, run = carry
            d = tile_at(dt_ref, t, h)
            dx = d * tile_at(xt_ref, t, h)
            new = tuple(
                jnp.exp2(a[n] * d) * state[n] + dx * row_of(bb_ref, t * DS + n) for n in range(DS)
            )
            return (new, run + d)

        zero = jnp.zeros((8, 128), F32)
        state, run = lax.fori_loop(0, rows, step, ((zero,) * DS, zero), unroll=4)
        for n in range(DS):
            end_ref[n, hs, :] = state[n]
            total_ref[n, hs, :] = jnp.exp2(a[n] * run)


def light_backward(dt_ref, gt_ref, cb_ref, a2_ref, adj_ref, rows):
    for h in range(2):
        hs = pl.ds(h * 8, 8)
        a = [a2_ref[n, hs, :] for n in range(DS)]

        def step(i, carry):
            t = rows - 1 - i
            d = tile_at(dt_ref, t, h)
            g = tile_at(gt_ref, t, h)
            return tuple(
                jnp.exp2(a[n] * d) * (carry[n] + g * row_of(cb_ref, t * DS + n)) for n in range(DS)
            )

        out = lax.fori_loop(0, rows, step, (jnp.zeros((8, 128), F32),) * DS, unroll=4)
        for n in range(DS):
            adj_ref[n, hs, :] = out[n]


def lightf_body(dt_ref, xt_ref, bb_ref, w0_ref, a2_ref, total_ref, end_ref):
    rows = dt_ref.shape[0] // 16
    for k in range(16):
        a2_ref[:, k, :] = -jnp.exp(w0_ref[ALOG0 : ALOG0 + DS, k * 128 : (k + 1) * 128]) * LOG2E
    light_forward(dt_ref, xt_ref, bb_ref, a2_ref, total_ref, end_ref, rows)


def gate_body(normed_ref, inz_ref, cot_ref, out_ref, dt_ref, cb_ref, a2_ref, gate_ref, gzp_ref, gt_ref, low_ref, adj_ref):
    rows, di = gate_ref.shape
    tiles = di // 128
    low_ref[...] = cot_ref[...].astype(BF16)
    width = 512

    def block(j, _):
        c = lanes(j, width)
        gate_ref[:, c] = dot(normed_ref[...], inz_ref[:, c])
        gzp_ref[:, c] = dot_nt(low_ref[...], out_ref[c, :])
        return 0

    lax.fori_loop(0, di // width, block, 0)

    def point(k, _):
        c = lanes(k)
        for q in range(4):
            r = slice(q * (rows // 4), (q + 1) * (rows // 4))
            z = gate_ref[r, c]
            gg = gzp_ref[r, c]
            s = sigmoid(z)
            gate = z * s
            gate_ref[r, c] = gate
            gzp_ref[r, c] = gg * s * (1.0 + z * (1.0 - s))
            gt_ref[pl.ds(q * (rows // 4) * tiles + k, rows // 4, stride=tiles), :] = gg * gate
        return 0

    lax.fori_loop(0, tiles, point, 0)
    light_backward(dt_ref, gt_ref, cb_ref, a2_ref, adj_ref, rows)


def forward_body(
    si_ref, dt_ref, xt_ref, bb_ref, cb_ref, a2_ref, w0_ref, gate_ref, gzp_ref, gt_ref, tok_ref, low_ref, normed_ref, out_ref,
    starts_ref, block_ref, gz_ref, ograd_ref, zgrad_ref, skipg_ref, yt, gated, low_t,
):
    chunks = starts_ref.shape[0]
    rows, di = gate_ref.shape
    tiles = di // 128
    size = rows // chunks
    for h in range(2):
        hs = pl.ds(h * 8, 8)
        a = [a2_ref[n, hs, :] for n in range(DS)]
        state = tuple(si_ref[n, hs, :] for n in range(DS))
        for chunk in range(chunks):
            for n in range(DS):
                starts_ref[chunk, n, hs, :] = state[n]

            def step(i, carry):
                t = chunk * size + i
                d = tile_at(dt_ref, t, h)
                dx = d * tile_at(xt_ref, t, h)
                new, parts = [], []
                for n in range(DS):
                    s = jnp.exp2(a[n] * d) * carry[n] + dx * row_of(bb_ref, t * DS + n)
                    parts.append(s * row_of(cb_ref, t * DS + n))
                    new.append(s)
                while len(parts) > 1:
                    parts = [parts[i] + parts[i + 1] for i in range(0, len(parts), 2)]
                yt[pl.ds(pl.multiple_of(t * 16 + h * 8, 8), 8), :] = parts[0]
                return tuple(new)

            state = lax.fori_loop(0, size, step, state, unroll=4)

    def point(k, _):
        c = lanes(k)
        total = jnp.zeros((8, 128), F32)
        for q in range(4):
            r = slice(q * (rows // 4), (q + 1) * (rows // 4))
            here = pl.ds(q * (rows // 4) * tiles + k, rows // 4, stride=tiles)
            x = xt_ref[here, :]
            y = yt[here, :] + w0_ref[6:7, c] * x
            gated[r, c] = (y * gate_ref[r, c]).astype(BF16)
            gz_ref[r, c] = (gzp_ref[r, c] * y).astype(BF16)
            total = total + jnp.sum((gt_ref[here, :] * x).reshape(-1, 8, 128), axis=0)
        skipg_ref[:, c] = jnp.sum(total, axis=0, keepdims=True)
        return 0

    lax.fori_loop(0, tiles, point, 0)

    def project(j, _):
        c = lanes(j, 256)
        block_ref[:, c] = tok_ref[:, c] + dot(gated[...], out_ref[:, c])
        return 0

    lax.fori_loop(0, tok_ref.shape[1] // 256, project, 0)

    def wide(j, _):
        c = lanes(j, 256)
        ograd_ref[c, :] = dot_tn(gated[:, c], low_ref[...]).astype(BF16)
        return 0

    lax.fori_loop(0, di // 256, wide, 0)

    def wide_z(j, _):
        c = lanes(j, 256)
        zgrad_ref[:, c] = dot_tn(normed_ref[...], gz_ref[:, c]).astype(BF16)
        return 0

    lax.fori_loop(0, di // 256, wide_z, 0)


def backward_body(
    so_ref, starts_ref, dt_ref, xt_ref, bb_ref, cb_ref, gt_ref, a2_ref,
    gdt_ref, gat_ref, gb_ref, gc_ref, ga_ref, keep, decays, pb, pc, rb, rc,
):
    chunks = starts_ref.shape[0]
    rows = dt_ref.shape[0] // 16
    size = rows // chunks
    zero = jnp.zeros((8, 128), F32)
    for h in range(2):
        hs = pl.ds(h * 8, 8)
        a = [a2_ref[n, hs, :] for n in range(DS)]
        for n in range(DS):
            ga_ref[n, hs, :] = zero
        later = tuple(so_ref[n, hs, :] for n in range(DS))
        for chunk in reversed(range(chunks)):
            base = chunk * size
            first = tuple(starts_ref[chunk, n, hs, :] for n in range(DS))
            for n in range(DS):
                keep[n * 8 : n * 8 + 8, :] = first[n]

            def again(i, carry):
                t = base + i
                d = tile_at(dt_ref, t, h)
                dx = d * tile_at(xt_ref, t, h)
                new = []
                for n in range(DS):
                    w = jnp.exp2(a[n] * d)
                    s = w * carry[n] + dx * row_of(bb_ref, t * DS + n)
                    o = pl.multiple_of(i * 128 + n * 8, 8)
                    decays[pl.ds(o, 8), :] = w
                    keep[pl.ds(pl.multiple_of(o + 128, 8), 8), :] = s
                    new.append(s)
                return tuple(new)

            lax.fori_loop(0, size, again, first, unroll=4)

            def back(j, carry):
                i = size - 1 - j
                t = base + i
                d = tile_at(dt_ref, t, h)
                x = tile_at(xt_ref, t, h)
                gy = tile_at(gt_ref, t, h)
                dx = d * x
                slot = (j % 2) * 128
                new = []
                weighted, through_a = [], []
                for n in range(DS):
                    o = pl.multiple_of(i * 128 + n * 8, 8)
                    w = decays[pl.ds(o, 8), :]
                    before = keep[pl.ds(o, 8), :]
                    now = keep[pl.ds(pl.multiple_of(o + 128, 8), 8), :]
                    g = carry[n] + gy * row_of(cb_ref, t * DS + n)
                    at = pl.ds(pl.multiple_of(slot + n * 8, 8), 8)
                    pc[at, :] = now * gy
                    pb[at, :] = g * dx
                    weighted.append(g * row_of(bb_ref, t * DS + n))
                    g = g * w
                    through = g * before
                    through_a.append(through * a[n])
                    ga_ref[n, hs, :] += through * d
                    new.append(g)
                while len(weighted) > 1:
                    weighted = [weighted[i] + weighted[i + 1] for i in range(0, len(weighted), 2)]
                    through_a = [through_a[i] + through_a[i + 1] for i in range(0, len(through_a), 2)]
                o = pl.ds(pl.multiple_of(t * 16 + h * 8, 8), 8)
                gdt_ref[o, :] = through_a[0] * LN2 + weighted[0] * x
                gat_ref[o, :] = weighted[0] * d
                for src, dst in ((pb, rb), (pc, rc)):
                    for m in range(2):
                        parts = [src[pl.ds(slot + m * 64 + s, 8, stride=8), :] for s in range(8)]
                        while len(parts) > 1:
                            parts = [parts[i] + parts[i + 1] for i in range(0, len(parts), 2)]
                        q = pl.ds(pl.multiple_of(t * 16 + m * 8, 8), 8)
                        if h == 0:
                            dst[q, :] = parts[0]
                        else:
                            dst[q, :] += parts[0]
                return tuple(new)

            later = lax.fori_loop(0, size, back, later, unroll=2)
    for n in range(DS):
        ga_ref[n] = ga_ref[n] * a2_ref[n] * LN2
    ones = jnp.ones((128, 128), BF16)
    pick = lax.broadcasted_iota(jnp.int32, (128, 128), 0) % DS == lax.broadcasted_iota(jnp.int32, (128, 128), 1)

    def collect(i, _):
        o = pl.ds(pl.multiple_of(i * 128, 128), 128)
        for src, dst in ((rb, gb_ref), (rc, gc_ref)):
            v = src[o, :]
            hi = v.astype(BF16)
            lo = (v - hi.astype(F32)).astype(BF16)
            s = jnp.where(pick, dot(hi, ones) + dot(lo, ones), 0.0)
            dst[pl.ds(pl.multiple_of(i * 8, 8), 8), :] = jnp.sum(s.reshape(8, DS, 128), axis=1)
        return 0

    lax.fori_loop(0, rows // 8, collect, 0)


def tail_body(
    gdt_ref, gat_ref, gb_ref, gc_ref, gt_ref, draw_ref, filt_ref, xin_ref, halo_ref, xs_ref, w0_ref, selt_ref,
    gf_ref, w0g_ref, selg_ref, proj, xp, raw_low, gproj, dw,
):
    rows, di = draw_ref.shape
    tiles = di // 128
    proj[:, 0:96] = dot_nt(xs_ref[...], selt_ref[...])
    low = proj[:, 0:DTR].astype(BF16)
    dw[...] = w0_ref[DELTA0 : DELTA0 + DTR, :].astype(BF16)

    def raw(k, _):
        c = lanes(k)
        g = gdt_ref[pl.ds(k, rows, stride=tiles), :] * sigmoid(draw_ref[:, c])
        w0g_ref[5:6, c] = jnp.sum(g, axis=0, keepdims=True)
        gl = g.astype(BF16)
        raw_low[:, c] = gl
        w0g_ref[DELTA0 : DELTA0 + DTR, c] = dot_tn(low, gl)
        return 0

    lax.fori_loop(0, tiles, raw, 0)
    gproj[:, 0:DTR] = dot_nt(raw_low[...], dw[...]).astype(BF16)
    gproj[:, DTR : DTR + DS] = gb_ref[:, 0:DS].astype(BF16)
    gproj[:, DTR + DS : DTR + 2 * DS] = gc_ref[:, 0:DS].astype(BF16)

    def point(k, _):
        c = lanes(k)
        gp = gproj[...]
        selg_ref[:, c] = dot_tn(gp, xs_ref[:, c])
        back = dot(gp, selt_ref[:, c])
        here = pl.ds(k, rows, stride=tiles)
        ga = gt_ref[here, :] * w0_ref[6:7, c] + gat_ref[here, :] + back
        f = filt_ref[:, c]
        s = sigmoid(f)
        gf = ga * (s * (1.0 + f * (1.0 - s)))
        gf_ref[:, c] = gf
        w0g_ref[4:5, c] = jnp.sum(gf, axis=0, keepdims=True)
        xp[0:16, :] = halo_ref[:, c].astype(F32)
        xp[16 : 16 + rows, :] = xin_ref[:, c].astype(F32)
        for tap in range(KW):
            lo = 16 - (KW - 1) + tap
            w0g_ref[tap : tap + 1, c] = jnp.sum(gf * xp[lo : lo + rows, :], axis=0, keepdims=True)
        return 0

    lax.fori_loop(0, tiles, point, 0)


def last_body(gf_ref, edge_ref, w0_ref, gz_ref, normed_ref, tok_ref, cot_ref, gain_ref, inx_ref, inz_ref, tgrad_ref, xgrad_ref, gaing_ref, gp, gx, gn):
    rows, di = gf_ref.shape
    tiles = di // 128

    def conv(k, _):
        c = lanes(k)
        gp[0:rows, :] = gf_ref[:, c]
        gp[rows : rows + 8, :] = edge_ref[:, c]
        total = jnp.zeros((rows, 128), F32)
        for tap in range(KW):
            lo = KW - 1 - tap
            total = total + w0_ref[tap : tap + 1, c] * gp[lo : lo + rows, :]
        gx[:, c] = total.astype(BF16)
        return 0

    lax.fori_loop(0, tiles, conv, 0)

    def wide(j, _):
        c = lanes(j, 256)
        xgrad_ref[:, c] = dot_tn(normed_ref[...], gx[:, c]).astype(BF16)
        return 0

    lax.fori_loop(0, di // 256, wide, 0)

    def back(j, _):
        c = lanes(j, 256)
        gn[:, c] = dot_nt(gx[...], inx_ref[c, :]) + dot_nt(gz_ref[...], inz_ref[c, :])
        return 0

    lax.fori_loop(0, inx_ref.shape[0] // 256, back, 0)

    def rows_of(i, total):
        r = pl.ds(pl.multiple_of(i * 8, 8), 8)
        u = tok_ref[r, :]
        g = gn[r, :]
        scale = lax.rsqrt(jnp.mean(u * u, axis=-1, keepdims=True) + EPS)
        v = g * gain_ref[...]
        mean = jnp.mean(v * u, axis=-1, keepdims=True)
        tgrad_ref[r, :] = cot_ref[r, :] + scale * v - u * (scale * scale * scale * mean)
        return total + g * u * scale

    total = lax.fori_loop(0, rows // 8, rows_of, jnp.zeros((8, tok_ref.shape[1]), F32))
    gaing_ref[...] = jnp.sum(total, axis=0, keepdims=True)


def unpack_body(pack_ref, w0_ref, selt_ref, gain_ref):
    devices = pack_ref.shape[0]
    low_half = lax.broadcasted_iota(jnp.int32, (PACK0, 128), 1) < 64
    for j in range(devices // 2):
        a = pack_ref[2 * j, 0:PACK0, :].astype(F32)
        b = pack_ref[2 * j + 1, 0:PACK0, :].astype(F32)
        c = slice(j * 128, (j + 1) * 128)
        w0_ref[:, c] = jnp.where(low_half, a, pltpu.roll(b, 64, 1))
        selt_ref[:, c] = jnp.where(low_half, pltpu.roll(a, 64, 1), b).astype(BF16)
    for j in range(devices // 4):
        v = sum(pack_ref[4 * j + i, PACK0 : PACK0 + 16, :].astype(F32) for i in range(4))
        gain_ref[:, j * 128 : (j + 1) * 128] = v[0:1, :]


def pack_body(w0g_ref, selg_ref, gaing_ref, skipg_ref, ga_ref, pack_ref):
    devices = pack_ref.shape[0]
    low_half = lax.broadcasted_iota(jnp.int32, (PACK0, 128), 1) < 64
    w0g_ref[6:7, :] = skipg_ref[...]
    w0g_ref[7:8, :] = jnp.zeros_like(skipg_ref)
    w0g_ref[DELTA0 + DTR : PACK0, :] = jnp.zeros((PACK0 - DELTA0 - DTR, w0g_ref.shape[1]), F32)
    for k in range(16):
        w0g_ref[ALOG0 : ALOG0 + DS, k * 128 : (k + 1) * 128] = ga_ref[:, k, :]
    for j in range(devices // 2):
        c = slice(j * 128, (j + 1) * 128)
        a, b = w0g_ref[:, c], selg_ref[:, c]
        pack_ref[2 * j, 0:PACK0, :] = jnp.where(low_half, a, pltpu.roll(b, 64, 1)).astype(BF16)
        pack_ref[2 * j + 1, 0:PACK0, :] = jnp.where(low_half, pltpu.roll(a, 64, 1), b).astype(BF16)
    for j in range(devices):
        v = gaing_ref[:, (j // 4) * 128 : (j // 4 + 1) * 128]
        pack_ref[j, PACK0 : PACK, :] = jnp.broadcast_to(v, (PACK - PACK0, 128)).astype(BF16)


def place():
    b, s = lax.axis_index("batch"), lax.axis_index("seq")
    return b // 2, b % 2, s // 2, s % 2


def device(y, c, z, x):
    return (y * 2 + c, z * 2 + x)


def greet(peers):
    barrier = pltpu.get_barrier_semaphore()
    for peer in peers:
        pl.semaphore_signal(barrier, inc=1, device_id=peer, device_id_type=MESH)
    pl.semaphore_wait(barrier, len(peers))


def remote(src, dst, send, recv, to):
    return pltpu.make_async_remote_copy(
        src_ref=src, dst_ref=dst, send_sem=send, recv_sem=recv, device_id=to, device_id_type=MESH
    )


def neighbours(y, c, z, x):
    return [device(y, c, z ^ k, x) for k in (1, 2, 3)] + [
        device(1 - y, c, z, x), device(y, c, z, 1 - x), device(y, 1 - c, z, x)
    ]


class Gather:
    COPIES = 14

    def __init__(self, src, out, send, recv, local):
        self.src, self.out, self.send, self.recv, self.local = src, out, send, recv, local
        self.at = place()
        self.count = 0
        self.copies = []

    def go(self, view, to):
        i = self.count
        self.count += 1
        source, target = view if isinstance(view, tuple) else (view, view)
        copy = remote(source, target, self.send.at[i], self.recv.at[i], to)
        copy.start()
        self.copies.append(copy)
        return copy

    def stage(self, k):
        y, c, z, x = self.at
        out = self.out
        half = out.shape[4] // 2
        top, bottom = pl.ds(0, half), pl.ds(half, half)
        to_y, to_x, to_c = device(1 - y, c, z, x), device(y, c, z, 1 - x), device(y, 1 - c, z, x)
        if k == 0:
            own = pltpu.make_async_copy(self.src, out.at[y, c, z, x], self.local)
            own.start()
            self.first = [self.go((self.src, out.at[y, c, z, x]), device(y, c, z ^ i, x)) for i in (1, 2, 3)]
            own.wait()
        elif k == 1:
            for copy in self.first:
                copy.wait_recv()
            self.a = self.go(out.at[y, c, :, x, top], to_y)
            self.b = self.go(out.at[y, c, :, x, bottom], to_x)
            self.go(out.at[y, c, :, x], to_c)
        elif k == 2:
            self.a.wait_recv()
            self.b.wait_recv()
            self.next = [self.go(out.at[i, c, :, x, top], to_x) for i in (0, 1)]
            self.next.append(self.go(out.at[y, c, :, :, bottom], to_y))
            self.go(out.at[1 - y, c, :, x, top], to_c)
            self.go(out.at[y, c, :, 1 - x, bottom], to_c)
        elif k == 3:
            for copy in self.next:
                copy.wait_recv()
            for i in (0, 1):
                self.go(out.at[i, c, :, 1 - x, top], to_c)
            self.go(out.at[1 - y, c, :, :, bottom], to_c)
        else:
            done = self.first + [self.a, self.b] + self.next
            for copy in self.copies:
                copy.wait_send()
                if not any(copy is other for other in done):
                    copy.wait_recv()


STAGES = 5


def gather_body(n, *refs):
    srcs, outs, (send, recv, local) = refs[:n], refs[n : 2 * n], refs[2 * n :]
    greet(neighbours(*place()))
    jobs = [Gather(srcs[i], outs[i], send.at[i], recv.at[i], local.at[i]) for i in range(n)]
    for step in range(n + STAGES - 1):
        for i in range(n):
            if 0 <= step - i < STAGES:
                jobs[i].stage(step - i)


def gather(shards):
    n = len(shards)
    outs = tuple(sds((2, 2, 4, 2) + s.shape, s.dtype) for s in shards)
    return pl.pallas_call(
        functools.partial(gather_body, n),
        out_shape=outs,
        in_specs=[ANY] * n,
        out_specs=(ANY,) * n,
        scratch_shapes=[
            pltpu.SemaphoreType.DMA((n, Gather.COPIES)),
            pltpu.SemaphoreType.DMA((n, Gather.COPIES)),
            pltpu.SemaphoreType.DMA((n,)),
        ],
        compiler_params=pltpu.CompilerParams(collective_id=0, has_side_effects=True),
    )(*shards)


class Scatter:
    COPIES = 10

    def __init__(self, g, out, own, r1, r2, r3, r4, send, recv, local):
        self.g, self.out, self.own, self.r1, self.r2, self.r3, self.r4 = g, out, own, r1, r2, r3, r4
        self.send, self.recv, self.local = send, recv, local
        self.at = place()
        self.count = 0
        self.copies = []

    def go(self, source, target, to):
        i = self.count
        self.count += 1
        copy = remote(source, target, self.send.at[i], self.recv.at[i], to)
        copy.start()
        self.copies.append(copy)
        return copy

    def add(self, index, more, other):
        self.own[index] = (self.own[index].astype(F32) + more[other].astype(F32)).astype(BF16)

    def stage(self, k):
        y, c, z, x = self.at
        g, own = self.g, self.own
        half = own.shape[3] // 2
        top, bottom = pl.ds(0, half), pl.ds(half, half)
        to_y, to_x, to_c = device(1 - y, c, z, x), device(y, c, z, 1 - x), device(y, 1 - c, z, x)
        if k == 0:
            self.wait = [self.go(g.at[i, 1 - c], self.r1.at[i], to_c) for i in (0, 1)]
            self.held = [pltpu.make_async_copy(g.at[i, c], own.at[i], self.local.at[i]) for i in (0, 1)]
            for copy in self.held:
                copy.start()
        elif k == 1:
            for copy in self.held:
                copy.wait()
            for copy in self.wait:
                copy.wait_recv()

            def piece(i, _):
                at = (i // 8, i // 2 % 4, i % 2)
                self.add(at, self.r1, at)
                return 0

            lax.fori_loop(0, 16, piece, 0)
            self.wait = [self.go(own.at[1 - y, :, :, top], self.r2.at[pl.ds(0, 4), :], to_y)]
            for i in (0, 1):
                self.wait.append(self.go(own.at[i, :, 1 - x, bottom], self.r2.at[pl.ds(4, 4), i], to_x))
        elif k == 2:
            for copy in self.wait:
                copy.wait_recv()

            def piece(i, _):
                b, d = i // 2, i % 2
                self.add((y, b, d, top), self.r2, (b, d))
                self.add((d, b, x, bottom), self.r2, (4 + b, d))
                return 0

            lax.fori_loop(0, 8, piece, 0)
            self.wait = [
                self.go(own.at[y, :, 1 - x, top], self.r3.at[0], to_x),
                self.go(own.at[1 - y, :, x, bottom], self.r3.at[1], to_y),
            ]
        elif k == 3:
            for copy in self.wait:
                copy.wait_recv()

            def piece(b, _):
                self.add((y, b, x, top), self.r3, (0, b))
                self.add((y, b, x, bottom), self.r3, (1, b))
                return 0

            lax.fori_loop(0, 4, piece, 0)
            self.wait = [
                self.go(own.at[y, z ^ i, x], self.r4.at[i - 1], device(y, c, z ^ i, x)) for i in (1, 2, 3)
            ]
        else:
            for copy in self.wait:
                copy.wait_recv()
            total = own[y, z, x].astype(F32)
            for i in range(3):
                total = total + self.r4[i].astype(F32)
            self.out[...] = total
            for copy in self.copies:
                copy.wait_send()


def scatter_body(n, *refs):
    gs, outs, rest = refs[:n], refs[n : 2 * n], refs[2 * n :]
    send, recv, local = rest[5 * n :]
    greet(neighbours(*place()))
    jobs = [
        Scatter(gs[i], outs[i], *rest[5 * i : 5 * i + 5], send.at[i], recv.at[i], local.at[i]) for i in range(n)
    ]
    for step in range(n + STAGES - 1):
        for i in range(n):
            if 0 <= step - i < STAGES:
                jobs[i].stage(step - i)


def scatter(grads):
    n = len(grads)
    outs = tuple(sds(g.shape[4:], F32) for g in grads)
    scratch = []
    for g in grads:
        rows, cols = g.shape[4:]
        scratch += [
            pltpu.VMEM((2, 4, 2, rows, cols), BF16),
            pltpu.VMEM((2, 4, 2, rows, cols), BF16),
            pltpu.VMEM((8, 2, rows // 2, cols), BF16),
            pltpu.VMEM((2, 4, rows // 2, cols), BF16),
            pltpu.VMEM((3, rows, cols), BF16),
        ]
    return pl.pallas_call(
        functools.partial(scatter_body, n),
        out_shape=outs,
        in_specs=[ANY] * n,
        out_specs=(VM,) * n,
        scratch_shapes=scratch
        + [pltpu.SemaphoreType.DMA((n, Scatter.COPIES))] * 2
        + [pltpu.SemaphoreType.DMA((n, 2))],
        compiler_params=pltpu.CompilerParams(
            collective_id=1, has_side_effects=True, vmem_limit_bytes=GRANT
        ),
    )(*grads)


def exchange_body(total_ref, end_ref, adj_ref, si_ref, so_ref, mine, got, back, final, send, recv):
    peers = mine.shape[0]
    pair = DS // peers
    b, s = lax.axis_index("batch"), lax.axis_index("seq")
    others = [(b, lax.rem(s + k, peers)) for k in range(1, peers)]
    greet(others)
    for j in range(peers):
        for i in range(pair):
            for m, ref in enumerate((total_ref, end_ref, adj_ref)):
                mine[j, m, i] = ref[j * pair + i].astype(BF16)
    first = []
    for k in range(1, peers):
        to = lax.rem(s + k, peers)
        copy = remote(mine.at[to], got.at[s], send.at[0, k], recv.at[0, k], (b, to))
        copy.start()
        first.append(copy)
    got[s] = mine[s]
    for copy in first:
        copy.wait_recv()
    shape = (pair,) + total_ref.shape[1:]
    state = jnp.zeros(shape, F32)
    for p in range(peers):
        back[p, 0] = state.astype(BF16)
        state = got[p, 0].astype(F32) * state + got[p, 1].astype(F32)
    state = jnp.zeros(shape, F32)
    for p in reversed(range(peers)):
        back[p, 1] = state.astype(BF16)
        state = got[p, 0].astype(F32) * state + got[p, 2].astype(F32)
    second = []
    for k in range(1, peers):
        to = lax.rem(s + k, peers)
        copy = remote(back.at[to], final.at[s], send.at[1, k], recv.at[1, k], (b, to))
        copy.start()
        second.append(copy)
    final[s] = back[s]
    for copy in second:
        copy.wait_recv()
    for j in range(peers):
        for i in range(pair):
            si_ref[j * pair + i] = final[j, 0, i].astype(F32)
            so_ref[j * pair + i] = final[j, 1, i].astype(F32)
    for copy in first + second:
        copy.wait_send()


def exchange(total, end, adj, peers):
    shape = total.shape
    pair = DS // peers
    return kernel_call(
        exchange_body,
        (sds(shape, F32), sds(shape, F32)),
        3,
        [
            pltpu.VMEM((peers, 3, pair) + shape[1:], BF16),
            pltpu.VMEM((peers, 3, pair) + shape[1:], BF16),
            pltpu.VMEM((peers, 2, pair) + shape[1:], BF16),
            pltpu.VMEM((peers, 2, pair) + shape[1:], BF16),
            pltpu.SemaphoreType.DMA((2, peers)),
            pltpu.SemaphoreType.DMA((2, peers)),
        ],
        collective_id=2,
        has_side_effects=True,
    )(total, end, adj)


def shift(value, by):
    peers = lax.axis_size("seq")
    pairs = [(i, i + by) for i in range(peers) if 0 <= i + by < peers]
    return lax.ppermute(value, "seq", pairs)


def carried_in(total, value, reverse):
    peers, index = lax.axis_size("seq"), lax.axis_index("seq")
    totals = lax.all_gather(total.astype(BF16), "seq")
    values = lax.all_gather(value.astype(BF16), "seq")

    def turn(k, before):
        at = peers - 1 - k if reverse else k
        reached = at > index if reverse else at < index
        new = totals[at].astype(F32) * before + values[at].astype(F32)
        return jnp.where(reached, new, before)

    return lax.fori_loop(0, peers, turn, jnp.zeros(value.shape, F32))


def on_device(tokens, cotangent, norm_gain, in_weight, conv_weight, conv_bias, select_weight, delta_weight, delta_bias, a_log, skip_gain, out_weight):
    axes = ("batch", "seq")
    sizes = (lax.axis_size("batch"), lax.axis_size("seq"))
    devices = sizes[0] * sizes[1]
    staged = sizes == (4, 8)
    me = lax.axis_index("batch") * sizes[1] + lax.axis_index("seq")
    tok, cot = tokens[0], cotangent[0]
    rows, width = tok.shape
    di = out_weight.shape[0] * devices
    tiles = di // 128
    own = conv_bias.shape[0]

    if staged:
        left = jnp.concatenate(
            [
                conv_weight, conv_bias[None], delta_bias[None], skip_gain[None], jnp.zeros((1, own), BF16),
                a_log, delta_weight, jnp.zeros((PACK0 - DELTA0 - DTR, own), BF16),
            ],
            axis=0,
        )
        gain_row = lax.dynamic_update_slice(jnp.zeros((128,), BF16), norm_gain, ((me % 4) * norm_gain.shape[0],))
        pack = jnp.concatenate(
            [
                jnp.concatenate([left, select_weight.T], axis=1),
                jnp.broadcast_to(gain_row[None], (PACK - PACK0, 128)),
            ],
            axis=0,
        )
        in_x, in_z, out_full, packs = gather((in_weight[:, :di], in_weight[:, di:], out_weight, pack))
        in_x, in_z = in_x.reshape(width, di), in_z.reshape(width, di)
        out_full = out_full.reshape(di, width)
        w0, sel_t, gain = kernel_call(
            unpack_body, (sds((PACK0, di), F32), sds((PACK0, di), BF16), sds((1, width), F32)), 1
        )(packs.reshape((devices,) + pack.shape))
    else:
        full = lambda v, axis: lax.all_gather(v, axes, axis=axis, tiled=True)
        in_full = full(in_weight, 0)
        in_x, in_z = in_full[:, :di], in_full[:, di:]
        out_full = full(out_weight, 0)
        sel_t = full(select_weight, 0).T
        gain = full(norm_gain, 0)[None].astype(F32)
        w0 = jnp.concatenate(
            [
                full(conv_weight, 1), full(conv_bias, 0)[None], full(delta_bias, 0)[None], full(skip_gain, 0)[None],
                jnp.zeros((1, di), BF16), full(a_log, 1), full(delta_weight, 1),
                jnp.zeros((PACK0 - DELTA0 - DTR, di), BF16),
            ],
            axis=0,
        ).astype(F32)

    flat = sds((rows * tiles, 128), F32)
    wide = sds((rows, di), F32)
    spread = sds((rows * DS, 128), F32)
    carry = sds((DS, tiles, 128), F32)

    normed, x_in = kernel_call(
        inproj_body, (sds((rows, width), BF16), sds((rows, di), BF16)), 3
    )(tok, gain, in_x)
    halo = shift(x_in[rows - 16 :], 1)
    filt, xs, xt, draw, dt, bb, cb = kernel_call(
        conv_body,
        (wide, sds((rows, di), BF16), flat, wide, flat, spread, spread),
        4,
        [pltpu.VMEM((rows, 128), F32), pltpu.VMEM((rows + 16, 128), F32)],
    )(x_in, halo, w0, sel_t)
    a2, total, end = kernel_call(lightf_body, (carry, carry, carry), 4)(dt, xt, bb, w0)
    gate, gzp, gt, low, adj = kernel_call(
        gate_body, (wide, wide, flat, sds((rows, width), BF16), carry), 7
    )(normed, in_z, cot, out_full, dt, cb, a2)
    if staged:
        state_in, state_out = exchange(total, end, adj, sizes[1])
    else:
        state_in = carried_in(total, end, False)
        state_out = carried_in(total, adj, True)
    chunks = rows // 64
    starts, block_out, gz, out_grad, z_grad, skip_grad = kernel_call(
        forward_body,
        (
            sds((chunks, DS, tiles, 128), F32), sds((rows, width), F32), sds((rows, di), BF16),
            sds((di, width), BF16), sds((width, di), BF16), sds((1, di), F32),
        ),
        14,
        [pltpu.VMEM((rows * tiles, 128), F32), pltpu.VMEM((rows, di), BF16), pltpu.VMEM((8, 128), F32)],
    )(state_in, dt, xt, bb, cb, a2, w0, gate, gzp, gt, tok, low, normed, out_full)
    tall = pltpu.VMEM((rows * DS, 128), F32)
    gdt, gat, gb, gc, ga = kernel_call(
        backward_body,
        (flat, flat, sds((rows, 128), F32), sds((rows, 128), F32), carry),
        8,
        [
            pltpu.VMEM((65 * 128, 128), F32), pltpu.VMEM((64 * 128, 128), F32), pltpu.VMEM((256, 128), F32),
            pltpu.VMEM((256, 128), F32), tall, tall,
        ],
    )(state_out, starts, dt, xt, bb, cb, gt, a2)
    gf, w0g, selg = kernel_call(
        tail_body,
        (wide, sds((PACK0, di), F32), sds((PACK0, di), F32)),
        12,
        [
            pltpu.VMEM((rows, 128), F32), pltpu.VMEM((rows + 16, 128), F32), pltpu.VMEM((rows, di), BF16),
            pltpu.VMEM((rows, PACK0), BF16), pltpu.VMEM((DTR, di), BF16),
        ],
    )(gdt, gat, gb, gc, gt, draw, filt, x_in, halo, xs, w0, sel_t)
    edge = shift(gf[:8], -1)
    tokens_grad, x_grad, gain_grad = kernel_call(
        last_body,
        (sds((rows, width), F32), sds((width, di), BF16), sds((1, width), F32)),
        10,
        [pltpu.VMEM((rows + 8, 128), F32), pltpu.VMEM((rows, di), BF16), pltpu.VMEM((rows, width), F32)],
    )(gf, edge, w0, gz, normed, tok, cot, gain, in_x, in_z)

    if staged:
        packed = kernel_call(pack_body, sds((devices, PACK, 128), BF16), 5)(
            w0g, selg, gain_grad, skip_grad, ga
        )
        lead = (2, 2, 4, 2)
        g_out, g_z, g_x, g_pack = scatter(
            (
                out_grad.reshape(lead + out_weight.shape),
                z_grad.reshape(lead + (width // devices, di)),
                x_grad.reshape(lead + (width // devices, di)),
                packed.reshape(lead + packed.shape[1:]),
            )
        )
        left, right = g_pack[:PACK0, :own], g_pack[:PACK0, own:]
        g_gain = lax.dynamic_slice(g_pack[PACK0], ((me % 4) * norm_gain.shape[0],), norm_gain.shape)
        grads = (
            g_gain, jnp.concatenate([g_x, g_z], axis=1), left[0:KW], left[4], right.T,
            left[DELTA0 : DELTA0 + DTR], left[5], left[ALOG0 : ALOG0 + DS], left[6], g_out,
        )
    else:
        share = lambda v, d: lax.psum_scatter(v.astype(F32), axes, scatter_dimension=d, tiled=True)
        ga_flat = ga.reshape(DS, di)
        grads = (
            share(gain_grad[0], 0), share(jnp.concatenate([x_grad, z_grad], axis=1), 0), share(w0g[0:KW], 1),
            share(w0g[4], 0), share(selg.T, 0), share(w0g[DELTA0 : DELTA0 + DTR], 1), share(w0g[5], 0),
            share(ga_flat, 1), share(skip_grad[0], 0), share(out_grad, 0),
        )
    return (block_out[None], tokens_grad[None]) + grads


def solution(mesh):
    both = ("batch", "seq")
    first, second = P(both), P(None, both)
    matrix = P(both, None)
    whole = P("batch", "seq", None)
    weights = (first, matrix, second, first, matrix, second, first, second, first, matrix)
    return jax.shard_map(
        on_device,
        mesh=mesh,
        in_specs=(whole, whole) + weights,
        out_specs=(whole, whole) + weights,
        check_vma=False,
    )
```

```python
import functools

import jax
import jax.numpy as jnp
from jax import lax
from jax.experimental import pallas as pl
from jax.experimental.pallas import tpu as pltpu
from jax.sharding import PartitionSpec as P

DS = 16
KW = 4
DTR = 64
EPS = 1e-05
LOG2E = 1.4426950408889634
LN2 = 0.6931471805599453
F32 = jnp.float32
BF16 = jnp.bfloat16
MESH = pl.DeviceIdType.MESH
VM = pl.BlockSpec(memory_space=pltpu.VMEM)
ANY = pl.BlockSpec(memory_space=pl.ANY)
GRANT = 60 << 20
ALOG0, DELTA0, PACK0, PACK = 8, 24, 96, 128


def sds(shape, dtype):
    return jax.ShapeDtypeStruct(shape, dtype)


def kernel_call(body, outs, n_in, scratch=(), flops=1e9, **params):
    return pl.pallas_call(
        body,
        out_shape=outs,
        in_specs=[VM] * n_in,
        out_specs=jax.tree.map(lambda _: VM, outs),
        scratch_shapes=list(scratch),
        cost_estimate=pl.CostEstimate(flops=int(flops), bytes_accessed=8 << 20, transcendentals=0),
        compiler_params=pltpu.CompilerParams(vmem_limit_bytes=GRANT, **params),
    )


def sigmoid(v):
    return 1.0 / (1.0 + jnp.exp(-v))


def dot(a, b):
    return jnp.dot(a, b, preferred_element_type=F32)


def dot_nt(a, b):
    return lax.dot_general(a, b, (((1,), (1,)), ((), ())), preferred_element_type=F32)


def dot_tn(a, b):
    return lax.dot_general(a, b, (((0,), (0,)), ((), ())), preferred_element_type=F32)


def lanes(k, width=128):
    return pl.ds(pl.multiple_of(k * width, width), width)


def inproj_body(tok_ref, gain_ref, inx_ref, normed_ref, xin_ref):
    rows = tok_ref.shape[0]

    def norm(i, _):
        r = pl.ds(pl.multiple_of(i * 16, 16), 16)
        u = tok_ref[r, :]
        scale = lax.rsqrt(jnp.mean(u * u, axis=-1, keepdims=True) + EPS)
        normed_ref[r, :] = (u * scale * gain_ref[...]).astype(BF16)
        return 0

    lax.fori_loop(0, rows // 16, norm, 0)
    width = 512

    def mm(j, _):
        c = lanes(j, width)
        xin_ref[:, c] = dot(normed_ref[...], inx_ref[:, c]).astype(BF16)
        return 0

    lax.fori_loop(0, inx_ref.shape[1] // width, mm, 0)


def conv_body(xin_ref, halo_ref, w0_ref, selt_ref, filt_ref, xs_ref, xt_ref, draw_ref, dt_ref, bb_ref, cb_ref, proj, xp):
    rows, di = xin_ref.shape
    tiles = di // 128
    xp_rows = 16 + rows

    def conv(k, _):
        c = lanes(k)
        xp[0:16, :] = halo_ref[:, c].astype(F32)
        xp[16:xp_rows, :] = xin_ref[:, c].astype(F32)
        for q in range(2):
            r0 = q * (rows // 2)
            f = w0_ref[4:5, c]
            for tap in range(KW):
                lo = 16 - (KW - 1) + tap + r0
                f = f + w0_ref[tap : tap + 1, c] * xp[lo : lo + rows // 2, :]
            s = (f * sigmoid(f)).astype(BF16)
            filt_ref[r0 : r0 + rows // 2, c] = f
            xs_ref[r0 : r0 + rows // 2, c] = s
            xt_ref[pl.ds(r0 * tiles + k, rows // 2, stride=tiles), :] = s.astype(F32)
        return 0

    lax.fori_loop(0, tiles, conv, 0)
    proj[:, 0:96] = dot_nt(xs_ref[...], selt_ref[...])
    low = proj[:, 0:DTR].astype(BF16)

    def delta(k, _):
        c = lanes(k)
        raw = dot(low, w0_ref[DELTA0 : DELTA0 + DTR, c].astype(BF16)) + w0_ref[5:6, c]
        draw_ref[:, c] = raw
        dt_ref[pl.ds(k, rows, stride=tiles), :] = jnp.maximum(raw, 0.0) + jnp.log1p(jnp.exp(-jnp.abs(raw)))
        return 0

    lax.fori_loop(0, tiles, delta, 0)
    row_ids = lax.broadcasted_iota(jnp.int32, (128, 128), 0) % DS
    lane_ids = lax.broadcasted_iota(jnp.int32, (128, 128), 1)
    ones = jnp.ones((128, 128), BF16)

    def spread(i, _):
        r = pl.ds(pl.multiple_of(i * 8, 8), 8)
        p = proj[r, :]
        tall = jnp.broadcast_to(p[:, None, :], (8, DS, 128)).reshape(128, 128)
        o = pl.ds(pl.multiple_of(i * 128, 128), 128)
        for first, ref in ((DTR, bb_ref), (DTR + DS, cb_ref)):
            v = jnp.where(lane_ids == row_ids + first, tall, 0.0)
            hi = v.astype(BF16)
            v = v - hi.astype(F32)
            mid = v.astype(BF16)
            lo = (v - mid.astype(F32)).astype(BF16)
            ref[o, :] = (dot(hi, ones) + dot(mid, ones)) + dot(lo, ones)
        return 0

    lax.fori_loop(0, rows // 8, spread, 0)


def row_of(ref, index):
    return ref[pl.ds(index, 8, stride=0), :]


def tile_at(ref, t, h):
    return ref[pl.ds(pl.multiple_of(t * 16 + h * 8, 8), 8), :]


def light_forward(dt_ref, xt_ref, bb_ref, a2_ref, total_ref, end_ref, rows):
    for h in range(2):
        hs = pl.ds(h * 8, 8)
        a = [a2_ref[n, hs, :] for n in range(DS)]

        def step(t, carry):
            state, run = carry
            d = tile_at(dt_ref, t, h)
            dx = d * tile_at(xt_ref, t, h)
            new = tuple(
                jnp.exp2(a[n] * d) * state[n] + dx * row_of(bb_ref, t * DS + n) for n in range(DS)
            )
            return (new, run + d)

        zero = jnp.zeros((8, 128), F32)
        state, run = lax.fori_loop(0, rows, step, ((zero,) * DS, zero), unroll=4)
        for n in range(DS):
            end_ref[n, hs, :] = state[n]
            total_ref[n, hs, :] = jnp.exp2(a[n] * run)


def light_backward(dt_ref, gt_ref, cb_ref, a2_ref, adj_ref, rows):
    for h in range(2):
        hs = pl.ds(h * 8, 8)
        a = [a2_ref[n, hs, :] for n in range(DS)]

        def step(i, carry):
            t = rows - 1 - i
            d = tile_at(dt_ref, t, h)
            g = tile_at(gt_ref, t, h)
            return tuple(
                jnp.exp2(a[n] * d) * (carry[n] + g * row_of(cb_ref, t * DS + n)) for n in range(DS)
            )

        out = lax.fori_loop(0, rows, step, (jnp.zeros((8, 128), F32),) * DS, unroll=4)
        for n in range(DS):
            adj_ref[n, hs, :] = out[n]


def lightf_body(dt_ref, xt_ref, bb_ref, w0_ref, a2_ref, total_ref, end_ref):
    rows = dt_ref.shape[0] // 16
    for k in range(16):
        a2_ref[:, k, :] = -jnp.exp(w0_ref[ALOG0 : ALOG0 + DS, k * 128 : (k + 1) * 128]) * LOG2E
    light_forward(dt_ref, xt_ref, bb_ref, a2_ref, total_ref, end_ref, rows)


def gate_body(normed_ref, inz_ref, cot_ref, out_ref, dt_ref, cb_ref, a2_ref, gate_ref, gzp_ref, gt_ref, low_ref, adj_ref):
    rows, di = gate_ref.shape
    tiles = di // 128
    low_ref[...] = cot_ref[...].astype(BF16)
    width = 512

    def block(j, _):
        c = lanes(j, width)
        gate_ref[:, c] = dot(normed_ref[...], inz_ref[:, c])
        gzp_ref[:, c] = dot_nt(low_ref[...], out_ref[c, :])
        return 0

    lax.fori_loop(0, di // width, block, 0)

    def point(k, _):
        c = lanes(k)
        for q in range(4):
            r = slice(q * (rows // 4), (q + 1) * (rows // 4))
            z = gate_ref[r, c]
            gg = gzp_ref[r, c]
            s = sigmoid(z)
            gate = z * s
            gate_ref[r, c] = gate
            gzp_ref[r, c] = gg * s * (1.0 + z * (1.0 - s))
            gt_ref[pl.ds(q * (rows // 4) * tiles + k, rows // 4, stride=tiles), :] = gg * gate
        return 0

    lax.fori_loop(0, tiles, point, 0)
    light_backward(dt_ref, gt_ref, cb_ref, a2_ref, adj_ref, rows)


def forward_body(
    si_ref, dt_ref, xt_ref, bb_ref, cb_ref, a2_ref, w0_ref, gate_ref, gzp_ref, gt_ref, tok_ref, low_ref, normed_ref, out_ref,
    starts_ref, block_ref, gz_ref, ograd_ref, zgrad_ref, skipg_ref, yt, gated, low_t,
):
    chunks = starts_ref.shape[0]
    rows, di = gate_ref.shape
    tiles = di // 128
    size = rows // chunks
    for h in range(2):
        hs = pl.ds(h * 8, 8)
        a = [a2_ref[n, hs, :] for n in range(DS)]
        state = tuple(si_ref[n, hs, :] for n in range(DS))
        for chunk in range(chunks):
            for n in range(DS):
                starts_ref[chunk, n, hs, :] = state[n]

            def step(i, carry):
                t = chunk * size + i
                d = tile_at(dt_ref, t, h)
                dx = d * tile_at(xt_ref, t, h)
                new, parts = [], []
                for n in range(DS):
                    s = jnp.exp2(a[n] * d) * carry[n] + dx * row_of(bb_ref, t * DS + n)
                    parts.append(s * row_of(cb_ref, t * DS + n))
                    new.append(s)
                while len(parts) > 1:
                    parts = [parts[i] + parts[i + 1] for i in range(0, len(parts), 2)]
                yt[pl.ds(pl.multiple_of(t * 16 + h * 8, 8), 8), :] = parts[0]
                return tuple(new)

            state = lax.fori_loop(0, size, step, state, unroll=4)

    def point(k, _):
        c = lanes(k)
        total = jnp.zeros((8, 128), F32)
        for q in range(4):
            r = slice(q * (rows // 4), (q + 1) * (rows // 4))
            here = pl.ds(q * (rows // 4) * tiles + k, rows // 4, stride=tiles)
            x = xt_ref[here, :]
            y = yt[here, :] + w0_ref[6:7, c] * x
            gated[r, c] = (y * gate_ref[r, c]).astype(BF16)
            gz_ref[r, c] = (gzp_ref[r, c] * y).astype(BF16)
            total = total + jnp.sum((gt_ref[here, :] * x).reshape(-1, 8, 128), axis=0)
        skipg_ref[:, c] = jnp.sum(total, axis=0, keepdims=True)
        return 0

    lax.fori_loop(0, tiles, point, 0)

    def project(j, _):
        c = lanes(j, 256)
        block_ref[:, c] = tok_ref[:, c] + dot(gated[...], out_ref[:, c])
        return 0

    lax.fori_loop(0, tok_ref.shape[1] // 256, project, 0)

    def wide(j, _):
        c = lanes(j, 256)
        ograd_ref[c, :] = dot_tn(gated[:, c], low_ref[...]).astype(BF16)
        return 0

    lax.fori_loop(0, di // 256, wide, 0)

    def wide_z(j, _):
        c = lanes(j, 256)
        zgrad_ref[:, c] = dot_tn(normed_ref[...], gz_ref[:, c]).astype(BF16)
        return 0

    lax.fori_loop(0, di // 256, wide_z, 0)


def backward_body(
    so_ref, starts_ref, dt_ref, xt_ref, bb_ref, cb_ref, gt_ref, a2_ref,
    gdt_ref, gat_ref, gb_ref, gc_ref, ga_ref, keep, decays, pb, pc, rb, rc,
):
    chunks = starts_ref.shape[0]
    rows = dt_ref.shape[0] // 16
    size = rows // chunks
    zero = jnp.zeros((8, 128), F32)
    for h in range(2):
        hs = pl.ds(h * 8, 8)
        a = [a2_ref[n, hs, :] for n in range(DS)]
        for n in range(DS):
            ga_ref[n, hs, :] = zero
        later = tuple(so_ref[n, hs, :] for n in range(DS))
        for chunk in reversed(range(chunks)):
            base = chunk * size
            first = tuple(starts_ref[chunk, n, hs, :] for n in range(DS))
            for n in range(DS):
                keep[n * 8 : n * 8 + 8, :] = first[n]

            def again(i, carry):
                t = base + i
                d = tile_at(dt_ref, t, h)
                dx = d * tile_at(xt_ref, t, h)
                new = []
                for n in range(DS):
                    w = jnp.exp2(a[n] * d)
                    s = w * carry[n] + dx * row_of(bb_ref, t * DS + n)
                    o = pl.multiple_of(i * 128 + n * 8, 8)
                    decays[pl.ds(o, 8), :] = w
                    keep[pl.ds(pl.multiple_of(o + 128, 8), 8), :] = s
                    new.append(s)
                return tuple(new)

            lax.fori_loop(0, size, again, first, unroll=4)

            def back(j, carry):
                i = size - 1 - j
                t = base + i
                d = tile_at(dt_ref, t, h)
                x = tile_at(xt_ref, t, h)
                gy = tile_at(gt_ref, t, h)
                dx = d * x
                slot = (j % 2) * 128
                new = []
                weighted, through_a = [], []
                for n in range(DS):
                    o = pl.multiple_of(i * 128 + n * 8, 8)
                    w = decays[pl.ds(o, 8), :]
                    before = keep[pl.ds(o, 8), :]
                    now = keep[pl.ds(pl.multiple_of(o + 128, 8), 8), :]
                    g = carry[n] + gy * row_of(cb_ref, t * DS + n)
                    at = pl.ds(pl.multiple_of(slot + n * 8, 8), 8)
                    pc[at, :] = now * gy
                    pb[at, :] = g * dx
                    weighted.append(g * row_of(bb_ref, t * DS + n))
                    g = g * w
                    through = g * before
                    through_a.append(through * a[n])
                    ga_ref[n, hs, :] += through * d
                    new.append(g)
                while len(weighted) > 1:
                    weighted = [weighted[i] + weighted[i + 1] for i in range(0, len(weighted), 2)]
                    through_a = [through_a[i] + through_a[i + 1] for i in range(0, len(through_a), 2)]
                o = pl.ds(pl.multiple_of(t * 16 + h * 8, 8), 8)
                gdt_ref[o, :] = through_a[0] * LN2 + weighted[0] * x
                gat_ref[o, :] = weighted[0] * d
                for src, dst in ((pb, rb), (pc, rc)):
                    for m in range(2):
                        parts = [src[pl.ds(slot + m * 64 + s, 8, stride=8), :] for s in range(8)]
                        while len(parts) > 1:
                            parts = [parts[i] + parts[i + 1] for i in range(0, len(parts), 2)]
                        q = pl.ds(pl.multiple_of(t * 16 + m * 8, 8), 8)
                        if h == 0:
                            dst[q, :] = parts[0]
                        else:
                            dst[q, :] += parts[0]
                return tuple(new)

            later = lax.fori_loop(0, size, back, later, unroll=2)
    for n in range(DS):
        ga_ref[n] = ga_ref[n] * a2_ref[n] * LN2
    ones = jnp.ones((128, 128), BF16)
    pick = lax.broadcasted_iota(jnp.int32, (128, 128), 0) % DS == lax.broadcasted_iota(jnp.int32, (128, 128), 1)

    def collect(i, _):
        o = pl.ds(pl.multiple_of(i * 128, 128), 128)
        for src, dst in ((rb, gb_ref), (rc, gc_ref)):
            v = src[o, :]
            hi = v.astype(BF16)
            lo = (v - hi.astype(F32)).astype(BF16)
            s = jnp.where(pick, dot(hi, ones) + dot(lo, ones), 0.0)
            dst[pl.ds(pl.multiple_of(i * 8, 8), 8), :] = jnp.sum(s.reshape(8, DS, 128), axis=1)
        return 0

    lax.fori_loop(0, rows // 8, collect, 0)


def tail_body(
    gdt_ref, gat_ref, gb_ref, gc_ref, gt_ref, draw_ref, filt_ref, xin_ref, halo_ref, xs_ref, w0_ref, selt_ref,
    gf_ref, w0g_ref, selg_ref, proj, xp, raw_low, gproj, dw,
):
    rows, di = draw_ref.shape
    tiles = di // 128
    proj[:, 0:96] = dot_nt(xs_ref[...], selt_ref[...])
    low = proj[:, 0:DTR].astype(BF16)
    dw[...] = w0_ref[DELTA0 : DELTA0 + DTR, :].astype(BF16)

    def raw(k, _):
        c = lanes(k)
        g = gdt_ref[pl.ds(k, rows, stride=tiles), :] * sigmoid(draw_ref[:, c])
        w0g_ref[5:6, c] = jnp.sum(g, axis=0, keepdims=True)
        gl = g.astype(BF16)
        raw_low[:, c] = gl
        w0g_ref[DELTA0 : DELTA0 + DTR, c] = dot_tn(low, gl)
        return 0

    lax.fori_loop(0, tiles, raw, 0)
    gproj[:, 0:DTR] = dot_nt(raw_low[...], dw[...]).astype(BF16)
    gproj[:, DTR : DTR + DS] = gb_ref[:, 0:DS].astype(BF16)
    gproj[:, DTR + DS : DTR + 2 * DS] = gc_ref[:, 0:DS].astype(BF16)

    def point(k, _):
        c = lanes(k)
        gp = gproj[...]
        selg_ref[:, c] = dot_tn(gp, xs_ref[:, c])
        back = dot(gp, selt_ref[:, c])
        here = pl.ds(k, rows, stride=tiles)
        ga = gt_ref[here, :] * w0_ref[6:7, c] + gat_ref[here, :] + back
        f = filt_ref[:, c]
        s = sigmoid(f)
        gf = ga * (s * (1.0 + f * (1.0 - s)))
        gf_ref[:, c] = gf
        w0g_ref[4:5, c] = jnp.sum(gf, axis=0, keepdims=True)
        xp[0:16, :] = halo_ref[:, c].astype(F32)
        xp[16 : 16 + rows, :] = xin_ref[:, c].astype(F32)
        for tap in range(KW):
            lo = 16 - (KW - 1) + tap
            w0g_ref[tap : tap + 1, c] = jnp.sum(gf * xp[lo : lo + rows, :], axis=0, keepdims=True)
        return 0

    lax.fori_loop(0, tiles, point, 0)


def last_body(gf_ref, edge_ref, w0_ref, gz_ref, normed_ref, tok_ref, cot_ref, gain_ref, inx_ref, inz_ref, tgrad_ref, xgrad_ref, gaing_ref, gp, gx, gn):
    rows, di = gf_ref.shape
    tiles = di // 128

    def conv(k, _):
        c = lanes(k)
        gp[0:rows, :] = gf_ref[:, c]
        gp[rows : rows + 8, :] = edge_ref[:, c]
        total = jnp.zeros((rows, 128), F32)
        for tap in range(KW):
            lo = KW - 1 - tap
            total = total + w0_ref[tap : tap + 1, c] * gp[lo : lo + rows, :]
        gx[:, c] = total.astype(BF16)
        return 0

    lax.fori_loop(0, tiles, conv, 0)

    def wide(j, _):
        c = lanes(j, 256)
        xgrad_ref[:, c] = dot_tn(normed_ref[...], gx[:, c]).astype(BF16)
        return 0

    lax.fori_loop(0, di // 256, wide, 0)

    def back(j, _):
        c = lanes(j, 256)
        gn[:, c] = dot_nt(gx[...], inx_ref[c, :]) + dot_nt(gz_ref[...], inz_ref[c, :])
        return 0

    lax.fori_loop(0, inx_ref.shape[0] // 256, back, 0)

    def rows_of(i, total):
        r = pl.ds(pl.multiple_of(i * 8, 8), 8)
        u = tok_ref[r, :]
        g = gn[r, :]
        scale = lax.rsqrt(jnp.mean(u * u, axis=-1, keepdims=True) + EPS)
        v = g * gain_ref[...]
        mean = jnp.mean(v * u, axis=-1, keepdims=True)
        tgrad_ref[r, :] = cot_ref[r, :] + scale * v - u * (scale * scale * scale * mean)
        return total + g * u * scale

    total = lax.fori_loop(0, rows // 8, rows_of, jnp.zeros((8, tok_ref.shape[1]), F32))
    gaing_ref[...] = jnp.sum(total, axis=0, keepdims=True)


def pack_body(w0g_ref, selg_ref, gaing_ref, skipg_ref, ga_ref, pack_ref):
    devices = pack_ref.shape[0]
    low_half = lax.broadcasted_iota(jnp.int32, (PACK0, 128), 1) < 64
    w0g_ref[6:7, :] = skipg_ref[...]
    w0g_ref[7:8, :] = jnp.zeros_like(skipg_ref)
    w0g_ref[DELTA0 + DTR : PACK0, :] = jnp.zeros((PACK0 - DELTA0 - DTR, w0g_ref.shape[1]), F32)
    for k in range(16):
        w0g_ref[ALOG0 : ALOG0 + DS, k * 128 : (k + 1) * 128] = ga_ref[:, k, :]
    for j in range(devices // 2):
        c = slice(j * 128, (j + 1) * 128)
        a, b = w0g_ref[:, c], selg_ref[:, c]
        pack_ref[2 * j, 0:PACK0, :] = jnp.where(low_half, a, pltpu.roll(b, 64, 1)).astype(BF16)
        pack_ref[2 * j + 1, 0:PACK0, :] = jnp.where(low_half, pltpu.roll(a, 64, 1), b).astype(BF16)
    for j in range(devices):
        v = gaing_ref[:, (j // 4) * 128 : (j // 4 + 1) * 128]
        pack_ref[j, PACK0 : PACK, :] = jnp.broadcast_to(v, (PACK - PACK0, 128)).astype(BF16)


def place():
    b, s = lax.axis_index("batch"), lax.axis_index("seq")
    return b // 2, b % 2, s // 2, s % 2


def device(y, c, z, x):
    return (y * 2 + c, z * 2 + x)


def greet(peers):
    barrier = pltpu.get_barrier_semaphore()
    for peer in peers:
        pl.semaphore_signal(barrier, inc=1, device_id=peer, device_id_type=MESH)
    pl.semaphore_wait(barrier, len(peers))


def remote(src, dst, send, recv, to):
    return pltpu.make_async_remote_copy(
        src_ref=src, dst_ref=dst, send_sem=send, recv_sem=recv, device_id=to, device_id_type=MESH
    )


def neighbours(y, c, z, x):
    return [device(y, c, z ^ k, x) for k in (1, 2, 3)] + [
        device(1 - y, c, z, x), device(y, c, z, 1 - x), device(y, 1 - c, z, x)
    ]


class Gather:
    COPIES = 14

    def __init__(self, src, out, send, recv, local):
        self.src, self.out, self.send, self.recv, self.local = src, out, send, recv, local
        self.at = place()
        self.count = 0
        self.copies = []

    def go(self, view, to):
        i = self.count
        self.count += 1
        source, target = view if isinstance(view, tuple) else (view, view)
        copy = remote(source, target, self.send.at[i], self.recv.at[i], to)
        copy.start()
        self.copies.append(copy)
        return copy

    def stage(self, k):
        y, c, z, x = self.at
        out = self.out
        half = out.shape[4] // 2
        top, bottom = pl.ds(0, half), pl.ds(half, half)
        to_y, to_x, to_c = device(1 - y, c, z, x), device(y, c, z, 1 - x), device(y, 1 - c, z, x)
        if k == 0:
            own = pltpu.make_async_copy(self.src, out.at[y, c, z, x], self.local)
            own.start()
            self.first = [self.go((self.src, out.at[y, c, z, x]), device(y, c, z ^ i, x)) for i in (1, 2, 3)]
            own.wait()
        elif k == 1:
            for copy in self.first:
                copy.wait_recv()
            self.a = self.go(out.at[y, c, :, x, top], to_y)
            self.b = self.go(out.at[y, c, :, x, bottom], to_x)
            self.go(out.at[y, c, :, x], to_c)
        elif k == 2:
            self.a.wait_recv()
            self.b.wait_recv()
            self.next = [self.go(out.at[i, c, :, x, top], to_x) for i in (0, 1)]
            self.next.append(self.go(out.at[y, c, :, :, bottom], to_y))
            self.go(out.at[1 - y, c, :, x, top], to_c)
            self.go(out.at[y, c, :, 1 - x, bottom], to_c)
        elif k == 3:
            for copy in self.next:
                copy.wait_recv()
            for i in (0, 1):
                self.go(out.at[i, c, :, 1 - x, top], to_c)
            self.go(out.at[1 - y, c, :, :, bottom], to_c)
        else:
            done = self.first + [self.a, self.b] + self.next
            for copy in self.copies:
                if not any(copy is other for other in done):
                    copy.wait_recv()

    def drain(self):
        for copy in self.copies:
            copy.wait_send()


STAGES = 5


class Scatter:
    COPIES = 10

    def __init__(self, g, out, own, r1, r2, r3, r4, send, recv, local):
        self.g, self.out, self.own, self.r1, self.r2, self.r3, self.r4 = g, out, own, r1, r2, r3, r4
        self.send, self.recv, self.local = send, recv, local
        self.at = place()
        self.count = 0
        self.copies = []

    def go(self, source, target, to):
        i = self.count
        self.count += 1
        copy = remote(source, target, self.send.at[i], self.recv.at[i], to)
        copy.start()
        self.copies.append(copy)
        return copy

    def add(self, index, more, other):
        self.own[index] = (self.own[index].astype(F32) + more[other].astype(F32)).astype(BF16)

    def stage(self, k):
        y, c, z, x = self.at
        g, own = self.g, self.own
        half = own.shape[3] // 2
        top, bottom = pl.ds(0, half), pl.ds(half, half)
        to_y, to_x, to_c = device(1 - y, c, z, x), device(y, c, z, 1 - x), device(y, 1 - c, z, x)
        if k == 0:
            self.wait = [self.go(g.at[i, 1 - c], self.r1.at[i], to_c) for i in (0, 1)]
            self.held = [pltpu.make_async_copy(g.at[i, c], own.at[i], self.local.at[i]) for i in (0, 1)]
            for copy in self.held:
                copy.start()
        elif k == 1:
            for copy in self.held:
                copy.wait()
            for copy in self.wait:
                copy.wait_recv()

            def piece(i, _):
                at = (i // 8, i // 2 % 4, i % 2)
                self.add(at, self.r1, at)
                return 0

            lax.fori_loop(0, 16, piece, 0)
            self.wait = [self.go(own.at[1 - y, :, :, top], self.r2.at[pl.ds(0, 4), :], to_y)]
            for i in (0, 1):
                self.wait.append(self.go(own.at[i, :, 1 - x, bottom], self.r2.at[pl.ds(4, 4), i], to_x))
        elif k == 2:
            for copy in self.wait:
                copy.wait_recv()

            def piece(i, _):
                b, d = i // 2, i % 2
                self.add((y, b, d, top), self.r2, (b, d))
                self.add((d, b, x, bottom), self.r2, (4 + b, d))
                return 0

            lax.fori_loop(0, 8, piece, 0)
            self.wait = [
                self.go(own.at[y, :, 1 - x, top], self.r3.at[0], to_x),
                self.go(own.at[1 - y, :, x, bottom], self.r3.at[1], to_y),
            ]
        elif k == 3:
            for copy in self.wait:
                copy.wait_recv()

            def piece(b, _):
                self.add((y, b, x, top), self.r3, (0, b))
                self.add((y, b, x, bottom), self.r3, (1, b))
                return 0

            lax.fori_loop(0, 4, piece, 0)
            self.wait = [
                self.go(own.at[y, z ^ i, x], self.r4.at[i - 1], device(y, c, z ^ i, x)) for i in (1, 2, 3)
            ]
        else:
            for copy in self.wait:
                copy.wait_recv()
            total = own[y, z, x].astype(F32)
            for i in range(3):
                total = total + self.r4[i].astype(F32)
            self.out[...] = total
            for copy in self.copies:
                copy.wait_send()


def scatter_body(n, *refs):
    gs, outs, rest = refs[:n], refs[n : 2 * n], refs[2 * n :]
    send, recv, local = rest[5 * n :]
    greet(neighbours(*place()))
    jobs = [
        Scatter(gs[i], outs[i], *rest[5 * i : 5 * i + 5], send.at[i], recv.at[i], local.at[i]) for i in range(n)
    ]
    for step in range(n + STAGES - 1):
        for i in range(n):
            if 0 <= step - i < STAGES:
                jobs[i].stage(step - i)


def scatter(grads):
    n = len(grads)
    outs = tuple(sds(g.shape[4:], F32) for g in grads)
    scratch = []
    for g in grads:
        rows, cols = g.shape[4:]
        scratch += [
            pltpu.VMEM((2, 4, 2, rows, cols), BF16),
            pltpu.VMEM((2, 4, 2, rows, cols), BF16),
            pltpu.VMEM((8, 2, rows // 2, cols), BF16),
            pltpu.VMEM((2, 4, rows // 2, cols), BF16),
            pltpu.VMEM((3, rows, cols), BF16),
        ]
    return pl.pallas_call(
        functools.partial(scatter_body, n),
        out_shape=outs,
        in_specs=[ANY] * n,
        out_specs=(VM,) * n,
        scratch_shapes=scratch
        + [pltpu.SemaphoreType.DMA((n, Scatter.COPIES))] * 2
        + [pltpu.SemaphoreType.DMA((n, 2))],
        compiler_params=pltpu.CompilerParams(
            collective_id=1, has_side_effects=True, vmem_limit_bytes=GRANT
        ),
    )(*grads)


def shift(value, by):
    peers = lax.axis_size("seq")
    pairs = [(i, i + by) for i in range(peers) if 0 <= i + by < peers]
    return lax.ppermute(value, "seq", pairs)


def carried_in(total, value, reverse):
    peers, index = lax.axis_size("seq"), lax.axis_index("seq")
    totals = lax.all_gather(total.astype(BF16), "seq")
    values = lax.all_gather(value.astype(BF16), "seq")

    def turn(k, before):
        at = peers - 1 - k if reverse else k
        reached = at > index if reverse else at < index
        new = totals[at].astype(F32) * before + values[at].astype(F32)
        return jnp.where(reached, new, before)

    return lax.fori_loop(0, peers, turn, jnp.zeros(value.shape, F32))


def unpack_weights(pk, w0_ref, selt_ref, gain_ref):
    low_half = lax.broadcasted_iota(jnp.int32, (PACK0, 128), 1) < 64

    def pair(j, _):
        at = (j // 8, j // 4 % 2, j % 4)
        a = pk[at + (0, pl.ds(0, PACK0))].astype(F32)
        b = pk[at + (1, pl.ds(0, PACK0))].astype(F32)
        c = lanes(j)
        w0_ref[:, c] = jnp.where(low_half, a, pltpu.roll(b, 64, 1))
        selt_ref[:, c] = jnp.where(low_half, pltpu.roll(a, 64, 1), b).astype(BF16)
        return 0

    lax.fori_loop(0, 16, pair, 0)

    def gains(j, _):
        total = jnp.zeros((16, 128), F32)
        for i in range(4):
            v = pk[(j // 4, j // 2 % 2, j % 2 * 2 + i // 2, i % 2, pl.ds(PACK0, 16))]
            total = total + v.astype(F32)
        gain_ref[:, lanes(j)] = total[0:8, :]
        return 0

    lax.fori_loop(0, 8, gains, 0)


def normalise(tok, gain, normed):
    rows = tok.shape[0]

    def norm(i, _):
        r = pl.ds(pl.multiple_of(i * 16, 16), 16)
        u = tok[r, :]
        scale = lax.rsqrt(jnp.mean(u * u, axis=-1, keepdims=True) + EPS)
        normed[r, :] = (u * scale * gain[0:1, :]).astype(BF16)
        return 0

    lax.fori_loop(0, rows // 16, norm, 0)


def conv_tiles(first, count, xin, halo, live, w0, filt, xs, xt, xp):
    rows, di = xin.shape
    tiles = di // 128

    def conv(k, _):
        c = lanes(k)
        xp[0:16, :] = halo[:, c].astype(F32) * live
        xp[16 : 16 + rows, :] = xin[:, c].astype(F32)
        for q in range(2):
            r0 = q * (rows // 2)
            f = w0[4:5, c]
            for tap in range(KW):
                lo = 16 - (KW - 1) + tap + r0
                f = f + w0[tap : tap + 1, c] * xp[lo : lo + rows // 2, :]
            s = (f * sigmoid(f)).astype(BF16)
            filt[r0 : r0 + rows // 2, c] = f
            xs[r0 : r0 + rows // 2, c] = s
            xt[pl.ds(r0 * tiles + k, rows // 2, stride=tiles), :] = s.astype(F32)
        return 0

    lax.fori_loop(first, first + count, conv, 0)


def step_sizes(proj, w0, draw, dt):
    rows, di = draw.shape
    tiles = di // 128
    low = proj[:, 0:DTR].astype(BF16)

    def delta(k, _):
        c = lanes(k)
        raw = dot(low, w0[DELTA0 : DELTA0 + DTR, c].astype(BF16)) + w0[5:6, c]
        draw[:, c] = raw
        dt[pl.ds(k, rows, stride=tiles), :] = jnp.maximum(raw, 0.0) + jnp.log1p(jnp.exp(-jnp.abs(raw)))
        return 0

    lax.fori_loop(0, tiles, delta, 0)


def spread_rows(proj, bb, cb):
    row_ids = lax.broadcasted_iota(jnp.int32, (128, 128), 0) % DS
    lane_ids = lax.broadcasted_iota(jnp.int32, (128, 128), 1)
    ones = jnp.ones((128, 128), BF16)

    def spread(i, _):
        p = proj[pl.ds(pl.multiple_of(i * 8, 8), 8), :]
        tall = jnp.broadcast_to(p[:, None, :], (8, DS, 128)).reshape(128, 128)
        o = pl.ds(pl.multiple_of(i * 128, 128), 128)
        for first, ref in ((DTR, bb), (DTR + DS, cb)):
            v = jnp.where(lane_ids == row_ids + first, tall, 0.0)
            hi = v.astype(BF16)
            v = v - hi.astype(F32)
            mid = v.astype(BF16)
            lo = (v - mid.astype(F32)).astype(BF16)
            ref[o, :] = (dot(hi, ones) + dot(mid, ones)) + dot(lo, ones)
        return 0

    lax.fori_loop(0, proj.shape[0] // 8, spread, 0)


def light_forward_half(h, dt, xt, bb, a2, total, end):
    rows = dt.shape[0] // 16
    hs = pl.ds(h * 8, 8)
    a = [a2[n, hs, :] for n in range(DS)]

    def step(t, carry):
        state, run = carry
        d = tile_at(dt, t, h)
        dx = d * tile_at(xt, t, h)
        new = tuple(jnp.exp2(a[n] * d) * state[n] + dx * row_of(bb, t * DS + n) for n in range(DS))
        return (new, run + d)

    zero = jnp.zeros((8, 128), F32)
    state, run = lax.fori_loop(0, rows, step, ((zero,) * DS, zero), unroll=4)
    for n in range(DS):
        end[n, hs, :] = state[n]
        total[n, hs, :] = jnp.exp2(a[n] * run)


def light_backward_half(h, dt, gt, cb, a2, adj):
    rows = dt.shape[0] // 16
    hs = pl.ds(h * 8, 8)
    a = [a2[n, hs, :] for n in range(DS)]

    def step(i, carry):
        t = rows - 1 - i
        d = tile_at(dt, t, h)
        g = tile_at(gt, t, h)
        return tuple(jnp.exp2(a[n] * d) * (carry[n] + g * row_of(cb, t * DS + n)) for n in range(DS))

    out = lax.fori_loop(0, rows, step, (jnp.zeros((8, 128), F32),) * DS, unroll=4)
    for n in range(DS):
        adj[n, hs, :] = out[n]


def forward_half(h, si, dt, xt, bb, cb, a2, starts, yt):
    chunks = starts.shape[0]
    size = dt.shape[0] // 16 // chunks
    hs = pl.ds(h * 8, 8)
    a = [a2[n, hs, :] for n in range(DS)]

    def chunk(q, state):
        for n in range(DS):
            starts[q, n, hs, :] = state[n]

        def step(i, carry):
            t = q * size + i
            d = tile_at(dt, t, h)
            dx = d * tile_at(xt, t, h)
            new, parts = [], []
            for n in range(DS):
                s = jnp.exp2(a[n] * d) * carry[n] + dx * row_of(bb, t * DS + n)
                parts.append(s * row_of(cb, t * DS + n))
                new.append(s)
            while len(parts) > 1:
                parts = [parts[i] + parts[i + 1] for i in range(0, len(parts), 2)]
            yt[pl.ds(pl.multiple_of(t * 16 + h * 8, 8), 8), :] = parts[0]
            return tuple(new)

        return lax.fori_loop(0, size, step, state, unroll=4)

    lax.fori_loop(0, chunks, chunk, tuple(si[n, hs, :] for n in range(DS)))


def carry_send(refs, mine, got, send, recv):
    peers = mine.shape[0]
    pair = DS // peers
    b, s = lax.axis_index("batch"), lax.axis_index("seq")
    for j in range(peers):
        for i in range(pair):
            for m, ref in enumerate(refs):
                mine[j, m, i] = ref[j * pair + i].astype(BF16)
    copies = []
    for k in range(1, peers):
        to = lax.rem(s + k, peers)
        copy = remote(mine.at[to], got.at[s], send.at[k - 1], recv.at[k - 1], (b, to))
        copy.start()
        copies.append(copy)
    got[s] = mine[s]
    return copies


def carry_back(back, final, send, recv):
    peers = back.shape[0]
    b, s = lax.axis_index("batch"), lax.axis_index("seq")
    copies = []
    for k in range(1, peers):
        to = lax.rem(s + k, peers)
        copy = remote(back.at[to], final.at[s], send.at[k - 1], recv.at[k - 1], (b, to))
        copy.start()
        copies.append(copy)
    final[s] = back[s]
    return copies


def arrived(copies):
    for copy in copies:
        copy.wait_recv()


WX, WZ, WO = 4, 2, 2


def front_body(tok_in, cot_in, inw_in, outw_in, pack_in, *refs):
    names = FRONT_OUTS
    o = dict(zip(names, refs[: len(names)]))
    v = dict(zip(FRONT_SCRATCH, refs[len(names) :]))
    stash_sem, load_sem, job_send, job_recv, job_local, ring_send, ring_recv, halo_send, halo_recv = (
        v[n] for n in ("stash", "load", "jsend", "jrecv", "jlocal", "rsend", "rrecv", "hsend", "hrecv")
    )
    y, c, z, x = place()
    b, s = lax.axis_index("batch"), lax.axis_index("seq")
    peers = v["mine"].shape[0]
    stash = []

    def put(*keys):
        for key in keys:
            copy = pltpu.make_async_copy(v[key], o[key], stash_sem.at[len(stash)])
            copy.start()
            stash.append(copy)

    load_tok = pltpu.make_async_copy(tok_in, v["tok"], load_sem.at[0])
    load_cot = pltpu.make_async_copy(cot_in, v["cot"], load_sem.at[1])
    load_tok.start()
    load_cot.start()
    greet([(b, lax.rem(s + k, peers)) for k in range(1, peers)] + [device(1 - y, c, z, x), device(y, 1 - c, z, x)])

    jobs = []

    def job(src, out):
        i = len(jobs)
        jobs.append(Gather(src, out, job_send.at[i], job_recv.at[i], job_local.at[i]))

    width = inw_in.shape[1] // 2 // WX
    wide_z = inw_in.shape[1] // 2 // WZ
    wide_o = outw_in.shape[1] // WO
    job(pack_in, v["pk"])
    for i in range(WX):
        job(inw_in.at[:, pl.ds(i * width, width)], v["inx"].at[i])
    for i in range(WZ):
        job(inw_in.at[:, pl.ds(inw_in.shape[1] // 2 + i * wide_z, wide_z)], v["inz"].at[i])
    for i in range(WO):
        job(outw_in.at[:, pl.ds(i * wide_o, wide_o)], v["wo"].at[i])
    tick = [0]

    def advance():
        for i, it in enumerate(jobs):
            k = tick[0] - i
            if 0 <= k < STAGES:
                it.stage(k)
        tick[0] += 1

    di = v["xin"].shape[1]
    rows = v["xin"].shape[0]
    tiles = di // 128
    per = tiles // WX
    live = jnp.where(s > 0, 1.0, 0.0)
    halos = []

    def project_x(i):
        cols = pl.ds(i * width, width)
        v["xin"][:, cols] = dot(v["normed"][...], v["inx"][i].reshape(-1, width)).astype(BF16)
        copy = remote(
            v["xin"].at[pl.ds(rows - 16, 16), cols], v["halo"].at[:, cols],
            halo_send.at[i], halo_recv.at[i], (b, lax.rem(s + 1, peers)),
        )
        copy.start()
        halos.append(copy)

    def conv(i):
        halos[i].wait_recv()
        conv_tiles(i * per, per, v["xin"], v["halo"], live, v["w0"], v["filt"], v["xs"], v["xt"], v["xp"])

    for _ in range(STAGES):
        advance()
    unpack_weights(v["pk"], v["w0"], v["selt"], v["gain"])
    load_tok.wait()
    normalise(v["tok"], v["gain"], v["normed"])
    put("w0", "selt", "gain", "normed")
    for k in range(16):
        v["a2"][:, k, :] = -jnp.exp(v["w0"][ALOG0 : ALOG0 + DS, k * 128 : (k + 1) * 128]) * LOG2E
    put("a2")
    for i in range(WX):
        advance()
        project_x(i)
        if i > 0:
            conv(i - 1)
    put("inx")
    conv(WX - 1)
    put("xin", "halo", "filt", "xs", "xt")
    load_cot.wait()
    v["low"][...] = v["cot"][...].astype(BF16)
    put("low")
    v["proj"][:, 0:PACK0] = dot_nt(v["xs"][...], v["selt"][...])
    step_sizes(v["proj"], v["w0"], v["draw"], v["dt"])
    put("draw", "dt")
    advance()
    spread_rows(v["proj"], v["bb"], v["cb"])
    put("bb", "cb")
    light_forward_half(0, v["dt"], v["xt"], v["bb"], v["a2"], v["total"], v["end"])
    advance()
    light_forward_half(1, v["dt"], v["xt"], v["bb"], v["a2"], v["total"], v["end"])

    sent = carry_send((v["total"], v["end"]), v["mine"], v["got"], ring_send.at[0], ring_recv.at[0])
    advance()
    for i in range(WZ):
        v["gate"][:, i * wide_z : (i + 1) * wide_z] = dot(v["normed"][...], v["inz"][i].reshape(-1, wide_z))
    put("inz")
    arrived(sent)
    state = jnp.zeros(v["back"].shape[1:], F32)
    for p in range(peers):
        v["back"][p] = state.astype(BF16)
        state = v["got"][p, 0].astype(F32) * state + v["got"][p, 1].astype(F32)
    more = carry_back(v["back"], v["final"], ring_send.at[1], ring_recv.at[1])
    sent += more
    advance()
    arrived(more)
    pair = DS // peers
    for j in range(peers):
        for i in range(pair):
            v["si"][j * pair + i] = v["final"][j, i].astype(F32)
    forward_half(0, v["si"], v["dt"], v["xt"], v["bb"], v["cb"], v["a2"], v["starts"], v["yt"])
    while tick[0] < len(jobs) + STAGES - 1:
        advance()
    forward_half(1, v["si"], v["dt"], v["xt"], v["bb"], v["cb"], v["a2"], v["starts"], v["yt"])
    put("starts")

    block = 512
    per_b = block // (di // 32)

    def gated_grad(j, _):
        out = jnp.zeros((rows, block), F32)
        for i in range(WO):
            w = v["wo"][i, j // 2, j % 2].reshape(block, wide_o)
            out = out + dot_nt(v["low"][:, i * wide_o : (i + 1) * wide_o], w)
        v["gzp"][:, lanes(j, block)] = out
        return 0

    lax.fori_loop(0, di // block, gated_grad, 0)

    def point(k, _):
        cols = lanes(k)
        for q in range(4):
            r = slice(q * (rows // 4), (q + 1) * (rows // 4))
            zz = v["gate"][r, cols]
            gg = v["gzp"][r, cols]
            sg = sigmoid(zz)
            gate = zz * sg
            v["gate"][r, cols] = gate
            v["gzp"][r, cols] = gg * sg * (1.0 + zz * (1.0 - sg))
            v["gt"][pl.ds(q * (rows // 4) * tiles + k, rows // 4, stride=tiles), :] = gg * gate
        return 0

    lax.fori_loop(0, tiles, point, 0)
    put("gt")
    for h in range(2):
        light_backward_half(h, v["dt"], v["gt"], v["cb"], v["a2"], v["adj"])
    again = carry_send((v["adj"],), v["mine2"], v["got2"], ring_send.at[2], ring_recv.at[2])
    sent += again

    def emit(k, _):
        cols = lanes(k)
        total = jnp.zeros((8, 128), F32)
        for q in range(4):
            r = slice(q * (rows // 4), (q + 1) * (rows // 4))
            here = pl.ds(q * (rows // 4) * tiles + k, rows // 4, stride=tiles)
            xx = v["xt"][here, :]
            yy = v["yt"][here, :] + v["w0"][6:7, cols] * xx
            v["gated"][r, cols] = (yy * v["gate"][r, cols]).astype(BF16)
            v["gz"][r, cols] = (v["gzp"][r, cols] * yy).astype(BF16)
            total = total + jnp.sum((v["gt"][here, :] * xx).reshape(-1, 8, 128), axis=0)
        v["skipg"][:, cols] = jnp.broadcast_to(jnp.sum(total, axis=0, keepdims=True), (8, 128))
        return 0

    lax.fori_loop(0, tiles, emit, 0)
    put("gated", "gz", "skipg")
    arrived(again)
    state = jnp.zeros(v["back2"].shape[1:], F32)
    for p in reversed(range(peers)):
        v["back2"][p] = state.astype(BF16)
        state = v["got"][p, 0].astype(F32) * state + v["got2"][p, 0].astype(F32)
    more = carry_back(v["back2"], v["final2"], ring_send.at[3], ring_recv.at[3])
    sent += more
    for i in range(WO):
        cols = pl.ds(i * wide_o, wide_o)
        w = v["wo"][i].reshape(di, wide_o)
        v["tok"][:, cols] = v["tok"][:, cols] + dot(v["gated"][...], w)
    copy = pltpu.make_async_copy(v["tok"], o["block"], load_sem.at[0])
    copy.start()
    arrived(more)
    for j in range(peers):
        for i in range(pair):
            v["so"][j * pair + i] = v["final2"][j, i].astype(F32)
    put("so")
    copy.wait()
    for it in jobs:
        it.drain()
    for it in sent + halos:
        it.wait_send()
    for it in stash:
        it.wait()


FRONT_OUTS = (
    "block", "w0", "selt", "gain", "normed", "a2", "inx", "xin", "halo", "filt", "xs", "xt", "low", "draw", "dt",
    "bb", "cb", "inz", "starts", "gt", "gated", "gz", "skipg", "so",
)
FRONT_SCRATCH = (
    "w0", "selt", "gain", "normed", "a2", "inx", "xin", "halo", "filt", "xs", "xt", "low", "draw", "dt",
    "bb", "cb", "inz", "starts", "gt", "gated", "gz", "skipg", "so",
    "tok", "cot", "pk", "wo", "proj", "xp", "gate", "gzp", "yt", "total", "end", "adj", "si",
    "mine", "got", "back", "final", "mine2", "got2", "back2", "final2",
    "stash", "load", "jsend", "jrecv", "jlocal", "rsend", "rrecv", "hsend", "hrecv",
)


def front(tok, cot, in_weight, out_weight, pack, peers, chunks):
    rows, width = tok.shape
    di = in_weight.shape[1] // 2
    tiles = di // 128
    lead = (2, 2, 4, 2)
    flat, wide, carry = ((rows * tiles, 128), F32), ((rows, di), F32), ((DS, tiles, 128), F32)
    spread, half = ((rows * DS, 128), F32), ((rows, di), BF16)
    pair = (DS // peers, tiles, 128)
    shapes = {
        "block": ((rows, width), F32), "w0": ((PACK0, di), F32), "selt": ((PACK0, di), BF16), "gain": ((8, width), F32),
        "normed": ((rows, width), BF16), "a2": carry, "inx": ((WX,) + lead + (in_weight.shape[0], di // WX), BF16),
        "xin": half, "halo": ((16, di), BF16), "filt": wide, "xs": half, "xt": flat, "low": ((rows, width), BF16),
        "draw": wide, "dt": flat, "bb": spread, "cb": spread,
        "inz": ((WZ,) + lead + (in_weight.shape[0], di // WZ), BF16), "starts": ((chunks, DS, tiles, 128), F32),
        "gt": flat, "gated": half, "gz": half, "skipg": ((8, di), F32), "so": carry,
        "tok": ((rows, width), F32), "cot": ((rows, width), F32), "pk": (lead + pack.shape, BF16),
        "wo": ((WO,) + lead + (out_weight.shape[0], width // WO), BF16), "proj": ((rows, 128), F32),
        "xp": ((rows + 16, 128), F32), "gate": wide, "gzp": wide, "yt": flat, "total": carry, "end": carry, "adj": carry,
        "si": carry, "mine": ((peers, 2) + pair, BF16), "got": ((peers, 2) + pair, BF16), "back": ((peers,) + pair, BF16),
        "final": ((peers,) + pair, BF16), "mine2": ((peers, 1) + pair, BF16), "got2": ((peers, 1) + pair, BF16),
        "back2": ((peers,) + pair, BF16), "final2": ((peers,) + pair, BF16),
    }
    n_jobs = 1 + WX + WZ + WO
    dma = pltpu.SemaphoreType.DMA
    sems = {
        "stash": dma((len(FRONT_OUTS) - 1,)), "load": dma((2,)), "jsend": dma((n_jobs, Gather.COPIES)),
        "jrecv": dma((n_jobs, Gather.COPIES)), "jlocal": dma((n_jobs,)), "rsend": dma((4, peers - 1)),
        "rrecv": dma((4, peers - 1)), "hsend": dma((WX,)), "hrecv": dma((WX,)),
    }
    outs = pl.pallas_call(
        front_body,
        out_shape=tuple(sds(*shapes[n]) for n in FRONT_OUTS),
        in_specs=[ANY] * 5,
        out_specs=(ANY,) * len(FRONT_OUTS),
        scratch_shapes=[sems[n] if n in sems else pltpu.VMEM(*shapes[n]) for n in FRONT_SCRATCH],
        compiler_params=pltpu.CompilerParams(collective_id=0, has_side_effects=True, vmem_limit_bytes=GRANT),
    )(tok, cot, in_weight, out_weight, pack)
    return dict(zip(FRONT_OUTS, outs))


def wide_body(gated_ref, low_ref, normed_ref, gz_ref, ograd_ref, zgrad_ref):
    di = gated_ref.shape[1]

    def wide(j, _):
        c = lanes(j, 256)
        ograd_ref[c, :] = dot_tn(gated_ref[:, c], low_ref[...]).astype(BF16)
        zgrad_ref[:, c] = dot_tn(normed_ref[...], gz_ref[:, c]).astype(BF16)
        return 0

    lax.fori_loop(0, di // 256, wide, 0)


def on_slice(tokens, cotangent, norm_gain, in_weight, conv_weight, conv_bias, select_weight, delta_weight, delta_bias, a_log, skip_gain, out_weight):
    sizes = (lax.axis_size("batch"), lax.axis_size("seq"))
    devices = sizes[0] * sizes[1]
    me = lax.axis_index("batch") * sizes[1] + lax.axis_index("seq")
    tok, cot = tokens[0], cotangent[0]
    rows, width = tok.shape
    di = out_weight.shape[0] * devices
    tiles = di // 128
    own = conv_bias.shape[0]
    left = jnp.concatenate(
        [
            conv_weight, conv_bias[None], delta_bias[None], skip_gain[None], jnp.zeros((1, own), BF16),
            a_log, delta_weight, jnp.zeros((PACK0 - DELTA0 - DTR, own), BF16),
        ],
        axis=0,
    )
    gain_row = lax.dynamic_update_slice(jnp.zeros((128,), BF16), norm_gain, ((me % 4) * norm_gain.shape[0],))
    pack = jnp.concatenate(
        [
            jnp.concatenate([left, select_weight.T], axis=1),
            jnp.broadcast_to(gain_row[None], (PACK - PACK0, 128)),
        ],
        axis=0,
    )
    f = front(tok, cot, in_weight, out_weight, pack, sizes[1], rows // 64)
    flat = sds((rows * tiles, 128), F32)
    wide = sds((rows, di), F32)
    carry = sds((DS, tiles, 128), F32)
    in_x = f["inx"].reshape(WX, width, -1).transpose(1, 0, 2).reshape(width, di)
    in_z = f["inz"].reshape(WZ, width, -1).transpose(1, 0, 2).reshape(width, di)
    gain, block_out, skip_grad = f["gain"][:1], f["block"], f["skipg"][:1]
    dt, xt, bb, cb, gt, a2, starts, state_out = (f[n] for n in ("dt", "xt", "bb", "cb", "gt", "a2", "starts", "so"))
    draw, filt, x_in, halo, xs, w0, sel_t, gz, normed = (
        f[n] for n in ("draw", "filt", "xin", "halo", "xs", "w0", "selt", "gz", "normed")
    )
    halo = jnp.where(lax.axis_index("seq") > 0, halo, jnp.zeros_like(halo))
    out_grad, z_grad = kernel_call(wide_body, (sds((di, width), BF16), sds((width, di), BF16)), 4)(
        f["gated"], f["low"], normed, gz
    )
    tall = pltpu.VMEM((rows * DS, 128), F32)
    gdt, gat, gb, gc, ga = kernel_call(
        backward_body,
        (flat, flat, sds((rows, 128), F32), sds((rows, 128), F32), carry),
        8,
        [
            pltpu.VMEM((65 * 128, 128), F32), pltpu.VMEM((64 * 128, 128), F32), pltpu.VMEM((256, 128), F32),
            pltpu.VMEM((256, 128), F32), tall, tall,
        ],
    )(state_out, starts, dt, xt, bb, cb, gt, a2)
    gf, w0g, selg = kernel_call(
        tail_body,
        (wide, sds((PACK0, di), F32), sds((PACK0, di), F32)),
        12,
        [
            pltpu.VMEM((rows, 128), F32), pltpu.VMEM((rows + 16, 128), F32), pltpu.VMEM((rows, di), BF16),
            pltpu.VMEM((rows, PACK0), BF16), pltpu.VMEM((DTR, di), BF16),
        ],
    )(gdt, gat, gb, gc, gt, draw, filt, x_in, halo, xs, w0, sel_t)
    edge = shift(gf[:8], -1)
    tokens_grad, x_grad, gain_grad = kernel_call(
        last_body,
        (sds((rows, width), F32), sds((width, di), BF16), sds((1, width), F32)),
        10,
        [pltpu.VMEM((rows + 8, 128), F32), pltpu.VMEM((rows, di), BF16), pltpu.VMEM((rows, width), F32)],
    )(gf, edge, w0, gz, normed, tok, cot, gain, in_x, in_z)

    packed = kernel_call(pack_body, sds((devices, PACK, 128), BF16), 5)(
        w0g, selg, gain_grad, skip_grad, ga
    )
    lead = (2, 2, 4, 2)
    g_out, g_z, g_x, g_pack = scatter(
        (
            out_grad.reshape(lead + out_weight.shape),
            z_grad.reshape(lead + (width // devices, di)),
            x_grad.reshape(lead + (width // devices, di)),
            packed.reshape(lead + packed.shape[1:]),
        )
    )
    left, right = g_pack[:PACK0, :own], g_pack[:PACK0, own:]
    g_gain = lax.dynamic_slice(g_pack[PACK0], ((me % 4) * norm_gain.shape[0],), norm_gain.shape)
    grads = (
        g_gain, jnp.concatenate([g_x, g_z], axis=1), left[0:KW], left[4], right.T,
        left[DELTA0 : DELTA0 + DTR], left[5], left[ALOG0 : ALOG0 + DS], left[6], g_out,
    )
    return (block_out[None], tokens_grad[None]) + grads


def on_device(tokens, cotangent, norm_gain, in_weight, conv_weight, conv_bias, select_weight, delta_weight, delta_bias, a_log, skip_gain, out_weight):
    axes = ("batch", "seq")
    sizes = (lax.axis_size("batch"), lax.axis_size("seq"))
    if sizes == (4, 8):
        return on_slice(
            tokens, cotangent, norm_gain, in_weight, conv_weight, conv_bias, select_weight, delta_weight, delta_bias,
            a_log, skip_gain, out_weight,
        )
    tok, cot = tokens[0], cotangent[0]
    rows, width = tok.shape
    di = out_weight.shape[0] * sizes[0] * sizes[1]
    tiles = di // 128
    full = lambda v, axis: lax.all_gather(v, axes, axis=axis, tiled=True)
    in_full = full(in_weight, 0)
    in_x, in_z = in_full[:, :di], in_full[:, di:]
    out_full = full(out_weight, 0)
    sel_t = full(select_weight, 0).T
    gain = full(norm_gain, 0)[None].astype(F32)
    w0 = jnp.concatenate(
        [
            full(conv_weight, 1), full(conv_bias, 0)[None], full(delta_bias, 0)[None], full(skip_gain, 0)[None],
            jnp.zeros((1, di), BF16), full(a_log, 1), full(delta_weight, 1),
            jnp.zeros((PACK0 - DELTA0 - DTR, di), BF16),
        ],
        axis=0,
    ).astype(F32)

    flat = sds((rows * tiles, 128), F32)
    wide = sds((rows, di), F32)
    spread = sds((rows * DS, 128), F32)
    carry = sds((DS, tiles, 128), F32)

    normed, x_in = kernel_call(
        inproj_body, (sds((rows, width), BF16), sds((rows, di), BF16)), 3
    )(tok, gain, in_x)
    halo = shift(x_in[rows - 16 :], 1)
    filt, xs, xt, draw, dt, bb, cb = kernel_call(
        conv_body,
        (wide, sds((rows, di), BF16), flat, wide, flat, spread, spread),
        4,
        [pltpu.VMEM((rows, 128), F32), pltpu.VMEM((rows + 16, 128), F32)],
    )(x_in, halo, w0, sel_t)
    a2, total, end = kernel_call(lightf_body, (carry, carry, carry), 4)(dt, xt, bb, w0)
    gate, gzp, gt, low, adj = kernel_call(
        gate_body, (wide, wide, flat, sds((rows, width), BF16), carry), 7
    )(normed, in_z, cot, out_full, dt, cb, a2)
    state_in = carried_in(total, end, False)
    state_out = carried_in(total, adj, True)
    chunks = rows // 64
    starts, block_out, gz, out_grad, z_grad, skip_grad = kernel_call(
        forward_body,
        (
            sds((chunks, DS, tiles, 128), F32), sds((rows, width), F32), sds((rows, di), BF16),
            sds((di, width), BF16), sds((width, di), BF16), sds((1, di), F32),
        ),
        14,
        [pltpu.VMEM((rows * tiles, 128), F32), pltpu.VMEM((rows, di), BF16), pltpu.VMEM((8, 128), F32)],
    )(state_in, dt, xt, bb, cb, a2, w0, gate, gzp, gt, tok, low, normed, out_full)
    tall = pltpu.VMEM((rows * DS, 128), F32)
    gdt, gat, gb, gc, ga = kernel_call(
        backward_body,
        (flat, flat, sds((rows, 128), F32), sds((rows, 128), F32), carry),
        8,
        [
            pltpu.VMEM((65 * 128, 128), F32), pltpu.VMEM((64 * 128, 128), F32), pltpu.VMEM((256, 128), F32),
            pltpu.VMEM((256, 128), F32), tall, tall,
        ],
    )(state_out, starts, dt, xt, bb, cb, gt, a2)
    gf, w0g, selg = kernel_call(
        tail_body,
        (wide, sds((PACK0, di), F32), sds((PACK0, di), F32)),
        12,
        [
            pltpu.VMEM((rows, 128), F32), pltpu.VMEM((rows + 16, 128), F32), pltpu.VMEM((rows, di), BF16),
            pltpu.VMEM((rows, PACK0), BF16), pltpu.VMEM((DTR, di), BF16),
        ],
    )(gdt, gat, gb, gc, gt, draw, filt, x_in, halo, xs, w0, sel_t)
    edge = shift(gf[:8], -1)
    tokens_grad, x_grad, gain_grad = kernel_call(
        last_body,
        (sds((rows, width), F32), sds((width, di), BF16), sds((1, width), F32)),
        10,
        [pltpu.VMEM((rows + 8, 128), F32), pltpu.VMEM((rows, di), BF16), pltpu.VMEM((rows, width), F32)],
    )(gf, edge, w0, gz, normed, tok, cot, gain, in_x, in_z)

    share = lambda v, d: lax.psum_scatter(v.astype(F32), axes, scatter_dimension=d, tiled=True)
    ga_flat = ga.reshape(DS, di)
    grads = (
        share(gain_grad[0], 0), share(jnp.concatenate([x_grad, z_grad], axis=1), 0), share(w0g[0:KW], 1),
        share(w0g[4], 0), share(selg.T, 0), share(w0g[DELTA0 : DELTA0 + DTR], 1), share(w0g[5], 0),
        share(ga_flat, 1), share(skip_grad[0], 0), share(out_grad, 0),
    )
    return (block_out[None], tokens_grad[None]) + grads


def solution(mesh):
    both = ("batch", "seq")
    first, second = P(both), P(None, both)
    matrix = P(both, None)
    whole = P("batch", "seq", None)
    weights = (first, matrix, second, first, matrix, second, first, second, first, matrix)
    return jax.shard_map(
        on_device,
        mesh=mesh,
        in_specs=(whole, whole) + weights,
        out_specs=(whole, whole) + weights,
        check_vma=False,
    )
```

```python
import functools

import jax
import jax.numpy as jnp
from jax import lax
from jax.experimental import pallas as pl
from jax.experimental.pallas import tpu as pltpu
from jax.sharding import PartitionSpec as P

DS = 16
KW = 4
DTR = 64
EPS = 1e-05
LOG2E = 1.4426950408889634
LN2 = 0.6931471805599453
F32 = jnp.float32
BF16 = jnp.bfloat16
MESH = pl.DeviceIdType.MESH
VM = pl.BlockSpec(memory_space=pltpu.VMEM)
ANY = pl.BlockSpec(memory_space=pl.ANY)
GRANT = 60 << 20
ALOG0, DELTA0, PACK0, PACK = 8, 24, 96, 128


def sds(shape, dtype):
    return jax.ShapeDtypeStruct(shape, dtype)


def kernel_call(body, outs, n_in, scratch=(), flops=1e9, **params):
    return pl.pallas_call(
        body,
        out_shape=outs,
        in_specs=[VM] * n_in,
        out_specs=jax.tree.map(lambda _: VM, outs),
        scratch_shapes=list(scratch),
        cost_estimate=pl.CostEstimate(flops=int(flops), bytes_accessed=8 << 20, transcendentals=0),
        compiler_params=pltpu.CompilerParams(vmem_limit_bytes=GRANT, **params),
    )


def sigmoid(v):
    return 1.0 / (1.0 + jnp.exp(-v))


def dot(a, b):
    return jnp.dot(a, b, preferred_element_type=F32)


def dot_nt(a, b):
    return lax.dot_general(a, b, (((1,), (1,)), ((), ())), preferred_element_type=F32)


def dot_tn(a, b):
    return lax.dot_general(a, b, (((0,), (0,)), ((), ())), preferred_element_type=F32)


def lanes(k, width=128):
    return pl.ds(pl.multiple_of(k * width, width), width)


def inproj_body(tok_ref, gain_ref, inx_ref, normed_ref, xin_ref):
    rows = tok_ref.shape[0]

    def norm(i, _):
        r = pl.ds(pl.multiple_of(i * 16, 16), 16)
        u = tok_ref[r, :]
        scale = lax.rsqrt(jnp.mean(u * u, axis=-1, keepdims=True) + EPS)
        normed_ref[r, :] = (u * scale * gain_ref[...]).astype(BF16)
        return 0

    lax.fori_loop(0, rows // 16, norm, 0)
    width = 512

    def mm(j, _):
        c = lanes(j, width)
        xin_ref[:, c] = dot(normed_ref[...], inx_ref[:, c]).astype(BF16)
        return 0

    lax.fori_loop(0, inx_ref.shape[1] // width, mm, 0)


def conv_body(xin_ref, halo_ref, w0_ref, selt_ref, filt_ref, xs_ref, xt_ref, draw_ref, dt_ref, bb_ref, cb_ref, proj, xp):
    rows, di = xin_ref.shape
    tiles = di // 128
    xp_rows = 16 + rows

    def conv(k, _):
        c = lanes(k)
        xp[0:16, :] = halo_ref[:, c].astype(F32)
        xp[16:xp_rows, :] = xin_ref[:, c].astype(F32)
        for q in range(2):
            r0 = q * (rows // 2)
            f = w0_ref[4:5, c]
            for tap in range(KW):
                lo = 16 - (KW - 1) + tap + r0
                f = f + w0_ref[tap : tap + 1, c] * xp[lo : lo + rows // 2, :]
            s = (f * sigmoid(f)).astype(BF16)
            filt_ref[r0 : r0 + rows // 2, c] = f
            xs_ref[r0 : r0 + rows // 2, c] = s
            xt_ref[pl.ds(r0 * tiles + k, rows // 2, stride=tiles), :] = s.astype(F32)
        return 0

    lax.fori_loop(0, tiles, conv, 0)
    proj[:, 0:96] = dot_nt(xs_ref[...], selt_ref[...])
    low = proj[:, 0:DTR].astype(BF16)

    def delta(k, _):
        c = lanes(k)
        raw = dot(low, w0_ref[DELTA0 : DELTA0 + DTR, c].astype(BF16)) + w0_ref[5:6, c]
        draw_ref[:, c] = raw
        dt_ref[pl.ds(k, rows, stride=tiles), :] = jnp.maximum(raw, 0.0) + jnp.log1p(jnp.exp(-jnp.abs(raw)))
        return 0

    lax.fori_loop(0, tiles, delta, 0)
    row_ids = lax.broadcasted_iota(jnp.int32, (128, 128), 0) % DS
    lane_ids = lax.broadcasted_iota(jnp.int32, (128, 128), 1)
    ones = jnp.ones((128, 128), BF16)

    def spread(i, _):
        r = pl.ds(pl.multiple_of(i * 8, 8), 8)
        p = proj[r, :]
        tall = jnp.broadcast_to(p[:, None, :], (8, DS, 128)).reshape(128, 128)
        o = pl.ds(pl.multiple_of(i * 128, 128), 128)
        for first, ref in ((DTR, bb_ref), (DTR + DS, cb_ref)):
            v = jnp.where(lane_ids == row_ids + first, tall, 0.0)
            hi = v.astype(BF16)
            v = v - hi.astype(F32)
            mid = v.astype(BF16)
            lo = (v - mid.astype(F32)).astype(BF16)
            ref[o, :] = (dot(hi, ones) + dot(mid, ones)) + dot(lo, ones)
        return 0

    lax.fori_loop(0, rows // 8, spread, 0)


def row_of(ref, index):
    return ref[pl.ds(index, 8, stride=0), :]


def tile_at(ref, t, h):
    return ref[pl.ds(pl.multiple_of(t * 16 + h * 8, 8), 8), :]


def light_forward(dt_ref, xt_ref, bb_ref, a2_ref, total_ref, end_ref, rows):
    for h in range(2):
        hs = pl.ds(h * 8, 8)
        a = [a2_ref[n, hs, :] for n in range(DS)]

        def step(t, carry):
            state, run = carry
            d = tile_at(dt_ref, t, h)
            dx = d * tile_at(xt_ref, t, h)
            new = tuple(
                jnp.exp2(a[n] * d) * state[n] + dx * row_of(bb_ref, t * DS + n) for n in range(DS)
            )
            return (new, run + d)

        zero = jnp.zeros((8, 128), F32)
        state, run = lax.fori_loop(0, rows, step, ((zero,) * DS, zero), unroll=4)
        for n in range(DS):
            end_ref[n, hs, :] = state[n]
            total_ref[n, hs, :] = jnp.exp2(a[n] * run)


def light_backward(dt_ref, gt_ref, cb_ref, a2_ref, adj_ref, rows):
    for h in range(2):
        hs = pl.ds(h * 8, 8)
        a = [a2_ref[n, hs, :] for n in range(DS)]

        def step(i, carry):
            t = rows - 1 - i
            d = tile_at(dt_ref, t, h)
            g = tile_at(gt_ref, t, h)
            return tuple(
                jnp.exp2(a[n] * d) * (carry[n] + g * row_of(cb_ref, t * DS + n)) for n in range(DS)
            )

        out = lax.fori_loop(0, rows, step, (jnp.zeros((8, 128), F32),) * DS, unroll=4)
        for n in range(DS):
            adj_ref[n, hs, :] = out[n]


def lightf_body(dt_ref, xt_ref, bb_ref, w0_ref, a2_ref, total_ref, end_ref):
    rows = dt_ref.shape[0] // 16
    for k in range(16):
        a2_ref[:, k, :] = -jnp.exp(w0_ref[ALOG0 : ALOG0 + DS, k * 128 : (k + 1) * 128]) * LOG2E
    light_forward(dt_ref, xt_ref, bb_ref, a2_ref, total_ref, end_ref, rows)


def gate_body(normed_ref, inz_ref, cot_ref, out_ref, dt_ref, cb_ref, a2_ref, gate_ref, gzp_ref, gt_ref, low_ref, adj_ref):
    rows, di = gate_ref.shape
    tiles = di // 128
    low_ref[...] = cot_ref[...].astype(BF16)
    width = 512

    def block(j, _):
        c = lanes(j, width)
        gate_ref[:, c] = dot(normed_ref[...], inz_ref[:, c])
        gzp_ref[:, c] = dot_nt(low_ref[...], out_ref[c, :])
        return 0

    lax.fori_loop(0, di // width, block, 0)

    def point(k, _):
        c = lanes(k)
        for q in range(4):
            r = slice(q * (rows // 4), (q + 1) * (rows // 4))
            z = gate_ref[r, c]
            gg = gzp_ref[r, c]
            s = sigmoid(z)
            gate = z * s
            gate_ref[r, c] = gate
            gzp_ref[r, c] = gg * s * (1.0 + z * (1.0 - s))
            gt_ref[pl.ds(q * (rows // 4) * tiles + k, rows // 4, stride=tiles), :] = gg * gate
        return 0

    lax.fori_loop(0, tiles, point, 0)
    light_backward(dt_ref, gt_ref, cb_ref, a2_ref, adj_ref, rows)


def forward_body(
    si_ref, dt_ref, xt_ref, bb_ref, cb_ref, a2_ref, w0_ref, gate_ref, gzp_ref, gt_ref, tok_ref, low_ref, normed_ref, out_ref,
    starts_ref, block_ref, gz_ref, ograd_ref, zgrad_ref, skipg_ref, yt, gated, low_t,
):
    chunks = starts_ref.shape[0]
    rows, di = gate_ref.shape
    tiles = di // 128
    size = rows // chunks
    for h in range(2):
        hs = pl.ds(h * 8, 8)
        a = [a2_ref[n, hs, :] for n in range(DS)]
        state = tuple(si_ref[n, hs, :] for n in range(DS))
        for chunk in range(chunks):
            for n in range(DS):
                starts_ref[chunk, n, hs, :] = state[n]

            def step(i, carry):
                t = chunk * size + i
                d = tile_at(dt_ref, t, h)
                dx = d * tile_at(xt_ref, t, h)
                new, parts = [], []
                for n in range(DS):
                    s = jnp.exp2(a[n] * d) * carry[n] + dx * row_of(bb_ref, t * DS + n)
                    parts.append(s * row_of(cb_ref, t * DS + n))
                    new.append(s)
                while len(parts) > 1:
                    parts = [parts[i] + parts[i + 1] for i in range(0, len(parts), 2)]
                yt[pl.ds(pl.multiple_of(t * 16 + h * 8, 8), 8), :] = parts[0]
                return tuple(new)

            state = lax.fori_loop(0, size, step, state, unroll=4)

    def point(k, _):
        c = lanes(k)
        total = jnp.zeros((8, 128), F32)
        for q in range(4):
            r = slice(q * (rows // 4), (q + 1) * (rows // 4))
            here = pl.ds(q * (rows // 4) * tiles + k, rows // 4, stride=tiles)
            x = xt_ref[here, :]
            y = yt[here, :] + w0_ref[6:7, c] * x
            gated[r, c] = (y * gate_ref[r, c]).astype(BF16)
            gz_ref[r, c] = (gzp_ref[r, c] * y).astype(BF16)
            total = total + jnp.sum((gt_ref[here, :] * x).reshape(-1, 8, 128), axis=0)
        skipg_ref[:, c] = jnp.sum(total, axis=0, keepdims=True)
        return 0

    lax.fori_loop(0, tiles, point, 0)

    def project(j, _):
        c = lanes(j, 256)
        block_ref[:, c] = tok_ref[:, c] + dot(gated[...], out_ref[:, c])
        return 0

    lax.fori_loop(0, tok_ref.shape[1] // 256, project, 0)

    def wide(j, _):
        c = lanes(j, 256)
        ograd_ref[c, :] = dot_tn(gated[:, c], low_ref[...]).astype(BF16)
        return 0

    lax.fori_loop(0, di // 256, wide, 0)

    def wide_z(j, _):
        c = lanes(j, 256)
        zgrad_ref[:, c] = dot_tn(normed_ref[...], gz_ref[:, c]).astype(BF16)
        return 0

    lax.fori_loop(0, di // 256, wide_z, 0)


def backward_body(
    so_ref, starts_ref, dt_ref, xt_ref, bb_ref, cb_ref, gt_ref, a2_ref,
    gdt_ref, gat_ref, gb_ref, gc_ref, ga_ref, keep, decays, pb, pc, rb, rc,
):
    chunks = starts_ref.shape[0]
    rows = dt_ref.shape[0] // 16
    size = rows // chunks
    zero = jnp.zeros((8, 128), F32)
    for h in range(2):
        hs = pl.ds(h * 8, 8)
        a = [a2_ref[n, hs, :] for n in range(DS)]
        for n in range(DS):
            ga_ref[n, hs, :] = zero
        later = tuple(so_ref[n, hs, :] for n in range(DS))
        for chunk in reversed(range(chunks)):
            base = chunk * size
            first = tuple(starts_ref[chunk, n, hs, :] for n in range(DS))
            for n in range(DS):
                keep[n * 8 : n * 8 + 8, :] = first[n]

            def again(i, carry):
                t = base + i
                d = tile_at(dt_ref, t, h)
                dx = d * tile_at(xt_ref, t, h)
                new = []
                for n in range(DS):
                    w = jnp.exp2(a[n] * d)
                    s = w * carry[n] + dx * row_of(bb_ref, t * DS + n)
                    o = pl.multiple_of(i * 128 + n * 8, 8)
                    decays[pl.ds(o, 8), :] = w
                    keep[pl.ds(pl.multiple_of(o + 128, 8), 8), :] = s
                    new.append(s)
                return tuple(new)

            lax.fori_loop(0, size, again, first, unroll=4)

            def back(j, carry):
                i = size - 1 - j
                t = base + i
                d = tile_at(dt_ref, t, h)
                x = tile_at(xt_ref, t, h)
                gy = tile_at(gt_ref, t, h)
                dx = d * x
                slot = (j % 2) * 128
                new = []
                weighted, through_a = [], []
                for n in range(DS):
                    o = pl.multiple_of(i * 128 + n * 8, 8)
                    w = decays[pl.ds(o, 8), :]
                    before = keep[pl.ds(o, 8), :]
                    now = keep[pl.ds(pl.multiple_of(o + 128, 8), 8), :]
                    g = carry[n] + gy * row_of(cb_ref, t * DS + n)
                    at = pl.ds(pl.multiple_of(slot + n * 8, 8), 8)
                    pc[at, :] = now * gy
                    pb[at, :] = g * dx
                    weighted.append(g * row_of(bb_ref, t * DS + n))
                    g = g * w
                    through = g * before
                    through_a.append(through * a[n])
                    ga_ref[n, hs, :] += through * d
                    new.append(g)
                while len(weighted) > 1:
                    weighted = [weighted[i] + weighted[i + 1] for i in range(0, len(weighted), 2)]
                    through_a = [through_a[i] + through_a[i + 1] for i in range(0, len(through_a), 2)]
                o = pl.ds(pl.multiple_of(t * 16 + h * 8, 8), 8)
                gdt_ref[o, :] = through_a[0] * LN2 + weighted[0] * x
                gat_ref[o, :] = weighted[0] * d
                for src, dst in ((pb, rb), (pc, rc)):
                    for m in range(2):
                        parts = [src[pl.ds(slot + m * 64 + s, 8, stride=8), :] for s in range(8)]
                        while len(parts) > 1:
                            parts = [parts[i] + parts[i + 1] for i in range(0, len(parts), 2)]
                        q = pl.ds(pl.multiple_of(t * 16 + m * 8, 8), 8)
                        if h == 0:
                            dst[q, :] = parts[0]
                        else:
                            dst[q, :] += parts[0]
                return tuple(new)

            later = lax.fori_loop(0, size, back, later, unroll=2)
    for n in range(DS):
        ga_ref[n] = ga_ref[n] * a2_ref[n] * LN2
    ones = jnp.ones((128, 128), BF16)
    pick = lax.broadcasted_iota(jnp.int32, (128, 128), 0) % DS == lax.broadcasted_iota(jnp.int32, (128, 128), 1)

    def collect(i, _):
        o = pl.ds(pl.multiple_of(i * 128, 128), 128)
        for src, dst in ((rb, gb_ref), (rc, gc_ref)):
            v = src[o, :]
            hi = v.astype(BF16)
            lo = (v - hi.astype(F32)).astype(BF16)
            s = jnp.where(pick, dot(hi, ones) + dot(lo, ones), 0.0)
            dst[pl.ds(pl.multiple_of(i * 8, 8), 8), :] = jnp.sum(s.reshape(8, DS, 128), axis=1)
        return 0

    lax.fori_loop(0, rows // 8, collect, 0)


def tail_body(
    gdt_ref, gat_ref, gb_ref, gc_ref, gt_ref, draw_ref, filt_ref, xin_ref, halo_ref, xs_ref, w0_ref, selt_ref,
    gf_ref, w0g_ref, selg_ref, proj, xp, raw_low, gproj, dw,
):
    rows, di = draw_ref.shape
    tiles = di // 128
    proj[:, 0:96] = dot_nt(xs_ref[...], selt_ref[...])
    low = proj[:, 0:DTR].astype(BF16)
    dw[...] = w0_ref[DELTA0 : DELTA0 + DTR, :].astype(BF16)

    def raw(k, _):
        c = lanes(k)
        g = gdt_ref[pl.ds(k, rows, stride=tiles), :] * sigmoid(draw_ref[:, c])
        w0g_ref[5:6, c] = jnp.sum(g, axis=0, keepdims=True)
        gl = g.astype(BF16)
        raw_low[:, c] = gl
        w0g_ref[DELTA0 : DELTA0 + DTR, c] = dot_tn(low, gl)
        return 0

    lax.fori_loop(0, tiles, raw, 0)
    gproj[:, 0:DTR] = dot_nt(raw_low[...], dw[...]).astype(BF16)
    gproj[:, DTR : DTR + DS] = gb_ref[:, 0:DS].astype(BF16)
    gproj[:, DTR + DS : DTR + 2 * DS] = gc_ref[:, 0:DS].astype(BF16)

    def point(k, _):
        c = lanes(k)
        gp = gproj[...]
        selg_ref[:, c] = dot_tn(gp, xs_ref[:, c])
        back = dot(gp, selt_ref[:, c])
        here = pl.ds(k, rows, stride=tiles)
        ga = gt_ref[here, :] * w0_ref[6:7, c] + gat_ref[here, :] + back
        f = filt_ref[:, c]
        s = sigmoid(f)
        gf = ga * (s * (1.0 + f * (1.0 - s)))
        gf_ref[:, c] = gf
        w0g_ref[4:5, c] = jnp.sum(gf, axis=0, keepdims=True)
        xp[0:16, :] = halo_ref[:, c].astype(F32)
        xp[16 : 16 + rows, :] = xin_ref[:, c].astype(F32)
        for tap in range(KW):
            lo = 16 - (KW - 1) + tap
            w0g_ref[tap : tap + 1, c] = jnp.sum(gf * xp[lo : lo + rows, :], axis=0, keepdims=True)
        return 0

    lax.fori_loop(0, tiles, point, 0)


def last_body(gf_ref, edge_ref, w0_ref, gz_ref, normed_ref, tok_ref, cot_ref, gain_ref, inx_ref, inz_ref, tgrad_ref, xgrad_ref, gaing_ref, gp, gx, gn):
    rows, di = gf_ref.shape
    tiles = di // 128

    def conv(k, _):
        c = lanes(k)
        gp[0:rows, :] = gf_ref[:, c]
        gp[rows : rows + 8, :] = edge_ref[:, c]
        total = jnp.zeros((rows, 128), F32)
        for tap in range(KW):
            lo = KW - 1 - tap
            total = total + w0_ref[tap : tap + 1, c] * gp[lo : lo + rows, :]
        gx[:, c] = total.astype(BF16)
        return 0

    lax.fori_loop(0, tiles, conv, 0)

    def wide(j, _):
        c = lanes(j, 256)
        xgrad_ref[:, c] = dot_tn(normed_ref[...], gx[:, c]).astype(BF16)
        return 0

    lax.fori_loop(0, di // 256, wide, 0)

    def back(j, _):
        c = lanes(j, 256)
        gn[:, c] = dot_nt(gx[...], inx_ref[c, :]) + dot_nt(gz_ref[...], inz_ref[c, :])
        return 0

    lax.fori_loop(0, inx_ref.shape[0] // 256, back, 0)

    def rows_of(i, total):
        r = pl.ds(pl.multiple_of(i * 8, 8), 8)
        u = tok_ref[r, :]
        g = gn[r, :]
        scale = lax.rsqrt(jnp.mean(u * u, axis=-1, keepdims=True) + EPS)
        v = g * gain_ref[...]
        mean = jnp.mean(v * u, axis=-1, keepdims=True)
        tgrad_ref[r, :] = cot_ref[r, :] + scale * v - u * (scale * scale * scale * mean)
        return total + g * u * scale

    total = lax.fori_loop(0, rows // 8, rows_of, jnp.zeros((8, tok_ref.shape[1]), F32))
    gaing_ref[...] = jnp.sum(total, axis=0, keepdims=True)


def place():
    b, s = lax.axis_index("batch"), lax.axis_index("seq")
    return b // 2, b % 2, s // 2, s % 2


def device(y, c, z, x):
    return (y * 2 + c, z * 2 + x)


def greet(peers):
    barrier = pltpu.get_barrier_semaphore()
    for peer in peers:
        pl.semaphore_signal(barrier, inc=1, device_id=peer, device_id_type=MESH)
    pl.semaphore_wait(barrier, len(peers))


def remote(src, dst, send, recv, to):
    return pltpu.make_async_remote_copy(
        src_ref=src, dst_ref=dst, send_sem=send, recv_sem=recv, device_id=to, device_id_type=MESH
    )


def neighbours(y, c, z, x):
    return [device(y, c, z ^ k, x) for k in (1, 2, 3)] + [
        device(1 - y, c, z, x), device(y, c, z, 1 - x), device(y, 1 - c, z, x)
    ]


class Gather:
    COPIES = 14

    def __init__(self, src, out, send, recv, local):
        self.src, self.out, self.send, self.recv, self.local = src, out, send, recv, local
        self.at = place()
        self.count = 0
        self.copies = []

    def go(self, view, to):
        i = self.count
        self.count += 1
        source, target = view if isinstance(view, tuple) else (view, view)
        copy = remote(source, target, self.send.at[i], self.recv.at[i], to)
        copy.start()
        self.copies.append(copy)
        return copy

    def stage(self, k):
        y, c, z, x = self.at
        out = self.out
        half = out.shape[4] // 2
        top, bottom = pl.ds(0, half), pl.ds(half, half)
        to_y, to_x, to_c = device(1 - y, c, z, x), device(y, c, z, 1 - x), device(y, 1 - c, z, x)
        if k == 0:
            own = pltpu.make_async_copy(self.src, out.at[y, c, z, x], self.local)
            own.start()
            self.first = [self.go((self.src, out.at[y, c, z, x]), device(y, c, z ^ i, x)) for i in (1, 2, 3)]
            own.wait()
        elif k == 1:
            for copy in self.first:
                copy.wait_recv()
            self.a = self.go(out.at[y, c, :, x, top], to_y)
            self.b = self.go(out.at[y, c, :, x, bottom], to_x)
            self.go(out.at[y, c, :, x], to_c)
        elif k == 2:
            self.a.wait_recv()
            self.b.wait_recv()
            self.next = [self.go(out.at[i, c, :, x, top], to_x) for i in (0, 1)]
            self.next.append(self.go(out.at[y, c, :, :, bottom], to_y))
            self.go(out.at[1 - y, c, :, x, top], to_c)
            self.go(out.at[y, c, :, 1 - x, bottom], to_c)
        elif k == 3:
            for copy in self.next:
                copy.wait_recv()
            for i in (0, 1):
                self.go(out.at[i, c, :, 1 - x, top], to_c)
            self.go(out.at[1 - y, c, :, :, bottom], to_c)
        else:
            done = self.first + [self.a, self.b] + self.next
            for copy in self.copies:
                if not any(copy is other for other in done):
                    copy.wait_recv()

    def drain(self):
        for copy in self.copies:
            copy.wait_send()


STAGES = 5


def shift(value, by):
    peers = lax.axis_size("seq")
    pairs = [(i, i + by) for i in range(peers) if 0 <= i + by < peers]
    return lax.ppermute(value, "seq", pairs)


def carried_in(total, value, reverse):
    peers, index = lax.axis_size("seq"), lax.axis_index("seq")
    totals = lax.all_gather(total.astype(BF16), "seq")
    values = lax.all_gather(value.astype(BF16), "seq")

    def turn(k, before):
        at = peers - 1 - k if reverse else k
        reached = at > index if reverse else at < index
        new = totals[at].astype(F32) * before + values[at].astype(F32)
        return jnp.where(reached, new, before)

    return lax.fori_loop(0, peers, turn, jnp.zeros(value.shape, F32))


def unpack_weights(pk, w0_ref, selt_ref, gain_ref):
    low_half = lax.broadcasted_iota(jnp.int32, (PACK0, 128), 1) < 64

    def pair(j, _):
        at = (j // 8, j // 4 % 2, j % 4)
        a = pk[at + (0, pl.ds(0, PACK0))].astype(F32)
        b = pk[at + (1, pl.ds(0, PACK0))].astype(F32)
        c = lanes(j)
        w0_ref[:, c] = jnp.where(low_half, a, pltpu.roll(b, 64, 1))
        selt_ref[:, c] = jnp.where(low_half, pltpu.roll(a, 64, 1), b).astype(BF16)
        return 0

    lax.fori_loop(0, 16, pair, 0)

    def gains(j, _):
        total = jnp.zeros((16, 128), F32)
        for i in range(4):
            v = pk[(j // 4, j // 2 % 2, j % 2 * 2 + i // 2, i % 2, pl.ds(PACK0, 16))]
            total = total + v.astype(F32)
        gain_ref[:, lanes(j)] = total[0:8, :]
        return 0

    lax.fori_loop(0, 8, gains, 0)


def normalise(tok, gain, normed):
    rows = tok.shape[0]

    def norm(i, _):
        r = pl.ds(pl.multiple_of(i * 16, 16), 16)
        u = tok[r, :]
        scale = lax.rsqrt(jnp.mean(u * u, axis=-1, keepdims=True) + EPS)
        normed[r, :] = (u * scale * gain[0:1, :]).astype(BF16)
        return 0

    lax.fori_loop(0, rows // 16, norm, 0)


def conv_tiles(first, count, xin, halo, live, w0, filt, xs, xt, xp):
    rows, di = xin.shape
    tiles = di // 128

    def conv(k, _):
        c = lanes(k)
        xp[0:16, :] = halo[:, c].astype(F32) * live
        xp[16 : 16 + rows, :] = xin[:, c].astype(F32)
        for q in range(2):
            r0 = q * (rows // 2)
            f = w0[4:5, c]
            for tap in range(KW):
                lo = 16 - (KW - 1) + tap + r0
                f = f + w0[tap : tap + 1, c] * xp[lo : lo + rows // 2, :]
            s = (f * sigmoid(f)).astype(BF16)
            filt[r0 : r0 + rows // 2, c] = f
            xs[r0 : r0 + rows // 2, c] = s
            xt[pl.ds(r0 * tiles + k, rows // 2, stride=tiles), :] = s.astype(F32)
        return 0

    lax.fori_loop(first, first + count, conv, 0)


def step_sizes(proj, w0, draw, dt):
    rows, di = draw.shape
    tiles = di // 128
    low = proj[:, 0:DTR].astype(BF16)

    def delta(k, _):
        c = lanes(k)
        raw = dot(low, w0[DELTA0 : DELTA0 + DTR, c].astype(BF16)) + w0[5:6, c]
        draw[:, c] = raw
        dt[pl.ds(k, rows, stride=tiles), :] = jnp.maximum(raw, 0.0) + jnp.log1p(jnp.exp(-jnp.abs(raw)))
        return 0

    lax.fori_loop(0, tiles, delta, 0)


def spread_rows(proj, bb, cb):
    row_ids = lax.broadcasted_iota(jnp.int32, (128, 128), 0) % DS
    lane_ids = lax.broadcasted_iota(jnp.int32, (128, 128), 1)
    ones = jnp.ones((128, 128), BF16)

    def spread(i, _):
        p = proj[pl.ds(pl.multiple_of(i * 8, 8), 8), :]
        tall = jnp.broadcast_to(p[:, None, :], (8, DS, 128)).reshape(128, 128)
        o = pl.ds(pl.multiple_of(i * 128, 128), 128)
        for first, ref in ((DTR, bb), (DTR + DS, cb)):
            v = jnp.where(lane_ids == row_ids + first, tall, 0.0)
            hi = v.astype(BF16)
            v = v - hi.astype(F32)
            mid = v.astype(BF16)
            lo = (v - mid.astype(F32)).astype(BF16)
            ref[o, :] = (dot(hi, ones) + dot(mid, ones)) + dot(lo, ones)
        return 0

    lax.fori_loop(0, proj.shape[0] // 8, spread, 0)


def light_forward_half(h, dt, xt, bb, a2, total, end):
    rows = dt.shape[0] // 16
    hs = pl.ds(h * 8, 8)
    a = [a2[n, hs, :] for n in range(DS)]

    def step(t, carry):
        state, run = carry
        d = tile_at(dt, t, h)
        dx = d * tile_at(xt, t, h)
        new = tuple(jnp.exp2(a[n] * d) * state[n] + dx * row_of(bb, t * DS + n) for n in range(DS))
        return (new, run + d)

    zero = jnp.zeros((8, 128), F32)
    state, run = lax.fori_loop(0, rows, step, ((zero,) * DS, zero), unroll=4)
    for n in range(DS):
        end[n, hs, :] = state[n]
        total[n, hs, :] = jnp.exp2(a[n] * run)


def light_backward_half(h, dt, gt, cb, a2, adj):
    rows = dt.shape[0] // 16
    hs = pl.ds(h * 8, 8)
    a = [a2[n, hs, :] for n in range(DS)]

    def step(i, carry):
        t = rows - 1 - i
        d = tile_at(dt, t, h)
        g = tile_at(gt, t, h)
        return tuple(jnp.exp2(a[n] * d) * (carry[n] + g * row_of(cb, t * DS + n)) for n in range(DS))

    out = lax.fori_loop(0, rows, step, (jnp.zeros((8, 128), F32),) * DS, unroll=4)
    for n in range(DS):
        adj[n, hs, :] = out[n]


def forward_half(h, si, dt, xt, bb, cb, a2, starts, yt):
    chunks = starts.shape[0]
    size = dt.shape[0] // 16 // chunks
    hs = pl.ds(h * 8, 8)
    a = [a2[n, hs, :] for n in range(DS)]

    def chunk(q, state):
        for n in range(DS):
            starts[q, n, hs, :] = state[n]

        def step(i, carry):
            t = q * size + i
            d = tile_at(dt, t, h)
            dx = d * tile_at(xt, t, h)
            new, parts = [], []
            for n in range(DS):
                s = jnp.exp2(a[n] * d) * carry[n] + dx * row_of(bb, t * DS + n)
                parts.append(s * row_of(cb, t * DS + n))
                new.append(s)
            while len(parts) > 1:
                parts = [parts[i] + parts[i + 1] for i in range(0, len(parts), 2)]
            yt[pl.ds(pl.multiple_of(t * 16 + h * 8, 8), 8), :] = parts[0]
            return tuple(new)

        return lax.fori_loop(0, size, step, state, unroll=4)

    lax.fori_loop(0, chunks, chunk, tuple(si[n, hs, :] for n in range(DS)))


def carry_send(refs, mine, got, send, recv):
    peers = mine.shape[0]
    pair = DS // peers
    b, s = lax.axis_index("batch"), lax.axis_index("seq")
    for j in range(peers):
        for i in range(pair):
            for m, ref in enumerate(refs):
                mine[j, m, i] = ref[j * pair + i].astype(BF16)
    copies = []
    for k in range(1, peers):
        to = lax.rem(s + k, peers)
        copy = remote(mine.at[to], got.at[s], send.at[k - 1], recv.at[k - 1], (b, to))
        copy.start()
        copies.append(copy)
    got[s] = mine[s]
    return copies


def carry_back(back, final, send, recv):
    peers = back.shape[0]
    b, s = lax.axis_index("batch"), lax.axis_index("seq")
    copies = []
    for k in range(1, peers):
        to = lax.rem(s + k, peers)
        copy = remote(back.at[to], final.at[s], send.at[k - 1], recv.at[k - 1], (b, to))
        copy.start()
        copies.append(copy)
    final[s] = back[s]
    return copies


def arrived(copies):
    for copy in copies:
        copy.wait_recv()


WX, WZ, WO = 4, 4, 2


def front_body(tok_in, cot_in, inw_in, outw_in, pack_in, *refs):
    names = FRONT_OUTS
    o = dict(zip(names, refs[: len(names)]))
    v = dict(zip(FRONT_SCRATCH, refs[len(names) :]))
    stash_sem, load_sem, job_send, job_recv, job_local, ring_send, ring_recv, halo_send, halo_recv = (
        v[n] for n in ("stash", "load", "jsend", "jrecv", "jlocal", "rsend", "rrecv", "hsend", "hrecv")
    )
    y, c, z, x = place()
    b, s = lax.axis_index("batch"), lax.axis_index("seq")
    peers = v["mine"].shape[0]
    stash = []

    def put(*keys):
        for key in keys:
            copy = pltpu.make_async_copy(v[key], o[key], stash_sem.at[len(stash)])
            copy.start()
            stash.append(copy)

    load_tok = pltpu.make_async_copy(tok_in, v["tok"], load_sem.at[0])
    load_cot = pltpu.make_async_copy(cot_in, v["cot"], load_sem.at[1])
    load_tok.start()
    load_cot.start()
    greet([(b, lax.rem(s + k, peers)) for k in range(1, peers)] + [device(1 - y, c, z, x), device(y, 1 - c, z, x)])

    jobs = []

    def job(src, out):
        i = len(jobs)
        jobs.append(Gather(src, out, job_send.at[i], job_recv.at[i], job_local.at[i]))

    width = inw_in.shape[1] // 2 // WX
    wide_z = inw_in.shape[1] // 2 // WZ
    wide_o = outw_in.shape[1] // WO
    job(pack_in, v["pk"])
    for i in range(WX):
        job(inw_in.at[:, pl.ds(i * width, width)], v["inx"].at[i])
    for i in range(WZ):
        job(inw_in.at[:, pl.ds(inw_in.shape[1] // 2 + i * wide_z, wide_z)], v["inz"].at[i])
    for i in range(WO):
        job(outw_in.at[:, pl.ds(i * wide_o, wide_o)], v["wo"].at[i])
    tick = [0]

    def advance():
        for i, it in enumerate(jobs):
            k = tick[0] - i
            if 0 <= k < STAGES:
                it.stage(k)
        tick[0] += 1

    di = v["xin"].shape[1]
    rows = v["xin"].shape[0]
    tiles = di // 128
    per = tiles // WX
    live = jnp.where(s > 0, 1.0, 0.0)
    halos = []

    def project_x(i):
        cols = pl.ds(i * width, width)
        v["xin"][:, cols] = dot(v["normed"][...], v["inx"][i].reshape(-1, width)).astype(BF16)
        copy = remote(
            v["xin"].at[pl.ds(rows - 16, 16), cols], v["halo"].at[:, cols],
            halo_send.at[i], halo_recv.at[i], (b, lax.rem(s + 1, peers)),
        )
        copy.start()
        halos.append(copy)

    def conv(i):
        halos[i].wait_recv()
        conv_tiles(i * per, per, v["xin"], v["halo"], live, v["w0"], v["filt"], v["xs"], v["xt"], v["xp"])

    for _ in range(STAGES):
        advance()
    unpack_weights(v["pk"], v["w0"], v["selt"], v["gain"])
    load_tok.wait()
    normalise(v["tok"], v["gain"], v["normed"])
    put("w0", "selt", "gain", "normed")
    for k in range(16):
        v["a2"][:, k, :] = -jnp.exp(v["w0"][ALOG0 : ALOG0 + DS, k * 128 : (k + 1) * 128]) * LOG2E
    put("a2")
    for i in range(WX):
        advance()
        project_x(i)
        if i > 0:
            conv(i - 1)
    put("inx")
    conv(WX - 1)
    put("xin", "halo", "filt", "xs", "xt")
    load_cot.wait()
    v["low"][...] = v["cot"][...].astype(BF16)
    put("low")
    v["proj"][:, 0:PACK0] = dot_nt(v["xs"][...], v["selt"][...])
    step_sizes(v["proj"], v["w0"], v["draw"], v["dt"])
    put("draw", "dt")
    advance()
    spread_rows(v["proj"], v["bb"], v["cb"])
    put("bb", "cb")
    light_forward_half(0, v["dt"], v["xt"], v["bb"], v["a2"], v["total"], v["end"])
    advance()
    light_forward_half(1, v["dt"], v["xt"], v["bb"], v["a2"], v["total"], v["end"])

    sent = carry_send((v["total"], v["end"]), v["mine"], v["got"], ring_send.at[0], ring_recv.at[0])
    advance()

    def project_z(i):
        v["gate"][:, i * wide_z : (i + 1) * wide_z] = dot(v["normed"][...], v["inz"][i].reshape(-1, wide_z))

    for i in range(WZ - 1):
        project_z(i)
    arrived(sent)
    state = jnp.zeros(v["back"].shape[1:], F32)
    for p in range(peers):
        v["back"][p] = state.astype(BF16)
        state = v["got"][p, 0].astype(F32) * state + v["got"][p, 1].astype(F32)
    more = carry_back(v["back"], v["final"], ring_send.at[1], ring_recv.at[1])
    sent += more
    advance()
    project_z(WZ - 1)
    put("inz")
    arrived(more)
    pair = DS // peers
    for j in range(peers):
        for i in range(pair):
            v["si"][j * pair + i] = v["final"][j, i].astype(F32)
    forward_half(0, v["si"], v["dt"], v["xt"], v["bb"], v["cb"], v["a2"], v["starts"], v["yt"])
    while tick[0] < len(jobs) + STAGES - 1:
        advance()
    forward_half(1, v["si"], v["dt"], v["xt"], v["bb"], v["cb"], v["a2"], v["starts"], v["yt"])
    put("starts")

    block = 512
    per_b = block // (di // 32)

    def gated_grad(j, _):
        out = jnp.zeros((rows, block), F32)
        for i in range(WO):
            w = v["wo"][i, j // 2, j % 2].reshape(block, wide_o)
            out = out + dot_nt(v["low"][:, i * wide_o : (i + 1) * wide_o], w)
        v["gzp"][:, lanes(j, block)] = out
        return 0

    lax.fori_loop(0, di // block, gated_grad, 0)

    def point(k, _):
        cols = lanes(k)
        for q in range(4):
            r = slice(q * (rows // 4), (q + 1) * (rows // 4))
            zz = v["gate"][r, cols]
            gg = v["gzp"][r, cols]
            sg = sigmoid(zz)
            gate = zz * sg
            v["gate"][r, cols] = gate
            v["gzp"][r, cols] = gg * sg * (1.0 + zz * (1.0 - sg))
            v["gt"][pl.ds(q * (rows // 4) * tiles + k, rows // 4, stride=tiles), :] = gg * gate
        return 0

    lax.fori_loop(0, tiles, point, 0)
    put("gt")
    for h in range(2):
        light_backward_half(h, v["dt"], v["gt"], v["cb"], v["a2"], v["adj"])
    again = carry_send((v["adj"],), v["mine2"], v["got2"], ring_send.at[2], ring_recv.at[2])
    sent += again

    def emit(k, _):
        cols = lanes(k)
        total = jnp.zeros((8, 128), F32)
        for q in range(4):
            r = slice(q * (rows // 4), (q + 1) * (rows // 4))
            here = pl.ds(q * (rows // 4) * tiles + k, rows // 4, stride=tiles)
            xx = v["xt"][here, :]
            yy = v["yt"][here, :] + v["w0"][6:7, cols] * xx
            v["gated"][r, cols] = (yy * v["gate"][r, cols]).astype(BF16)
            v["gz"][r, cols] = (v["gzp"][r, cols] * yy).astype(BF16)
            total = total + jnp.sum((v["gt"][here, :] * xx).reshape(-1, 8, 128), axis=0)
        v["skipg"][:, cols] = jnp.broadcast_to(jnp.sum(total, axis=0, keepdims=True), (8, 128))
        return 0

    lax.fori_loop(0, tiles, emit, 0)
    put("gated", "gz", "skipg")
    arrived(again)
    state = jnp.zeros(v["back2"].shape[1:], F32)
    for p in reversed(range(peers)):
        v["back2"][p] = state.astype(BF16)
        state = v["got"][p, 0].astype(F32) * state + v["got2"][p, 0].astype(F32)
    more = carry_back(v["back2"], v["final2"], ring_send.at[3], ring_recv.at[3])
    sent += more
    for i in range(WO):
        cols = pl.ds(i * wide_o, wide_o)
        w = v["wo"][i].reshape(di, wide_o)
        v["tok"][:, cols] = v["tok"][:, cols] + dot(v["gated"][...], w)
    copy = pltpu.make_async_copy(v["tok"], o["block"], load_sem.at[0])
    copy.start()
    arrived(more)
    for j in range(peers):
        for i in range(pair):
            v["so"][j * pair + i] = v["final2"][j, i].astype(F32)
    put("so")
    copy.wait()
    for it in jobs:
        it.drain()
    for it in sent + halos:
        it.wait_send()
    for it in stash:
        it.wait()


FRONT_OUTS = (
    "block", "w0", "selt", "gain", "normed", "a2", "inx", "xin", "halo", "filt", "xs", "xt", "low", "draw", "dt",
    "bb", "cb", "inz", "starts", "gt", "gated", "gz", "skipg", "so",
)
FRONT_SCRATCH = (
    "w0", "selt", "gain", "normed", "a2", "inx", "xin", "halo", "filt", "xs", "xt", "low", "draw", "dt",
    "bb", "cb", "inz", "starts", "gt", "gated", "gz", "skipg", "so",
    "tok", "cot", "pk", "wo", "proj", "xp", "gate", "gzp", "yt", "total", "end", "adj", "si",
    "mine", "got", "back", "final", "mine2", "got2", "back2", "final2",
    "stash", "load", "jsend", "jrecv", "jlocal", "rsend", "rrecv", "hsend", "hrecv",
)


def front(tok, cot, in_weight, out_weight, pack, peers, chunks):
    rows, width = tok.shape
    di = in_weight.shape[1] // 2
    tiles = di // 128
    lead = (2, 2, 4, 2)
    flat, wide, carry = ((rows * tiles, 128), F32), ((rows, di), F32), ((DS, tiles, 128), F32)
    spread, half = ((rows * DS, 128), F32), ((rows, di), BF16)
    pair = (DS // peers, tiles, 128)
    shapes = {
        "block": ((rows, width), F32), "w0": ((PACK0, di), F32), "selt": ((PACK0, di), BF16), "gain": ((8, width), F32),
        "normed": ((rows, width), BF16), "a2": carry, "inx": ((WX,) + lead + (in_weight.shape[0], di // WX), BF16),
        "xin": half, "halo": ((16, di), BF16), "filt": wide, "xs": half, "xt": flat, "low": ((rows, width), BF16),
        "draw": wide, "dt": flat, "bb": spread, "cb": spread,
        "inz": ((WZ,) + lead + (in_weight.shape[0], di // WZ), BF16), "starts": ((chunks, DS, tiles, 128), F32),
        "gt": flat, "gated": half, "gz": half, "skipg": ((8, di), F32), "so": carry,
        "tok": ((rows, width), F32), "cot": ((rows, width), F32), "pk": (lead + pack.shape, BF16),
        "wo": ((WO,) + lead + (out_weight.shape[0], width // WO), BF16), "proj": ((rows, 128), F32),
        "xp": ((rows + 16, 128), F32), "gate": wide, "gzp": wide, "yt": flat, "total": carry, "end": carry, "adj": carry,
        "si": carry, "mine": ((peers, 2) + pair, BF16), "got": ((peers, 2) + pair, BF16), "back": ((peers,) + pair, BF16),
        "final": ((peers,) + pair, BF16), "mine2": ((peers, 1) + pair, BF16), "got2": ((peers, 1) + pair, BF16),
        "back2": ((peers,) + pair, BF16), "final2": ((peers,) + pair, BF16),
    }
    n_jobs = 1 + WX + WZ + WO
    dma = pltpu.SemaphoreType.DMA
    sems = {
        "stash": dma((len(FRONT_OUTS) - 1,)), "load": dma((2,)), "jsend": dma((n_jobs, Gather.COPIES)),
        "jrecv": dma((n_jobs, Gather.COPIES)), "jlocal": dma((n_jobs,)), "rsend": dma((4, peers - 1)),
        "rrecv": dma((4, peers - 1)), "hsend": dma((WX,)), "hrecv": dma((WX,)),
    }
    outs = pl.pallas_call(
        front_body,
        out_shape=tuple(sds(*shapes[n]) for n in FRONT_OUTS),
        in_specs=[ANY] * 5,
        out_specs=(ANY,) * len(FRONT_OUTS),
        scratch_shapes=[sems[n] if n in sems else pltpu.VMEM(*shapes[n]) for n in FRONT_SCRATCH],
        compiler_params=pltpu.CompilerParams(collective_id=0, has_side_effects=True, vmem_limit_bytes=GRANT),
    )(tok, cot, in_weight, out_weight, pack)
    return dict(zip(FRONT_OUTS, outs))


class Share:
    COPIES = 10

    def __init__(self, own, other, r1, r2, r3, r4, out, send, recv):
        self.own, self.other, self.r1, self.r2, self.r3, self.r4, self.out = own, other, r1, r2, r3, r4, out
        self.send, self.recv = send, recv
        self.at = place()
        self.copies = []

    def go(self, source, target, to):
        i = len(self.copies)
        copy = remote(source, target, self.send.at[i], self.recv.at[i], to)
        copy.start()
        self.copies.append(copy)
        return copy

    def stage(self, k):
        y, c, z, x = self.at
        own = self.own
        half = own.shape[3] // 2
        top, bottom = pl.ds(0, half), pl.ds(half, half)
        to_y, to_x, to_c = device(1 - y, c, z, x), device(y, c, z, 1 - x), device(y, 1 - c, z, x)
        if k > 0:
            arrived(self.wait)
        if k == 0:
            self.wait = [self.go(self.other.at[i], self.r1.at[i], to_c) for i in (0, 1)]
        elif k == 1:

            def piece(i, _):
                at = (i // 8, i // 2 % 4, i % 2)
                own[at] = own[at] + self.r1[at]
                return 0

            lax.fori_loop(0, 16, piece, 0)
            self.wait = [self.go(own.at[1 - y, :, :, top], self.r2.at[pl.ds(0, 4), :], to_y)]
            for i in (0, 1):
                self.wait.append(self.go(own.at[i, :, 1 - x, bottom], self.r2.at[pl.ds(4, 4), i], to_x))
        elif k == 2:

            def piece(i, _):
                b, d = i // 2, i % 2
                own[y, b, d, top] = own[y, b, d, top] + self.r2[b, d]
                own[d, b, x, bottom] = own[d, b, x, bottom] + self.r2[4 + b, d]
                return 0

            lax.fori_loop(0, 8, piece, 0)
            self.wait = [
                self.go(own.at[y, :, 1 - x, top], self.r3.at[0], to_x),
                self.go(own.at[1 - y, :, x, bottom], self.r3.at[1], to_y),
            ]
        elif k == 3:

            def piece(b, _):
                own[y, b, x, top] = own[y, b, x, top] + self.r3[0, b]
                own[y, b, x, bottom] = own[y, b, x, bottom] + self.r3[1, b]
                return 0

            lax.fori_loop(0, 4, piece, 0)
            self.wait = [
                self.go(own.at[y, z ^ i, x], self.r4.at[i - 1], device(y, c, z ^ i, x)) for i in (1, 2, 3)
            ]
        else:
            total = own[y, z, x].astype(F32)
            for i in range(3):
                total = total + self.r4[i].astype(F32)
            self.out[...] = total

    def drain(self):
        for copy in self.copies:
            copy.wait_send()
        self.copies = []


def adjoint_part(chunk, h, dt, xt, bb, cb, gt, a2, starts, later, keep, decays, pb, pc, rb, rc, ga, size):
    hs = pl.ds(h * 8, 8)
    a = [a2[n, hs, :] for n in range(DS)]
    base = chunk * size
    first = tuple(starts[chunk, n, hs, :] for n in range(DS))
    for n in range(DS):
        keep[n * 8 : n * 8 + 8, :] = first[n]

    def again(i, carry):
        t = base + i
        d = tile_at(dt, t, h)
        dx = d * tile_at(xt, t, h)
        new = []
        for n in range(DS):
            w = jnp.exp2(a[n] * d)
            s = w * carry[n] + dx * row_of(bb, t * DS + n)
            o = pl.multiple_of(i * 128 + n * 8, 8)
            decays[pl.ds(o, 8), :] = w
            keep[pl.ds(pl.multiple_of(o + 128, 8), 8), :] = s
            new.append(s)
        return tuple(new)

    lax.fori_loop(0, size, again, first, unroll=4)

    def back(j, carry):
        i = size - 1 - j
        t = base + i
        d = tile_at(dt, t, h)
        x = tile_at(xt, t, h)
        gy = tile_at(gt, t, h)
        dx = d * x
        slot = (j % 2) * 128
        new = []
        weighted, through_a = [], []
        for n in range(DS):
            o = pl.multiple_of(i * 128 + n * 8, 8)
            w = decays[pl.ds(o, 8), :]
            before = keep[pl.ds(o, 8), :]
            now = keep[pl.ds(pl.multiple_of(o + 128, 8), 8), :]
            g = carry[n] + gy * row_of(cb, t * DS + n)
            at = pl.ds(pl.multiple_of(slot + n * 8, 8), 8)
            pc[at, :] = now * gy
            pb[at, :] = g * dx
            weighted.append(g * row_of(bb, t * DS + n))
            g = g * w
            through = g * before
            through_a.append(through * a[n])
            ga[n, hs, :] += through * d
            new.append(g)
        while len(weighted) > 1:
            weighted = [weighted[i] + weighted[i + 1] for i in range(0, len(weighted), 2)]
            through_a = [through_a[i] + through_a[i + 1] for i in range(0, len(through_a), 2)]
        o = pl.ds(pl.multiple_of(t * 16 + h * 8, 8), 8)
        dt[o, :] = through_a[0] * LN2 + weighted[0] * x
        xt[o, :] = weighted[0] * d
        for src, dst in ((pb, rb), (pc, rc)):
            for m in range(2):
                parts = [src[pl.ds(slot + m * 64 + s, 8, stride=8), :] for s in range(8)]
                while len(parts) > 1:
                    parts = [parts[i] + parts[i + 1] for i in range(0, len(parts), 2)]
                q = pl.ds(pl.multiple_of(i * 16 + m * 8, 8), 8)
                if h == 0:
                    dst[q, :] = parts[0]
                else:
                    dst[q, :] += parts[0]
        return tuple(new)

    out = lax.fori_loop(0, size, back, tuple(later[n, hs, :] for n in range(DS)), unroll=2)
    for n in range(DS):
        later[n, hs, :] = out[n]


def collect_rows(chunk, size, rb, rc, gb, gc):
    ones = jnp.ones((128, 128), BF16)
    pick = lax.broadcasted_iota(jnp.int32, (128, 128), 0) % DS == lax.broadcasted_iota(jnp.int32, (128, 128), 1)

    def collect(i, _):
        o = pl.ds(pl.multiple_of(i * 128, 128), 128)
        for src, dst in ((rb, gb), (rc, gc)):
            v = src[o, :]
            hi = v.astype(BF16)
            lo = (v - hi.astype(F32)).astype(BF16)
            s = jnp.where(pick, dot(hi, ones) + dot(lo, ones), 0.0)
            dst[pl.ds(pl.multiple_of(chunk * size + i * 8, 8), 8), :] = jnp.sum(s.reshape(8, DS, 128), axis=1)
        return 0

    lax.fori_loop(0, size // 8, collect, 0)


BACK_IN = (
    "gated", "low", "normed", "gz", "dt", "xt", "bb", "cb", "gt", "a2", "starts", "so", "draw", "xs", "w0", "selt",
    "filt", "xin", "halo", "inx", "inz", "gain", "skipg", "tok", "cot",
)
BACK_LOAD = tuple(n for n in BACK_IN if n not in ("inx", "inz"))
BACK_OUT = ("tgrad", "gin", "gout", "gpack")
BACK_SCRATCH = BACK_LOAD + (
    "wbuf", "keep", "decays", "pb", "pc", "rb", "rc", "ga", "gb", "gc", "proj", "xp", "gp", "rawlow", "gproj", "dw", "w0g",
    "selg", "edge", "gx", "gn", "gaing",
    "own", "other", "r1", "r2", "r3", "r4", "pown", "pother", "p1", "p2", "p3", "p4",
    "load", "wsem", "send", "recv", "esend", "erecv",
)
BLOCKS = 4


def back_body(*refs):
    hbm = dict(zip(BACK_IN, refs))
    refs = refs[len(BACK_IN) :]
    o = dict(zip(BACK_OUT, refs))
    v = dict(zip(BACK_SCRATCH, refs[len(BACK_OUT) :]))
    loads = {}
    for i, name in enumerate(BACK_LOAD):
        loads[name] = pltpu.make_async_copy(hbm[name], v[name], v["load"].at[i])
        loads[name].start()

    def need(*names):
        for name in names:
            loads[name].wait()

    y, c, z, x = place()
    b, s = lax.axis_index("batch"), lax.axis_index("seq")
    peers = lax.axis_size("seq")
    greet(neighbours(y, c, z, x) + [(b, lax.rem(s + 1, peers)), (b, lax.rem(s + peers - 1, peers))])

    rows, di = v["gz"].shape
    width = v["normed"].shape[1]
    tiles = di // 128
    cols = di // BLOCKS
    half = width // 2
    owned = v["own"].shape[4]
    jobs = []

    def job(out):
        i = len(jobs)
        at = i % (2 * BLOCKS)
        jobs.append(
            Share(
                v["own"].at[at], v["other"].at[at], v["r1"].at[i], v["r2"].at[i], v["r3"].at[i], v["r4"].at[i],
                out, v["send"].at[i], v["recv"].at[i],
            )
        )

    for i in range(4):
        job(o["gout"].at[i // 2 * owned : (i // 2 + 1) * owned, i % 2 * half : (i % 2 + 1) * half])
    for i in range(BLOCKS):
        job(o["gin"].at[:, di + i * cols : di + (i + 1) * cols])
    for i in range(BLOCKS):
        job(o["gin"].at[:, i * cols : (i + 1) * cols])
    last = len(jobs)
    jobs.append(
        Share(
            v["pown"], v["pother"], v["p1"], v["p2"], v["p3"], v["p4"], o["gpack"], v["send"].at[last], v["recv"].at[last]
        )
    )
    tick = [0]
    begun, ready = [0], [0]

    def advance():
        for i in range(begun[0], ready[0]):
            k = tick[0] - i
            if 0 <= k < STAGES:
                jobs[i].stage(k)
        tick[0] += 1

    need("gated", "low")

    def out_blocks(core, dst):
        def block(i, _):
            first = pl.multiple_of(((i // 2) * 2 + core) * (di // 4) + (i % 2) * 256, 256)
            g = v["gated"][:, pl.ds(first, 256)]
            for q in range(2):
                r = dot_tn(g, v["low"][:, q * half : (q + 1) * half]).astype(BF16).reshape(2, 2, 2, owned, half)
                for p in range(2):
                    dst[p * 2 + q, i // 2, pl.ds((i % 2) * 2, 2)] = r[:, :, p]
            return 0

        lax.fori_loop(0, 4, block, 0)

    def in_blocks(core, dst, first, right):
        def block(i, _):
            n = v["normed"][:, pl.ds(pl.multiple_of((i * 2 + core) * (width // 4), 256), width // 4)]
            for q, g in enumerate(right):
                dst[first + q, i] = dot_tn(n, g()).astype(BF16).reshape(4, 2, owned, cols)
            return 0

        lax.fori_loop(0, 2, block, 0)

    out_blocks(1 - c, v["other"])
    ready[0] = 4
    advance()
    out_blocks(c, v["own"])
    need("normed", "gz")
    z_right = [lambda q=q: v["gz"][:, q * cols : (q + 1) * cols] for q in range(BLOCKS)]
    in_blocks(1 - c, v["other"], BLOCKS, z_right)
    ready[0] = 8
    advance()
    in_blocks(c, v["own"], BLOCKS, z_right)

    need("dt", "xt", "bb", "cb", "gt", "a2", "starts", "so")
    v["ga"][...] = jnp.zeros_like(v["ga"])
    chunks = v["starts"].shape[0]
    size = rows // chunks
    for chunk in reversed(range(chunks)):
        for h in range(2):
            adjoint_part(
                chunk, h, v["dt"], v["xt"], v["bb"], v["cb"], v["gt"], v["a2"], v["starts"], v["so"], v["keep"],
                v["decays"], v["pb"], v["pc"], v["rb"], v["rc"], v["ga"], size,
            )
            if tick[0] < 8 + STAGES - 1:
                advance()
        collect_rows(chunk, size, v["rb"], v["rc"], v["gb"], v["gc"])
    while tick[0] < 8 + STAGES - 1:
        advance()
    tick[0] = begun[0] = 2 * BLOCKS

    need("draw", "xs", "w0", "selt")
    v["proj"][:, 0:PACK0] = dot_nt(v["xs"][...], v["selt"][...])
    low = v["proj"][:, 0:DTR].astype(BF16)
    v["dw"][...] = v["w0"][DELTA0 : DELTA0 + DTR, :].astype(BF16)
    w0g = v["w0g"]

    def raw(k, _):
        at = lanes(k)
        g = v["dt"][pl.ds(k, rows, stride=tiles), :] * sigmoid(v["draw"][:, at])
        w0g[5:6, at] = jnp.sum(g, axis=0, keepdims=True)
        gl = g.astype(BF16)
        v["rawlow"][:, at] = gl
        w0g[DELTA0 : DELTA0 + DTR, at] = dot_tn(low, gl)
        return 0

    lax.fori_loop(0, tiles, raw, 0)
    v["gproj"][:, 0:DTR] = dot_nt(v["rawlow"][...], v["dw"][...]).astype(BF16)
    v["gproj"][:, DTR : DTR + DS] = v["gb"][:, 0:DS].astype(BF16)
    v["gproj"][:, DTR + DS : DTR + 2 * DS] = v["gc"][:, 0:DS].astype(BF16)
    need("filt", "xin", "halo")
    not_first = jnp.where(s > 0, 1.0, 0.0)
    not_last = jnp.where(s < peers - 1, 1.0, 0.0)

    def point(k, _):
        at = lanes(k)
        gp = v["gproj"][...]
        v["selg"][:, at] = dot_tn(gp, v["xs"][:, at])
        into = dot(gp, v["selt"][:, at])
        here = pl.ds(k, rows, stride=tiles)
        g = v["gt"][here, :] * v["w0"][6:7, at] + v["xt"][here, :] + into
        f = v["filt"][:, at]
        sg = sigmoid(f)
        gf = g * (sg * (1.0 + f * (1.0 - sg)))
        v["filt"][:, at] = gf
        w0g[4:5, at] = jnp.sum(gf, axis=0, keepdims=True)
        v["xp"][0:16, :] = v["halo"][:, at].astype(F32) * not_first
        v["xp"][16 : 16 + rows, :] = v["xin"][:, at].astype(F32)
        for tap in range(KW):
            lo = 16 - (KW - 1) + tap
            w0g[tap : tap + 1, at] = jnp.sum(gf * v["xp"][lo : lo + rows, :], axis=0, keepdims=True)
        return 0

    edges = []

    def points(q):
        lax.fori_loop(q * (tiles // BLOCKS), (q + 1) * (tiles // BLOCKS), point, 0)
        at = pl.ds(q * cols, cols)
        copy = remote(
            v["filt"].at[pl.ds(0, 8), at], v["edge"].at[:, at], v["esend"].at[q], v["erecv"].at[q],
            (b, lax.rem(s + peers - 1, peers)),
        )
        copy.start()
        edges.append(copy)

    weights = {}

    def fetch(i):
        source = hbm["inx"].at[i] if i < WX else hbm["inz"].at[i - WX]
        weights[i] = pltpu.make_async_copy(source, v["wbuf"].at[i % 2], v["wsem"].at[i])
        weights[i].start()

    fetch(0)
    fetch(1)

    def blocks(q):
        edges[q].wait_recv()

        def conv(k, _):
            at = lanes(k)
            v["gp"][0:rows, :] = v["filt"][:, at]
            v["gp"][rows : rows + 8, :] = v["edge"][:, at] * not_last
            total = jnp.zeros((rows, 128), F32)
            for tap in range(KW):
                lo = KW - 1 - tap
                total = total + v["w0"][tap : tap + 1, at] * v["gp"][lo : lo + rows, :]
            v["gx"][:, at] = total.astype(BF16)
            return 0

        lax.fori_loop(q * (tiles // BLOCKS), (q + 1) * (tiles // BLOCKS), conv, 0)
        right = [lambda: v["gx"][:, q * cols : (q + 1) * cols]]
        jobs[q].drain()
        in_blocks(1 - c, v["other"], q, right)
        ready[0] = 2 * BLOCKS + q + 1
        advance()
        in_blocks(c, v["own"], q, right)

    def into_rows(i):
        weights[i].wait()
        g = v["gx"] if i < WX else v["gz"]
        q = i % WX
        for d in range(2):
            w = v["wbuf"][i % 2].reshape(width, cols)[d * half : (d + 1) * half]
            part = dot_nt(g[:, q * cols : (q + 1) * cols], w)
            at = slice(d * half, (d + 1) * half)
            v["gn"][:, at] = part if i == 0 else v["gn"][:, at] + part
        if i + 2 < 2 * WX:
            fetch(i + 2)

    points(0)
    for q in range(1, BLOCKS):
        points(q)
        blocks(q - 1)
    into_rows(0)
    blocks(BLOCKS - 1)
    into_rows(1)
    into_rows(2)
    advance()
    into_rows(3)
    into_rows(4)
    into_rows(5)
    advance()
    into_rows(6)
    into_rows(7)
    need("tok", "cot", "gain")
    advance()

    def rows_of(i, total):
        r = pl.ds(pl.multiple_of(i * 8, 8), 8)
        u = v["tok"][r, :]
        g = v["gn"][r, :]
        scale = lax.rsqrt(jnp.mean(u * u, axis=-1, keepdims=True) + EPS)
        w = g * v["gain"][0:1, :]
        mean = jnp.mean(w * u, axis=-1, keepdims=True)
        o["tgrad"][r, :] = v["cot"][r, :] + scale * w - u * (scale * scale * scale * mean)
        return total + g * u * scale

    total = lax.fori_loop(0, rows // 8, rows_of, jnp.zeros((8, width), F32))
    v["gaing"][...] = jnp.broadcast_to(jnp.sum(total, axis=0, keepdims=True), (8, width))
    need("skipg")
    w0g[6:7, :] = v["skipg"][0:1, :]
    w0g[7:8, :] = jnp.zeros((1, di), F32)
    w0g[DELTA0 + DTR : PACK0, :] = jnp.zeros((PACK0 - DELTA0 - DTR, di), F32)
    for k in range(tiles):
        w0g[ALOG0 : ALOG0 + DS, k * 128 : (k + 1) * 128] = v["ga"][:, k, :] * v["a2"][:, k, :] * LN2
    low_half = lax.broadcasted_iota(jnp.int32, (PACK0, 128), 1) < 64

    def pack(core, dst):
        def pair(i, _):
            j = i // 4 * 8 + core * 4 + i % 4
            at = lanes(j)
            l, r = w0g[:, at], v["selg"][:, at]
            dst[i // 4, i % 4, 0, 0:PACK0, :] = jnp.where(low_half, l, pltpu.roll(r, 64, 1)).astype(BF16)
            dst[i // 4, i % 4, 1, 0:PACK0, :] = jnp.where(low_half, pltpu.roll(l, 64, 1), r).astype(BF16)
            g = jnp.broadcast_to(v["gaing"][0:1, lanes(j // 2)], (PACK - PACK0, 128)).astype(BF16)
            for d in range(2):
                dst[i // 4, i % 4, d, PACK0:PACK, :] = g
            return 0

        lax.fori_loop(0, 8, pair, 0)

    pack(1 - c, v["pother"])
    ready[0] = last + 1
    jobs[last].stage(0)
    pack(c, v["pown"])
    k = 1
    while k < STAGES or tick[0] < last + STAGES - 1:
        if tick[0] < last + STAGES - 1:
            ready[0] = last
            advance()
        if k < STAGES:
            jobs[last].stage(k)
            k += 1
    for it in jobs:
        it.drain()
    for it in edges:
        it.wait_send()


def back(f, tok, cot):
    rows, di = f["gz"].shape
    width = tok.shape[1]
    tiles = di // 128
    cols = di // BLOCKS
    chunks = f["starts"].shape[0]
    size = rows // chunks
    lead = (2, 4, 2)
    owned = width // 32
    inputs = dict(f, tok=tok, cot=cot)
    shapes = {n: (inputs[n].shape, inputs[n].dtype) for n in BACK_IN}
    shapes["a2"] = shapes["so"] = ((DS, tiles, 128), F32)

    def sums(prefix, n, rows, cols, held):
        names = ("own", "other", "r1", "r2", "r3", "r4") if not prefix else ("pown", "pother", "p1", "p2", "p3", "p4")
        dims = (
            lead + (rows, cols), lead + (rows, cols), lead + (rows, cols), (8, 2, rows // 2, cols),
            (2, 4, rows // 2, cols), (3, rows, cols),
        )
        for i, (name, d) in enumerate(zip(names, dims)):
            k = (held if i < 2 else n,) if not prefix else ()
            shapes[name] = (k + d, BF16)

    sums("", 3 * BLOCKS, owned, cols, 2 * BLOCKS)
    sums("p", 1, PACK, 128, 1)
    tall = ((size * DS, 128), F32)
    shapes.update(
        wbuf=((2, 2, 2, 4, 2, owned, cols), BF16), keep=(((size + 1) * 128, 128), F32), decays=((size * 128, 128), F32),
        pb=((256, 128), F32), pc=((256, 128), F32), rb=tall, rc=tall, ga=((DS, tiles, 128), F32), gb=((rows, 128), F32),
        gc=((rows, 128), F32), proj=((rows, 128), F32), xp=((rows + 16, 128), F32), gp=((rows + 8, 128), F32),
        rawlow=((rows, di), BF16), gproj=((rows, PACK0), BF16), dw=((DTR, di), BF16), w0g=((PACK0, di), F32),
        selg=((PACK0, di), F32), edge=((8, di), F32), gx=((rows, di), BF16), gn=((rows, width), F32), gaing=((8, width), F32),
    )
    dma = pltpu.SemaphoreType.DMA
    n_jobs = 3 * BLOCKS + 1
    sems = {
        "load": dma((len(BACK_LOAD),)), "wsem": dma((2 * WX,)), "send": dma((n_jobs, Share.COPIES)),
        "recv": dma((n_jobs, Share.COPIES)), "esend": dma((BLOCKS,)), "erecv": dma((BLOCKS,)),
    }
    return pl.pallas_call(
        back_body,
        out_shape=(
            sds((rows, width), F32), sds((owned, 2 * di), F32), sds((di // 32, width), F32), sds((PACK, 128), F32),
        ),
        in_specs=[ANY] * len(BACK_IN),
        out_specs=(VM,) * 4,
        scratch_shapes=[sems[n] if n in sems else pltpu.VMEM(*shapes[n]) for n in BACK_SCRATCH],
        compiler_params=pltpu.CompilerParams(collective_id=1, has_side_effects=True, vmem_limit_bytes=GRANT),
    )(*(inputs[n] for n in BACK_IN))


def on_slice(tokens, cotangent, norm_gain, in_weight, conv_weight, conv_bias, select_weight, delta_weight, delta_bias, a_log, skip_gain, out_weight):
    sizes = (lax.axis_size("batch"), lax.axis_size("seq"))
    me = lax.axis_index("batch") * sizes[1] + lax.axis_index("seq")
    tok, cot = tokens[0], cotangent[0]
    rows = tok.shape[0]
    own = conv_bias.shape[0]
    left = jnp.concatenate(
        [
            conv_weight, conv_bias[None], delta_bias[None], skip_gain[None], jnp.zeros((1, own), BF16),
            a_log, delta_weight, jnp.zeros((PACK0 - DELTA0 - DTR, own), BF16),
        ],
        axis=0,
    )
    gain_row = lax.dynamic_update_slice(jnp.zeros((128,), BF16), norm_gain, ((me % 4) * norm_gain.shape[0],))
    pack = jnp.concatenate(
        [
            jnp.concatenate([left, select_weight.T], axis=1),
            jnp.broadcast_to(gain_row[None], (PACK - PACK0, 128)),
        ],
        axis=0,
    )
    f = front(tok, cot, in_weight, out_weight, pack, sizes[1], rows // 32)
    tokens_grad, g_in, g_out, g_pack = back(f, tok, cot)
    left, right = g_pack[:PACK0, :own], g_pack[:PACK0, own:]
    g_gain = lax.dynamic_slice(g_pack[PACK0], ((me % 4) * norm_gain.shape[0],), norm_gain.shape)
    grads = (
        g_gain, g_in, left[0:KW], left[4], right.T,
        left[DELTA0 : DELTA0 + DTR], left[5], left[ALOG0 : ALOG0 + DS], left[6], g_out,
    )
    return (f["block"][None], tokens_grad[None]) + grads


def on_device(tokens, cotangent, norm_gain, in_weight, conv_weight, conv_bias, select_weight, delta_weight, delta_bias, a_log, skip_gain, out_weight):
    axes = ("batch", "seq")
    sizes = (lax.axis_size("batch"), lax.axis_size("seq"))
    if sizes == (4, 8):
        return on_slice(
            tokens, cotangent, norm_gain, in_weight, conv_weight, conv_bias, select_weight, delta_weight, delta_bias,
            a_log, skip_gain, out_weight,
        )
    tok, cot = tokens[0], cotangent[0]
    rows, width = tok.shape
    di = out_weight.shape[0] * sizes[0] * sizes[1]
    tiles = di // 128
    full = lambda v, axis: lax.all_gather(v, axes, axis=axis, tiled=True)
    in_full = full(in_weight, 0)
    in_x, in_z = in_full[:, :di], in_full[:, di:]
    out_full = full(out_weight, 0)
    sel_t = full(select_weight, 0).T
    gain = full(norm_gain, 0)[None].astype(F32)
    w0 = jnp.concatenate(
        [
            full(conv_weight, 1), full(conv_bias, 0)[None], full(delta_bias, 0)[None], full(skip_gain, 0)[None],
            jnp.zeros((1, di), BF16), full(a_log, 1), full(delta_weight, 1),
            jnp.zeros((PACK0 - DELTA0 - DTR, di), BF16),
        ],
        axis=0,
    ).astype(F32)

    flat = sds((rows * tiles, 128), F32)
    wide = sds((rows, di), F32)
    spread = sds((rows * DS, 128), F32)
    carry = sds((DS, tiles, 128), F32)

    normed, x_in = kernel_call(
        inproj_body, (sds((rows, width), BF16), sds((rows, di), BF16)), 3
    )(tok, gain, in_x)
    halo = shift(x_in[rows - 16 :], 1)
    filt, xs, xt, draw, dt, bb, cb = kernel_call(
        conv_body,
        (wide, sds((rows, di), BF16), flat, wide, flat, spread, spread),
        4,
        [pltpu.VMEM((rows, 128), F32), pltpu.VMEM((rows + 16, 128), F32)],
    )(x_in, halo, w0, sel_t)
    a2, total, end = kernel_call(lightf_body, (carry, carry, carry), 4)(dt, xt, bb, w0)
    gate, gzp, gt, low, adj = kernel_call(
        gate_body, (wide, wide, flat, sds((rows, width), BF16), carry), 7
    )(normed, in_z, cot, out_full, dt, cb, a2)
    state_in = carried_in(total, end, False)
    state_out = carried_in(total, adj, True)
    chunks = rows // 64
    starts, block_out, gz, out_grad, z_grad, skip_grad = kernel_call(
        forward_body,
        (
            sds((chunks, DS, tiles, 128), F32), sds((rows, width), F32), sds((rows, di), BF16),
            sds((di, width), BF16), sds((width, di), BF16), sds((1, di), F32),
        ),
        14,
        [pltpu.VMEM((rows * tiles, 128), F32), pltpu.VMEM((rows, di), BF16), pltpu.VMEM((8, 128), F32)],
    )(state_in, dt, xt, bb, cb, a2, w0, gate, gzp, gt, tok, low, normed, out_full)
    tall = pltpu.VMEM((rows * DS, 128), F32)
    gdt, gat, gb, gc, ga = kernel_call(
        backward_body,
        (flat, flat, sds((rows, 128), F32), sds((rows, 128), F32), carry),
        8,
        [
            pltpu.VMEM((65 * 128, 128), F32), pltpu.VMEM((64 * 128, 128), F32), pltpu.VMEM((256, 128), F32),
            pltpu.VMEM((256, 128), F32), tall, tall,
        ],
    )(state_out, starts, dt, xt, bb, cb, gt, a2)
    gf, w0g, selg = kernel_call(
        tail_body,
        (wide, sds((PACK0, di), F32), sds((PACK0, di), F32)),
        12,
        [
            pltpu.VMEM((rows, 128), F32), pltpu.VMEM((rows + 16, 128), F32), pltpu.VMEM((rows, di), BF16),
            pltpu.VMEM((rows, PACK0), BF16), pltpu.VMEM((DTR, di), BF16),
        ],
    )(gdt, gat, gb, gc, gt, draw, filt, x_in, halo, xs, w0, sel_t)
    edge = shift(gf[:8], -1)
    tokens_grad, x_grad, gain_grad = kernel_call(
        last_body,
        (sds((rows, width), F32), sds((width, di), BF16), sds((1, width), F32)),
        10,
        [pltpu.VMEM((rows + 8, 128), F32), pltpu.VMEM((rows, di), BF16), pltpu.VMEM((rows, width), F32)],
    )(gf, edge, w0, gz, normed, tok, cot, gain, in_x, in_z)

    share = lambda v, d: lax.psum_scatter(v.astype(F32), axes, scatter_dimension=d, tiled=True)
    ga_flat = ga.reshape(DS, di)
    grads = (
        share(gain_grad[0], 0), share(jnp.concatenate([x_grad, z_grad], axis=1), 0), share(w0g[0:KW], 1),
        share(w0g[4], 0), share(selg.T, 0), share(w0g[DELTA0 : DELTA0 + DTR], 1), share(w0g[5], 0),
        share(ga_flat, 1), share(skip_grad[0], 0), share(out_grad, 0),
    )
    return (block_out[None], tokens_grad[None]) + grads


def solution(mesh):
    both = ("batch", "seq")
    first, second = P(both), P(None, both)
    matrix = P(both, None)
    whole = P("batch", "seq", None)
    weights = (first, matrix, second, first, matrix, second, first, second, first, matrix)
    return jax.shard_map(
        on_device,
        mesh=mesh,
        in_specs=(whole, whole) + weights,
        out_specs=(whole, whole) + weights,
        check_vma=False,
    )
```

```python
import functools

import jax
import jax.numpy as jnp
from jax import lax
from jax.experimental import pallas as pl
from jax.experimental.pallas import tpu as pltpu
from jax.sharding import PartitionSpec as P

DS = 16
KW = 4
DTR = 64
EPS = 1e-05
LOG2E = 1.4426950408889634
LN2 = 0.6931471805599453
F32 = jnp.float32
BF16 = jnp.bfloat16
MESH = pl.DeviceIdType.MESH
VM = pl.BlockSpec(memory_space=pltpu.VMEM)
ANY = pl.BlockSpec(memory_space=pl.ANY)
GRANT = 60 << 20
ALOG0, DELTA0, PACK0, PACK = 8, 24, 96, 128


def sds(shape, dtype):
    return jax.ShapeDtypeStruct(shape, dtype)


def kernel_call(body, outs, n_in, scratch=(), flops=1e9, **params):
    return pl.pallas_call(
        body,
        out_shape=outs,
        in_specs=[VM] * n_in,
        out_specs=jax.tree.map(lambda _: VM, outs),
        scratch_shapes=list(scratch),
        cost_estimate=pl.CostEstimate(flops=int(flops), bytes_accessed=8 << 20, transcendentals=0),
        compiler_params=pltpu.CompilerParams(vmem_limit_bytes=GRANT, **params),
    )


def sigmoid(v):
    return 1.0 / (1.0 + jnp.exp(-v))


def dot(a, b):
    return jnp.dot(a, b, preferred_element_type=F32)


def dot_nt(a, b):
    return lax.dot_general(a, b, (((1,), (1,)), ((), ())), preferred_element_type=F32)


def dot_tn(a, b):
    return lax.dot_general(a, b, (((0,), (0,)), ((), ())), preferred_element_type=F32)


def lanes(k, width=128):
    return pl.ds(pl.multiple_of(k * width, width), width)


def inproj_body(tok_ref, gain_ref, inx_ref, normed_ref, xin_ref):
    rows = tok_ref.shape[0]

    def norm(i, _):
        r = pl.ds(pl.multiple_of(i * 16, 16), 16)
        u = tok_ref[r, :]
        scale = lax.rsqrt(jnp.mean(u * u, axis=-1, keepdims=True) + EPS)
        normed_ref[r, :] = (u * scale * gain_ref[...]).astype(BF16)
        return 0

    lax.fori_loop(0, rows // 16, norm, 0)
    width = 512

    def mm(j, _):
        c = lanes(j, width)
        xin_ref[:, c] = dot(normed_ref[...], inx_ref[:, c]).astype(BF16)
        return 0

    lax.fori_loop(0, inx_ref.shape[1] // width, mm, 0)


def conv_body(xin_ref, halo_ref, w0_ref, selt_ref, filt_ref, xs_ref, xt_ref, draw_ref, dt_ref, bb_ref, cb_ref, proj, xp):
    rows, di = xin_ref.shape
    tiles = di // 128
    xp_rows = 16 + rows

    def conv(k, _):
        c = lanes(k)
        xp[0:16, :] = halo_ref[:, c].astype(F32)
        xp[16:xp_rows, :] = xin_ref[:, c].astype(F32)
        for q in range(2):
            r0 = q * (rows // 2)
            f = w0_ref[4:5, c]
            for tap in range(KW):
                lo = 16 - (KW - 1) + tap + r0
                f = f + w0_ref[tap : tap + 1, c] * xp[lo : lo + rows // 2, :]
            s = (f * sigmoid(f)).astype(BF16)
            filt_ref[r0 : r0 + rows // 2, c] = f
            xs_ref[r0 : r0 + rows // 2, c] = s
            xt_ref[pl.ds(r0 * tiles + k, rows // 2, stride=tiles), :] = s.astype(F32)
        return 0

    lax.fori_loop(0, tiles, conv, 0)
    proj[:, 0:96] = dot_nt(xs_ref[...], selt_ref[...])
    low = proj[:, 0:DTR].astype(BF16)

    def delta(k, _):
        c = lanes(k)
        raw = dot(low, w0_ref[DELTA0 : DELTA0 + DTR, c].astype(BF16)) + w0_ref[5:6, c]
        draw_ref[:, c] = raw
        dt_ref[pl.ds(k, rows, stride=tiles), :] = jnp.maximum(raw, 0.0) + jnp.log1p(jnp.exp(-jnp.abs(raw)))
        return 0

    lax.fori_loop(0, tiles, delta, 0)
    row_ids = lax.broadcasted_iota(jnp.int32, (128, 128), 0) % DS
    lane_ids = lax.broadcasted_iota(jnp.int32, (128, 128), 1)
    ones = jnp.ones((128, 128), BF16)

    def spread(i, _):
        r = pl.ds(pl.multiple_of(i * 8, 8), 8)
        p = proj[r, :]
        tall = jnp.broadcast_to(p[:, None, :], (8, DS, 128)).reshape(128, 128)
        o = pl.ds(pl.multiple_of(i * 128, 128), 128)
        for first, ref in ((DTR, bb_ref), (DTR + DS, cb_ref)):
            v = jnp.where(lane_ids == row_ids + first, tall, 0.0)
            hi = v.astype(BF16)
            v = v - hi.astype(F32)
            mid = v.astype(BF16)
            lo = (v - mid.astype(F32)).astype(BF16)
            ref[o, :] = (dot(hi, ones) + dot(mid, ones)) + dot(lo, ones)
        return 0

    lax.fori_loop(0, rows // 8, spread, 0)


def row_of(ref, index):
    return ref[pl.ds(index, 8, stride=0), :]


def tile_at(ref, t, h):
    return ref[pl.ds(pl.multiple_of(t * 16 + h * 8, 8), 8), :]


def light_forward(dt_ref, xt_ref, bb_ref, a2_ref, total_ref, end_ref, rows):
    for h in range(2):
        hs = pl.ds(h * 8, 8)
        a = [a2_ref[n, hs, :] for n in range(DS)]

        def step(t, carry):
            state, run = carry
            d = tile_at(dt_ref, t, h)
            dx = d * tile_at(xt_ref, t, h)
            new = tuple(
                jnp.exp2(a[n] * d) * state[n] + dx * row_of(bb_ref, t * DS + n) for n in range(DS)
            )
            return (new, run + d)

        zero = jnp.zeros((8, 128), F32)
        state, run = lax.fori_loop(0, rows, step, ((zero,) * DS, zero), unroll=4)
        for n in range(DS):
            end_ref[n, hs, :] = state[n]
            total_ref[n, hs, :] = jnp.exp2(a[n] * run)


def light_backward(dt_ref, gt_ref, cb_ref, a2_ref, adj_ref, rows):
    for h in range(2):
        hs = pl.ds(h * 8, 8)
        a = [a2_ref[n, hs, :] for n in range(DS)]

        def step(i, carry):
            t = rows - 1 - i
            d = tile_at(dt_ref, t, h)
            g = tile_at(gt_ref, t, h)
            return tuple(
                jnp.exp2(a[n] * d) * (carry[n] + g * row_of(cb_ref, t * DS + n)) for n in range(DS)
            )

        out = lax.fori_loop(0, rows, step, (jnp.zeros((8, 128), F32),) * DS, unroll=4)
        for n in range(DS):
            adj_ref[n, hs, :] = out[n]


def lightf_body(dt_ref, xt_ref, bb_ref, w0_ref, a2_ref, total_ref, end_ref):
    rows = dt_ref.shape[0] // 16
    for k in range(16):
        a2_ref[:, k, :] = -jnp.exp(w0_ref[ALOG0 : ALOG0 + DS, k * 128 : (k + 1) * 128]) * LOG2E
    light_forward(dt_ref, xt_ref, bb_ref, a2_ref, total_ref, end_ref, rows)


def gate_body(normed_ref, inz_ref, cot_ref, out_ref, dt_ref, cb_ref, a2_ref, gate_ref, gzp_ref, gt_ref, low_ref, adj_ref):
    rows, di = gate_ref.shape
    tiles = di // 128
    low_ref[...] = cot_ref[...].astype(BF16)
    width = 512

    def block(j, _):
        c = lanes(j, width)
        gate_ref[:, c] = dot(normed_ref[...], inz_ref[:, c])
        gzp_ref[:, c] = dot_nt(low_ref[...], out_ref[c, :])
        return 0

    lax.fori_loop(0, di // width, block, 0)

    def point(k, _):
        c = lanes(k)
        for q in range(4):
            r = slice(q * (rows // 4), (q + 1) * (rows // 4))
            z = gate_ref[r, c]
            gg = gzp_ref[r, c]
            s = sigmoid(z)
            gate = z * s
            gate_ref[r, c] = gate
            gzp_ref[r, c] = gg * s * (1.0 + z * (1.0 - s))
            gt_ref[pl.ds(q * (rows // 4) * tiles + k, rows // 4, stride=tiles), :] = gg * gate
        return 0

    lax.fori_loop(0, tiles, point, 0)
    light_backward(dt_ref, gt_ref, cb_ref, a2_ref, adj_ref, rows)


def forward_body(
    si_ref, dt_ref, xt_ref, bb_ref, cb_ref, a2_ref, w0_ref, gate_ref, gzp_ref, gt_ref, tok_ref, low_ref, normed_ref, out_ref,
    starts_ref, block_ref, gz_ref, ograd_ref, zgrad_ref, skipg_ref, yt, gated, low_t,
):
    chunks = starts_ref.shape[0]
    rows, di = gate_ref.shape
    tiles = di // 128
    size = rows // chunks
    for h in range(2):
        hs = pl.ds(h * 8, 8)
        a = [a2_ref[n, hs, :] for n in range(DS)]
        state = tuple(si_ref[n, hs, :] for n in range(DS))
        for chunk in range(chunks):
            for n in range(DS):
                starts_ref[chunk, n, hs, :] = state[n]

            def step(i, carry):
                t = chunk * size + i
                d = tile_at(dt_ref, t, h)
                dx = d * tile_at(xt_ref, t, h)
                new, parts = [], []
                for n in range(DS):
                    s = jnp.exp2(a[n] * d) * carry[n] + dx * row_of(bb_ref, t * DS + n)
                    parts.append(s * row_of(cb_ref, t * DS + n))
                    new.append(s)
                while len(parts) > 1:
                    parts = [parts[i] + parts[i + 1] for i in range(0, len(parts), 2)]
                yt[pl.ds(pl.multiple_of(t * 16 + h * 8, 8), 8), :] = parts[0]
                return tuple(new)

            state = lax.fori_loop(0, size, step, state, unroll=4)

    def point(k, _):
        c = lanes(k)
        total = jnp.zeros((8, 128), F32)
        for q in range(4):
            r = slice(q * (rows // 4), (q + 1) * (rows // 4))
            here = pl.ds(q * (rows // 4) * tiles + k, rows // 4, stride=tiles)
            x = xt_ref[here, :]
            y = yt[here, :] + w0_ref[6:7, c] * x
            gated[r, c] = (y * gate_ref[r, c]).astype(BF16)
            gz_ref[r, c] = (gzp_ref[r, c] * y).astype(BF16)
            total = total + jnp.sum((gt_ref[here, :] * x).reshape(-1, 8, 128), axis=0)
        skipg_ref[:, c] = jnp.sum(total, axis=0, keepdims=True)
        return 0

    lax.fori_loop(0, tiles, point, 0)

    def project(j, _):
        c = lanes(j, 256)
        block_ref[:, c] = tok_ref[:, c] + dot(gated[...], out_ref[:, c])
        return 0

    lax.fori_loop(0, tok_ref.shape[1] // 256, project, 0)

    def wide(j, _):
        c = lanes(j, 256)
        ograd_ref[c, :] = dot_tn(gated[:, c], low_ref[...]).astype(BF16)
        return 0

    lax.fori_loop(0, di // 256, wide, 0)

    def wide_z(j, _):
        c = lanes(j, 256)
        zgrad_ref[:, c] = dot_tn(normed_ref[...], gz_ref[:, c]).astype(BF16)
        return 0

    lax.fori_loop(0, di // 256, wide_z, 0)


def backward_body(
    so_ref, starts_ref, dt_ref, xt_ref, bb_ref, cb_ref, gt_ref, a2_ref,
    gdt_ref, gat_ref, gb_ref, gc_ref, ga_ref, keep, decays, pb, pc, rb, rc,
):
    chunks = starts_ref.shape[0]
    rows = dt_ref.shape[0] // 16
    size = rows // chunks
    zero = jnp.zeros((8, 128), F32)
    for h in range(2):
        hs = pl.ds(h * 8, 8)
        a = [a2_ref[n, hs, :] for n in range(DS)]
        for n in range(DS):
            ga_ref[n, hs, :] = zero
        later = tuple(so_ref[n, hs, :] for n in range(DS))
        for chunk in reversed(range(chunks)):
            base = chunk * size
            first = tuple(starts_ref[chunk, n, hs, :] for n in range(DS))
            for n in range(DS):
                keep[n * 8 : n * 8 + 8, :] = first[n]

            def again(i, carry):
                t = base + i
                d = tile_at(dt_ref, t, h)
                dx = d * tile_at(xt_ref, t, h)
                new = []
                for n in range(DS):
                    w = jnp.exp2(a[n] * d)
                    s = w * carry[n] + dx * row_of(bb_ref, t * DS + n)
                    o = pl.multiple_of(i * 128 + n * 8, 8)
                    decays[pl.ds(o, 8), :] = w
                    keep[pl.ds(pl.multiple_of(o + 128, 8), 8), :] = s
                    new.append(s)
                return tuple(new)

            lax.fori_loop(0, size, again, first, unroll=4)

            def back(j, carry):
                i = size - 1 - j
                t = base + i
                d = tile_at(dt_ref, t, h)
                x = tile_at(xt_ref, t, h)
                gy = tile_at(gt_ref, t, h)
                dx = d * x
                slot = (j % 2) * 128
                new = []
                weighted, through_a = [], []
                for n in range(DS):
                    o = pl.multiple_of(i * 128 + n * 8, 8)
                    w = decays[pl.ds(o, 8), :]
                    before = keep[pl.ds(o, 8), :]
                    now = keep[pl.ds(pl.multiple_of(o + 128, 8), 8), :]
                    g = carry[n] + gy * row_of(cb_ref, t * DS + n)
                    at = pl.ds(pl.multiple_of(slot + n * 8, 8), 8)
                    pc[at, :] = now * gy
                    pb[at, :] = g * dx
                    weighted.append(g * row_of(bb_ref, t * DS + n))
                    g = g * w
                    through = g * before
                    through_a.append(through * a[n])
                    ga_ref[n, hs, :] += through * d
                    new.append(g)
                while len(weighted) > 1:
                    weighted = [weighted[i] + weighted[i + 1] for i in range(0, len(weighted), 2)]
                    through_a = [through_a[i] + through_a[i + 1] for i in range(0, len(through_a), 2)]
                o = pl.ds(pl.multiple_of(t * 16 + h * 8, 8), 8)
                gdt_ref[o, :] = through_a[0] * LN2 + weighted[0] * x
                gat_ref[o, :] = weighted[0] * d
                for src, dst in ((pb, rb), (pc, rc)):
                    for m in range(2):
                        parts = [src[pl.ds(slot + m * 64 + s, 8, stride=8), :] for s in range(8)]
                        while len(parts) > 1:
                            parts = [parts[i] + parts[i + 1] for i in range(0, len(parts), 2)]
                        q = pl.ds(pl.multiple_of(t * 16 + m * 8, 8), 8)
                        if h == 0:
                            dst[q, :] = parts[0]
                        else:
                            dst[q, :] += parts[0]
                return tuple(new)

            later = lax.fori_loop(0, size, back, later, unroll=2)
    for n in range(DS):
        ga_ref[n] = ga_ref[n] * a2_ref[n] * LN2
    ones = jnp.ones((128, 128), BF16)
    pick = lax.broadcasted_iota(jnp.int32, (128, 128), 0) % DS == lax.broadcasted_iota(jnp.int32, (128, 128), 1)

    def collect(i, _):
        o = pl.ds(pl.multiple_of(i * 128, 128), 128)
        for src, dst in ((rb, gb_ref), (rc, gc_ref)):
            v = src[o, :]
            hi = v.astype(BF16)
            lo = (v - hi.astype(F32)).astype(BF16)
            s = jnp.where(pick, dot(hi, ones) + dot(lo, ones), 0.0)
            dst[pl.ds(pl.multiple_of(i * 8, 8), 8), :] = jnp.sum(s.reshape(8, DS, 128), axis=1)
        return 0

    lax.fori_loop(0, rows // 8, collect, 0)


def tail_body(
    gdt_ref, gat_ref, gb_ref, gc_ref, gt_ref, draw_ref, filt_ref, xin_ref, halo_ref, xs_ref, w0_ref, selt_ref,
    gf_ref, w0g_ref, selg_ref, proj, xp, raw_low, gproj, dw,
):
    rows, di = draw_ref.shape
    tiles = di // 128
    proj[:, 0:96] = dot_nt(xs_ref[...], selt_ref[...])
    low = proj[:, 0:DTR].astype(BF16)
    dw[...] = w0_ref[DELTA0 : DELTA0 + DTR, :].astype(BF16)

    def raw(k, _):
        c = lanes(k)
        g = gdt_ref[pl.ds(k, rows, stride=tiles), :] * sigmoid(draw_ref[:, c])
        w0g_ref[5:6, c] = jnp.sum(g, axis=0, keepdims=True)
        gl = g.astype(BF16)
        raw_low[:, c] = gl
        w0g_ref[DELTA0 : DELTA0 + DTR, c] = dot_tn(low, gl)
        return 0

    lax.fori_loop(0, tiles, raw, 0)
    gproj[:, 0:DTR] = dot_nt(raw_low[...], dw[...]).astype(BF16)
    gproj[:, DTR : DTR + DS] = gb_ref[:, 0:DS].astype(BF16)
    gproj[:, DTR + DS : DTR + 2 * DS] = gc_ref[:, 0:DS].astype(BF16)

    def point(k, _):
        c = lanes(k)
        gp = gproj[...]
        selg_ref[:, c] = dot_tn(gp, xs_ref[:, c])
        back = dot(gp, selt_ref[:, c])
        here = pl.ds(k, rows, stride=tiles)
        ga = gt_ref[here, :] * w0_ref[6:7, c] + gat_ref[here, :] + back
        f = filt_ref[:, c]
        s = sigmoid(f)
        gf = ga * (s * (1.0 + f * (1.0 - s)))
        gf_ref[:, c] = gf
        w0g_ref[4:5, c] = jnp.sum(gf, axis=0, keepdims=True)
        xp[0:16, :] = halo_ref[:, c].astype(F32)
        xp[16 : 16 + rows, :] = xin_ref[:, c].astype(F32)
        for tap in range(KW):
            lo = 16 - (KW - 1) + tap
            w0g_ref[tap : tap + 1, c] = jnp.sum(gf * xp[lo : lo + rows, :], axis=0, keepdims=True)
        return 0

    lax.fori_loop(0, tiles, point, 0)


def last_body(gf_ref, edge_ref, w0_ref, gz_ref, normed_ref, tok_ref, cot_ref, gain_ref, inx_ref, inz_ref, tgrad_ref, xgrad_ref, gaing_ref, gp, gx, gn):
    rows, di = gf_ref.shape
    tiles = di // 128

    def conv(k, _):
        c = lanes(k)
        gp[0:rows, :] = gf_ref[:, c]
        gp[rows : rows + 8, :] = edge_ref[:, c]
        total = jnp.zeros((rows, 128), F32)
        for tap in range(KW):
            lo = KW - 1 - tap
            total = total + w0_ref[tap : tap + 1, c] * gp[lo : lo + rows, :]
        gx[:, c] = total.astype(BF16)
        return 0

    lax.fori_loop(0, tiles, conv, 0)

    def wide(j, _):
        c = lanes(j, 256)
        xgrad_ref[:, c] = dot_tn(normed_ref[...], gx[:, c]).astype(BF16)
        return 0

    lax.fori_loop(0, di // 256, wide, 0)

    def back(j, _):
        c = lanes(j, 256)
        gn[:, c] = dot_nt(gx[...], inx_ref[c, :]) + dot_nt(gz_ref[...], inz_ref[c, :])
        return 0

    lax.fori_loop(0, inx_ref.shape[0] // 256, back, 0)

    def rows_of(i, total):
        r = pl.ds(pl.multiple_of(i * 8, 8), 8)
        u = tok_ref[r, :]
        g = gn[r, :]
        scale = lax.rsqrt(jnp.mean(u * u, axis=-1, keepdims=True) + EPS)
        v = g * gain_ref[...]
        mean = jnp.mean(v * u, axis=-1, keepdims=True)
        tgrad_ref[r, :] = cot_ref[r, :] + scale * v - u * (scale * scale * scale * mean)
        return total + g * u * scale

    total = lax.fori_loop(0, rows // 8, rows_of, jnp.zeros((8, tok_ref.shape[1]), F32))
    gaing_ref[...] = jnp.sum(total, axis=0, keepdims=True)


def place():
    b, s = lax.axis_index("batch"), lax.axis_index("seq")
    return b // 2, b % 2, s // 2, s % 2


def device(y, c, z, x):
    return (y * 2 + c, z * 2 + x)


def greet(peers):
    barrier = pltpu.get_barrier_semaphore()
    for peer in peers:
        pl.semaphore_signal(barrier, inc=1, device_id=peer, device_id_type=MESH)
    pl.semaphore_wait(barrier, len(peers))


def remote(src, dst, send, recv, to):
    return pltpu.make_async_remote_copy(
        src_ref=src, dst_ref=dst, send_sem=send, recv_sem=recv, device_id=to, device_id_type=MESH
    )


def neighbours(y, c, z, x):
    return [device(y, c, z ^ k, x) for k in (1, 2, 3)] + [
        device(1 - y, c, z, x), device(y, c, z, 1 - x), device(y, 1 - c, z, x)
    ]


class Gather:
    COPIES = 14

    def __init__(self, src, out, send, recv, local):
        self.src, self.out, self.send, self.recv, self.local = src, out, send, recv, local
        self.at = place()
        self.count = 0
        self.copies = []

    def go(self, view, to):
        i = self.count
        self.count += 1
        source, target = view if isinstance(view, tuple) else (view, view)
        copy = remote(source, target, self.send.at[i], self.recv.at[i], to)
        copy.start()
        self.copies.append(copy)
        return copy

    def stage(self, k):
        y, c, z, x = self.at
        out = self.out
        half = out.shape[4] // 2
        top, bottom = pl.ds(0, half), pl.ds(half, half)
        to_y, to_x, to_c = device(1 - y, c, z, x), device(y, c, z, 1 - x), device(y, 1 - c, z, x)
        if k == 0:
            own = pltpu.make_async_copy(self.src, out.at[y, c, z, x], self.local)
            own.start()
            self.first = [self.go((self.src, out.at[y, c, z, x]), device(y, c, z ^ i, x)) for i in (1, 2, 3)]
            own.wait()
        elif k == 1:
            for copy in self.first:
                copy.wait_recv()
            self.a = self.go(out.at[y, c, :, x, top], to_y)
            self.b = self.go(out.at[y, c, :, x, bottom], to_x)
            self.go(out.at[y, c, :, x], to_c)
        elif k == 2:
            self.a.wait_recv()
            self.b.wait_recv()
            self.next = [self.go(out.at[i, c, :, x, top], to_x) for i in (0, 1)]
            self.next.append(self.go(out.at[y, c, :, :, bottom], to_y))
            self.go(out.at[1 - y, c, :, x, top], to_c)
            self.go(out.at[y, c, :, 1 - x, bottom], to_c)
        elif k == 3:
            for copy in self.next:
                copy.wait_recv()
            for i in (0, 1):
                self.go(out.at[i, c, :, 1 - x, top], to_c)
            self.go(out.at[1 - y, c, :, :, bottom], to_c)
        else:
            done = self.first + [self.a, self.b] + self.next
            for copy in self.copies:
                if not any(copy is other for other in done):
                    copy.wait_recv()

    def drain(self):
        for copy in self.copies:
            copy.wait_send()


STAGES = 5
STEPS = (0, 2, 4, 6, 7)
PACE = 1.0
DELAY = 0
STEPS_BACK = (0, 2, 4, 6, 8)
STEPS_LAST = (0, 1, 2, 3, 4)
PACE_BACK = 1.0


def shift(value, by):
    peers = lax.axis_size("seq")
    pairs = [(i, i + by) for i in range(peers) if 0 <= i + by < peers]
    return lax.ppermute(value, "seq", pairs)


def carried_in(total, value, reverse):
    peers, index = lax.axis_size("seq"), lax.axis_index("seq")
    totals = lax.all_gather(total.astype(BF16), "seq")
    values = lax.all_gather(value.astype(BF16), "seq")

    def turn(k, before):
        at = peers - 1 - k if reverse else k
        reached = at > index if reverse else at < index
        new = totals[at].astype(F32) * before + values[at].astype(F32)
        return jnp.where(reached, new, before)

    return lax.fori_loop(0, peers, turn, jnp.zeros(value.shape, F32))


def unpack_weights(pk, w0_ref, selt_ref, gain_ref):
    low_half = lax.broadcasted_iota(jnp.int32, (PACK0, 128), 1) < 64

    def pair(j, _):
        at = (j // 8, j // 4 % 2, j % 4)
        a = pk[at + (0, pl.ds(0, PACK0))].astype(F32)
        b = pk[at + (1, pl.ds(0, PACK0))].astype(F32)
        c = lanes(j)
        w0_ref[:, c] = jnp.where(low_half, a, pltpu.roll(b, 64, 1))
        selt_ref[:, c] = jnp.where(low_half, pltpu.roll(a, 64, 1), b).astype(BF16)
        return 0

    lax.fori_loop(0, 16, pair, 0)

    def gains(j, _):
        total = jnp.zeros((16, 128), F32)
        for i in range(4):
            v = pk[(j // 4, j // 2 % 2, j % 2 * 2 + i // 2, i % 2, pl.ds(PACK0, 16))]
            total = total + v.astype(F32)
        gain_ref[:, lanes(j)] = total[0:8, :]
        return 0

    lax.fori_loop(0, 8, gains, 0)


def normalise(tok, gain, normed):
    rows = tok.shape[0]

    def norm(i, _):
        r = pl.ds(pl.multiple_of(i * 16, 16), 16)
        u = tok[r, :]
        scale = lax.rsqrt(jnp.mean(u * u, axis=-1, keepdims=True) + EPS)
        normed[r, :] = (u * scale * gain[0:1, :]).astype(BF16)
        return 0

    lax.fori_loop(0, rows // 16, norm, 0)


def conv_tiles(first, count, xin, halo, live, w0, filt, xs, xt, xp):
    rows, di = xin.shape
    tiles = di // 128

    def conv(k, _):
        c = lanes(k)
        xp[0:16, :] = halo[:, c].astype(F32) * live
        xp[16 : 16 + rows, :] = xin[:, c].astype(F32)
        for q in range(2):
            r0 = q * (rows // 2)
            f = w0[4:5, c]
            for tap in range(KW):
                lo = 16 - (KW - 1) + tap + r0
                f = f + w0[tap : tap + 1, c] * xp[lo : lo + rows // 2, :]
            s = (f * sigmoid(f)).astype(BF16)
            filt[r0 : r0 + rows // 2, c] = f
            xs[r0 : r0 + rows // 2, c] = s
            xt[pl.ds(r0 * tiles + k, rows // 2, stride=tiles), :] = s.astype(F32)
        return 0

    lax.fori_loop(first, first + count, conv, 0)


def step_sizes(first, count, proj, w0, draw, dt):
    rows, di = draw.shape
    tiles = di // 128
    low = proj[:, 0:DTR].astype(BF16)

    def delta(k, _):
        c = lanes(k)
        raw = dot(low, w0[DELTA0 : DELTA0 + DTR, c].astype(BF16)) + w0[5:6, c]
        draw[:, c] = raw
        dt[pl.ds(k, rows, stride=tiles), :] = jnp.maximum(raw, 0.0) + jnp.log1p(jnp.exp(-jnp.abs(raw)))
        return 0

    lax.fori_loop(first, first + count, delta, 0)


def spread_rows(part, parts, proj, first, ref):
    row_ids = lax.broadcasted_iota(jnp.int32, (128, 128), 0) % DS
    lane_ids = lax.broadcasted_iota(jnp.int32, (128, 128), 1)
    ones = jnp.ones((128, 128), BF16)

    def spread(i, _):
        p = proj[pl.ds(pl.multiple_of(i * 8, 8), 8), :]
        tall = jnp.broadcast_to(p[:, None, :], (8, DS, 128)).reshape(128, 128)
        o = pl.ds(pl.multiple_of(i * 128, 128), 128)
        v = jnp.where(lane_ids == row_ids + first, tall, 0.0)
        hi = v.astype(BF16)
        v = v - hi.astype(F32)
        mid = v.astype(BF16)
        lo = (v - mid.astype(F32)).astype(BF16)
        ref[o, :] = (dot(hi, ones) + dot(mid, ones)) + dot(lo, ones)
        return 0

    count = proj.shape[0] // 8 // parts
    lax.fori_loop(part * count, (part + 1) * count, spread, 0)


def light_forward_part(h, part, parts, dt, xt, bb, a2, total, end, run):
    rows = dt.shape[0] // 16
    size = rows // parts
    hs = pl.ds(h * 8, 8)
    a = [a2[n, hs, :] for n in range(DS)]

    def step(i, carry):
        state, past = carry
        t = part * size + i
        d = tile_at(dt, t, h)
        dx = d * tile_at(xt, t, h)
        new = tuple(jnp.exp2(a[n] * d) * state[n] + dx * row_of(bb, t * DS + n) for n in range(DS))
        return (new, past + d)

    zero = jnp.zeros((8, 128), F32)
    start = ((zero,) * DS, zero) if part == 0 else (tuple(end[n, hs, :] for n in range(DS)), run[hs, :])
    state, past = lax.fori_loop(0, size, step, start, unroll=4)
    run[hs, :] = past
    for n in range(DS):
        end[n, hs, :] = state[n]
        if part == parts - 1:
            total[n, hs, :] = jnp.exp2(a[n] * past)


def light_backward_half(h, dt, gt, cb, a2, adj):
    rows = dt.shape[0] // 16
    hs = pl.ds(h * 8, 8)
    a = [a2[n, hs, :] for n in range(DS)]

    def step(i, carry):
        t = rows - 1 - i
        d = tile_at(dt, t, h)
        g = tile_at(gt, t, h)
        return tuple(jnp.exp2(a[n] * d) * (carry[n] + g * row_of(cb, t * DS + n)) for n in range(DS))

    out = lax.fori_loop(0, rows, step, (jnp.zeros((8, 128), F32),) * DS, unroll=4)
    for n in range(DS):
        adj[n, hs, :] = out[n]


def forward_part(h, q, si, dt, xt, bb, cb, a2, starts, yt):
    size = dt.shape[0] // 16 // starts.shape[0]
    hs = pl.ds(h * 8, 8)
    a = [a2[n, hs, :] for n in range(DS)]
    state = tuple(si[n, hs, :] for n in range(DS))
    for n in range(DS):
        starts[q, n, hs, :] = state[n]

    def step(i, carry):
        t = q * size + i
        d = tile_at(dt, t, h)
        dx = d * tile_at(xt, t, h)
        new, parts = [], []
        for n in range(DS):
            s = jnp.exp2(a[n] * d) * carry[n] + dx * row_of(bb, t * DS + n)
            parts.append(s * row_of(cb, t * DS + n))
            new.append(s)
        while len(parts) > 1:
            parts = [parts[i] + parts[i + 1] for i in range(0, len(parts), 2)]
        yt[pl.ds(pl.multiple_of(t * 16 + h * 8, 8), 8), :] = parts[0]
        return tuple(new)

    state = lax.fori_loop(0, size, step, state, unroll=4)
    for n in range(DS):
        si[n, hs, :] = state[n]


def carry_send(refs, mine, got, send, recv):
    peers = mine.shape[0]
    pair = DS // peers
    b, s = lax.axis_index("batch"), lax.axis_index("seq")
    for j in range(peers):
        for i in range(pair):
            for m, ref in enumerate(refs):
                mine[j, m, i] = ref[j * pair + i].astype(BF16)
    copies = []
    for k in range(1, peers):
        to = lax.rem(s + k, peers)
        copy = remote(mine.at[to], got.at[s], send.at[k - 1], recv.at[k - 1], (b, to))
        copy.start()
        copies.append(copy)
    got[s] = mine[s]
    return copies


def carry_back(back, final, send, recv):
    peers = back.shape[0]
    b, s = lax.axis_index("batch"), lax.axis_index("seq")
    copies = []
    for k in range(1, peers):
        to = lax.rem(s + k, peers)
        copy = remote(back.at[to], final.at[s], send.at[k - 1], recv.at[k - 1], (b, to))
        copy.start()
        copies.append(copy)
    final[s] = back[s]
    return copies


def arrived(copies):
    for copy in copies:
        copy.wait_recv()


WX, WZ, WO = 4, 4, 4


def pack_small(refs, out, me):
    gain, conv, conv_bias, select, delta, delta_bias, a_log, skip = (ref[...].astype(F32) for ref in refs)
    own = conv.shape[1]
    none = jnp.zeros((1, own), F32)
    left = jnp.concatenate([conv, conv_bias, delta_bias, skip, none, a_log, delta, jnp.zeros((PACK0 - DELTA0 - DTR, own), F32)], axis=0)
    right = jnp.concatenate([select, jnp.zeros((own, 128 - PACK0), F32)], axis=1).T[0:PACK0]
    out[0:PACK0, :] = jnp.concatenate([left, right], axis=1).astype(BF16)
    part = gain.shape[1]
    tile = jnp.concatenate([gain] * (128 // part), axis=1)
    mine = lax.broadcasted_iota(jnp.int32, tile.shape, 1) // part == me % (128 // part)
    out[PACK0:PACK, :] = jnp.broadcast_to(jnp.where(mine, tile, 0.0), (PACK - PACK0, 128)).astype(BF16)


def front_body(tok_in, cot_in, inw_in, outw_in, *refs):
    small, refs = refs[:8], refs[8:]
    names = FRONT_OUTS
    o = dict(zip(names, refs[: len(names)]))
    v = dict(zip(FRONT_SCRATCH, refs[len(names) :]))
    stash_sem, load_sem, job_send, job_recv, job_local, ring_send, ring_recv, halo_send, halo_recv = (
        v[n] for n in ("stash", "load", "jsend", "jrecv", "jlocal", "rsend", "rrecv", "hsend", "hrecv")
    )
    y, c, z, x = place()
    b, s = lax.axis_index("batch"), lax.axis_index("seq")
    peers = v["mine"].shape[0]
    stash = []

    def put(*keys):
        for key in keys:
            copy = pltpu.make_async_copy(v[key], o[key], stash_sem.at[len(stash)])
            copy.start()
            stash.append(copy)

    load_tok = pltpu.make_async_copy(tok_in, v["tok"], load_sem.at[0])
    load_cot = pltpu.make_async_copy(cot_in, v["cot"], load_sem.at[1])
    load_tok.start()
    load_cot.start()
    pack_small(small, v["packed"], b * peers + s)
    greet([(b, lax.rem(s + k, peers)) for k in range(1, peers)] + [device(1 - y, c, z, x), device(y, 1 - c, z, x)])

    jobs = []

    def job(src, out):
        i = len(jobs)
        jobs.append(Gather(src, out, job_send.at[i], job_recv.at[i], job_local.at[i]))

    width = inw_in.shape[1] // 2 // WX
    wide_z = inw_in.shape[1] // 2 // WZ
    wide_o = outw_in.shape[1] // WO
    job(v["packed"], v["pk"])
    for i in range(WX):
        job(inw_in.at[:, pl.ds(i * width, width)], v["inx"].at[i])
    for i in range(WZ):
        job(inw_in.at[:, pl.ds(inw_in.shape[1] // 2 + i * wide_z, wide_z)], v["inz"].at[i])
    for i in range(WO):
        job(outw_in.at[:, pl.ds(i * wide_o, wide_o)], v["wo"].at[i])
    events = sorted(
        ((i if i <= WX else i + DELAY) + STEPS[k], -k, i) for i in range(len(jobs)) for k in range(STAGES)
    )
    clock = [0.0]

    def advance():
        _, k, i = events.pop(0)
        jobs[i].stage(-k)

    def landed(i):
        while any(e[2] == i for e in events):
            advance()
            clock[0] = 0.0

    def spend(time):
        clock[0] += time
        while clock[0] >= PACE:
            clock[0] -= PACE
            if events:
                advance()

    di = v["xin"].shape[1]
    rows = v["xin"].shape[0]
    tiles = di // 128
    per = tiles // WX
    live = jnp.where(s > 0, 1.0, 0.0)
    halos = []

    def project_x(i):
        cols = pl.ds(i * width, width)
        v["xin"][:, cols] = dot(v["normed"][...], v["inx"][i].reshape(-1, width)).astype(BF16)
        copy = remote(
            v["xin"].at[pl.ds(rows - 16, 16), cols], v["halo"].at[:, cols],
            halo_send.at[i], halo_recv.at[i], (b, lax.rem(s + 1, peers)),
        )
        copy.start()
        halos.append(copy)

    def conv(i):
        halos[i].wait_recv()
        conv_tiles(i * per, per, v["xin"], v["halo"], live, v["w0"], v["filt"], v["xs"], v["xt"], v["xp"])

    landed(0)
    unpack_weights(v["pk"], v["w0"], v["selt"], v["gain"])
    load_tok.wait()
    normalise(v["tok"], v["gain"], v["normed"])
    put("w0", "selt", "gain", "normed")
    for k in range(16):
        v["a2"][:, k, :] = -jnp.exp(v["w0"][ALOG0 : ALOG0 + DS, k * 128 : (k + 1) * 128]) * LOG2E
    put("a2")
    for i in range(WX):
        landed(1 + i)
        project_x(i)
        if i > 0:
            conv(i - 1)
    put("inx")
    load_cot.wait()
    v["low"][...] = v["cot"][...].astype(BF16)
    put("low")
    conv(WX - 1)
    put("xin", "halo", "filt", "xs", "xt")
    v["proj"][:, 0:PACK0] = dot_nt(v["xs"][...], v["selt"][...])
    spend(1.5)
    for q in range(4):
        step_sizes(q * (tiles // 4), tiles // 4, v["proj"], v["w0"], v["draw"], v["dt"])
        spend(1.0)
    put("draw", "dt")
    for q in range(4):
        spread_rows(q, 4, v["proj"], DTR, v["bb"])
        spend(0.85)
    put("bb")
    for h in range(2):
        for q in range(4):
            light_forward_part(h, q, 4, v["dt"], v["xt"], v["bb"], v["a2"], v["total"], v["end"], v["run"])
            spend(0.8)

    sent = carry_send((v["total"], v["end"]), v["mine"], v["got"], ring_send.at[0], ring_recv.at[0])

    def project_z(i):
        landed(1 + WX + i)
        v["gate"][:, i * wide_z : (i + 1) * wide_z] = dot(v["normed"][...], v["inz"][i].reshape(-1, wide_z))

    for q in range(4):
        spread_rows(q, 4, v["proj"], DTR + DS, v["cb"])
        spend(0.85)
    put("cb")
    arrived(sent)
    state = jnp.zeros(v["back"].shape[1:], F32)
    for p in range(peers):
        v["back"][p] = state.astype(BF16)
        state = v["got"][p, 0].astype(F32) * state + v["got"][p, 1].astype(F32)
    more = carry_back(v["back"], v["final"], ring_send.at[1], ring_recv.at[1])
    sent += more
    for i in range(WZ - 1):
        project_z(i)
    arrived(more)
    pair = DS // peers
    for j in range(peers):
        for i in range(pair):
            v["si"][j * pair + i] = v["final"][j, i].astype(F32)
    clock[0] = 0.0
    for q in range(v["starts"].shape[0]):
        for h in range(2):
            forward_part(h, q, v["si"], v["dt"], v["xt"], v["bb"], v["cb"], v["a2"], v["starts"], v["yt"])
            spend(0.6)
    put("starts")
    project_z(3)
    put("inz")
    landed(len(jobs) - 1)

    block = 512
    per_b = block // (di // 32)

    def gated_grad(j, _):
        out = jnp.zeros((rows, block), F32)
        for i in range(WO):
            w = v["wo"][i, j // 2, j % 2].reshape(block, wide_o)
            out = out + dot_nt(v["low"][:, i * wide_o : (i + 1) * wide_o], w)
        v["gzp"][:, lanes(j, block)] = out
        return 0

    lax.fori_loop(0, di // block, gated_grad, 0)

    def point(k, _):
        cols = lanes(k)
        for q in range(4):
            r = slice(q * (rows // 4), (q + 1) * (rows // 4))
            zz = v["gate"][r, cols]
            gg = v["gzp"][r, cols]
            sg = sigmoid(zz)
            gate = zz * sg
            v["gate"][r, cols] = gate
            v["gzp"][r, cols] = gg * sg * (1.0 + zz * (1.0 - sg))
            v["gt"][pl.ds(q * (rows // 4) * tiles + k, rows // 4, stride=tiles), :] = gg * gate
        return 0

    lax.fori_loop(0, tiles, point, 0)
    put("gt")
    for h in range(2):
        light_backward_half(h, v["dt"], v["gt"], v["cb"], v["a2"], v["adj"])
    again = carry_send((v["adj"],), v["mine2"], v["got2"], ring_send.at[2], ring_recv.at[2])
    sent += again

    def emit(k, _):
        cols = lanes(k)
        total = jnp.zeros((8, 128), F32)
        for q in range(4):
            r = slice(q * (rows // 4), (q + 1) * (rows // 4))
            here = pl.ds(q * (rows // 4) * tiles + k, rows // 4, stride=tiles)
            xx = v["xt"][here, :]
            yy = v["yt"][here, :] + v["w0"][6:7, cols] * xx
            v["gated"][r, cols] = (yy * v["gate"][r, cols]).astype(BF16)
            v["gz"][r, cols] = (v["gzp"][r, cols] * yy).astype(BF16)
            total = total + jnp.sum((v["gt"][here, :] * xx).reshape(-1, 8, 128), axis=0)
        v["skipg"][:, cols] = jnp.broadcast_to(jnp.sum(total, axis=0, keepdims=True), (8, 128))
        return 0

    lax.fori_loop(0, tiles, emit, 0)
    put("gated", "gz", "skipg")
    for i in range(WO):
        cols = pl.ds(i * wide_o, wide_o)
        w = v["wo"][i].reshape(di, wide_o)
        v["tok"][:, cols] = v["tok"][:, cols] + dot(v["gated"][...], w)
    copy = pltpu.make_async_copy(v["tok"], o["block"], load_sem.at[0])
    copy.start()
    arrived(again)
    state = jnp.zeros(v["back2"].shape[1:], F32)
    for p in reversed(range(peers)):
        v["back2"][p] = state.astype(BF16)
        state = v["got"][p, 0].astype(F32) * state + v["got2"][p, 0].astype(F32)
    put("back2")
    copy.wait()
    for it in jobs:
        it.drain()
    for it in sent + halos:
        it.wait_send()
    for it in stash:
        it.wait()


FRONT_OUTS = (
    "block", "w0", "selt", "gain", "normed", "a2", "inx", "xin", "halo", "filt", "xs", "xt", "low", "draw", "dt",
    "bb", "cb", "inz", "starts", "gt", "gated", "gz", "skipg", "back2",
)
FRONT_SCRATCH = (
    "w0", "selt", "gain", "normed", "a2", "inx", "xin", "halo", "filt", "xs", "xt", "low", "draw", "dt",
    "bb", "cb", "inz", "starts", "gt", "gated", "gz", "skipg", "back2",
    "tok", "cot", "pk", "wo", "proj", "xp", "gate", "gzp", "yt", "total", "end", "adj", "si",
    "mine", "got", "back", "final", "mine2", "got2", "run", "packed",
    "stash", "load", "jsend", "jrecv", "jlocal", "rsend", "rrecv", "hsend", "hrecv",
)


def front(tok, cot, in_weight, out_weight, small, peers, chunks):
    rows, width = tok.shape
    di = in_weight.shape[1] // 2
    tiles = di // 128
    lead = (2, 2, 4, 2)
    flat, wide, carry = ((rows * tiles, 128), F32), ((rows, di), F32), ((DS, tiles, 128), F32)
    spread, half = ((rows * DS, 128), F32), ((rows, di), BF16)
    pair = (DS // peers, tiles, 128)
    shapes = {
        "block": ((rows, width), F32), "w0": ((PACK0, di), F32), "selt": ((PACK0, di), BF16), "gain": ((8, width), F32),
        "normed": ((rows, width), BF16), "a2": carry, "inx": ((WX,) + lead + (in_weight.shape[0], di // WX), BF16),
        "xin": half, "halo": ((16, di), BF16), "filt": wide, "xs": half, "xt": flat, "low": ((rows, width), BF16),
        "draw": wide, "dt": flat, "bb": spread, "cb": spread,
        "inz": ((WZ,) + lead + (in_weight.shape[0], di // WZ), BF16), "starts": ((chunks, DS, tiles, 128), F32),
        "gt": flat, "gated": half, "gz": half, "skipg": ((8, di), F32),
        "tok": ((rows, width), F32), "cot": ((rows, width), F32), "pk": (lead + (PACK, 128), BF16),
        "wo": ((WO,) + lead + (out_weight.shape[0], width // WO), BF16), "proj": ((rows, 128), F32),
        "xp": ((rows + 16, 128), F32), "gate": wide, "gzp": wide, "yt": flat, "total": carry, "end": carry, "adj": carry,
        "si": carry, "mine": ((peers, 2) + pair, BF16), "got": ((peers, 2) + pair, BF16), "back": ((peers,) + pair, BF16),
        "final": ((peers,) + pair, BF16), "mine2": ((peers, 1) + pair, BF16), "got2": ((peers, 1) + pair, BF16),
        "back2": ((peers,) + pair, BF16), "packed": ((PACK, 128), BF16), "run": ((tiles, 128), F32),
    }
    n_jobs = 1 + WX + WZ + WO
    dma = pltpu.SemaphoreType.DMA
    sems = {
        "stash": dma((len(FRONT_OUTS) - 1,)), "load": dma((2,)), "jsend": dma((n_jobs, Gather.COPIES)),
        "jrecv": dma((n_jobs, Gather.COPIES)), "jlocal": dma((n_jobs,)), "rsend": dma((3, peers - 1)),
        "rrecv": dma((3, peers - 1)), "hsend": dma((WX,)), "hrecv": dma((WX,)),
    }
    outs = pl.pallas_call(
        front_body,
        out_shape=tuple(sds(*shapes[n]) for n in FRONT_OUTS),
        in_specs=[ANY] * 4 + [VM] * len(small),
        out_specs=(ANY,) * len(FRONT_OUTS),
        scratch_shapes=[sems[n] if n in sems else pltpu.VMEM(*shapes[n]) for n in FRONT_SCRATCH],
        compiler_params=pltpu.CompilerParams(collective_id=0, has_side_effects=True, vmem_limit_bytes=GRANT),
    )(tok, cot, in_weight, out_weight, *small)
    return dict(zip(FRONT_OUTS, outs))


class Share:
    COPIES = 10

    def __init__(self, own, other, r1, r2, r3, r4, out, send, recv):
        self.own, self.other, self.r1, self.r2, self.r3, self.r4, self.out = own, other, r1, r2, r3, r4, out
        self.send, self.recv = send, recv
        self.at = place()
        self.copies = []

    def go(self, source, target, to):
        i = len(self.copies)
        copy = remote(source, target, self.send.at[i], self.recv.at[i], to)
        copy.start()
        self.copies.append(copy)
        return copy

    def stage(self, k):
        y, c, z, x = self.at
        own = self.own
        half = own.shape[3] // 2
        top, bottom = pl.ds(0, half), pl.ds(half, half)
        to_y, to_x, to_c = device(1 - y, c, z, x), device(y, c, z, 1 - x), device(y, 1 - c, z, x)
        if k > 0:
            arrived(self.wait)
        if k == 0:
            self.wait = [self.go(self.other.at[i], self.r1.at[i], to_c) for i in (0, 1)]
        elif k == 1:

            def piece(i, _):
                at = (i // 8, i // 2 % 4, i % 2)
                own[at] = own[at] + self.r1[at]
                return 0

            lax.fori_loop(0, 16, piece, 0)
            self.wait = [self.go(own.at[1 - y, :, :, top], self.r2.at[pl.ds(0, 4), :], to_y)]
            for i in (0, 1):
                self.wait.append(self.go(own.at[i, :, 1 - x, bottom], self.r2.at[pl.ds(4, 4), i], to_x))
        elif k == 2:

            def piece(i, _):
                b, d = i // 2, i % 2
                own[y, b, d, top] = own[y, b, d, top] + self.r2[b, d]
                own[d, b, x, bottom] = own[d, b, x, bottom] + self.r2[4 + b, d]
                return 0

            lax.fori_loop(0, 8, piece, 0)
            self.wait = [
                self.go(own.at[y, :, 1 - x, top], self.r3.at[0], to_x),
                self.go(own.at[1 - y, :, x, bottom], self.r3.at[1], to_y),
            ]
        elif k == 3:

            def piece(b, _):
                own[y, b, x, top] = own[y, b, x, top] + self.r3[0, b]
                own[y, b, x, bottom] = own[y, b, x, bottom] + self.r3[1, b]
                return 0

            lax.fori_loop(0, 4, piece, 0)
            self.wait = [
                self.go(own.at[y, z ^ i, x], self.r4.at[i - 1], device(y, c, z ^ i, x)) for i in (1, 2, 3)
            ]
        else:
            total = own[y, z, x].astype(F32)
            for i in range(3):
                total = total + self.r4[i].astype(F32)
            self.out[...] = total

    def drain(self):
        for copy in self.copies:
            copy.wait_send()
        self.copies = []


def adjoint_part(chunk, h, dt, xt, bb, cb, gt, a2, starts, later, keep, decays, pb, pc, rb, rc, ga, size):
    hs = pl.ds(h * 8, 8)
    a = [a2[n, hs, :] for n in range(DS)]
    base = chunk * size
    first = tuple(starts[chunk, n, hs, :] for n in range(DS))
    for n in range(DS):
        keep[n * 8 : n * 8 + 8, :] = first[n]

    def again(i, carry):
        t = base + i
        d = tile_at(dt, t, h)
        dx = d * tile_at(xt, t, h)
        new = []
        for n in range(DS):
            w = jnp.exp2(a[n] * d)
            s = w * carry[n] + dx * row_of(bb, t * DS + n)
            o = pl.multiple_of(i * 128 + n * 8, 8)
            decays[pl.ds(o, 8), :] = w
            keep[pl.ds(pl.multiple_of(o + 128, 8), 8), :] = s
            new.append(s)
        return tuple(new)

    lax.fori_loop(0, size, again, first, unroll=4)

    def back(j, carry):
        i = size - 1 - j
        t = base + i
        d = tile_at(dt, t, h)
        x = tile_at(xt, t, h)
        gy = tile_at(gt, t, h)
        dx = d * x
        slot = (j % 2) * 128
        new = []
        weighted, through_a = [], []
        for n in range(DS):
            o = pl.multiple_of(i * 128 + n * 8, 8)
            w = decays[pl.ds(o, 8), :]
            before = keep[pl.ds(o, 8), :]
            now = keep[pl.ds(pl.multiple_of(o + 128, 8), 8), :]
            g = carry[n] + gy * row_of(cb, t * DS + n)
            at = pl.ds(pl.multiple_of(slot + n * 8, 8), 8)
            pc[at, :] = now * gy
            pb[at, :] = g * dx
            weighted.append(g * row_of(bb, t * DS + n))
            g = g * w
            through = g * before
            through_a.append(through * a[n])
            ga[n, hs, :] += through * d
            new.append(g)
        while len(weighted) > 1:
            weighted = [weighted[i] + weighted[i + 1] for i in range(0, len(weighted), 2)]
            through_a = [through_a[i] + through_a[i + 1] for i in range(0, len(through_a), 2)]
        o = pl.ds(pl.multiple_of(t * 16 + h * 8, 8), 8)
        dt[o, :] = through_a[0] * LN2 + weighted[0] * x
        xt[o, :] = weighted[0] * d
        for src, dst in ((pb, rb), (pc, rc)):
            for m in range(2):
                parts = [src[pl.ds(slot + m * 64 + s, 8, stride=8), :] for s in range(8)]
                while len(parts) > 1:
                    parts = [parts[i] + parts[i + 1] for i in range(0, len(parts), 2)]
                q = pl.ds(pl.multiple_of(i * 16 + m * 8, 8), 8)
                if h == 0:
                    dst[q, :] = parts[0]
                else:
                    dst[q, :] += parts[0]
        return tuple(new)

    out = lax.fori_loop(0, size, back, tuple(later[n, hs, :] for n in range(DS)), unroll=2)
    for n in range(DS):
        later[n, hs, :] = out[n]


def collect_rows(chunk, size, rb, rc, gb, gc):
    ones = jnp.ones((128, 128), BF16)
    pick = lax.broadcasted_iota(jnp.int32, (128, 128), 0) % DS == lax.broadcasted_iota(jnp.int32, (128, 128), 1)

    def collect(i, _):
        o = pl.ds(pl.multiple_of(i * 128, 128), 128)
        for src, dst in ((rb, gb), (rc, gc)):
            v = src[o, :]
            hi = v.astype(BF16)
            lo = (v - hi.astype(F32)).astype(BF16)
            s = jnp.where(pick, dot(hi, ones) + dot(lo, ones), 0.0)
            dst[pl.ds(pl.multiple_of(chunk * size + i * 8, 8), 8), :] = jnp.sum(s.reshape(8, DS, 128), axis=1)
        return 0

    lax.fori_loop(0, size // 8, collect, 0)


BACK_IN = (
    "back2", "gated", "low", "normed", "gz", "dt", "xt", "bb", "cb", "gt", "a2", "starts", "draw", "xs", "w0", "selt",
    "filt", "xin", "halo", "inx", "inz", "gain", "skipg", "tok", "cot",
)
BACK_LOAD = tuple(n for n in BACK_IN if n not in ("inx", "inz"))
BACK_OUT = ("tgrad", "gin", "gout", "gpack")
BACK_SCRATCH = BACK_LOAD[:-1] + (
    "wbuf", "keep", "decays", "pb", "pc", "rb", "rc", "ga", "gb", "gc", "proj", "xp", "gp", "rawlow", "gproj", "dw", "w0g",
    "selg", "edge", "gx", "gn", "gaing",
    "own", "other", "r1", "r2", "r3", "r4", "pown", "pother", "p1", "p2", "p3", "p4",
    "so", "final2",
    "load", "wsem", "send", "recv", "esend", "erecv", "rsend", "rrecv",
)
BLOCKS = 4


def back_body(*refs):
    hbm = dict(zip(BACK_IN, refs))
    refs = refs[len(BACK_IN) :]
    o = dict(zip(BACK_OUT, refs))
    v = dict(zip(BACK_SCRATCH, refs[len(BACK_OUT) :]))
    loads = {}
    for i, name in enumerate(BACK_LOAD):
        loads[name] = pltpu.make_async_copy(hbm[name], o["tgrad"] if name == "cot" else v[name], v["load"].at[i])
        loads[name].start()

    def need(*names):
        for name in names:
            loads[name].wait()

    y, c, z, x = place()
    b, s = lax.axis_index("batch"), lax.axis_index("seq")
    peers = lax.axis_size("seq")
    greet([(b, lax.rem(s + k, peers)) for k in range(1, peers)] + [device(1 - y, c, z, x), device(y, 1 - c, z, x)])
    need("back2")
    sent = carry_back(v["back2"], v["final2"], v["rsend"].at[0], v["rrecv"].at[0])

    rows, di = v["gz"].shape
    width = v["normed"].shape[1]
    tiles = di // 128
    cols = di // BLOCKS
    half = width // 2
    owned = v["own"].shape[4]
    jobs = []

    def job(out):
        i = len(jobs)
        at = i % (2 * BLOCKS)
        jobs.append(
            Share(
                v["own"].at[at], v["other"].at[at], v["r1"].at[i], v["r2"].at[i], v["r3"].at[i], v["r4"].at[i],
                out, v["send"].at[i], v["recv"].at[i],
            )
        )

    for i in range(4):
        job(o["gout"].at[i // 2 * owned : (i // 2 + 1) * owned, i % 2 * half : (i % 2 + 1) * half])
    for i in range(BLOCKS):
        job(o["gin"].at[:, di + i * cols : di + (i + 1) * cols])
    for i in range(BLOCKS):
        job(o["gin"].at[:, i * cols : (i + 1) * cols])
    last = len(jobs)
    jobs.append(
        Share(
            v["pown"], v["pother"], v["p1"], v["p2"], v["p3"], v["p4"], o["gpack"], v["send"].at[last], v["recv"].at[last]
        )
    )
    events, now, clock = [], [0], [0.0]
    first = [0]

    def enter(*blocks, steps=STEPS_BACK):
        for i in blocks:
            first[0] = max(first[0] + 1, now[0])
            events.extend((first[0] + steps[k], -k, i) for k in range(STAGES))
        events.sort()

    def advance():
        now[0], k, i = events.pop(0)
        jobs[i].stage(-k)

    def spend(time):
        clock[0] += time
        while clock[0] >= PACE_BACK:
            clock[0] -= PACE_BACK
            if events:
                advance()

    def finish(i):
        while any(e[2] == i for e in events):
            advance()
        jobs[i].drain()

    need("gated", "low")

    def out_blocks(core, dst):
        def block(i, _):
            first = pl.multiple_of(((i // 2) * 2 + core) * (di // 4) + (i % 2) * 256, 256)
            g = v["gated"][:, pl.ds(first, 256)]
            for q in range(2):
                r = dot_tn(g, v["low"][:, q * half : (q + 1) * half]).astype(BF16).reshape(2, 2, 2, owned, half)
                for p in range(2):
                    dst[p * 2 + q, i // 2, pl.ds((i % 2) * 2, 2)] = r[:, :, p]
            return 0

        lax.fori_loop(0, 4, block, 0)

    def in_blocks(core, dst, first, right):
        def block(i, _):
            n = v["normed"][:, pl.ds(pl.multiple_of((i * 2 + core) * (width // 4), 256), width // 4)]
            for q, g in enumerate(right):
                dst[first + q, i] = dot_tn(n, g()).astype(BF16).reshape(4, 2, owned, cols)
            return 0

        lax.fori_loop(0, 2, block, 0)

    out_blocks(1 - c, v["other"])
    enter(0, 1, 2, 3)
    advance()
    advance()
    out_blocks(c, v["own"])
    need("normed", "gz")
    z_right = [lambda q=q: v["gz"][:, q * cols : (q + 1) * cols] for q in range(BLOCKS)]
    in_blocks(1 - c, v["other"], BLOCKS, z_right)
    enter(4, 5, 6, 7)
    in_blocks(c, v["own"], BLOCKS, z_right)
    spend(3.0)
    arrived(sent)
    pair = DS // peers
    for j in range(peers):
        for i in range(pair):
            v["so"][j * pair + i] = v["final2"][j, i].astype(F32)

    need("dt", "xt", "bb", "cb", "gt", "a2", "starts")
    v["ga"][...] = jnp.zeros_like(v["ga"])
    chunks = v["starts"].shape[0]
    size = rows // chunks
    for chunk in reversed(range(chunks)):
        for h in range(2):
            adjoint_part(
                chunk, h, v["dt"], v["xt"], v["bb"], v["cb"], v["gt"], v["a2"], v["starts"], v["so"], v["keep"],
                v["decays"], v["pb"], v["pc"], v["rb"], v["rc"], v["ga"], size,
            )
            spend(2.0)
        collect_rows(chunk, size, v["rb"], v["rc"], v["gb"], v["gc"])
        spend(0.75)

    need("draw", "xs", "w0", "selt")
    v["proj"][:, 0:PACK0] = dot_nt(v["xs"][...], v["selt"][...])
    low = v["proj"][:, 0:DTR].astype(BF16)
    v["dw"][...] = v["w0"][DELTA0 : DELTA0 + DTR, :].astype(BF16)
    w0g = v["w0g"]

    def raw(k, _):
        at = lanes(k)
        g = v["dt"][pl.ds(k, rows, stride=tiles), :] * sigmoid(v["draw"][:, at])
        w0g[5:6, at] = jnp.sum(g, axis=0, keepdims=True)
        gl = g.astype(BF16)
        v["rawlow"][:, at] = gl
        w0g[DELTA0 : DELTA0 + DTR, at] = dot_tn(low, gl)
        return 0

    spend(0.5)
    for q in range(BLOCKS):
        lax.fori_loop(q * (tiles // BLOCKS), (q + 1) * (tiles // BLOCKS), raw, 0)
        spend(0.85)
    v["gproj"][:, 0:DTR] = dot_nt(v["rawlow"][...], v["dw"][...]).astype(BF16)
    v["gproj"][:, DTR : DTR + DS] = v["gb"][:, 0:DS].astype(BF16)
    v["gproj"][:, DTR + DS : DTR + 2 * DS] = v["gc"][:, 0:DS].astype(BF16)
    need("filt", "xin", "halo")
    not_first = jnp.where(s > 0, 1.0, 0.0)
    not_last = jnp.where(s < peers - 1, 1.0, 0.0)

    def point(k, _):
        at = lanes(k)
        gp = v["gproj"][...]
        v["selg"][:, at] = dot_tn(gp, v["xs"][:, at])
        into = dot(gp, v["selt"][:, at])
        here = pl.ds(k, rows, stride=tiles)
        g = v["gt"][here, :] * v["w0"][6:7, at] + v["xt"][here, :] + into
        f = v["filt"][:, at]
        sg = sigmoid(f)
        gf = g * (sg * (1.0 + f * (1.0 - sg)))
        v["filt"][:, at] = gf
        w0g[4:5, at] = jnp.sum(gf, axis=0, keepdims=True)
        v["xp"][0:16, :] = v["halo"][:, at].astype(F32) * not_first
        v["xp"][16 : 16 + rows, :] = v["xin"][:, at].astype(F32)
        for tap in range(KW):
            lo = 16 - (KW - 1) + tap
            w0g[tap : tap + 1, at] = jnp.sum(gf * v["xp"][lo : lo + rows, :], axis=0, keepdims=True)
        return 0

    edges = []

    def points(q):
        lax.fori_loop(q * (tiles // BLOCKS), (q + 1) * (tiles // BLOCKS), point, 0)
        at = pl.ds(q * cols, cols)
        copy = remote(
            v["filt"].at[pl.ds(0, 8), at], v["edge"].at[:, at], v["esend"].at[q], v["erecv"].at[q],
            (b, lax.rem(s + peers - 1, peers)),
        )
        copy.start()
        edges.append(copy)

    weights = {}

    def fetch(i):
        source = hbm["inx"].at[i] if i < WX else hbm["inz"].at[i - WX]
        weights[i] = pltpu.make_async_copy(source, v["wbuf"].at[i % 2], v["wsem"].at[i])
        weights[i].start()

    fetch(0)
    fetch(1)

    def blocks(q):
        edges[q].wait_recv()

        def conv(k, _):
            at = lanes(k)
            v["gp"][0:rows, :] = v["filt"][:, at]
            v["gp"][rows : rows + 8, :] = v["edge"][:, at] * not_last
            total = jnp.zeros((rows, 128), F32)
            for tap in range(KW):
                lo = KW - 1 - tap
                total = total + v["w0"][tap : tap + 1, at] * v["gp"][lo : lo + rows, :]
            v["gx"][:, at] = total.astype(BF16)
            return 0

        lax.fori_loop(q * (tiles // BLOCKS), (q + 1) * (tiles // BLOCKS), conv, 0)
        right = [lambda: v["gx"][:, q * cols : (q + 1) * cols]]
        finish(q)
        in_blocks(1 - c, v["other"], q, right)
        jobs[2 * BLOCKS + q].stage(0)
        enter(2 * BLOCKS + q, steps=STEPS_LAST)
        events.remove((first[0], 0, 2 * BLOCKS + q))
        in_blocks(c, v["own"], q, right)
        while events and events[0][0] <= first[0]:
            advance()

    def into_rows(i):
        weights[i].wait()
        g = v["gx"] if i < WX else v["gz"]
        q = i % WX
        for d in range(2):
            w = v["wbuf"][i % 2].reshape(width, cols)[d * half : (d + 1) * half]
            part = dot_nt(g[:, q * cols : (q + 1) * cols], w)
            at = slice(d * half, (d + 1) * half)
            v["gn"][:, at] = part if i == 0 else v["gn"][:, at] + part
        if i + 2 < 2 * WX:
            fetch(i + 2)
        spend(0.5)

    points(0)
    points(1)
    for q in range(2, BLOCKS):
        points(q)
        blocks(q - 2)
    blocks(BLOCKS - 2)
    blocks(BLOCKS - 1)
    for i in range(2 * WX):
        into_rows(i)
    need("tok", "cot", "gain")

    def rows_of(i, total):
        r = pl.ds(pl.multiple_of(i * 8, 8), 8)
        u = v["tok"][r, :]
        g = v["gn"][r, :]
        scale = lax.rsqrt(jnp.mean(u * u, axis=-1, keepdims=True) + EPS)
        w = g * v["gain"][0:1, :]
        mean = jnp.mean(w * u, axis=-1, keepdims=True)
        o["tgrad"][r, :] = o["tgrad"][r, :] + scale * w - u * (scale * scale * scale * mean)
        return total + g * u * scale

    total = lax.fori_loop(0, rows // 8, rows_of, jnp.zeros((8, width), F32))
    v["gaing"][...] = jnp.broadcast_to(jnp.sum(total, axis=0, keepdims=True), (8, width))
    need("skipg")
    w0g[6:7, :] = v["skipg"][0:1, :]
    w0g[7:8, :] = jnp.zeros((1, di), F32)
    w0g[DELTA0 + DTR : PACK0, :] = jnp.zeros((PACK0 - DELTA0 - DTR, di), F32)
    for k in range(tiles):
        w0g[ALOG0 : ALOG0 + DS, k * 128 : (k + 1) * 128] = v["ga"][:, k, :] * v["a2"][:, k, :] * LN2
    low_half = lax.broadcasted_iota(jnp.int32, (PACK0, 128), 1) < 64

    def pack(core, dst):
        def pair(i, _):
            j = i // 4 * 8 + core * 4 + i % 4
            at = lanes(j)
            l, r = w0g[:, at], v["selg"][:, at]
            dst[i // 4, i % 4, 0, 0:PACK0, :] = jnp.where(low_half, l, pltpu.roll(r, 64, 1)).astype(BF16)
            dst[i // 4, i % 4, 1, 0:PACK0, :] = jnp.where(low_half, pltpu.roll(l, 64, 1), r).astype(BF16)
            g = jnp.broadcast_to(v["gaing"][0:1, lanes(j // 2)], (PACK - PACK0, 128)).astype(BF16)
            for d in range(2):
                dst[i // 4, i % 4, d, PACK0:PACK, :] = g
            return 0

        lax.fori_loop(0, 8, pair, 0)

    spend(3.0)
    pack(1 - c, v["pother"])
    jobs[last].stage(0)
    pack(c, v["pown"])
    enter(last, steps=STEPS_LAST)
    events.remove((first[0], 0, last))
    while events:
        advance()
    for it in jobs:
        it.drain()
    for it in edges + sent:
        it.wait_send()


def back(f, tok, cot):
    rows, di = f["gz"].shape
    width = tok.shape[1]
    tiles = di // 128
    cols = di // BLOCKS
    chunks = f["starts"].shape[0]
    size = rows // chunks
    lead = (2, 4, 2)
    owned = width // 32
    inputs = dict(f, tok=tok, cot=cot)
    shapes = {n: (inputs[n].shape, inputs[n].dtype) for n in BACK_IN}
    peers = f["back2"].shape[0]
    pair = (DS // peers, tiles, 128)
    shapes.update(
        so=((DS, tiles, 128), F32), final2=((peers,) + pair, BF16),
    )

    def sums(prefix, n, rows, cols, held):
        names = ("own", "other", "r1", "r2", "r3", "r4") if not prefix else ("pown", "pother", "p1", "p2", "p3", "p4")
        dims = (
            lead + (rows, cols), lead + (rows, cols), lead + (rows, cols), (8, 2, rows // 2, cols),
            (2, 4, rows // 2, cols), (3, rows, cols),
        )
        for i, (name, d) in enumerate(zip(names, dims)):
            k = (held if i < 2 else n,) if not prefix else ()
            shapes[name] = (k + d, BF16)

    sums("", 3 * BLOCKS, owned, cols, 2 * BLOCKS)
    sums("p", 1, PACK, 128, 1)
    tall = ((size * DS, 128), F32)
    shapes.update(
        wbuf=((2, 2, 2, 4, 2, owned, cols), BF16), keep=(((size + 1) * 128, 128), F32), decays=((size * 128, 128), F32),
        pb=((256, 128), F32), pc=((256, 128), F32), rb=tall, rc=tall, ga=((DS, tiles, 128), F32), gb=((rows, 128), F32),
        gc=((rows, 128), F32), proj=((rows, 128), F32), xp=((rows + 16, 128), F32), gp=((rows + 8, 128), F32),
        rawlow=((rows, di), BF16), gproj=((rows, PACK0), BF16), dw=((DTR, di), BF16), w0g=((PACK0, di), F32),
        selg=((PACK0, di), F32), edge=((8, di), F32), gx=((rows, di), BF16), gn=((rows, width), F32), gaing=((8, width), F32),
    )
    dma = pltpu.SemaphoreType.DMA
    n_jobs = 3 * BLOCKS + 1
    sems = {
        "load": dma((len(BACK_LOAD),)), "wsem": dma((2 * WX,)), "send": dma((n_jobs, Share.COPIES)),
        "recv": dma((n_jobs, Share.COPIES)), "esend": dma((BLOCKS,)), "erecv": dma((BLOCKS,)),
        "rsend": dma((1, peers - 1)), "rrecv": dma((1, peers - 1)),
    }
    return pl.pallas_call(
        back_body,
        out_shape=(
            sds((rows, width), F32), sds((owned, 2 * di), F32), sds((di // 32, width), F32), sds((PACK, 128), F32),
        ),
        in_specs=[ANY] * len(BACK_IN),
        out_specs=(VM,) * 4,
        scratch_shapes=[sems[n] if n in sems else pltpu.VMEM(*shapes[n]) for n in BACK_SCRATCH],
        compiler_params=pltpu.CompilerParams(collective_id=1, has_side_effects=True, vmem_limit_bytes=GRANT),
    )(*(inputs[n] for n in BACK_IN))


def finish_body(*refs):
    big, pack = refs[:4], refs[4]
    outs, small, sem = refs[5:9], refs[9:17], refs[17]
    copies = [pltpu.make_async_copy(src, dst, sem.at[i]) for i, (src, dst) in enumerate(zip(big, outs))]
    for copy in copies:
        copy.start()
    gain, conv, conv_bias, select, delta, delta_bias, a_log, skip = small
    own = conv.shape[1]
    conv[...] = pack[0:KW, 0:own]
    for row, ref in ((4, conv_bias), (5, delta_bias), (6, skip)):
        ref[...] = pack[row : row + 1, 0:own]
    a_log[...] = pack[ALOG0 : ALOG0 + DS, 0:own]
    delta[...] = pack[DELTA0 : DELTA0 + DTR, 0:own]
    select[...] = pack[...].T[own : 2 * own, 0:PACK0]
    part = gain.shape[1]
    parts = 128 // part
    me = (lax.axis_index("batch") * lax.axis_size("seq") + lax.axis_index("seq")) % parts
    tile = pack[PACK0 : PACK0 + 1, :]
    total = jnp.zeros((1, part), F32)
    for i in range(parts):
        total = total + jnp.where(me == i, tile[:, i * part : (i + 1) * part], 0.0)
    gain[...] = total
    for copy in copies:
        copy.wait()


def finish(whole, small):
    block, tgrad, gin, gout, pack = whole
    big = (block, tgrad, gin, gout)
    return pl.pallas_call(
        finish_body,
        out_shape=tuple(sds(v.shape, F32) for v in big + small),
        in_specs=[VM] * 5,
        out_specs=(ANY,) * 4 + (VM,) * 8,
        scratch_shapes=[pltpu.SemaphoreType.DMA((4,))],
        compiler_params=pltpu.CompilerParams(vmem_limit_bytes=GRANT),
    )(*big, pack)


def on_slice(tokens, cotangent, norm_gain, in_weight, conv_weight, conv_bias, select_weight, delta_weight, delta_bias, a_log, skip_gain, out_weight):
    sizes = (lax.axis_size("batch"), lax.axis_size("seq"))
    tok, cot = tokens[0], cotangent[0]
    rows = tok.shape[0]
    small = (
        norm_gain[None], conv_weight, conv_bias[None], select_weight, delta_weight, delta_bias[None], a_log, skip_gain[None],
    )
    f = front(tok, cot, in_weight, out_weight, small, sizes[1], rows // 32)
    whole = (f["block"],) + back(f, tok, cot)
    block_out, tokens_grad, g_in, g_out, *grads = finish(whole, small)
    g_gain, g_conv, g_conv_bias, g_select, g_delta, g_delta_bias, g_a_log, g_skip = grads
    return (
        block_out[None], tokens_grad[None], g_gain[0], g_in, g_conv, g_conv_bias[0], g_select, g_delta, g_delta_bias[0],
        g_a_log, g_skip[0], g_out,
    )


def on_device(tokens, cotangent, norm_gain, in_weight, conv_weight, conv_bias, select_weight, delta_weight, delta_bias, a_log, skip_gain, out_weight):
    axes = ("batch", "seq")
    sizes = (lax.axis_size("batch"), lax.axis_size("seq"))
    if sizes == (4, 8):
        return on_slice(
            tokens, cotangent, norm_gain, in_weight, conv_weight, conv_bias, select_weight, delta_weight, delta_bias,
            a_log, skip_gain, out_weight,
        )
    tok, cot = tokens[0], cotangent[0]
    rows, width = tok.shape
    di = out_weight.shape[0] * sizes[0] * sizes[1]
    tiles = di // 128
    full = lambda v, axis: lax.all_gather(v, axes, axis=axis, tiled=True)
    in_full = full(in_weight, 0)
    in_x, in_z = in_full[:, :di], in_full[:, di:]
    out_full = full(out_weight, 0)
    sel_t = full(select_weight, 0).T
    gain = full(norm_gain, 0)[None].astype(F32)
    w0 = jnp.concatenate(
        [
            full(conv_weight, 1), full(conv_bias, 0)[None], full(delta_bias, 0)[None], full(skip_gain, 0)[None],
            jnp.zeros((1, di), BF16), full(a_log, 1), full(delta_weight, 1),
            jnp.zeros((PACK0 - DELTA0 - DTR, di), BF16),
        ],
        axis=0,
    ).astype(F32)

    flat = sds((rows * tiles, 128), F32)
    wide = sds((rows, di), F32)
    spread = sds((rows * DS, 128), F32)
    carry = sds((DS, tiles, 128), F32)

    normed, x_in = kernel_call(
        inproj_body, (sds((rows, width), BF16), sds((rows, di), BF16)), 3
    )(tok, gain, in_x)
    halo = shift(x_in[rows - 16 :], 1)
    filt, xs, xt, draw, dt, bb, cb = kernel_call(
        conv_body,
        (wide, sds((rows, di), BF16), flat, wide, flat, spread, spread),
        4,
        [pltpu.VMEM((rows, 128), F32), pltpu.VMEM((rows + 16, 128), F32)],
    )(x_in, halo, w0, sel_t)
    a2, total, end = kernel_call(lightf_body, (carry, carry, carry), 4)(dt, xt, bb, w0)
    gate, gzp, gt, low, adj = kernel_call(
        gate_body, (wide, wide, flat, sds((rows, width), BF16), carry), 7
    )(normed, in_z, cot, out_full, dt, cb, a2)
    state_in = carried_in(total, end, False)
    state_out = carried_in(total, adj, True)
    chunks = rows // 64
    starts, block_out, gz, out_grad, z_grad, skip_grad = kernel_call(
        forward_body,
        (
            sds((chunks, DS, tiles, 128), F32), sds((rows, width), F32), sds((rows, di), BF16),
            sds((di, width), BF16), sds((width, di), BF16), sds((1, di), F32),
        ),
        14,
        [pltpu.VMEM((rows * tiles, 128), F32), pltpu.VMEM((rows, di), BF16), pltpu.VMEM((8, 128), F32)],
    )(state_in, dt, xt, bb, cb, a2, w0, gate, gzp, gt, tok, low, normed, out_full)
    tall = pltpu.VMEM((rows * DS, 128), F32)
    gdt, gat, gb, gc, ga = kernel_call(
        backward_body,
        (flat, flat, sds((rows, 128), F32), sds((rows, 128), F32), carry),
        8,
        [
            pltpu.VMEM((65 * 128, 128), F32), pltpu.VMEM((64 * 128, 128), F32), pltpu.VMEM((256, 128), F32),
            pltpu.VMEM((256, 128), F32), tall, tall,
        ],
    )(state_out, starts, dt, xt, bb, cb, gt, a2)
    gf, w0g, selg = kernel_call(
        tail_body,
        (wide, sds((PACK0, di), F32), sds((PACK0, di), F32)),
        12,
        [
            pltpu.VMEM((rows, 128), F32), pltpu.VMEM((rows + 16, 128), F32), pltpu.VMEM((rows, di), BF16),
            pltpu.VMEM((rows, PACK0), BF16), pltpu.VMEM((DTR, di), BF16),
        ],
    )(gdt, gat, gb, gc, gt, draw, filt, x_in, halo, xs, w0, sel_t)
    edge = shift(gf[:8], -1)
    tokens_grad, x_grad, gain_grad = kernel_call(
        last_body,
        (sds((rows, width), F32), sds((width, di), BF16), sds((1, width), F32)),
        10,
        [pltpu.VMEM((rows + 8, 128), F32), pltpu.VMEM((rows, di), BF16), pltpu.VMEM((rows, width), F32)],
    )(gf, edge, w0, gz, normed, tok, cot, gain, in_x, in_z)

    share = lambda v, d: lax.psum_scatter(v.astype(F32), axes, scatter_dimension=d, tiled=True)
    ga_flat = ga.reshape(DS, di)
    grads = (
        share(gain_grad[0], 0), share(jnp.concatenate([x_grad, z_grad], axis=1), 0), share(w0g[0:KW], 1),
        share(w0g[4], 0), share(selg.T, 0), share(w0g[DELTA0 : DELTA0 + DTR], 1), share(w0g[5], 0),
        share(ga_flat, 1), share(skip_grad[0], 0), share(out_grad, 0),
    )
    return (block_out[None], tokens_grad[None]) + grads


def solution(mesh):
    both = ("batch", "seq")
    first, second = P(both), P(None, both)
    matrix = P(both, None)
    whole = P("batch", "seq", None)
    weights = (first, matrix, second, first, matrix, second, first, second, first, matrix)
    return jax.shard_map(
        on_device,
        mesh=mesh,
        in_specs=(whole, whole) + weights,
        out_specs=(whole, whole) + weights,
        check_vma=False,
    )
```

```python
import functools

import jax
import jax.numpy as jnp
from jax import lax
from jax.experimental import pallas as pl
from jax.experimental.pallas import tpu as pltpu
from jax.sharding import PartitionSpec as P

DS = 16
KW = 4
DTR = 64
EPS = 1e-05
LOG2E = 1.4426950408889634
LN2 = 0.6931471805599453
F32 = jnp.float32
BF16 = jnp.bfloat16
MESH = pl.DeviceIdType.MESH
VM = pl.BlockSpec(memory_space=pltpu.VMEM)
ANY = pl.BlockSpec(memory_space=pl.ANY)
GRANT = 60 << 20
ALOG0, DELTA0, PACK0, PACK = 8, 24, 96, 128


def sds(shape, dtype):
    return jax.ShapeDtypeStruct(shape, dtype)


def kernel_call(body, outs, n_in, scratch=(), flops=1e9, **params):
    return pl.pallas_call(
        body,
        out_shape=outs,
        in_specs=[VM] * n_in,
        out_specs=jax.tree.map(lambda _: VM, outs),
        scratch_shapes=list(scratch),
        cost_estimate=pl.CostEstimate(flops=int(flops), bytes_accessed=8 << 20, transcendentals=0),
        compiler_params=pltpu.CompilerParams(vmem_limit_bytes=GRANT, **params),
    )


def sigmoid(v):
    return 1.0 / (1.0 + jnp.exp(-v))


def dot(a, b):
    return jnp.dot(a, b, preferred_element_type=F32)


def dot_nt(a, b):
    return lax.dot_general(a, b, (((1,), (1,)), ((), ())), preferred_element_type=F32)


def dot_tn(a, b):
    return lax.dot_general(a, b, (((0,), (0,)), ((), ())), preferred_element_type=F32)


def lanes(k, width=128):
    return pl.ds(pl.multiple_of(k * width, width), width)


def inproj_body(tok_ref, gain_ref, inx_ref, normed_ref, xin_ref):
    rows = tok_ref.shape[0]

    def norm(i, _):
        r = pl.ds(pl.multiple_of(i * 16, 16), 16)
        u = tok_ref[r, :]
        scale = lax.rsqrt(jnp.mean(u * u, axis=-1, keepdims=True) + EPS)
        normed_ref[r, :] = (u * scale * gain_ref[...]).astype(BF16)
        return 0

    lax.fori_loop(0, rows // 16, norm, 0)
    width = 512

    def mm(j, _):
        c = lanes(j, width)
        xin_ref[:, c] = dot(normed_ref[...], inx_ref[:, c]).astype(BF16)
        return 0

    lax.fori_loop(0, inx_ref.shape[1] // width, mm, 0)


def conv_body(xin_ref, halo_ref, w0_ref, selt_ref, filt_ref, xs_ref, xt_ref, draw_ref, dt_ref, bb_ref, cb_ref, proj, xp):
    rows, di = xin_ref.shape
    tiles = di // 128
    xp_rows = 16 + rows

    def conv(k, _):
        c = lanes(k)
        xp[0:16, :] = halo_ref[:, c].astype(F32)
        xp[16:xp_rows, :] = xin_ref[:, c].astype(F32)
        for q in range(2):
            r0 = q * (rows // 2)
            f = w0_ref[4:5, c]
            for tap in range(KW):
                lo = 16 - (KW - 1) + tap + r0
                f = f + w0_ref[tap : tap + 1, c] * xp[lo : lo + rows // 2, :]
            s = (f * sigmoid(f)).astype(BF16)
            filt_ref[r0 : r0 + rows // 2, c] = f
            xs_ref[r0 : r0 + rows // 2, c] = s
            xt_ref[pl.ds(r0 * tiles + k, rows // 2, stride=tiles), :] = s.astype(F32)
        return 0

    lax.fori_loop(0, tiles, conv, 0)
    proj[:, 0:96] = dot_nt(xs_ref[...], selt_ref[...])
    low = proj[:, 0:DTR].astype(BF16)

    def delta(k, _):
        c = lanes(k)
        raw = dot(low, w0_ref[DELTA0 : DELTA0 + DTR, c].astype(BF16)) + w0_ref[5:6, c]
        draw_ref[:, c] = raw
        dt_ref[pl.ds(k, rows, stride=tiles), :] = jnp.maximum(raw, 0.0) + jnp.log1p(jnp.exp(-jnp.abs(raw)))
        return 0

    lax.fori_loop(0, tiles, delta, 0)
    row_ids = lax.broadcasted_iota(jnp.int32, (128, 128), 0) % DS
    lane_ids = lax.broadcasted_iota(jnp.int32, (128, 128), 1)
    ones = jnp.ones((128, 128), BF16)

    def spread(i, _):
        r = pl.ds(pl.multiple_of(i * 8, 8), 8)
        p = proj[r, :]
        tall = jnp.broadcast_to(p[:, None, :], (8, DS, 128)).reshape(128, 128)
        o = pl.ds(pl.multiple_of(i * 128, 128), 128)
        for first, ref in ((DTR, bb_ref), (DTR + DS, cb_ref)):
            v = jnp.where(lane_ids == row_ids + first, tall, 0.0)
            hi = v.astype(BF16)
            v = v - hi.astype(F32)
            mid = v.astype(BF16)
            lo = (v - mid.astype(F32)).astype(BF16)
            ref[o, :] = (dot(hi, ones) + dot(mid, ones)) + dot(lo, ones)
        return 0

    lax.fori_loop(0, rows // 8, spread, 0)


def row_of(ref, index):
    return ref[pl.ds(index, 8, stride=0), :]


def tile_at(ref, t, h):
    return ref[pl.ds(pl.multiple_of(t * 16 + h * 8, 8), 8), :]


def light_forward(dt_ref, xt_ref, bb_ref, a2_ref, total_ref, end_ref, rows):
    for h in range(2):
        hs = pl.ds(h * 8, 8)
        a = [a2_ref[n, hs, :] for n in range(DS)]

        def step(t, carry):
            state, run = carry
            d = tile_at(dt_ref, t, h)
            dx = d * tile_at(xt_ref, t, h)
            new = tuple(
                jnp.exp2(a[n] * d) * state[n] + dx * row_of(bb_ref, t * DS + n) for n in range(DS)
            )
            return (new, run + d)

        zero = jnp.zeros((8, 128), F32)
        state, run = lax.fori_loop(0, rows, step, ((zero,) * DS, zero), unroll=4)
        for n in range(DS):
            end_ref[n, hs, :] = state[n]
            total_ref[n, hs, :] = jnp.exp2(a[n] * run)


def light_backward(dt_ref, gt_ref, cb_ref, a2_ref, adj_ref, rows):
    for h in range(2):
        hs = pl.ds(h * 8, 8)
        a = [a2_ref[n, hs, :] for n in range(DS)]

        def step(i, carry):
            t = rows - 1 - i
            d = tile_at(dt_ref, t, h)
            g = tile_at(gt_ref, t, h)
            return tuple(
                jnp.exp2(a[n] * d) * (carry[n] + g * row_of(cb_ref, t * DS + n)) for n in range(DS)
            )

        out = lax.fori_loop(0, rows, step, (jnp.zeros((8, 128), F32),) * DS, unroll=4)
        for n in range(DS):
            adj_ref[n, hs, :] = out[n]


def lightf_body(dt_ref, xt_ref, bb_ref, w0_ref, a2_ref, total_ref, end_ref):
    rows = dt_ref.shape[0] // 16
    for k in range(16):
        a2_ref[:, k, :] = -jnp.exp(w0_ref[ALOG0 : ALOG0 + DS, k * 128 : (k + 1) * 128]) * LOG2E
    light_forward(dt_ref, xt_ref, bb_ref, a2_ref, total_ref, end_ref, rows)


def gate_body(normed_ref, inz_ref, cot_ref, out_ref, dt_ref, cb_ref, a2_ref, gate_ref, gzp_ref, gt_ref, low_ref, adj_ref):
    rows, di = gate_ref.shape
    tiles = di // 128
    low_ref[...] = cot_ref[...].astype(BF16)
    width = 512

    def block(j, _):
        c = lanes(j, width)
        gate_ref[:, c] = dot(normed_ref[...], inz_ref[:, c])
        gzp_ref[:, c] = dot_nt(low_ref[...], out_ref[c, :])
        return 0

    lax.fori_loop(0, di // width, block, 0)

    def point(k, _):
        c = lanes(k)
        for q in range(4):
            r = slice(q * (rows // 4), (q + 1) * (rows // 4))
            z = gate_ref[r, c]
            gg = gzp_ref[r, c]
            s = sigmoid(z)
            gate = z * s
            gate_ref[r, c] = gate
            gzp_ref[r, c] = gg * s * (1.0 + z * (1.0 - s))
            gt_ref[pl.ds(q * (rows // 4) * tiles + k, rows // 4, stride=tiles), :] = gg * gate
        return 0

    lax.fori_loop(0, tiles, point, 0)
    light_backward(dt_ref, gt_ref, cb_ref, a2_ref, adj_ref, rows)


def forward_body(
    si_ref, dt_ref, xt_ref, bb_ref, cb_ref, a2_ref, w0_ref, gate_ref, gzp_ref, gt_ref, tok_ref, low_ref, normed_ref, out_ref,
    starts_ref, block_ref, gz_ref, ograd_ref, zgrad_ref, skipg_ref, yt, gated, low_t,
):
    chunks = starts_ref.shape[0]
    rows, di = gate_ref.shape
    tiles = di // 128
    size = rows // chunks
    for h in range(2):
        hs = pl.ds(h * 8, 8)
        a = [a2_ref[n, hs, :] for n in range(DS)]
        state = tuple(si_ref[n, hs, :] for n in range(DS))
        for chunk in range(chunks):
            for n in range(DS):
                starts_ref[chunk, n, hs, :] = state[n]

            def step(i, carry):
                t = chunk * size + i
                d = tile_at(dt_ref, t, h)
                dx = d * tile_at(xt_ref, t, h)
                new, parts = [], []
                for n in range(DS):
                    s = jnp.exp2(a[n] * d) * carry[n] + dx * row_of(bb_ref, t * DS + n)
                    parts.append(s * row_of(cb_ref, t * DS + n))
                    new.append(s)
                while len(parts) > 1:
                    parts = [parts[i] + parts[i + 1] for i in range(0, len(parts), 2)]
                yt[pl.ds(pl.multiple_of(t * 16 + h * 8, 8), 8), :] = parts[0]
                return tuple(new)

            state = lax.fori_loop(0, size, step, state, unroll=4)

    def point(k, _):
        c = lanes(k)
        total = jnp.zeros((8, 128), F32)
        for q in range(4):
            r = slice(q * (rows // 4), (q + 1) * (rows // 4))
            here = pl.ds(q * (rows // 4) * tiles + k, rows // 4, stride=tiles)
            x = xt_ref[here, :]
            y = yt[here, :] + w0_ref[6:7, c] * x
            gated[r, c] = (y * gate_ref[r, c]).astype(BF16)
            gz_ref[r, c] = (gzp_ref[r, c] * y).astype(BF16)
            total = total + jnp.sum((gt_ref[here, :] * x).reshape(-1, 8, 128), axis=0)
        skipg_ref[:, c] = jnp.sum(total, axis=0, keepdims=True)
        return 0

    lax.fori_loop(0, tiles, point, 0)

    def project(j, _):
        c = lanes(j, 256)
        block_ref[:, c] = tok_ref[:, c] + dot(gated[...], out_ref[:, c])
        return 0

    lax.fori_loop(0, tok_ref.shape[1] // 256, project, 0)

    def wide(j, _):
        c = lanes(j, 256)
        ograd_ref[c, :] = dot_tn(gated[:, c], low_ref[...]).astype(BF16)
        return 0

    lax.fori_loop(0, di // 256, wide, 0)

    def wide_z(j, _):
        c = lanes(j, 256)
        zgrad_ref[:, c] = dot_tn(normed_ref[...], gz_ref[:, c]).astype(BF16)
        return 0

    lax.fori_loop(0, di // 256, wide_z, 0)


def backward_body(
    so_ref, starts_ref, dt_ref, xt_ref, bb_ref, cb_ref, gt_ref, a2_ref,
    gdt_ref, gat_ref, gb_ref, gc_ref, ga_ref, keep, decays, pb, pc, rb, rc,
):
    chunks = starts_ref.shape[0]
    rows = dt_ref.shape[0] // 16
    size = rows // chunks
    zero = jnp.zeros((8, 128), F32)
    for h in range(2):
        hs = pl.ds(h * 8, 8)
        a = [a2_ref[n, hs, :] for n in range(DS)]
        for n in range(DS):
            ga_ref[n, hs, :] = zero
        later = tuple(so_ref[n, hs, :] for n in range(DS))
        for chunk in reversed(range(chunks)):
            base = chunk * size
            first = tuple(starts_ref[chunk, n, hs, :] for n in range(DS))
            for n in range(DS):
                keep[n * 8 : n * 8 + 8, :] = first[n]

            def again(i, carry):
                t = base + i
                d = tile_at(dt_ref, t, h)
                dx = d * tile_at(xt_ref, t, h)
                new = []
                for n in range(DS):
                    w = jnp.exp2(a[n] * d)
                    s = w * carry[n] + dx * row_of(bb_ref, t * DS + n)
                    o = pl.multiple_of(i * 128 + n * 8, 8)
                    decays[pl.ds(o, 8), :] = w
                    keep[pl.ds(pl.multiple_of(o + 128, 8), 8), :] = s
                    new.append(s)
                return tuple(new)

            lax.fori_loop(0, size, again, first, unroll=4)

            def back(j, carry):
                i = size - 1 - j
                t = base + i
                d = tile_at(dt_ref, t, h)
                x = tile_at(xt_ref, t, h)
                gy = tile_at(gt_ref, t, h)
                dx = d * x
                slot = (j % 2) * 128
                new = []
                weighted, through_a = [], []
                for n in range(DS):
                    o = pl.multiple_of(i * 128 + n * 8, 8)
                    w = decays[pl.ds(o, 8), :]
                    before = keep[pl.ds(o, 8), :]
                    now = keep[pl.ds(pl.multiple_of(o + 128, 8), 8), :]
                    g = carry[n] + gy * row_of(cb_ref, t * DS + n)
                    at = pl.ds(pl.multiple_of(slot + n * 8, 8), 8)
                    pc[at, :] = now * gy
                    pb[at, :] = g * dx
                    weighted.append(g * row_of(bb_ref, t * DS + n))
                    g = g * w
                    through = g * before
                    through_a.append(through * a[n])
                    ga_ref[n, hs, :] += through * d
                    new.append(g)
                while len(weighted) > 1:
                    weighted = [weighted[i] + weighted[i + 1] for i in range(0, len(weighted), 2)]
                    through_a = [through_a[i] + through_a[i + 1] for i in range(0, len(through_a), 2)]
                o = pl.ds(pl.multiple_of(t * 16 + h * 8, 8), 8)
                gdt_ref[o, :] = through_a[0] * LN2 + weighted[0] * x
                gat_ref[o, :] = weighted[0] * d
                for src, dst in ((pb, rb), (pc, rc)):
                    for m in range(2):
                        parts = [src[pl.ds(slot + m * 64 + s, 8, stride=8), :] for s in range(8)]
                        while len(parts) > 1:
                            parts = [parts[i] + parts[i + 1] for i in range(0, len(parts), 2)]
                        q = pl.ds(pl.multiple_of(t * 16 + m * 8, 8), 8)
                        if h == 0:
                            dst[q, :] = parts[0]
                        else:
                            dst[q, :] += parts[0]
                return tuple(new)

            later = lax.fori_loop(0, size, back, later, unroll=2)
    for n in range(DS):
        ga_ref[n] = ga_ref[n] * a2_ref[n] * LN2
    ones = jnp.ones((128, 128), BF16)
    pick = lax.broadcasted_iota(jnp.int32, (128, 128), 0) % DS == lax.broadcasted_iota(jnp.int32, (128, 128), 1)

    def collect(i, _):
        o = pl.ds(pl.multiple_of(i * 128, 128), 128)
        for src, dst in ((rb, gb_ref), (rc, gc_ref)):
            v = src[o, :]
            hi = v.astype(BF16)
            lo = (v - hi.astype(F32)).astype(BF16)
            s = jnp.where(pick, dot(hi, ones) + dot(lo, ones), 0.0)
            dst[pl.ds(pl.multiple_of(i * 8, 8), 8), :] = jnp.sum(s.reshape(8, DS, 128), axis=1)
        return 0

    lax.fori_loop(0, rows // 8, collect, 0)


def tail_body(
    gdt_ref, gat_ref, gb_ref, gc_ref, gt_ref, draw_ref, filt_ref, xin_ref, halo_ref, xs_ref, w0_ref, selt_ref,
    gf_ref, w0g_ref, selg_ref, proj, xp, raw_low, gproj, dw,
):
    rows, di = draw_ref.shape
    tiles = di // 128
    proj[:, 0:96] = dot_nt(xs_ref[...], selt_ref[...])
    low = proj[:, 0:DTR].astype(BF16)
    dw[...] = w0_ref[DELTA0 : DELTA0 + DTR, :].astype(BF16)

    def raw(k, _):
        c = lanes(k)
        g = gdt_ref[pl.ds(k, rows, stride=tiles), :] * sigmoid(draw_ref[:, c])
        w0g_ref[5:6, c] = jnp.sum(g, axis=0, keepdims=True)
        gl = g.astype(BF16)
        raw_low[:, c] = gl
        w0g_ref[DELTA0 : DELTA0 + DTR, c] = dot_tn(low, gl)
        return 0

    lax.fori_loop(0, tiles, raw, 0)
    gproj[:, 0:DTR] = dot_nt(raw_low[...], dw[...]).astype(BF16)
    gproj[:, DTR : DTR + DS] = gb_ref[:, 0:DS].astype(BF16)
    gproj[:, DTR + DS : DTR + 2 * DS] = gc_ref[:, 0:DS].astype(BF16)

    def point(k, _):
        c = lanes(k)
        gp = gproj[...]
        selg_ref[:, c] = dot_tn(gp, xs_ref[:, c])
        back = dot(gp, selt_ref[:, c])
        here = pl.ds(k, rows, stride=tiles)
        ga = gt_ref[here, :] * w0_ref[6:7, c] + gat_ref[here, :] + back
        f = filt_ref[:, c]
        s = sigmoid(f)
        gf = ga * (s * (1.0 + f * (1.0 - s)))
        gf_ref[:, c] = gf
        w0g_ref[4:5, c] = jnp.sum(gf, axis=0, keepdims=True)
        xp[0:16, :] = halo_ref[:, c].astype(F32)
        xp[16 : 16 + rows, :] = xin_ref[:, c].astype(F32)
        for tap in range(KW):
            lo = 16 - (KW - 1) + tap
            w0g_ref[tap : tap + 1, c] = jnp.sum(gf * xp[lo : lo + rows, :], axis=0, keepdims=True)
        return 0

    lax.fori_loop(0, tiles, point, 0)


def last_body(gf_ref, edge_ref, w0_ref, gz_ref, normed_ref, tok_ref, cot_ref, gain_ref, inx_ref, inz_ref, tgrad_ref, xgrad_ref, gaing_ref, gp, gx, gn):
    rows, di = gf_ref.shape
    tiles = di // 128

    def conv(k, _):
        c = lanes(k)
        gp[0:rows, :] = gf_ref[:, c]
        gp[rows : rows + 8, :] = edge_ref[:, c]
        total = jnp.zeros((rows, 128), F32)
        for tap in range(KW):
            lo = KW - 1 - tap
            total = total + w0_ref[tap : tap + 1, c] * gp[lo : lo + rows, :]
        gx[:, c] = total.astype(BF16)
        return 0

    lax.fori_loop(0, tiles, conv, 0)

    def wide(j, _):
        c = lanes(j, 256)
        xgrad_ref[:, c] = dot_tn(normed_ref[...], gx[:, c]).astype(BF16)
        return 0

    lax.fori_loop(0, di // 256, wide, 0)

    def back(j, _):
        c = lanes(j, 256)
        gn[:, c] = dot_nt(gx[...], inx_ref[c, :]) + dot_nt(gz_ref[...], inz_ref[c, :])
        return 0

    lax.fori_loop(0, inx_ref.shape[0] // 256, back, 0)

    def rows_of(i, total):
        r = pl.ds(pl.multiple_of(i * 8, 8), 8)
        u = tok_ref[r, :]
        g = gn[r, :]
        scale = lax.rsqrt(jnp.mean(u * u, axis=-1, keepdims=True) + EPS)
        v = g * gain_ref[...]
        mean = jnp.mean(v * u, axis=-1, keepdims=True)
        tgrad_ref[r, :] = cot_ref[r, :] + scale * v - u * (scale * scale * scale * mean)
        return total + g * u * scale

    total = lax.fori_loop(0, rows // 8, rows_of, jnp.zeros((8, tok_ref.shape[1]), F32))
    gaing_ref[...] = jnp.sum(total, axis=0, keepdims=True)


def place():
    b, s = lax.axis_index("batch"), lax.axis_index("seq")
    return b // 2, b % 2, s // 2, s % 2


def device(y, c, z, x):
    return (y * 2 + c, z * 2 + x)


def greet(peers):
    barrier = pltpu.get_barrier_semaphore()
    for peer in peers:
        pl.semaphore_signal(barrier, inc=1, device_id=peer, device_id_type=MESH)
    pl.semaphore_wait(barrier, len(peers))


def remote(src, dst, send, recv, to):
    return pltpu.make_async_remote_copy(
        src_ref=src, dst_ref=dst, send_sem=send, recv_sem=recv, device_id=to, device_id_type=MESH
    )


def neighbours(y, c, z, x):
    return [device(y, c, z ^ k, x) for k in (1, 2, 3)] + [
        device(1 - y, c, z, x), device(y, c, z, 1 - x), device(y, 1 - c, z, x)
    ]


class Gather:
    COPIES = 14

    def __init__(self, src, out, send, recv, local):
        self.src, self.out, self.send, self.recv, self.local = src, out, send, recv, local
        self.at = place()
        self.count = 0
        self.copies = []

    def go(self, view, to):
        i = self.count
        self.count += 1
        source, target = view if isinstance(view, tuple) else (view, view)
        copy = remote(source, target, self.send.at[i], self.recv.at[i], to)
        copy.start()
        self.copies.append(copy)
        return copy

    def stage(self, k):
        y, c, z, x = self.at
        out = self.out
        half = out.shape[4] // 2
        top, bottom = pl.ds(0, half), pl.ds(half, half)
        to_y, to_x, to_c = device(1 - y, c, z, x), device(y, c, z, 1 - x), device(y, 1 - c, z, x)
        if k == 0:
            own = pltpu.make_async_copy(self.src, out.at[y, c, z, x], self.local)
            own.start()
            self.first = [self.go((self.src, out.at[y, c, z, x]), device(y, c, z ^ i, x)) for i in (1, 2, 3)]
            own.wait()
        elif k == 1:
            for copy in self.first:
                copy.wait_recv()
            self.a = self.go(out.at[y, c, :, x, top], to_y)
            self.b = self.go(out.at[y, c, :, x, bottom], to_x)
            self.go(out.at[y, c, :, x], to_c)
        elif k == 2:
            self.a.wait_recv()
            self.b.wait_recv()
            self.next = [self.go(out.at[i, c, :, x, top], to_x) for i in (0, 1)]
            self.next.append(self.go(out.at[y, c, :, :, bottom], to_y))
            self.go(out.at[1 - y, c, :, x, top], to_c)
            self.go(out.at[y, c, :, 1 - x, bottom], to_c)
        elif k == 3:
            for copy in self.next:
                copy.wait_recv()
            for i in (0, 1):
                self.go(out.at[i, c, :, 1 - x, top], to_c)
            self.go(out.at[1 - y, c, :, :, bottom], to_c)
        else:
            done = self.first + [self.a, self.b] + self.next
            for copy in self.copies:
                if not any(copy is other for other in done):
                    copy.wait_recv()

    def drain(self):
        for copy in self.copies:
            copy.wait_send()


STAGES = 5
STEPS = (0, 2, 4, 6, 7)
PACE = 1.0
DELAY = 0
STEPS_LATE = (0, 3, 6, 9, 11)
STEPS_BACK = (0, 3, 6, 9, 12)
STEPS_LAST = (0, 3, 6, 9, 12)
STEPS_PACK = (0, 1, 2, 3, 4)
PACE_BACK = 1.0


def shift(value, by):
    peers = lax.axis_size("seq")
    pairs = [(i, i + by) for i in range(peers) if 0 <= i + by < peers]
    return lax.ppermute(value, "seq", pairs)


def carried_in(total, value, reverse):
    peers, index = lax.axis_size("seq"), lax.axis_index("seq")
    totals = lax.all_gather(total.astype(BF16), "seq")
    values = lax.all_gather(value.astype(BF16), "seq")

    def turn(k, before):
        at = peers - 1 - k if reverse else k
        reached = at > index if reverse else at < index
        new = totals[at].astype(F32) * before + values[at].astype(F32)
        return jnp.where(reached, new, before)

    return lax.fori_loop(0, peers, turn, jnp.zeros(value.shape, F32))


def unpack_weights(pk, w0_ref, selt_ref, gain_ref):
    low_half = lax.broadcasted_iota(jnp.int32, (PACK0, 128), 1) < 64

    def pair(j, _):
        at = (j // 8, j // 4 % 2, j % 4)
        a = pk[at + (0, pl.ds(0, PACK0))].astype(F32)
        b = pk[at + (1, pl.ds(0, PACK0))].astype(F32)
        c = lanes(j)
        w0_ref[:, c] = jnp.where(low_half, a, pltpu.roll(b, 64, 1))
        selt_ref[:, c] = jnp.where(low_half, pltpu.roll(a, 64, 1), b).astype(BF16)
        return 0

    lax.fori_loop(0, 16, pair, 0)

    def gains(j, _):
        total = jnp.zeros((16, 128), F32)
        for i in range(4):
            v = pk[(j // 4, j // 2 % 2, j % 2 * 2 + i // 2, i % 2, pl.ds(PACK0, 16))]
            total = total + v.astype(F32)
        gain_ref[:, lanes(j)] = total[0:8, :]
        return 0

    lax.fori_loop(0, 8, gains, 0)


def normalise(tok, gain, normed):
    rows = tok.shape[0]

    def norm(i, _):
        r = pl.ds(pl.multiple_of(i * 16, 16), 16)
        u = tok[r, :]
        scale = lax.rsqrt(jnp.mean(u * u, axis=-1, keepdims=True) + EPS)
        normed[r, :] = (u * scale * gain[0:1, :]).astype(BF16)
        return 0

    lax.fori_loop(0, rows // 16, norm, 0)


def conv_tiles(first, count, xin, halo, live, w0, filt, xs, xt, xp):
    rows, di = xin.shape
    tiles = di // 128

    def conv(k, _):
        c = lanes(k)
        xp[0:16, :] = halo[:, c].astype(F32) * live
        xp[16 : 16 + rows, :] = xin[:, c].astype(F32)
        for q in range(2):
            r0 = q * (rows // 2)
            f = w0[4:5, c]
            for tap in range(KW):
                lo = 16 - (KW - 1) + tap + r0
                f = f + w0[tap : tap + 1, c] * xp[lo : lo + rows // 2, :]
            s = (f * sigmoid(f)).astype(BF16)
            filt[r0 : r0 + rows // 2, c] = f
            xs[r0 : r0 + rows // 2, c] = s
            xt[pl.ds(r0 * tiles + k, rows // 2, stride=tiles), :] = s.astype(F32)
        return 0

    lax.fori_loop(first, first + count, conv, 0)


def step_sizes(first, count, proj, w0, draw, dt):
    rows, di = draw.shape
    tiles = di // 128
    low = proj[:, 0:DTR].astype(BF16)

    def delta(k, _):
        c = lanes(k)
        raw = dot(low, w0[DELTA0 : DELTA0 + DTR, c].astype(BF16)) + w0[5:6, c]
        draw[:, c] = raw
        dt[pl.ds(k, rows, stride=tiles), :] = jnp.maximum(raw, 0.0) + jnp.log1p(jnp.exp(-jnp.abs(raw)))
        return 0

    lax.fori_loop(first, first + count, delta, 0)


def spread_rows(part, parts, proj, first, ref):
    row_ids = lax.broadcasted_iota(jnp.int32, (128, 128), 0) % DS
    lane_ids = lax.broadcasted_iota(jnp.int32, (128, 128), 1)
    ones = jnp.ones((128, 128), BF16)

    def spread(i, _):
        p = proj[pl.ds(pl.multiple_of(i * 8, 8), 8), :]
        tall = jnp.broadcast_to(p[:, None, :], (8, DS, 128)).reshape(128, 128)
        o = pl.ds(pl.multiple_of(i * 128, 128), 128)
        v = jnp.where(lane_ids == row_ids + first, tall, 0.0)
        hi = v.astype(BF16)
        v = v - hi.astype(F32)
        mid = v.astype(BF16)
        lo = (v - mid.astype(F32)).astype(BF16)
        ref[o, :] = (dot(hi, ones) + dot(mid, ones)) + dot(lo, ones)
        return 0

    count = proj.shape[0] // 8 // parts
    lax.fori_loop(part * count, (part + 1) * count, spread, 0)


def light_forward_part(h, part, parts, dt, xt, bb, a2, total, end, run):
    rows = dt.shape[0] // 16
    size = rows // parts
    hs = pl.ds(h * 8, 8)
    a = [a2[n, hs, :] for n in range(DS)]

    def step(i, carry):
        state, past = carry
        t = part * size + i
        d = tile_at(dt, t, h)
        dx = d * tile_at(xt, t, h)
        new = tuple(jnp.exp2(a[n] * d) * state[n] + dx * row_of(bb, t * DS + n) for n in range(DS))
        return (new, past + d)

    zero = jnp.zeros((8, 128), F32)
    start = ((zero,) * DS, zero) if part == 0 else (tuple(end[n, hs, :] for n in range(DS)), run[hs, :])
    state, past = lax.fori_loop(0, size, step, start, unroll=4)
    run[hs, :] = past
    for n in range(DS):
        end[n, hs, :] = state[n]
        if part == parts - 1:
            total[n, hs, :] = jnp.exp2(a[n] * past)


def light_backward_half(h, dt, gt, cb, a2, adj):
    rows = dt.shape[0] // 16
    hs = pl.ds(h * 8, 8)
    a = [a2[n, hs, :] for n in range(DS)]

    def step(i, carry):
        t = rows - 1 - i
        d = tile_at(dt, t, h)
        g = tile_at(gt, t, h)
        return tuple(jnp.exp2(a[n] * d) * (carry[n] + g * row_of(cb, t * DS + n)) for n in range(DS))

    out = lax.fori_loop(0, rows, step, (jnp.zeros((8, 128), F32),) * DS, unroll=4)
    for n in range(DS):
        adj[n, hs, :] = out[n]


def forward_part(h, q, si, dt, xt, bb, cb, a2, starts, yt):
    size = dt.shape[0] // 16 // starts.shape[0]
    hs = pl.ds(h * 8, 8)
    a = [a2[n, hs, :] for n in range(DS)]
    state = tuple(si[n, hs, :] for n in range(DS))
    for n in range(DS):
        starts[q, n, hs, :] = state[n]

    def step(i, carry):
        t = q * size + i
        d = tile_at(dt, t, h)
        dx = d * tile_at(xt, t, h)
        new, parts = [], []
        for n in range(DS):
            s = jnp.exp2(a[n] * d) * carry[n] + dx * row_of(bb, t * DS + n)
            parts.append(s * row_of(cb, t * DS + n))
            new.append(s)
        while len(parts) > 1:
            parts = [parts[i] + parts[i + 1] for i in range(0, len(parts), 2)]
        yt[pl.ds(pl.multiple_of(t * 16 + h * 8, 8), 8), :] = parts[0]
        return tuple(new)

    state = lax.fori_loop(0, size, step, state, unroll=4)
    for n in range(DS):
        si[n, hs, :] = state[n]


def carry_send(refs, mine, got, send, recv):
    peers = mine.shape[0]
    pair = DS // peers
    b, s = lax.axis_index("batch"), lax.axis_index("seq")
    for j in range(peers):
        for i in range(pair):
            for m, ref in enumerate(refs):
                mine[j, m, i] = ref[j * pair + i].astype(BF16)
    copies = []
    for k in range(1, peers):
        to = lax.rem(s + k, peers)
        copy = remote(mine.at[to], got.at[s], send.at[k - 1], recv.at[k - 1], (b, to))
        copy.start()
        copies.append(copy)
    got[s] = mine[s]
    return copies


def carry_back(back, final, send, recv):
    peers = back.shape[0]
    b, s = lax.axis_index("batch"), lax.axis_index("seq")
    copies = []
    for k in range(1, peers):
        to = lax.rem(s + k, peers)
        copy = remote(back.at[to], final.at[s], send.at[k - 1], recv.at[k - 1], (b, to))
        copy.start()
        copies.append(copy)
    final[s] = back[s]
    return copies


def arrived(copies):
    for copy in copies:
        copy.wait_recv()


WX, WZ, WO = 4, 4, 4


def pack_small(refs, out, me):
    gain, conv, conv_bias, select, delta, delta_bias, a_log, skip = (ref[...].astype(F32) for ref in refs)
    own = conv.shape[1]
    none = jnp.zeros((1, own), F32)
    left = jnp.concatenate([conv, conv_bias, delta_bias, skip, none, a_log, delta, jnp.zeros((PACK0 - DELTA0 - DTR, own), F32)], axis=0)
    right = jnp.concatenate([select, jnp.zeros((own, 128 - PACK0), F32)], axis=1).T[0:PACK0]
    out[0:PACK0, :] = jnp.concatenate([left, right], axis=1).astype(BF16)
    part = gain.shape[1]
    tile = jnp.concatenate([gain] * (128 // part), axis=1)
    mine = lax.broadcasted_iota(jnp.int32, tile.shape, 1) // part == me % (128 // part)
    out[PACK0:PACK, :] = jnp.broadcast_to(jnp.where(mine, tile, 0.0), (PACK - PACK0, 128)).astype(BF16)


def front_body(tok_in, cot_in, inw_in, outw_in, *refs):
    small, refs = refs[:8], refs[8:]
    names = FRONT_OUTS
    o = dict(zip(names, refs[: len(names)]))
    v = dict(zip(FRONT_SCRATCH, refs[len(names) :]))
    stash_sem, load_sem, job_send, job_recv, job_local, ring_send, ring_recv, halo_send, halo_recv = (
        v[n] for n in ("stash", "load", "jsend", "jrecv", "jlocal", "rsend", "rrecv", "hsend", "hrecv")
    )
    y, c, z, x = place()
    b, s = lax.axis_index("batch"), lax.axis_index("seq")
    peers = v["mine"].shape[0]
    stash = []

    def put(*keys):
        for key in keys:
            copy = pltpu.make_async_copy(v[key], o[key], stash_sem.at[len(stash)])
            copy.start()
            stash.append(copy)

    load_tok = pltpu.make_async_copy(tok_in, v["tok"], load_sem.at[0])
    load_cot = pltpu.make_async_copy(cot_in, v["cot"], load_sem.at[1])
    load_tok.start()
    load_cot.start()
    pack_small(small, v["packed"], b * peers + s)
    greet([(b, lax.rem(s + k, peers)) for k in range(1, peers)] + [device(1 - y, c, z, x), device(y, 1 - c, z, x)])

    jobs = []

    def job(src, out):
        i = len(jobs)
        jobs.append(Gather(src, out, job_send.at[i], job_recv.at[i], job_local.at[i]))

    width = inw_in.shape[1] // 2 // WX
    wide_z = inw_in.shape[1] // 2 // WZ
    wide_o = outw_in.shape[1] // WO
    job(v["packed"], v["pk"])
    for i in range(WX):
        job(inw_in.at[:, pl.ds(i * width, width)], v["inx"].at[i])
    for i in range(WZ):
        job(inw_in.at[:, pl.ds(inw_in.shape[1] // 2 + i * wide_z, wide_z)], v["inz"].at[i])
    for i in range(WO):
        job(outw_in.at[:, pl.ds(i * wide_o, wide_o)], v["wo"].at[i])
    events = sorted(
        (i + STEPS[k] if i <= WX else i + DELAY + STEPS_LATE[k], -k, i) for i in range(len(jobs)) for k in range(STAGES)
    )
    clock = [0.0]

    def advance():
        _, k, i = events.pop(0)
        jobs[i].stage(-k)

    def landed(i):
        while any(e[2] == i for e in events):
            advance()
            clock[0] = 0.0

    def spend(time):
        clock[0] += time
        while clock[0] >= PACE:
            clock[0] -= PACE
            if events:
                advance()

    di = v["xin"].shape[1]
    rows = v["xin"].shape[0]
    tiles = di // 128
    per = tiles // WX
    live = jnp.where(s > 0, 1.0, 0.0)
    halos = []

    def project_x(i):
        cols = pl.ds(i * width, width)
        v["xin"][:, cols] = dot(v["normed"][...], v["inx"][i].reshape(-1, width)).astype(BF16)
        copy = remote(
            v["xin"].at[pl.ds(rows - 16, 16), cols], v["halo"].at[:, cols],
            halo_send.at[i], halo_recv.at[i], (b, lax.rem(s + 1, peers)),
        )
        copy.start()
        halos.append(copy)

    def conv(i):
        halos[i].wait_recv()
        conv_tiles(i * per, per, v["xin"], v["halo"], live, v["w0"], v["filt"], v["xs"], v["xt"], v["xp"])

    landed(0)
    unpack_weights(v["pk"], v["w0"], v["selt"], v["gain"])
    load_tok.wait()
    normalise(v["tok"], v["gain"], v["normed"])
    put("w0", "selt", "gain", "normed")
    for k in range(16):
        v["a2"][:, k, :] = -jnp.exp(v["w0"][ALOG0 : ALOG0 + DS, k * 128 : (k + 1) * 128]) * LOG2E
    put("a2")
    for i in range(WX):
        landed(1 + i)
        project_x(i)
        if i > 0:
            conv(i - 1)
    put("inx")
    load_cot.wait()
    v["low"][...] = v["cot"][...].astype(BF16)
    put("low")
    conv(WX - 1)
    put("xin", "halo", "filt", "xs", "xt")
    v["proj"][:, 0:PACK0] = dot_nt(v["xs"][...], v["selt"][...])
    spend(1.5)
    for q in range(4):
        step_sizes(q * (tiles // 4), tiles // 4, v["proj"], v["w0"], v["draw"], v["dt"])
        spend(1.0)
    put("draw", "dt")
    for q in range(4):
        spread_rows(q, 4, v["proj"], DTR, v["bb"])
        spend(0.85)
    put("bb")
    for h in range(2):
        for q in range(4):
            light_forward_part(h, q, 4, v["dt"], v["xt"], v["bb"], v["a2"], v["total"], v["end"], v["run"])
            spend(0.8)

    sent = carry_send((v["total"], v["end"]), v["mine"], v["got"], ring_send.at[0], ring_recv.at[0])

    def project_z(i):
        landed(1 + WX + i)
        v["gate"][:, i * wide_z : (i + 1) * wide_z] = dot(v["normed"][...], v["inz"][i].reshape(-1, wide_z))

    for q in range(4):
        spread_rows(q, 4, v["proj"], DTR + DS, v["cb"])
        spend(0.85)
    put("cb")
    arrived(sent)
    state = jnp.zeros(v["back"].shape[1:], F32)
    for p in range(peers):
        v["back"][p] = state.astype(BF16)
        state = v["got"][p, 0].astype(F32) * state + v["got"][p, 1].astype(F32)
    more = carry_back(v["back"], v["final"], ring_send.at[1], ring_recv.at[1])
    sent += more
    for i in range(WZ - 1):
        project_z(i)
    arrived(more)
    pair = DS // peers
    for j in range(peers):
        for i in range(pair):
            v["si"][j * pair + i] = v["final"][j, i].astype(F32)
    clock[0] = 0.0
    for q in range(v["starts"].shape[0]):
        for h in range(2):
            forward_part(h, q, v["si"], v["dt"], v["xt"], v["bb"], v["cb"], v["a2"], v["starts"], v["yt"])
            spend(0.6)
    put("starts")
    project_z(3)
    put("inz")
    landed(len(jobs) - 1)

    block = 512
    per_b = block // (di // 32)

    def gated_grad(j, _):
        out = jnp.zeros((rows, block), F32)
        for i in range(WO):
            w = v["wo"][i, j // 2, j % 2].reshape(block, wide_o)
            out = out + dot_nt(v["low"][:, i * wide_o : (i + 1) * wide_o], w)
        v["gzp"][:, lanes(j, block)] = out
        return 0

    lax.fori_loop(0, di // block, gated_grad, 0)

    def point(k, _):
        cols = lanes(k)
        for q in range(4):
            r = slice(q * (rows // 4), (q + 1) * (rows // 4))
            zz = v["gate"][r, cols]
            gg = v["gzp"][r, cols]
            sg = sigmoid(zz)
            gate = zz * sg
            v["gate"][r, cols] = gate
            v["gzp"][r, cols] = gg * sg * (1.0 + zz * (1.0 - sg))
            v["gt"][pl.ds(q * (rows // 4) * tiles + k, rows // 4, stride=tiles), :] = gg * gate
        return 0

    lax.fori_loop(0, tiles, point, 0)
    put("gt")
    for h in range(2):
        light_backward_half(h, v["dt"], v["gt"], v["cb"], v["a2"], v["adj"])
    again = carry_send((v["adj"],), v["mine2"], v["got2"], ring_send.at[2], ring_recv.at[2])
    sent += again

    def emit(k, _):
        cols = lanes(k)
        total = jnp.zeros((8, 128), F32)
        for q in range(4):
            r = slice(q * (rows // 4), (q + 1) * (rows // 4))
            here = pl.ds(q * (rows // 4) * tiles + k, rows // 4, stride=tiles)
            xx = v["xt"][here, :]
            yy = v["yt"][here, :] + v["w0"][6:7, cols] * xx
            v["gated"][r, cols] = (yy * v["gate"][r, cols]).astype(BF16)
            v["gz"][r, cols] = (v["gzp"][r, cols] * yy).astype(BF16)
            total = total + jnp.sum((v["gt"][here, :] * xx).reshape(-1, 8, 128), axis=0)
        v["skipg"][:, cols] = jnp.broadcast_to(jnp.sum(total, axis=0, keepdims=True), (8, 128))
        return 0

    lax.fori_loop(0, tiles, emit, 0)
    put("gated", "gz", "skipg")
    for i in range(WO):
        cols = pl.ds(i * wide_o, wide_o)
        w = v["wo"][i].reshape(di, wide_o)
        v["tok"][:, cols] = v["tok"][:, cols] + dot(v["gated"][...], w)
    copy = pltpu.make_async_copy(v["tok"], o["block"], load_sem.at[0])
    copy.start()
    arrived(again)
    state = jnp.zeros(v["back2"].shape[1:], F32)
    for p in reversed(range(peers)):
        v["back2"][p] = state.astype(BF16)
        state = v["got"][p, 0].astype(F32) * state + v["got2"][p, 0].astype(F32)
    put("back2")
    copy.wait()
    for it in jobs:
        it.drain()
    for it in sent + halos:
        it.wait_send()
    for it in stash:
        it.wait()


FRONT_OUTS = (
    "block", "w0", "selt", "gain", "normed", "a2", "inx", "xin", "halo", "filt", "xs", "xt", "low", "draw", "dt",
    "bb", "cb", "inz", "starts", "gt", "gated", "gz", "skipg", "back2",
)
FRONT_SCRATCH = (
    "w0", "selt", "gain", "normed", "a2", "inx", "xin", "halo", "filt", "xs", "xt", "low", "draw", "dt",
    "bb", "cb", "inz", "starts", "gt", "gated", "gz", "skipg", "back2",
    "tok", "cot", "pk", "wo", "proj", "xp", "gate", "gzp", "yt", "total", "end", "adj", "si",
    "mine", "got", "back", "final", "mine2", "got2", "run", "packed",
    "stash", "load", "jsend", "jrecv", "jlocal", "rsend", "rrecv", "hsend", "hrecv",
)


def front(tok, cot, in_weight, out_weight, small, peers, chunks):
    rows, width = tok.shape
    di = in_weight.shape[1] // 2
    tiles = di // 128
    lead = (2, 2, 4, 2)
    flat, wide, carry = ((rows * tiles, 128), F32), ((rows, di), F32), ((DS, tiles, 128), F32)
    spread, half = ((rows * DS, 128), F32), ((rows, di), BF16)
    pair = (DS // peers, tiles, 128)
    shapes = {
        "block": ((rows, width), F32), "w0": ((PACK0, di), F32), "selt": ((PACK0, di), BF16), "gain": ((8, width), F32),
        "normed": ((rows, width), BF16), "a2": carry, "inx": ((WX,) + lead + (in_weight.shape[0], di // WX), BF16),
        "xin": half, "halo": ((16, di), BF16), "filt": wide, "xs": half, "xt": flat, "low": ((rows, width), BF16),
        "draw": wide, "dt": flat, "bb": spread, "cb": spread,
        "inz": ((WZ,) + lead + (in_weight.shape[0], di // WZ), BF16), "starts": ((chunks, DS, tiles, 128), F32),
        "gt": flat, "gated": half, "gz": half, "skipg": ((8, di), F32),
        "tok": ((rows, width), F32), "cot": ((rows, width), F32), "pk": (lead + (PACK, 128), BF16),
        "wo": ((WO,) + lead + (out_weight.shape[0], width // WO), BF16), "proj": ((rows, 128), F32),
        "xp": ((rows + 16, 128), F32), "gate": wide, "gzp": wide, "yt": flat, "total": carry, "end": carry, "adj": carry,
        "si": carry, "mine": ((peers, 2) + pair, BF16), "got": ((peers, 2) + pair, BF16), "back": ((peers,) + pair, BF16),
        "final": ((peers,) + pair, BF16), "mine2": ((peers, 1) + pair, BF16), "got2": ((peers, 1) + pair, BF16),
        "back2": ((peers,) + pair, BF16), "packed": ((PACK, 128), BF16), "run": ((tiles, 128), F32),
    }
    n_jobs = 1 + WX + WZ + WO
    dma = pltpu.SemaphoreType.DMA
    sems = {
        "stash": dma((len(FRONT_OUTS) - 1,)), "load": dma((2,)), "jsend": dma((n_jobs, Gather.COPIES)),
        "jrecv": dma((n_jobs, Gather.COPIES)), "jlocal": dma((n_jobs,)), "rsend": dma((3, peers - 1)),
        "rrecv": dma((3, peers - 1)), "hsend": dma((WX,)), "hrecv": dma((WX,)),
    }
    outs = pl.pallas_call(
        front_body,
        out_shape=tuple(sds(*shapes[n]) for n in FRONT_OUTS),
        in_specs=[ANY] * 4 + [VM] * len(small),
        out_specs=(ANY,) * len(FRONT_OUTS),
        scratch_shapes=[sems[n] if n in sems else pltpu.VMEM(*shapes[n]) for n in FRONT_SCRATCH],
        compiler_params=pltpu.CompilerParams(collective_id=0, has_side_effects=True, vmem_limit_bytes=GRANT),
    )(tok, cot, in_weight, out_weight, *small)
    return dict(zip(FRONT_OUTS, outs))


class Share:
    COPIES = 10

    def __init__(self, own, other, r1, r2, r3, r4, out, send, recv):
        self.own, self.other, self.r1, self.r2, self.r3, self.r4, self.out = own, other, r1, r2, r3, r4, out
        self.send, self.recv = send, recv
        self.at = place()
        self.copies = []

    def go(self, source, target, to):
        i = len(self.copies)
        copy = remote(source, target, self.send.at[i], self.recv.at[i], to)
        copy.start()
        self.copies.append(copy)
        return copy

    def stage(self, k):
        y, c, z, x = self.at
        own = self.own
        half = own.shape[3] // 2
        top, bottom = pl.ds(0, half), pl.ds(half, half)
        to_y, to_x, to_c = device(1 - y, c, z, x), device(y, c, z, 1 - x), device(y, 1 - c, z, x)
        if k > 0:
            arrived(self.wait)
        if k == 0:
            self.wait = [self.go(self.other.at[i], self.r1.at[i], to_c) for i in (0, 1)]
        elif k == 1:

            def piece(i, _):
                at = (i // 8, i // 2 % 4, i % 2)
                own[at] = own[at] + self.r1[at]
                return 0

            lax.fori_loop(0, 16, piece, 0)
            self.wait = [self.go(own.at[1 - y, :, :, top], self.r2.at[pl.ds(0, 4), :], to_y)]
            for i in (0, 1):
                self.wait.append(self.go(own.at[i, :, 1 - x, bottom], self.r2.at[pl.ds(4, 4), i], to_x))
        elif k == 2:

            def piece(i, _):
                b, d = i // 2, i % 2
                own[y, b, d, top] = own[y, b, d, top] + self.r2[b, d]
                own[d, b, x, bottom] = own[d, b, x, bottom] + self.r2[4 + b, d]
                return 0

            lax.fori_loop(0, 8, piece, 0)
            self.wait = [
                self.go(own.at[y, :, 1 - x, top], self.r3.at[0], to_x),
                self.go(own.at[1 - y, :, x, bottom], self.r3.at[1], to_y),
            ]
        elif k == 3:

            def piece(b, _):
                own[y, b, x, top] = own[y, b, x, top] + self.r3[0, b]
                own[y, b, x, bottom] = own[y, b, x, bottom] + self.r3[1, b]
                return 0

            lax.fori_loop(0, 4, piece, 0)
            self.wait = [
                self.go(own.at[y, z ^ i, x], self.r4.at[i - 1], device(y, c, z ^ i, x)) for i in (1, 2, 3)
            ]
        else:
            total = own[y, z, x].astype(F32)
            for i in range(3):
                total = total + self.r4[i].astype(F32)
            self.out[...] = total

    def drain(self):
        for copy in self.copies:
            copy.wait_send()
        self.copies = []


def adjoint_part(chunk, h, dt, xt, bb, cb, gt, a2, starts, later, keep, decays, pb, pc, rb, rc, ga, size):
    hs = pl.ds(h * 8, 8)
    base = chunk * size
    first = tuple(starts[chunk, n, hs, :] for n in range(DS))
    for n in range(DS):
        keep[n * 8 : n * 8 + 8, :] = first[n]

    def again(i, carry):
        t = base + i
        d = tile_at(dt, t, h)
        dx = d * tile_at(xt, t, h)
        new = []
        for n in range(DS):
            w = jnp.exp2(a2[n, hs, :] * d)
            s = w * carry[n] + dx * row_of(bb, t * DS + n)
            o = pl.multiple_of(i * 128 + n * 8, 8)
            decays[pl.ds(o, 8), :] = w
            keep[pl.ds(pl.multiple_of(o + 128, 8), 8), :] = s
            new.append(s)
        return tuple(new)

    lax.fori_loop(0, size, again, first, unroll=4)

    def back(j, carry):
        i = size - 1 - j
        t = base + i
        d = tile_at(dt, t, h)
        x = tile_at(xt, t, h)
        gy = tile_at(gt, t, h)
        dx = d * x
        slot = (j % 2) * 128
        new = []
        weighted, through_a = [], []
        for n in range(DS):
            o = pl.multiple_of(i * 128 + n * 8, 8)
            w = decays[pl.ds(o, 8), :]
            before = keep[pl.ds(o, 8), :]
            now = keep[pl.ds(pl.multiple_of(o + 128, 8), 8), :]
            g = carry[n] + gy * row_of(cb, t * DS + n)
            at = pl.ds(pl.multiple_of(slot + n * 8, 8), 8)
            pc[at, :] = now * gy
            pb[at, :] = g * dx
            weighted.append(g * row_of(bb, t * DS + n))
            g = g * w
            through = g * before
            through_a.append(through * a2[n, hs, :])
            ga[n, hs, :] += through * d
            new.append(g)
        while len(weighted) > 1:
            weighted = [weighted[i] + weighted[i + 1] for i in range(0, len(weighted), 2)]
            through_a = [through_a[i] + through_a[i + 1] for i in range(0, len(through_a), 2)]
        o = pl.ds(pl.multiple_of(t * 16 + h * 8, 8), 8)
        dt[o, :] = through_a[0] * LN2 + weighted[0] * x
        xt[o, :] = weighted[0] * d
        for src, dst in ((pb, rb), (pc, rc)):
            for m in range(2):
                parts = [src[pl.ds(slot + m * 64 + s, 8, stride=8), :] for s in range(8)]
                while len(parts) > 1:
                    parts = [parts[i] + parts[i + 1] for i in range(0, len(parts), 2)]
                q = pl.ds(pl.multiple_of(i * 16 + m * 8, 8), 8)
                if h == 0:
                    dst[q, :] = parts[0]
                else:
                    dst[q, :] += parts[0]
        return tuple(new)

    out = lax.fori_loop(0, size, back, tuple(later[n, hs, :] for n in range(DS)), unroll=2)
    for n in range(DS):
        later[n, hs, :] = out[n]


def collect_rows(chunk, size, rb, rc, gb, gc):
    ones = jnp.ones((8, 128), BF16)
    per = size * DS // 128
    for src, dst in ((rb, gb), (rc, gc)):
        v = src[...]
        hi = v.astype(BF16)
        lo = (v - hi.astype(F32)).astype(BF16)
        s = dot_nt(ones, hi) + dot_nt(ones, lo)
        for i in range(per):
            dst[chunk * per + i : chunk * per + i + 1, :] = s[0:1, i * 128 : (i + 1) * 128]


BACK_IN = (
    "back2", "gated", "low", "normed", "gz", "dt", "xt", "bb", "cb", "gt", "a2", "starts", "draw", "xs", "w0", "selt",
    "filt", "xin", "halo", "inx", "inz", "gain", "skipg", "tok", "cot",
)
BACK_LOAD = tuple(n for n in BACK_IN if n not in ("inx", "inz"))
BACK_OUT = ("tgrad", "gin", "gout", "gpack")
BACK_SCRATCH = BACK_LOAD[:-1] + (
    "wbuf", "keep", "decays", "pb", "pc", "rb", "rc", "ga", "gb", "gc", "proj", "xp", "gp", "rawlow", "gproj", "dw", "w0g",
    "selg", "edge", "gx", "gn", "gaing",
    "own", "other", "r1", "r2", "r3", "r4", "pown", "pother", "p1", "p2", "p3", "p4",
    "so", "final2",
    "load", "wsem", "send", "recv", "esend", "erecv", "rsend", "rrecv",
)
BLOCKS = 4


def back_body(*refs):
    hbm = dict(zip(BACK_IN, refs))
    refs = refs[len(BACK_IN) :]
    o = dict(zip(BACK_OUT, refs))
    v = dict(zip(BACK_SCRATCH, refs[len(BACK_OUT) :]))
    loads = {}
    for i, name in enumerate(BACK_LOAD):
        loads[name] = pltpu.make_async_copy(hbm[name], o["tgrad"] if name == "cot" else v[name], v["load"].at[i])
        loads[name].start()

    def need(*names):
        for name in names:
            loads[name].wait()

    y, c, z, x = place()
    b, s = lax.axis_index("batch"), lax.axis_index("seq")
    peers = lax.axis_size("seq")
    greet([(b, lax.rem(s + k, peers)) for k in range(1, peers)] + [device(1 - y, c, z, x), device(y, 1 - c, z, x)])
    need("back2")
    sent = carry_back(v["back2"], v["final2"], v["rsend"].at[0], v["rrecv"].at[0])

    rows, di = v["gz"].shape
    width = v["normed"].shape[1]
    tiles = di // 128
    cols = di // BLOCKS
    half = width // 2
    owned = v["own"].shape[4]
    jobs = []

    def job(out):
        i = len(jobs)
        at = i % (2 * BLOCKS)
        jobs.append(
            Share(
                v["own"].at[at], v["other"].at[at], v["r1"].at[i], v["r2"].at[i], v["r3"].at[i], v["r4"].at[i],
                out, v["send"].at[i], v["recv"].at[i],
            )
        )

    for i in range(4):
        job(o["gout"].at[i // 2 * owned : (i // 2 + 1) * owned, i % 2 * half : (i % 2 + 1) * half])
    for i in range(BLOCKS):
        job(o["gin"].at[:, di + i * cols : di + (i + 1) * cols])
    for i in range(BLOCKS):
        job(o["gin"].at[:, i * cols : (i + 1) * cols])
    last = len(jobs)
    jobs.append(
        Share(
            v["pown"], v["pother"], v["p1"], v["p2"], v["p3"], v["p4"], o["gpack"], v["send"].at[last], v["recv"].at[last]
        )
    )
    events, now, clock = [], [0], [0.0]
    first = [0]

    def enter(*blocks, steps=STEPS_BACK):
        for i in blocks:
            first[0] = max(first[0] + 1, now[0])
            events.extend((first[0] + steps[k], -k, i) for k in range(STAGES))
        events.sort()

    def advance():
        now[0], k, i = events.pop(0)
        jobs[i].stage(-k)

    def spend(time):
        clock[0] += time
        while clock[0] >= PACE_BACK:
            clock[0] -= PACE_BACK
            if events:
                advance()

    def finish(i):
        while any(e[2] == i for e in events):
            advance()
        jobs[i].drain()

    need("gated", "low")

    def out_blocks(core, dst):
        def block(i, _):
            first = pl.multiple_of(((i // 2) * 2 + core) * (di // 4) + (i % 2) * 256, 256)
            g = v["gated"][:, pl.ds(first, 256)]
            for q in range(2):
                r = dot_tn(g, v["low"][:, q * half : (q + 1) * half]).astype(BF16).reshape(2, 2, 2, owned, half)
                for p in range(2):
                    dst[p * 2 + q, i // 2, pl.ds((i % 2) * 2, 2)] = r[:, :, p]
            return 0

        lax.fori_loop(0, 4, block, 0)

    def in_blocks(core, dst, first, right):
        def block(i, _):
            n = v["normed"][:, pl.ds(pl.multiple_of((i * 2 + core) * (width // 4), 256), width // 4)]
            for q, g in enumerate(right):
                dst[first + q, i] = dot_tn(n, g()).astype(BF16).reshape(4, 2, owned, cols)
            return 0

        lax.fori_loop(0, 2, block, 0)

    out_blocks(1 - c, v["other"])
    enter(0, 1, 2, 3)
    advance()
    advance()
    out_blocks(c, v["own"])
    need("normed", "gz")
    z_right = [lambda q=q: v["gz"][:, q * cols : (q + 1) * cols] for q in range(BLOCKS)]
    in_blocks(1 - c, v["other"], BLOCKS, z_right)
    enter(4, 5, 6, 7)
    in_blocks(c, v["own"], BLOCKS, z_right)
    spend(3.0)
    arrived(sent)
    pair = DS // peers
    for j in range(peers):
        for i in range(pair):
            v["so"][j * pair + i] = v["final2"][j, i].astype(F32)

    need("dt", "xt", "bb", "cb", "gt", "a2", "starts")
    v["ga"][...] = jnp.zeros_like(v["ga"])
    chunks = v["starts"].shape[0]
    size = rows // chunks
    for chunk in reversed(range(chunks)):
        for h in range(2):
            adjoint_part(
                chunk, h, v["dt"], v["xt"], v["bb"], v["cb"], v["gt"], v["a2"], v["starts"], v["so"], v["keep"],
                v["decays"], v["pb"], v["pc"], v["rb"], v["rc"], v["ga"], size,
            )
            spend(2.0)
        collect_rows(chunk, size, v["rb"], v["rc"], v["gb"], v["gc"])
        spend(0.75)

    need("draw", "xs", "w0", "selt")
    v["proj"][:, 0:PACK0] = dot_nt(v["xs"][...], v["selt"][...])
    low = v["proj"][:, 0:DTR].astype(BF16)
    v["dw"][...] = v["w0"][DELTA0 : DELTA0 + DTR, :].astype(BF16)
    w0g = v["w0g"]

    def raw(k, _):
        at = lanes(k)
        g = v["dt"][pl.ds(k, rows, stride=tiles), :] * sigmoid(v["draw"][:, at])
        w0g[5:6, at] = jnp.sum(g, axis=0, keepdims=True)
        gl = g.astype(BF16)
        v["rawlow"][:, at] = gl
        w0g[DELTA0 : DELTA0 + DTR, at] = dot_tn(low, gl)
        return 0

    spend(0.5)
    for q in range(BLOCKS):
        lax.fori_loop(q * (tiles // BLOCKS), (q + 1) * (tiles // BLOCKS), raw, 0)
        spend(0.85)
    v["gproj"][:, 0:DTR] = dot_nt(v["rawlow"][...], v["dw"][...]).astype(BF16)
    per = 128 // DS
    for first_lane, src in ((DTR, v["gb"]), (DTR + DS, v["gc"])):
        for i in range(per):
            v["proj"][pl.ds(i, rows // per, stride=per), 0:DS] = src[:, i * DS : (i + 1) * DS]
        v["gproj"][:, first_lane : first_lane + DS] = v["proj"][:, 0:DS].astype(BF16)
    need("filt", "xin", "halo")
    not_first = jnp.where(s > 0, 1.0, 0.0)
    not_last = jnp.where(s < peers - 1, 1.0, 0.0)

    def point(k, _):
        at = lanes(k)
        gp = v["gproj"][...]
        v["selg"][:, at] = dot_tn(gp, v["xs"][:, at])
        into = dot(gp, v["selt"][:, at])
        here = pl.ds(k, rows, stride=tiles)
        g = v["gt"][here, :] * v["w0"][6:7, at] + v["xt"][here, :] + into
        f = v["filt"][:, at]
        sg = sigmoid(f)
        gf = g * (sg * (1.0 + f * (1.0 - sg)))
        v["filt"][:, at] = gf
        w0g[4:5, at] = jnp.sum(gf, axis=0, keepdims=True)
        v["xp"][0:16, :] = v["halo"][:, at].astype(F32) * not_first
        v["xp"][16 : 16 + rows, :] = v["xin"][:, at].astype(F32)
        for tap in range(KW):
            lo = 16 - (KW - 1) + tap
            w0g[tap : tap + 1, at] = jnp.sum(gf * v["xp"][lo : lo + rows, :], axis=0, keepdims=True)
        return 0

    edges = []

    def points(q):
        lax.fori_loop(q * (tiles // BLOCKS), (q + 1) * (tiles // BLOCKS), point, 0)
        at = pl.ds(q * cols, cols)
        copy = remote(
            v["filt"].at[pl.ds(0, 8), at], v["edge"].at[:, at], v["esend"].at[q], v["erecv"].at[q],
            (b, lax.rem(s + peers - 1, peers)),
        )
        copy.start()
        edges.append(copy)

    weights = {}

    def fetch(i):
        source = hbm["inx"].at[i] if i < WX else hbm["inz"].at[i - WX]
        weights[i] = pltpu.make_async_copy(source, v["wbuf"].at[i % 2], v["wsem"].at[i])
        weights[i].start()

    fetch(0)
    fetch(1)

    def blocks(q):
        edges[q].wait_recv()

        def conv(k, _):
            at = lanes(k)
            v["gp"][0:rows, :] = v["filt"][:, at]
            v["gp"][rows : rows + 8, :] = v["edge"][:, at] * not_last
            total = jnp.zeros((rows, 128), F32)
            for tap in range(KW):
                lo = KW - 1 - tap
                total = total + v["w0"][tap : tap + 1, at] * v["gp"][lo : lo + rows, :]
            v["gx"][:, at] = total.astype(BF16)
            return 0

        lax.fori_loop(q * (tiles // BLOCKS), (q + 1) * (tiles // BLOCKS), conv, 0)
        right = [lambda: v["gx"][:, q * cols : (q + 1) * cols]]
        finish(q)
        in_blocks(1 - c, v["other"], q, right)
        jobs[2 * BLOCKS + q].stage(0)
        enter(2 * BLOCKS + q, steps=STEPS_LAST)
        events.remove((first[0], 0, 2 * BLOCKS + q))
        in_blocks(c, v["own"], q, right)
        while events and events[0][0] <= first[0]:
            advance()

    def into_rows(i):
        weights[i].wait()
        g = v["gx"] if i < WX else v["gz"]
        q = i % WX
        for d in range(2):
            w = v["wbuf"][i % 2].reshape(width, cols)[d * half : (d + 1) * half]
            part = dot_nt(g[:, q * cols : (q + 1) * cols], w)
            at = slice(d * half, (d + 1) * half)
            v["gn"][:, at] = part if i == 0 else v["gn"][:, at] + part
        if i + 2 < 2 * WX:
            fetch(i + 2)
        spend(0.5)

    points(0)
    points(1)
    for q in range(2, BLOCKS):
        points(q)
        blocks(q - 2)
    blocks(BLOCKS - 2)
    blocks(BLOCKS - 1)
    for i in range(2 * WX):
        into_rows(i)
    need("tok", "cot", "gain")

    def rows_of(i, total):
        r = pl.ds(pl.multiple_of(i * 8, 8), 8)
        u = v["tok"][r, :]
        g = v["gn"][r, :]
        scale = lax.rsqrt(jnp.mean(u * u, axis=-1, keepdims=True) + EPS)
        w = g * v["gain"][0:1, :]
        mean = jnp.mean(w * u, axis=-1, keepdims=True)
        o["tgrad"][r, :] = o["tgrad"][r, :] + scale * w - u * (scale * scale * scale * mean)
        return total + g * u * scale

    total = lax.fori_loop(0, rows // 8, rows_of, jnp.zeros((8, width), F32))
    v["gaing"][...] = jnp.broadcast_to(jnp.sum(total, axis=0, keepdims=True), (8, width))
    need("skipg")
    w0g[6:7, :] = v["skipg"][0:1, :]
    w0g[7:8, :] = jnp.zeros((1, di), F32)
    w0g[DELTA0 + DTR : PACK0, :] = jnp.zeros((PACK0 - DELTA0 - DTR, di), F32)
    for k in range(tiles):
        w0g[ALOG0 : ALOG0 + DS, k * 128 : (k + 1) * 128] = v["ga"][:, k, :] * v["a2"][:, k, :] * LN2
    low_half = lax.broadcasted_iota(jnp.int32, (PACK0, 128), 1) < 64

    def pack(core, dst):
        def pair(i, _):
            j = i // 4 * 8 + core * 4 + i % 4
            at = lanes(j)
            l, r = w0g[:, at], v["selg"][:, at]
            dst[i // 4, i % 4, 0, 0:PACK0, :] = jnp.where(low_half, l, pltpu.roll(r, 64, 1)).astype(BF16)
            dst[i // 4, i % 4, 1, 0:PACK0, :] = jnp.where(low_half, pltpu.roll(l, 64, 1), r).astype(BF16)
            g = jnp.broadcast_to(v["gaing"][0:1, lanes(j // 2)], (PACK - PACK0, 128)).astype(BF16)
            for d in range(2):
                dst[i // 4, i % 4, d, PACK0:PACK, :] = g
            return 0

        lax.fori_loop(0, 8, pair, 0)

    spend(3.0)
    pack(1 - c, v["pother"])
    jobs[last].stage(0)
    pack(c, v["pown"])
    first[0] = now[0] - 1
    enter(last, steps=STEPS_PACK)
    events.remove((first[0], 0, last))
    while events:
        advance()
    for it in jobs:
        it.drain()
    for it in edges + sent:
        it.wait_send()


def back(f, tok, cot):
    rows, di = f["gz"].shape
    width = tok.shape[1]
    tiles = di // 128
    cols = di // BLOCKS
    chunks = f["starts"].shape[0]
    size = rows // chunks
    lead = (2, 4, 2)
    owned = width // 32
    inputs = dict(f, tok=tok, cot=cot)
    shapes = {n: (inputs[n].shape, inputs[n].dtype) for n in BACK_IN}
    peers = f["back2"].shape[0]
    pair = (DS // peers, tiles, 128)
    shapes.update(
        so=((DS, tiles, 128), F32), final2=((peers,) + pair, BF16),
    )

    def sums(prefix, n, rows, cols, held):
        names = ("own", "other", "r1", "r2", "r3", "r4") if not prefix else ("pown", "pother", "p1", "p2", "p3", "p4")
        dims = (
            lead + (rows, cols), lead + (rows, cols), lead + (rows, cols), (8, 2, rows // 2, cols),
            (2, 4, rows // 2, cols), (3, rows, cols),
        )
        for i, (name, d) in enumerate(zip(names, dims)):
            k = (held if i < 2 else n,) if not prefix else ()
            shapes[name] = (k + d, BF16)

    sums("", 3 * BLOCKS, owned, cols, 2 * BLOCKS)
    sums("p", 1, PACK, 128, 1)
    tall = ((size * DS, 128), F32)
    shapes.update(
        wbuf=((2, 2, 2, 4, 2, owned, cols), BF16), keep=(((size + 1) * 128, 128), F32), decays=((size * 128, 128), F32),
        pb=((256, 128), F32), pc=((256, 128), F32), rb=tall, rc=tall, ga=((DS, tiles, 128), F32), gb=((rows * DS // 128, 128), F32),
        gc=((rows * DS // 128, 128), F32), proj=((rows, 128), F32), xp=((rows + 16, 128), F32), gp=((rows + 8, 128), F32),
        rawlow=((rows, di), BF16), gproj=((rows, PACK0), BF16), dw=((DTR, di), BF16), w0g=((PACK0, di), F32),
        selg=((PACK0, di), F32), edge=((8, di), F32), gx=((rows, di), BF16), gn=((rows, width), F32), gaing=((8, width), F32),
    )
    dma = pltpu.SemaphoreType.DMA
    n_jobs = 3 * BLOCKS + 1
    sems = {
        "load": dma((len(BACK_LOAD),)), "wsem": dma((2 * WX,)), "send": dma((n_jobs, Share.COPIES)),
        "recv": dma((n_jobs, Share.COPIES)), "esend": dma((BLOCKS,)), "erecv": dma((BLOCKS,)),
        "rsend": dma((1, peers - 1)), "rrecv": dma((1, peers - 1)),
    }
    return pl.pallas_call(
        back_body,
        out_shape=(
            sds((rows, width), F32), sds((owned, 2 * di), F32), sds((di // 32, width), F32), sds((PACK, 128), F32),
        ),
        in_specs=[ANY] * len(BACK_IN),
        out_specs=(VM,) * 4,
        scratch_shapes=[sems[n] if n in sems else pltpu.VMEM(*shapes[n]) for n in BACK_SCRATCH],
        compiler_params=pltpu.CompilerParams(collective_id=1, has_side_effects=True, vmem_limit_bytes=GRANT),
    )(*(inputs[n] for n in BACK_IN))


def finish_body(*refs):
    big, pack = refs[:4], refs[4]
    outs, small, sem = refs[5:9], refs[9:17], refs[17]
    copies = [pltpu.make_async_copy(src, dst, sem.at[i]) for i, (src, dst) in enumerate(zip(big, outs))]
    for copy in copies:
        copy.start()
    gain, conv, conv_bias, select, delta, delta_bias, a_log, skip = small
    own = conv.shape[1]
    conv[...] = pack[0:KW, 0:own]
    for row, ref in ((4, conv_bias), (5, delta_bias), (6, skip)):
        ref[...] = pack[row : row + 1, 0:own]
    a_log[...] = pack[ALOG0 : ALOG0 + DS, 0:own]
    delta[...] = pack[DELTA0 : DELTA0 + DTR, 0:own]
    select[...] = pack[...].T[own : 2 * own, 0:PACK0]
    part = gain.shape[1]
    parts = 128 // part
    me = (lax.axis_index("batch") * lax.axis_size("seq") + lax.axis_index("seq")) % parts
    tile = pack[PACK0 : PACK0 + 1, :]
    total = jnp.zeros((1, part), F32)
    for i in range(parts):
        total = total + jnp.where(me == i, tile[:, i * part : (i + 1) * part], 0.0)
    gain[...] = total
    for copy in copies:
        copy.wait()


def finish(whole, small):
    block, tgrad, gin, gout, pack = whole
    big = (block, tgrad, gin, gout)
    return pl.pallas_call(
        finish_body,
        out_shape=tuple(sds(v.shape, F32) for v in big + small),
        in_specs=[VM] * 5,
        out_specs=(ANY,) * 4 + (VM,) * 8,
        scratch_shapes=[pltpu.SemaphoreType.DMA((4,))],
        compiler_params=pltpu.CompilerParams(vmem_limit_bytes=GRANT),
    )(*big, pack)


def on_slice(tokens, cotangent, norm_gain, in_weight, conv_weight, conv_bias, select_weight, delta_weight, delta_bias, a_log, skip_gain, out_weight):
    sizes = (lax.axis_size("batch"), lax.axis_size("seq"))
    tok, cot = tokens[0], cotangent[0]
    rows = tok.shape[0]
    small = (
        norm_gain[None], conv_weight, conv_bias[None], select_weight, delta_weight, delta_bias[None], a_log, skip_gain[None],
    )
    f = front(tok, cot, in_weight, out_weight, small, sizes[1], rows // 32)
    whole = (f["block"],) + back(f, tok, cot)
    block_out, tokens_grad, g_in, g_out, *grads = finish(whole, small)
    g_gain, g_conv, g_conv_bias, g_select, g_delta, g_delta_bias, g_a_log, g_skip = grads
    return (
        block_out[None], tokens_grad[None], g_gain[0], g_in, g_conv, g_conv_bias[0], g_select, g_delta, g_delta_bias[0],
        g_a_log, g_skip[0], g_out,
    )


def on_device(tokens, cotangent, norm_gain, in_weight, conv_weight, conv_bias, select_weight, delta_weight, delta_bias, a_log, skip_gain, out_weight):
    axes = ("batch", "seq")
    sizes = (lax.axis_size("batch"), lax.axis_size("seq"))
    if sizes == (4, 8):
        return on_slice(
            tokens, cotangent, norm_gain, in_weight, conv_weight, conv_bias, select_weight, delta_weight, delta_bias,
            a_log, skip_gain, out_weight,
        )
    tok, cot = tokens[0], cotangent[0]
    rows, width = tok.shape
    di = out_weight.shape[0] * sizes[0] * sizes[1]
    tiles = di // 128
    full = lambda v, axis: lax.all_gather(v, axes, axis=axis, tiled=True)
    in_full = full(in_weight, 0)
    in_x, in_z = in_full[:, :di], in_full[:, di:]
    out_full = full(out_weight, 0)
    sel_t = full(select_weight, 0).T
    gain = full(norm_gain, 0)[None].astype(F32)
    w0 = jnp.concatenate(
        [
            full(conv_weight, 1), full(conv_bias, 0)[None], full(delta_bias, 0)[None], full(skip_gain, 0)[None],
            jnp.zeros((1, di), BF16), full(a_log, 1), full(delta_weight, 1),
            jnp.zeros((PACK0 - DELTA0 - DTR, di), BF16),
        ],
        axis=0,
    ).astype(F32)

    flat = sds((rows * tiles, 128), F32)
    wide = sds((rows, di), F32)
    spread = sds((rows * DS, 128), F32)
    carry = sds((DS, tiles, 128), F32)

    normed, x_in = kernel_call(
        inproj_body, (sds((rows, width), BF16), sds((rows, di), BF16)), 3
    )(tok, gain, in_x)
    halo = shift(x_in[rows - 16 :], 1)
    filt, xs, xt, draw, dt, bb, cb = kernel_call(
        conv_body,
        (wide, sds((rows, di), BF16), flat, wide, flat, spread, spread),
        4,
        [pltpu.VMEM((rows, 128), F32), pltpu.VMEM((rows + 16, 128), F32)],
    )(x_in, halo, w0, sel_t)
    a2, total, end = kernel_call(lightf_body, (carry, carry, carry), 4)(dt, xt, bb, w0)
    gate, gzp, gt, low, adj = kernel_call(
        gate_body, (wide, wide, flat, sds((rows, width), BF16), carry), 7
    )(normed, in_z, cot, out_full, dt, cb, a2)
    state_in = carried_in(total, end, False)
    state_out = carried_in(total, adj, True)
    chunks = rows // 64
    starts, block_out, gz, out_grad, z_grad, skip_grad = kernel_call(
        forward_body,
        (
            sds((chunks, DS, tiles, 128), F32), sds((rows, width), F32), sds((rows, di), BF16),
            sds((di, width), BF16), sds((width, di), BF16), sds((1, di), F32),
        ),
        14,
        [pltpu.VMEM((rows * tiles, 128), F32), pltpu.VMEM((rows, di), BF16), pltpu.VMEM((8, 128), F32)],
    )(state_in, dt, xt, bb, cb, a2, w0, gate, gzp, gt, tok, low, normed, out_full)
    tall = pltpu.VMEM((rows * DS, 128), F32)
    gdt, gat, gb, gc, ga = kernel_call(
        backward_body,
        (flat, flat, sds((rows, 128), F32), sds((rows, 128), F32), carry),
        8,
        [
            pltpu.VMEM((65 * 128, 128), F32), pltpu.VMEM((64 * 128, 128), F32), pltpu.VMEM((256, 128), F32),
            pltpu.VMEM((256, 128), F32), tall, tall,
        ],
    )(state_out, starts, dt, xt, bb, cb, gt, a2)
    gf, w0g, selg = kernel_call(
        tail_body,
        (wide, sds((PACK0, di), F32), sds((PACK0, di), F32)),
        12,
        [
            pltpu.VMEM((rows, 128), F32), pltpu.VMEM((rows + 16, 128), F32), pltpu.VMEM((rows, di), BF16),
            pltpu.VMEM((rows, PACK0), BF16), pltpu.VMEM((DTR, di), BF16),
        ],
    )(gdt, gat, gb, gc, gt, draw, filt, x_in, halo, xs, w0, sel_t)
    edge = shift(gf[:8], -1)
    tokens_grad, x_grad, gain_grad = kernel_call(
        last_body,
        (sds((rows, width), F32), sds((width, di), BF16), sds((1, width), F32)),
        10,
        [pltpu.VMEM((rows + 8, 128), F32), pltpu.VMEM((rows, di), BF16), pltpu.VMEM((rows, width), F32)],
    )(gf, edge, w0, gz, normed, tok, cot, gain, in_x, in_z)

    share = lambda v, d: lax.psum_scatter(v.astype(F32), axes, scatter_dimension=d, tiled=True)
    ga_flat = ga.reshape(DS, di)
    grads = (
        share(gain_grad[0], 0), share(jnp.concatenate([x_grad, z_grad], axis=1), 0), share(w0g[0:KW], 1),
        share(w0g[4], 0), share(selg.T, 0), share(w0g[DELTA0 : DELTA0 + DTR], 1), share(w0g[5], 0),
        share(ga_flat, 1), share(skip_grad[0], 0), share(out_grad, 0),
    )
    return (block_out[None], tokens_grad[None]) + grads


def solution(mesh):
    both = ("batch", "seq")
    first, second = P(both), P(None, both)
    matrix = P(both, None)
    whole = P("batch", "seq", None)
    weights = (first, matrix, second, first, matrix, second, first, second, first, matrix)
    return jax.shard_map(
        on_device,
        mesh=mesh,
        in_specs=(whole, whole) + weights,
        out_specs=(whole, whole) + weights,
        check_vma=False,
    )
```

```python
import functools

import jax
import jax.numpy as jnp
from jax import lax
from jax.experimental import pallas as pl
from jax.experimental.pallas import tpu as pltpu
from jax.sharding import PartitionSpec as P

DS = 16
KW = 4
DTR = 64
EPS = 1e-05
LOG2E = 1.4426950408889634
LN2 = 0.6931471805599453
F32 = jnp.float32
BF16 = jnp.bfloat16
MESH = pl.DeviceIdType.MESH
VM = pl.BlockSpec(memory_space=pltpu.VMEM)
ANY = pl.BlockSpec(memory_space=pl.ANY)
GRANT = 60 << 20
ALOG0, DELTA0, PACK0, PACK = 8, 24, 96, 128


def sds(shape, dtype):
    return jax.ShapeDtypeStruct(shape, dtype)


def kernel_call(body, outs, n_in, scratch=(), flops=1e9, **params):
    return pl.pallas_call(
        body,
        out_shape=outs,
        in_specs=[VM] * n_in,
        out_specs=jax.tree.map(lambda _: VM, outs),
        scratch_shapes=list(scratch),
        cost_estimate=pl.CostEstimate(flops=int(flops), bytes_accessed=8 << 20, transcendentals=0),
        compiler_params=pltpu.CompilerParams(vmem_limit_bytes=GRANT, **params),
    )


def sigmoid(v):
    return 1.0 / (1.0 + jnp.exp(-v))


def dot(a, b):
    return jnp.dot(a, b, preferred_element_type=F32)


def dot_nt(a, b):
    return lax.dot_general(a, b, (((1,), (1,)), ((), ())), preferred_element_type=F32)


def dot_tn(a, b):
    return lax.dot_general(a, b, (((0,), (0,)), ((), ())), preferred_element_type=F32)


def lanes(k, width=128):
    return pl.ds(pl.multiple_of(k * width, width), width)


def inproj_body(tok_ref, gain_ref, inx_ref, normed_ref, xin_ref):
    rows = tok_ref.shape[0]

    def norm(i, _):
        r = pl.ds(pl.multiple_of(i * 16, 16), 16)
        u = tok_ref[r, :]
        scale = lax.rsqrt(jnp.mean(u * u, axis=-1, keepdims=True) + EPS)
        normed_ref[r, :] = (u * scale * gain_ref[...]).astype(BF16)
        return 0

    lax.fori_loop(0, rows // 16, norm, 0)
    width = 512

    def mm(j, _):
        c = lanes(j, width)
        xin_ref[:, c] = dot(normed_ref[...], inx_ref[:, c]).astype(BF16)
        return 0

    lax.fori_loop(0, inx_ref.shape[1] // width, mm, 0)


def conv_body(xin_ref, halo_ref, w0_ref, selt_ref, filt_ref, xs_ref, xt_ref, draw_ref, dt_ref, bb_ref, cb_ref, proj, xp):
    rows, di = xin_ref.shape
    tiles = di // 128
    xp_rows = 16 + rows

    def conv(k, _):
        c = lanes(k)
        xp[0:16, :] = halo_ref[:, c].astype(F32)
        xp[16:xp_rows, :] = xin_ref[:, c].astype(F32)
        for q in range(2):
            r0 = q * (rows // 2)
            f = w0_ref[4:5, c]
            for tap in range(KW):
                lo = 16 - (KW - 1) + tap + r0
                f = f + w0_ref[tap : tap + 1, c] * xp[lo : lo + rows // 2, :]
            s = (f * sigmoid(f)).astype(BF16)
            filt_ref[r0 : r0 + rows // 2, c] = f
            xs_ref[r0 : r0 + rows // 2, c] = s
            xt_ref[pl.ds(r0 * tiles + k, rows // 2, stride=tiles), :] = s.astype(F32)
        return 0

    lax.fori_loop(0, tiles, conv, 0)
    proj[:, 0:96] = dot_nt(xs_ref[...], selt_ref[...])
    low = proj[:, 0:DTR].astype(BF16)

    def delta(k, _):
        c = lanes(k)
        raw = dot(low, w0_ref[DELTA0 : DELTA0 + DTR, c].astype(BF16)) + w0_ref[5:6, c]
        draw_ref[:, c] = raw
        dt_ref[pl.ds(k, rows, stride=tiles), :] = jnp.maximum(raw, 0.0) + jnp.log1p(jnp.exp(-jnp.abs(raw)))
        return 0

    lax.fori_loop(0, tiles, delta, 0)
    row_ids = lax.broadcasted_iota(jnp.int32, (128, 128), 0) % DS
    lane_ids = lax.broadcasted_iota(jnp.int32, (128, 128), 1)
    ones = jnp.ones((128, 128), BF16)

    def spread(i, _):
        r = pl.ds(pl.multiple_of(i * 8, 8), 8)
        p = proj[r, :]
        tall = jnp.broadcast_to(p[:, None, :], (8, DS, 128)).reshape(128, 128)
        o = pl.ds(pl.multiple_of(i * 128, 128), 128)
        for first, ref in ((DTR, bb_ref), (DTR + DS, cb_ref)):
            v = jnp.where(lane_ids == row_ids + first, tall, 0.0)
            hi = v.astype(BF16)
            v = v - hi.astype(F32)
            mid = v.astype(BF16)
            lo = (v - mid.astype(F32)).astype(BF16)
            ref[o, :] = (dot(hi, ones) + dot(mid, ones)) + dot(lo, ones)
        return 0

    lax.fori_loop(0, rows // 8, spread, 0)


def row_of(ref, index):
    return ref[pl.ds(index, 8, stride=0), :]


def tile_at(ref, t, h):
    return ref[pl.ds(pl.multiple_of(t * 16 + h * 8, 8), 8), :]


def light_forward(dt_ref, xt_ref, bb_ref, a2_ref, total_ref, end_ref, rows):
    for h in range(2):
        hs = pl.ds(h * 8, 8)
        a = [a2_ref[n, hs, :] for n in range(DS)]

        def step(t, carry):
            state, run = carry
            d = tile_at(dt_ref, t, h)
            dx = d * tile_at(xt_ref, t, h)
            new = tuple(
                jnp.exp2(a[n] * d) * state[n] + dx * row_of(bb_ref, t * DS + n) for n in range(DS)
            )
            return (new, run + d)

        zero = jnp.zeros((8, 128), F32)
        state, run = lax.fori_loop(0, rows, step, ((zero,) * DS, zero), unroll=4)
        for n in range(DS):
            end_ref[n, hs, :] = state[n]
            total_ref[n, hs, :] = jnp.exp2(a[n] * run)


def light_backward(dt_ref, gt_ref, cb_ref, a2_ref, adj_ref, rows):
    for h in range(2):
        hs = pl.ds(h * 8, 8)
        a = [a2_ref[n, hs, :] for n in range(DS)]

        def step(i, carry):
            t = rows - 1 - i
            d = tile_at(dt_ref, t, h)
            g = tile_at(gt_ref, t, h)
            return tuple(
                jnp.exp2(a[n] * d) * (carry[n] + g * row_of(cb_ref, t * DS + n)) for n in range(DS)
            )

        out = lax.fori_loop(0, rows, step, (jnp.zeros((8, 128), F32),) * DS, unroll=4)
        for n in range(DS):
            adj_ref[n, hs, :] = out[n]


def lightf_body(dt_ref, xt_ref, bb_ref, w0_ref, a2_ref, total_ref, end_ref):
    rows = dt_ref.shape[0] // 16
    for k in range(16):
        a2_ref[:, k, :] = -jnp.exp(w0_ref[ALOG0 : ALOG0 + DS, k * 128 : (k + 1) * 128]) * LOG2E
    light_forward(dt_ref, xt_ref, bb_ref, a2_ref, total_ref, end_ref, rows)


def gate_body(normed_ref, inz_ref, cot_ref, out_ref, dt_ref, cb_ref, a2_ref, gate_ref, gzp_ref, gt_ref, low_ref, adj_ref):
    rows, di = gate_ref.shape
    tiles = di // 128
    low_ref[...] = cot_ref[...].astype(BF16)
    width = 512

    def block(j, _):
        c = lanes(j, width)
        gate_ref[:, c] = dot(normed_ref[...], inz_ref[:, c])
        gzp_ref[:, c] = dot_nt(low_ref[...], out_ref[c, :])
        return 0

    lax.fori_loop(0, di // width, block, 0)

    def point(k, _):
        c = lanes(k)
        for q in range(4):
            r = slice(q * (rows // 4), (q + 1) * (rows // 4))
            z = gate_ref[r, c]
            gg = gzp_ref[r, c]
            s = sigmoid(z)
            gate = z * s
            gate_ref[r, c] = gate
            gzp_ref[r, c] = gg * s * (1.0 + z * (1.0 - s))
            gt_ref[pl.ds(q * (rows // 4) * tiles + k, rows // 4, stride=tiles), :] = gg * gate
        return 0

    lax.fori_loop(0, tiles, point, 0)
    light_backward(dt_ref, gt_ref, cb_ref, a2_ref, adj_ref, rows)


def forward_body(
    si_ref, dt_ref, xt_ref, bb_ref, cb_ref, a2_ref, w0_ref, gate_ref, gzp_ref, gt_ref, tok_ref, low_ref, normed_ref, out_ref,
    starts_ref, block_ref, gz_ref, ograd_ref, zgrad_ref, skipg_ref, yt, gated, low_t,
):
    chunks = starts_ref.shape[0]
    rows, di = gate_ref.shape
    tiles = di // 128
    size = rows // chunks
    for h in range(2):
        hs = pl.ds(h * 8, 8)
        a = [a2_ref[n, hs, :] for n in range(DS)]
        state = tuple(si_ref[n, hs, :] for n in range(DS))
        for chunk in range(chunks):
            for n in range(DS):
                starts_ref[chunk, n, hs, :] = state[n]

            def step(i, carry):
                t = chunk * size + i
                d = tile_at(dt_ref, t, h)
                dx = d * tile_at(xt_ref, t, h)
                new, parts = [], []
                for n in range(DS):
                    s = jnp.exp2(a[n] * d) * carry[n] + dx * row_of(bb_ref, t * DS + n)
                    parts.append(s * row_of(cb_ref, t * DS + n))
                    new.append(s)
                while len(parts) > 1:
                    parts = [parts[i] + parts[i + 1] for i in range(0, len(parts), 2)]
                yt[pl.ds(pl.multiple_of(t * 16 + h * 8, 8), 8), :] = parts[0]
                return tuple(new)

            state = lax.fori_loop(0, size, step, state, unroll=4)

    def point(k, _):
        c = lanes(k)
        total = jnp.zeros((8, 128), F32)
        for q in range(4):
            r = slice(q * (rows // 4), (q + 1) * (rows // 4))
            here = pl.ds(q * (rows // 4) * tiles + k, rows // 4, stride=tiles)
            x = xt_ref[here, :]
            y = yt[here, :] + w0_ref[6:7, c] * x
            gated[r, c] = (y * gate_ref[r, c]).astype(BF16)
            gz_ref[r, c] = (gzp_ref[r, c] * y).astype(BF16)
            total = total + jnp.sum((gt_ref[here, :] * x).reshape(-1, 8, 128), axis=0)
        skipg_ref[:, c] = jnp.sum(total, axis=0, keepdims=True)
        return 0

    lax.fori_loop(0, tiles, point, 0)

    def project(j, _):
        c = lanes(j, 256)
        block_ref[:, c] = tok_ref[:, c] + dot(gated[...], out_ref[:, c])
        return 0

    lax.fori_loop(0, tok_ref.shape[1] // 256, project, 0)

    def wide(j, _):
        c = lanes(j, 256)
        ograd_ref[c, :] = dot_tn(gated[:, c], low_ref[...]).astype(BF16)
        return 0

    lax.fori_loop(0, di // 256, wide, 0)

    def wide_z(j, _):
        c = lanes(j, 256)
        zgrad_ref[:, c] = dot_tn(normed_ref[...], gz_ref[:, c]).astype(BF16)
        return 0

    lax.fori_loop(0, di // 256, wide_z, 0)


def backward_body(
    so_ref, starts_ref, dt_ref, xt_ref, bb_ref, cb_ref, gt_ref, a2_ref,
    gdt_ref, gat_ref, gb_ref, gc_ref, ga_ref, keep, decays, pb, pc, rb, rc,
):
    chunks = starts_ref.shape[0]
    rows = dt_ref.shape[0] // 16
    size = rows // chunks
    zero = jnp.zeros((8, 128), F32)
    for h in range(2):
        hs = pl.ds(h * 8, 8)
        a = [a2_ref[n, hs, :] for n in range(DS)]
        for n in range(DS):
            ga_ref[n, hs, :] = zero
        later = tuple(so_ref[n, hs, :] for n in range(DS))
        for chunk in reversed(range(chunks)):
            base = chunk * size
            first = tuple(starts_ref[chunk, n, hs, :] for n in range(DS))
            for n in range(DS):
                keep[n * 8 : n * 8 + 8, :] = first[n]

            def again(i, carry):
                t = base + i
                d = tile_at(dt_ref, t, h)
                dx = d * tile_at(xt_ref, t, h)
                new = []
                for n in range(DS):
                    w = jnp.exp2(a[n] * d)
                    s = w * carry[n] + dx * row_of(bb_ref, t * DS + n)
                    o = pl.multiple_of(i * 128 + n * 8, 8)
                    decays[pl.ds(o, 8), :] = w
                    keep[pl.ds(pl.multiple_of(o + 128, 8), 8), :] = s
                    new.append(s)
                return tuple(new)

            lax.fori_loop(0, size, again, first, unroll=4)

            def back(j, carry):
                i = size - 1 - j
                t = base + i
                d = tile_at(dt_ref, t, h)
                x = tile_at(xt_ref, t, h)
                gy = tile_at(gt_ref, t, h)
                dx = d * x
                slot = (j % 2) * 128
                new = []
                weighted, through_a = [], []
                for n in range(DS):
                    o = pl.multiple_of(i * 128 + n * 8, 8)
                    w = decays[pl.ds(o, 8), :]
                    before = keep[pl.ds(o, 8), :]
                    now = keep[pl.ds(pl.multiple_of(o + 128, 8), 8), :]
                    g = carry[n] + gy * row_of(cb_ref, t * DS + n)
                    at = pl.ds(pl.multiple_of(slot + n * 8, 8), 8)
                    pc[at, :] = now * gy
                    pb[at, :] = g * dx
                    weighted.append(g * row_of(bb_ref, t * DS + n))
                    g = g * w
                    through = g * before
                    through_a.append(through * a[n])
                    ga_ref[n, hs, :] += through * d
                    new.append(g)
                while len(weighted) > 1:
                    weighted = [weighted[i] + weighted[i + 1] for i in range(0, len(weighted), 2)]
                    through_a = [through_a[i] + through_a[i + 1] for i in range(0, len(through_a), 2)]
                o = pl.ds(pl.multiple_of(t * 16 + h * 8, 8), 8)
                gdt_ref[o, :] = through_a[0] * LN2 + weighted[0] * x
                gat_ref[o, :] = weighted[0] * d
                for src, dst in ((pb, rb), (pc, rc)):
                    for m in range(2):
                        parts = [src[pl.ds(slot + m * 64 + s, 8, stride=8), :] for s in range(8)]
                        while len(parts) > 1:
                            parts = [parts[i] + parts[i + 1] for i in range(0, len(parts), 2)]
                        q = pl.ds(pl.multiple_of(t * 16 + m * 8, 8), 8)
                        if h == 0:
                            dst[q, :] = parts[0]
                        else:
                            dst[q, :] += parts[0]
                return tuple(new)

            later = lax.fori_loop(0, size, back, later, unroll=2)
    for n in range(DS):
        ga_ref[n] = ga_ref[n] * a2_ref[n] * LN2
    ones = jnp.ones((128, 128), BF16)
    pick = lax.broadcasted_iota(jnp.int32, (128, 128), 0) % DS == lax.broadcasted_iota(jnp.int32, (128, 128), 1)

    def collect(i, _):
        o = pl.ds(pl.multiple_of(i * 128, 128), 128)
        for src, dst in ((rb, gb_ref), (rc, gc_ref)):
            v = src[o, :]
            hi = v.astype(BF16)
            lo = (v - hi.astype(F32)).astype(BF16)
            s = jnp.where(pick, dot(hi, ones) + dot(lo, ones), 0.0)
            dst[pl.ds(pl.multiple_of(i * 8, 8), 8), :] = jnp.sum(s.reshape(8, DS, 128), axis=1)
        return 0

    lax.fori_loop(0, rows // 8, collect, 0)


def tail_body(
    gdt_ref, gat_ref, gb_ref, gc_ref, gt_ref, draw_ref, filt_ref, xin_ref, halo_ref, xs_ref, w0_ref, selt_ref,
    gf_ref, w0g_ref, selg_ref, proj, xp, raw_low, gproj, dw,
):
    rows, di = draw_ref.shape
    tiles = di // 128
    proj[:, 0:96] = dot_nt(xs_ref[...], selt_ref[...])
    low = proj[:, 0:DTR].astype(BF16)
    dw[...] = w0_ref[DELTA0 : DELTA0 + DTR, :].astype(BF16)

    def raw(k, _):
        c = lanes(k)
        g = gdt_ref[pl.ds(k, rows, stride=tiles), :] * sigmoid(draw_ref[:, c])
        w0g_ref[5:6, c] = jnp.sum(g, axis=0, keepdims=True)
        gl = g.astype(BF16)
        raw_low[:, c] = gl
        w0g_ref[DELTA0 : DELTA0 + DTR, c] = dot_tn(low, gl)
        return 0

    lax.fori_loop(0, tiles, raw, 0)
    gproj[:, 0:DTR] = dot_nt(raw_low[...], dw[...]).astype(BF16)
    gproj[:, DTR : DTR + DS] = gb_ref[:, 0:DS].astype(BF16)
    gproj[:, DTR + DS : DTR + 2 * DS] = gc_ref[:, 0:DS].astype(BF16)

    def point(k, _):
        c = lanes(k)
        gp = gproj[...]
        selg_ref[:, c] = dot_tn(gp, xs_ref[:, c])
        back = dot(gp, selt_ref[:, c])
        here = pl.ds(k, rows, stride=tiles)
        ga = gt_ref[here, :] * w0_ref[6:7, c] + gat_ref[here, :] + back
        f = filt_ref[:, c]
        s = sigmoid(f)
        gf = ga * (s * (1.0 + f * (1.0 - s)))
        gf_ref[:, c] = gf
        w0g_ref[4:5, c] = jnp.sum(gf, axis=0, keepdims=True)
        xp[0:16, :] = halo_ref[:, c].astype(F32)
        xp[16 : 16 + rows, :] = xin_ref[:, c].astype(F32)
        for tap in range(KW):
            lo = 16 - (KW - 1) + tap
            w0g_ref[tap : tap + 1, c] = jnp.sum(gf * xp[lo : lo + rows, :], axis=0, keepdims=True)
        return 0

    lax.fori_loop(0, tiles, point, 0)


def last_body(gf_ref, edge_ref, w0_ref, gz_ref, normed_ref, tok_ref, cot_ref, gain_ref, inx_ref, inz_ref, tgrad_ref, xgrad_ref, gaing_ref, gp, gx, gn):
    rows, di = gf_ref.shape
    tiles = di // 128

    def conv(k, _):
        c = lanes(k)
        gp[0:rows, :] = gf_ref[:, c]
        gp[rows : rows + 8, :] = edge_ref[:, c]
        total = jnp.zeros((rows, 128), F32)
        for tap in range(KW):
            lo = KW - 1 - tap
            total = total + w0_ref[tap : tap + 1, c] * gp[lo : lo + rows, :]
        gx[:, c] = total.astype(BF16)
        return 0

    lax.fori_loop(0, tiles, conv, 0)

    def wide(j, _):
        c = lanes(j, 256)
        xgrad_ref[:, c] = dot_tn(normed_ref[...], gx[:, c]).astype(BF16)
        return 0

    lax.fori_loop(0, di // 256, wide, 0)

    def back(j, _):
        c = lanes(j, 256)
        gn[:, c] = dot_nt(gx[...], inx_ref[c, :]) + dot_nt(gz_ref[...], inz_ref[c, :])
        return 0

    lax.fori_loop(0, inx_ref.shape[0] // 256, back, 0)

    def rows_of(i, total):
        r = pl.ds(pl.multiple_of(i * 8, 8), 8)
        u = tok_ref[r, :]
        g = gn[r, :]
        scale = lax.rsqrt(jnp.mean(u * u, axis=-1, keepdims=True) + EPS)
        v = g * gain_ref[...]
        mean = jnp.mean(v * u, axis=-1, keepdims=True)
        tgrad_ref[r, :] = cot_ref[r, :] + scale * v - u * (scale * scale * scale * mean)
        return total + g * u * scale

    total = lax.fori_loop(0, rows // 8, rows_of, jnp.zeros((8, tok_ref.shape[1]), F32))
    gaing_ref[...] = jnp.sum(total, axis=0, keepdims=True)


def place():
    b, s = lax.axis_index("batch"), lax.axis_index("seq")
    return b // 2, b % 2, s // 2, s % 2


def device(y, c, z, x):
    return (y * 2 + c, z * 2 + x)


def greet(peers):
    barrier = pltpu.get_barrier_semaphore()
    for peer in peers:
        pl.semaphore_signal(barrier, inc=1, device_id=peer, device_id_type=MESH)
    pl.semaphore_wait(barrier, len(peers))


def remote(src, dst, send, recv, to):
    return pltpu.make_async_remote_copy(
        src_ref=src, dst_ref=dst, send_sem=send, recv_sem=recv, device_id=to, device_id_type=MESH
    )


def neighbours(y, c, z, x):
    return [device(y, c, z ^ k, x) for k in (1, 2, 3)] + [
        device(1 - y, c, z, x), device(y, c, z, 1 - x), device(y, 1 - c, z, x)
    ]


class Gather:
    COPIES = 14

    def __init__(self, src, out, send, recv, local):
        self.src, self.out, self.send, self.recv, self.local = src, out, send, recv, local
        self.at = place()
        self.count = 0
        self.copies = []

    def go(self, view, to):
        i = self.count
        self.count += 1
        source, target = view if isinstance(view, tuple) else (view, view)
        copy = remote(source, target, self.send.at[i], self.recv.at[i], to)
        copy.start()
        self.copies.append(copy)
        return copy

    def stage(self, k):
        y, c, z, x = self.at
        out = self.out
        half = out.shape[4] // 2
        top, bottom = pl.ds(0, half), pl.ds(half, half)
        to_y, to_x, to_c = device(1 - y, c, z, x), device(y, c, z, 1 - x), device(y, 1 - c, z, x)
        if k == 0:
            own = pltpu.make_async_copy(self.src, out.at[y, c, z, x], self.local)
            own.start()
            self.first = [self.go((self.src, out.at[y, c, z, x]), device(y, c, z ^ i, x)) for i in (1, 2, 3)]
            own.wait()
        elif k == 1:
            for copy in self.first:
                copy.wait_recv()
            self.a = self.go(out.at[y, c, :, x, top], to_y)
            self.b = self.go(out.at[y, c, :, x, bottom], to_x)
            self.go(out.at[y, c, :, x], to_c)
        elif k == 2:
            self.a.wait_recv()
            self.b.wait_recv()
            self.next = [self.go(out.at[i, c, :, x, top], to_x) for i in (0, 1)]
            self.next.append(self.go(out.at[y, c, :, :, bottom], to_y))
            self.go(out.at[1 - y, c, :, x, top], to_c)
            self.go(out.at[y, c, :, 1 - x, bottom], to_c)
        elif k == 3:
            for copy in self.next:
                copy.wait_recv()
            for i in (0, 1):
                self.go(out.at[i, c, :, 1 - x, top], to_c)
            self.go(out.at[1 - y, c, :, :, bottom], to_c)
        else:
            done = self.first + [self.a, self.b] + self.next
            for copy in self.copies:
                if not any(copy is other for other in done):
                    copy.wait_recv()

    def drain(self):
        for copy in self.copies:
            copy.wait_send()


STAGES = 5
STEPS = (0, 2, 4, 6, 7)
PACE = 1.2
DELAY = 0
STEPS_LATE = (0, 3, 6, 9, 11)
STEPS_BACK = (0, 3, 6, 9, 12)
STEPS_LAST = (0, 3, 6, 9, 12)
STEPS_PACK = (0, 1, 2, 3, 4)
PACE_BACK = 1.0


def shift(value, by):
    peers = lax.axis_size("seq")
    pairs = [(i, i + by) for i in range(peers) if 0 <= i + by < peers]
    return lax.ppermute(value, "seq", pairs)


def carried_in(total, value, reverse):
    peers, index = lax.axis_size("seq"), lax.axis_index("seq")
    totals = lax.all_gather(total.astype(BF16), "seq")
    values = lax.all_gather(value.astype(BF16), "seq")

    def turn(k, before):
        at = peers - 1 - k if reverse else k
        reached = at > index if reverse else at < index
        new = totals[at].astype(F32) * before + values[at].astype(F32)
        return jnp.where(reached, new, before)

    return lax.fori_loop(0, peers, turn, jnp.zeros(value.shape, F32))


def unpack_weights(pk, w0_ref, selt_ref, gain_ref):
    low_half = lax.broadcasted_iota(jnp.int32, (PACK0, 128), 1) < 64

    def pair(j, _):
        at = (j // 8, j // 4 % 2, j % 4)
        a = pk[at + (0, pl.ds(0, PACK0))].astype(F32)
        b = pk[at + (1, pl.ds(0, PACK0))].astype(F32)
        c = lanes(j)
        w0_ref[:, c] = jnp.where(low_half, a, pltpu.roll(b, 64, 1))
        selt_ref[:, c] = jnp.where(low_half, pltpu.roll(a, 64, 1), b).astype(BF16)
        return 0

    lax.fori_loop(0, 16, pair, 0)

    def gains(j, _):
        total = jnp.zeros((16, 128), F32)
        for i in range(4):
            v = pk[(j // 4, j // 2 % 2, j % 2 * 2 + i // 2, i % 2, pl.ds(PACK0, 16))]
            total = total + v.astype(F32)
        gain_ref[:, lanes(j)] = total[0:8, :]
        return 0

    lax.fori_loop(0, 8, gains, 0)


def normalise(tok, gain, normed):
    rows = tok.shape[0]

    def norm(i, _):
        r = pl.ds(pl.multiple_of(i * 16, 16), 16)
        u = tok[r, :]
        scale = lax.rsqrt(jnp.mean(u * u, axis=-1, keepdims=True) + EPS)
        normed[r, :] = (u * scale * gain[0:1, :]).astype(BF16)
        return 0

    lax.fori_loop(0, rows // 16, norm, 0, unroll=2)


def conv_tiles(first, count, xin, halo, live, w0, filt, xs, xt, xp):
    rows, di = xin.shape
    tiles = di // 128

    def conv(k, _):
        c = lanes(k)
        xp[0:16, :] = halo[:, c].astype(F32) * live
        xp[16 : 16 + rows, :] = xin[:, c].astype(F32)
        for q in range(2):
            r0 = q * (rows // 2)
            f = w0[4:5, c]
            for tap in range(KW):
                lo = 16 - (KW - 1) + tap + r0
                f = f + w0[tap : tap + 1, c] * xp[lo : lo + rows // 2, :]
            s = (f * sigmoid(f)).astype(BF16)
            filt[r0 : r0 + rows // 2, c] = f
            xs[r0 : r0 + rows // 2, c] = s
            xt[pl.ds(r0 * tiles + k, rows // 2, stride=tiles), :] = s.astype(F32)
        return 0

    lax.fori_loop(first, first + count, conv, 0)


def step_sizes(first, count, proj, w0, draw, dt):
    rows, di = draw.shape
    tiles = di // 128
    low = proj[:, 0:DTR].astype(BF16)

    def delta(k, _):
        c = lanes(k)
        raw = dot(low, w0[DELTA0 : DELTA0 + DTR, c].astype(BF16)) + w0[5:6, c]
        draw[:, c] = raw
        dt[pl.ds(k, rows, stride=tiles), :] = jnp.maximum(raw, 0.0) + jnp.log1p(jnp.exp(-jnp.abs(raw)))
        return 0

    lax.fori_loop(first, first + count, delta, 0, unroll=2)


def spread_rows(part, parts, proj, first, ref):
    row_ids = lax.broadcasted_iota(jnp.int32, (128, 128), 0) % DS
    lane_ids = lax.broadcasted_iota(jnp.int32, (128, 128), 1)
    ones = jnp.ones((128, 128), BF16)

    def spread(i, _):
        p = proj[pl.ds(pl.multiple_of(i * 8, 8), 8), :]
        tall = jnp.broadcast_to(p[:, None, :], (8, DS, 128)).reshape(128, 128)
        o = pl.ds(pl.multiple_of(i * 128, 128), 128)
        v = jnp.where(lane_ids == row_ids + first, tall, 0.0)
        hi = v.astype(BF16)
        v = v - hi.astype(F32)
        mid = v.astype(BF16)
        lo = (v - mid.astype(F32)).astype(BF16)
        ref[o, :] = (dot(hi, ones) + dot(mid, ones)) + dot(lo, ones)
        return 0

    count = proj.shape[0] // 8 // parts
    lax.fori_loop(part * count, (part + 1) * count, spread, 0, unroll=4)


def light_forward_part(h, part, parts, dt, xt, bb, a2, total, end, run):
    rows = dt.shape[0] // 16
    size = rows // parts
    hs = pl.ds(h * 8, 8)
    a = [a2[n, hs, :] for n in range(DS)]

    def step(i, carry):
        state, past = carry
        t = part * size + i
        d = tile_at(dt, t, h)
        dx = d * tile_at(xt, t, h)
        new = tuple(jnp.exp2(a[n] * d) * state[n] + dx * row_of(bb, t * DS + n) for n in range(DS))
        return (new, past + d)

    zero = jnp.zeros((8, 128), F32)
    start = ((zero,) * DS, zero) if part == 0 else (tuple(end[n, hs, :] for n in range(DS)), run[hs, :])
    state, past = lax.fori_loop(0, size, step, start, unroll=4)
    run[hs, :] = past
    for n in range(DS):
        end[n, hs, :] = state[n]
        if part == parts - 1:
            total[n, hs, :] = jnp.exp2(a[n] * past)


def light_backward_half(h, dt, gt, cb, a2, adj):
    rows = dt.shape[0] // 16
    hs = pl.ds(h * 8, 8)
    a = [a2[n, hs, :] for n in range(DS)]

    def step(i, carry):
        t = rows - 1 - i
        d = tile_at(dt, t, h)
        g = tile_at(gt, t, h)
        return tuple(jnp.exp2(a[n] * d) * (carry[n] + g * row_of(cb, t * DS + n)) for n in range(DS))

    out = lax.fori_loop(0, rows, step, (jnp.zeros((8, 128), F32),) * DS, unroll=4)
    for n in range(DS):
        adj[n, hs, :] = out[n]


def forward_part(h, q, si, dt, xt, bb, cb, a2, starts, yt):
    size = dt.shape[0] // 16 // starts.shape[0]
    hs = pl.ds(h * 8, 8)
    a = [a2[n, hs, :] for n in range(DS)]
    state = tuple(si[n, hs, :] for n in range(DS))
    for n in range(DS):
        starts[q, n, hs, :] = state[n]

    def step(i, carry):
        t = q * size + i
        d = tile_at(dt, t, h)
        dx = d * tile_at(xt, t, h)
        new, parts = [], []
        for n in range(DS):
            s = jnp.exp2(a[n] * d) * carry[n] + dx * row_of(bb, t * DS + n)
            parts.append(s * row_of(cb, t * DS + n))
            new.append(s)
        while len(parts) > 1:
            parts = [parts[i] + parts[i + 1] for i in range(0, len(parts), 2)]
        yt[pl.ds(pl.multiple_of(t * 16 + h * 8, 8), 8), :] = parts[0]
        return tuple(new)

    state = lax.fori_loop(0, size, step, state, unroll=4)
    for n in range(DS):
        si[n, hs, :] = state[n]


def carry_send(refs, mine, got, send, recv):
    peers = mine.shape[0]
    pair = DS // peers
    b, s = lax.axis_index("batch"), lax.axis_index("seq")
    for j in range(peers):
        for i in range(pair):
            for m, ref in enumerate(refs):
                mine[j, m, i] = ref[j * pair + i].astype(BF16)
    copies = []
    for k in range(1, peers):
        to = lax.rem(s + k, peers)
        copy = remote(mine.at[to], got.at[s], send.at[k - 1], recv.at[k - 1], (b, to))
        copy.start()
        copies.append(copy)
    got[s] = mine[s]
    return copies


def carry_back(back, final, send, recv):
    peers = back.shape[0]
    b, s = lax.axis_index("batch"), lax.axis_index("seq")
    copies = []
    for k in range(1, peers):
        to = lax.rem(s + k, peers)
        copy = remote(back.at[to], final.at[s], send.at[k - 1], recv.at[k - 1], (b, to))
        copy.start()
        copies.append(copy)
    final[s] = back[s]
    return copies


def arrived(copies):
    for copy in copies:
        copy.wait_recv()


WX, WZ, WO = 4, 4, 4


def pack_small(refs, out, me):
    gain, conv, conv_bias, select, delta, delta_bias, a_log, skip = (ref[...].astype(F32) for ref in refs)
    own = conv.shape[1]
    none = jnp.zeros((1, own), F32)
    left = jnp.concatenate([conv, conv_bias, delta_bias, skip, none, a_log, delta, jnp.zeros((PACK0 - DELTA0 - DTR, own), F32)], axis=0)
    right = jnp.concatenate([select, jnp.zeros((own, 128 - PACK0), F32)], axis=1).T[0:PACK0]
    out[0:PACK0, :] = jnp.concatenate([left, right], axis=1).astype(BF16)
    part = gain.shape[1]
    tile = jnp.concatenate([gain] * (128 // part), axis=1)
    mine = lax.broadcasted_iota(jnp.int32, tile.shape, 1) // part == me % (128 // part)
    out[PACK0:PACK, :] = jnp.broadcast_to(jnp.where(mine, tile, 0.0), (PACK - PACK0, 128)).astype(BF16)


def front_body(tok_in, cot_in, inw_in, outw_in, *refs):
    small, refs = refs[:8], refs[8:]
    names = FRONT_OUTS
    o = dict(zip(names, refs[: len(names)]))
    v = dict(zip(FRONT_SCRATCH, refs[len(names) :]))
    stash_sem, load_sem, job_send, job_recv, job_local, ring_send, ring_recv, halo_send, halo_recv = (
        v[n] for n in ("stash", "load", "jsend", "jrecv", "jlocal", "rsend", "rrecv", "hsend", "hrecv")
    )
    y, c, z, x = place()
    b, s = lax.axis_index("batch"), lax.axis_index("seq")
    peers = v["mine"].shape[0]
    stash = []

    def put(*keys):
        for key in keys:
            copy = pltpu.make_async_copy(v[key], o[key], stash_sem.at[len(stash)])
            copy.start()
            stash.append(copy)

    load_tok = pltpu.make_async_copy(tok_in, v["tok"], load_sem.at[0])
    load_cot = pltpu.make_async_copy(cot_in, v["cot"], load_sem.at[1])
    load_tok.start()
    load_cot.start()
    pack_small(small, v["packed"], b * peers + s)
    greet([(b, lax.rem(s + k, peers)) for k in range(1, peers)] + [device(1 - y, c, z, x), device(y, 1 - c, z, x)])

    jobs = []

    def job(src, out):
        i = len(jobs)
        jobs.append(Gather(src, out, job_send.at[i], job_recv.at[i], job_local.at[i]))

    width = inw_in.shape[1] // 2 // WX
    wide_z = inw_in.shape[1] // 2 // WZ
    wide_o = outw_in.shape[1] // WO
    job(v["packed"], v["pk"])
    for i in range(WX):
        job(inw_in.at[:, pl.ds(i * width, width)], v["inx"].at[i])
    for i in range(WZ):
        job(inw_in.at[:, pl.ds(inw_in.shape[1] // 2 + i * wide_z, wide_z)], v["inz"].at[i])
    for i in range(WO):
        job(outw_in.at[:, pl.ds(i * wide_o, wide_o)], v["wo"].at[i])
    events = sorted(
        (i + STEPS[k] if i <= WX else i + DELAY + STEPS_LATE[k], -k, i) for i in range(len(jobs)) for k in range(STAGES)
    )
    clock = [0.0]

    def advance():
        _, k, i = events.pop(0)
        jobs[i].stage(-k)

    def landed(i):
        while any(e[2] == i for e in events):
            advance()
            clock[0] = 0.0

    def spend(time):
        clock[0] += time
        while clock[0] >= PACE:
            clock[0] -= PACE
            if events:
                advance()

    di = v["xin"].shape[1]
    rows = v["xin"].shape[0]
    tiles = di // 128
    per = tiles // WX
    live = jnp.where(s > 0, 1.0, 0.0)
    halos = []

    def project_x(i):
        cols = pl.ds(i * width, width)
        v["xin"][:, cols] = dot(v["normed"][...], v["inx"][i].reshape(-1, width)).astype(BF16)
        copy = remote(
            v["xin"].at[pl.ds(rows - 16, 16), cols], v["halo"].at[:, cols],
            halo_send.at[i], halo_recv.at[i], (b, lax.rem(s + 1, peers)),
        )
        copy.start()
        halos.append(copy)

    def conv(i):
        halos[i].wait_recv()
        conv_tiles(i * per, per, v["xin"], v["halo"], live, v["w0"], v["filt"], v["xs"], v["xt"], v["xp"])

    landed(0)
    unpack_weights(v["pk"], v["w0"], v["selt"], v["gain"])
    load_tok.wait()
    normalise(v["tok"], v["gain"], v["normed"])
    put("w0", "selt", "gain", "normed")
    for k in range(16):
        v["a2"][:, k, :] = -jnp.exp(v["w0"][ALOG0 : ALOG0 + DS, k * 128 : (k + 1) * 128]) * LOG2E
    put("a2")
    for i in range(WX):
        landed(1 + i)
        project_x(i)
        if i > 0:
            conv(i - 1)
    put("inx")
    load_cot.wait()
    v["low"][...] = v["cot"][...].astype(BF16)
    put("low")
    conv(WX - 1)
    put("xin", "halo", "filt", "xs", "xt")
    v["proj"][:, 0:PACK0] = dot_nt(v["xs"][...], v["selt"][...])
    spend(1.5)
    for q in range(4):
        step_sizes(q * (tiles // 4), tiles // 4, v["proj"], v["w0"], v["draw"], v["dt"])
        spend(1.0)
    put("draw", "dt")
    for q in range(4):
        spread_rows(q, 4, v["proj"], DTR, v["bb"])
        spend(0.85)
    put("bb")
    for h in range(2):
        for q in range(4):
            light_forward_part(h, q, 4, v["dt"], v["xt"], v["bb"], v["a2"], v["total"], v["end"], v["run"])
            spend(0.8)

    sent = carry_send((v["total"], v["end"]), v["mine"], v["got"], ring_send.at[0], ring_recv.at[0])

    def project_z(i):
        landed(1 + WX + i)
        v["gate"][:, i * wide_z : (i + 1) * wide_z] = dot(v["normed"][...], v["inz"][i].reshape(-1, wide_z))

    for q in range(4):
        spread_rows(q, 4, v["proj"], DTR + DS, v["cb"])
        spend(0.85)
    put("cb")
    arrived(sent)
    state = jnp.zeros(v["back"].shape[1:], F32)
    for p in range(peers):
        v["back"][p] = state.astype(BF16)
        state = v["got"][p, 0].astype(F32) * state + v["got"][p, 1].astype(F32)
    more = carry_back(v["back"], v["final"], ring_send.at[1], ring_recv.at[1])
    sent += more
    for i in range(WZ - 1):
        project_z(i)
    arrived(more)
    pair = DS // peers
    for j in range(peers):
        for i in range(pair):
            v["si"][j * pair + i] = v["final"][j, i].astype(F32)
    clock[0] = 0.0
    for q in range(v["starts"].shape[0]):
        for h in range(2):
            forward_part(h, q, v["si"], v["dt"], v["xt"], v["bb"], v["cb"], v["a2"], v["starts"], v["yt"])
            spend(0.6)
    put("starts")
    project_z(3)
    put("inz")
    landed(len(jobs) - 1)

    block = 512
    per_b = block // (di // 32)

    def gated_grad(j, _):
        out = jnp.zeros((rows, block), F32)
        for i in range(WO):
            w = v["wo"][i, j // 2, j % 2].reshape(block, wide_o)
            out = out + dot_nt(v["low"][:, i * wide_o : (i + 1) * wide_o], w)
        v["gzp"][:, lanes(j, block)] = out
        return 0

    lax.fori_loop(0, di // block, gated_grad, 0)

    def point(k, _):
        cols = lanes(k)
        for q in range(4):
            r = slice(q * (rows // 4), (q + 1) * (rows // 4))
            zz = v["gate"][r, cols]
            gg = v["gzp"][r, cols]
            sg = sigmoid(zz)
            gate = zz * sg
            v["gate"][r, cols] = gate
            v["gzp"][r, cols] = gg * sg * (1.0 + zz * (1.0 - sg))
            v["gt"][pl.ds(q * (rows // 4) * tiles + k, rows // 4, stride=tiles), :] = gg * gate
        return 0

    lax.fori_loop(0, tiles, point, 0)
    put("gt")
    for h in range(2):
        light_backward_half(h, v["dt"], v["gt"], v["cb"], v["a2"], v["adj"])
    again = carry_send((v["adj"],), v["mine2"], v["got2"], ring_send.at[2], ring_recv.at[2])
    sent += again

    def emit(k, _):
        cols = lanes(k)
        total = jnp.zeros((8, 128), F32)
        for q in range(4):
            r = slice(q * (rows // 4), (q + 1) * (rows // 4))
            here = pl.ds(q * (rows // 4) * tiles + k, rows // 4, stride=tiles)
            xx = v["xt"][here, :]
            yy = v["yt"][here, :] + v["w0"][6:7, cols] * xx
            v["gated"][r, cols] = (yy * v["gate"][r, cols]).astype(BF16)
            v["gz"][r, cols] = (v["gzp"][r, cols] * yy).astype(BF16)
            total = total + jnp.sum((v["gt"][here, :] * xx).reshape(-1, 8, 128), axis=0)
        v["skipg"][:, cols] = jnp.broadcast_to(jnp.sum(total, axis=0, keepdims=True), (8, 128))
        return 0

    lax.fori_loop(0, tiles, emit, 0)
    put("gated", "gz", "skipg")
    for i in range(WO):
        cols = pl.ds(i * wide_o, wide_o)
        w = v["wo"][i].reshape(di, wide_o)
        v["tok"][:, cols] = v["tok"][:, cols] + dot(v["gated"][...], w)
    copy = pltpu.make_async_copy(v["tok"], o["block"], load_sem.at[0])
    copy.start()
    arrived(again)
    state = jnp.zeros(v["back2"].shape[1:], F32)
    for p in reversed(range(peers)):
        v["back2"][p] = state.astype(BF16)
        state = v["got"][p, 0].astype(F32) * state + v["got2"][p, 0].astype(F32)
    put("back2")
    copy.wait()
    for it in jobs:
        it.drain()
    for it in sent + halos:
        it.wait_send()
    for it in stash:
        it.wait()


FRONT_OUTS = (
    "block", "w0", "selt", "gain", "normed", "a2", "inx", "xin", "halo", "filt", "xs", "xt", "low", "draw", "dt",
    "bb", "cb", "inz", "starts", "gt", "gated", "gz", "skipg", "back2",
)
FRONT_SCRATCH = (
    "w0", "selt", "gain", "normed", "a2", "inx", "xin", "halo", "filt", "xs", "xt", "low", "draw", "dt",
    "bb", "cb", "inz", "starts", "gt", "gated", "gz", "skipg", "back2",
    "tok", "cot", "pk", "wo", "proj", "xp", "gate", "gzp", "yt", "total", "end", "adj", "si",
    "mine", "got", "back", "final", "mine2", "got2", "run", "packed",
    "stash", "load", "jsend", "jrecv", "jlocal", "rsend", "rrecv", "hsend", "hrecv",
)


def front(tok, cot, in_weight, out_weight, small, peers, chunks):
    rows, width = tok.shape
    di = in_weight.shape[1] // 2
    tiles = di // 128
    lead = (2, 2, 4, 2)
    flat, wide, carry = ((rows * tiles, 128), F32), ((rows, di), F32), ((DS, tiles, 128), F32)
    spread, half = ((rows * DS, 128), F32), ((rows, di), BF16)
    pair = (DS // peers, tiles, 128)
    shapes = {
        "block": ((rows, width), F32), "w0": ((PACK0, di), F32), "selt": ((PACK0, di), BF16), "gain": ((8, width), F32),
        "normed": ((rows, width), BF16), "a2": carry, "inx": ((WX,) + lead + (in_weight.shape[0], di // WX), BF16),
        "xin": half, "halo": ((16, di), BF16), "filt": wide, "xs": half, "xt": flat, "low": ((rows, width), BF16),
        "draw": wide, "dt": flat, "bb": spread, "cb": spread,
        "inz": ((WZ,) + lead + (in_weight.shape[0], di // WZ), BF16), "starts": ((chunks, DS, tiles, 128), F32),
        "gt": flat, "gated": half, "gz": half, "skipg": ((8, di), F32),
        "tok": ((rows, width), F32), "cot": ((rows, width), F32), "pk": (lead + (PACK, 128), BF16),
        "wo": ((WO,) + lead + (out_weight.shape[0], width // WO), BF16), "proj": ((rows, 128), F32),
        "xp": ((rows + 16, 128), F32), "gate": wide, "gzp": wide, "yt": flat, "total": carry, "end": carry, "adj": carry,
        "si": carry, "mine": ((peers, 2) + pair, BF16), "got": ((peers, 2) + pair, BF16), "back": ((peers,) + pair, BF16),
        "final": ((peers,) + pair, BF16), "mine2": ((peers, 1) + pair, BF16), "got2": ((peers, 1) + pair, BF16),
        "back2": ((peers,) + pair, BF16), "packed": ((PACK, 128), BF16), "run": ((tiles, 128), F32),
    }
    n_jobs = 1 + WX + WZ + WO
    dma = pltpu.SemaphoreType.DMA
    sems = {
        "stash": dma((len(FRONT_OUTS) - 1,)), "load": dma((2,)), "jsend": dma((n_jobs, Gather.COPIES)),
        "jrecv": dma((n_jobs, Gather.COPIES)), "jlocal": dma((n_jobs,)), "rsend": dma((3, peers - 1)),
        "rrecv": dma((3, peers - 1)), "hsend": dma((WX,)), "hrecv": dma((WX,)),
    }
    outs = pl.pallas_call(
        front_body,
        out_shape=tuple(sds(*shapes[n]) for n in FRONT_OUTS),
        in_specs=[ANY] * 4 + [VM] * len(small),
        out_specs=(ANY,) * len(FRONT_OUTS),
        scratch_shapes=[sems[n] if n in sems else pltpu.VMEM(*shapes[n]) for n in FRONT_SCRATCH],
        compiler_params=pltpu.CompilerParams(collective_id=0, has_side_effects=True, vmem_limit_bytes=GRANT),
    )(tok, cot, in_weight, out_weight, *small)
    return dict(zip(FRONT_OUTS, outs))


class Share:
    COPIES = 10

    def __init__(self, own, other, r1, r2, r3, r4, out, send, recv):
        self.own, self.other, self.r1, self.r2, self.r3, self.r4, self.out = own, other, r1, r2, r3, r4, out
        self.send, self.recv = send, recv
        self.at = place()
        self.copies = []

    def go(self, source, target, to):
        i = len(self.copies)
        copy = remote(source, target, self.send.at[i], self.recv.at[i], to)
        copy.start()
        self.copies.append(copy)
        return copy

    def stage(self, k):
        y, c, z, x = self.at
        own = self.own
        half = own.shape[3] // 2
        top, bottom = pl.ds(0, half), pl.ds(half, half)
        to_y, to_x, to_c = device(1 - y, c, z, x), device(y, c, z, 1 - x), device(y, 1 - c, z, x)
        if k > 0:
            arrived(self.wait)
        if k == 0:
            self.wait = [self.go(self.other.at[i], self.r1.at[i], to_c) for i in (0, 1)]
        elif k == 1:

            def piece(i, _):
                at = (i // 8, i // 2 % 4, i % 2)
                own[at] = own[at] + self.r1[at]
                return 0

            lax.fori_loop(0, 16, piece, 0)
            self.wait = [self.go(own.at[1 - y, :, :, top], self.r2.at[pl.ds(0, 4), :], to_y)]
            for i in (0, 1):
                self.wait.append(self.go(own.at[i, :, 1 - x, bottom], self.r2.at[pl.ds(4, 4), i], to_x))
        elif k == 2:

            def piece(i, _):
                b, d = i // 2, i % 2
                own[y, b, d, top] = own[y, b, d, top] + self.r2[b, d]
                own[d, b, x, bottom] = own[d, b, x, bottom] + self.r2[4 + b, d]
                return 0

            lax.fori_loop(0, 8, piece, 0)
            self.wait = [
                self.go(own.at[y, :, 1 - x, top], self.r3.at[0], to_x),
                self.go(own.at[1 - y, :, x, bottom], self.r3.at[1], to_y),
            ]
        elif k == 3:

            def piece(b, _):
                own[y, b, x, top] = own[y, b, x, top] + self.r3[0, b]
                own[y, b, x, bottom] = own[y, b, x, bottom] + self.r3[1, b]
                return 0

            lax.fori_loop(0, 4, piece, 0)
            self.wait = [
                self.go(own.at[y, z ^ i, x], self.r4.at[i - 1], device(y, c, z ^ i, x)) for i in (1, 2, 3)
            ]
        else:
            total = own[y, z, x].astype(F32)
            for i in range(3):
                total = total + self.r4[i].astype(F32)
            self.out[...] = total

    def drain(self):
        for copy in self.copies:
            copy.wait_send()
        self.copies = []


def adjoint_part(chunk, h, dt, xt, bb, cb, gt, a2, starts, later, keep, decays, pb, pc, rb, rc, ga, size):
    hs = pl.ds(h * 8, 8)
    base = chunk * size
    first = tuple(starts[chunk, n, hs, :] for n in range(DS))
    for n in range(DS):
        keep[n * 8 : n * 8 + 8, :] = first[n]

    def again(i, carry):
        t = base + i
        d = tile_at(dt, t, h)
        dx = d * tile_at(xt, t, h)
        new = []
        for n in range(DS):
            w = jnp.exp2(a2[n, hs, :] * d)
            s = w * carry[n] + dx * row_of(bb, t * DS + n)
            o = pl.multiple_of(i * 128 + n * 8, 8)
            decays[pl.ds(o, 8), :] = w
            keep[pl.ds(pl.multiple_of(o + 128, 8), 8), :] = s
            new.append(s)
        return tuple(new)

    lax.fori_loop(0, size, again, first, unroll=4)

    def back(j, carry):
        i = size - 1 - j
        t = base + i
        d = tile_at(dt, t, h)
        x = tile_at(xt, t, h)
        gy = tile_at(gt, t, h)
        dx = d * x
        slot = (j % 2) * 128
        new = []
        weighted, through_a = [], []
        for n in range(DS):
            o = pl.multiple_of(i * 128 + n * 8, 8)
            w = decays[pl.ds(o, 8), :]
            before = keep[pl.ds(o, 8), :]
            now = keep[pl.ds(pl.multiple_of(o + 128, 8), 8), :]
            g = carry[n] + gy * row_of(cb, t * DS + n)
            at = pl.ds(pl.multiple_of(slot + n * 8, 8), 8)
            pc[at, :] = now * gy
            pb[at, :] = g * dx
            weighted.append(g * row_of(bb, t * DS + n))
            g = g * w
            through = g * before
            through_a.append(through * a2[n, hs, :])
            ga[n, hs, :] += through * d
            new.append(g)
        while len(weighted) > 1:
            weighted = [weighted[i] + weighted[i + 1] for i in range(0, len(weighted), 2)]
            through_a = [through_a[i] + through_a[i + 1] for i in range(0, len(through_a), 2)]
        o = pl.ds(pl.multiple_of(t * 16 + h * 8, 8), 8)
        dt[o, :] = through_a[0] * LN2 + weighted[0] * x
        xt[o, :] = weighted[0] * d
        for src, dst in ((pb, rb), (pc, rc)):
            for m in range(2):
                parts = [src[pl.ds(slot + m * 64 + s, 8, stride=8), :] for s in range(8)]
                while len(parts) > 1:
                    parts = [parts[i] + parts[i + 1] for i in range(0, len(parts), 2)]
                q = pl.ds(pl.multiple_of(i * 16 + m * 8, 8), 8)
                if h == 0:
                    dst[q, :] = parts[0]
                else:
                    dst[q, :] += parts[0]
        return tuple(new)

    out = lax.fori_loop(0, size, back, tuple(later[n, hs, :] for n in range(DS)), unroll=2)
    for n in range(DS):
        later[n, hs, :] = out[n]


def collect_rows(chunk, size, rb, rc, gb, gc):
    ones = jnp.ones((8, 128), BF16)
    per = size * DS // 128
    for src, dst in ((rb, gb), (rc, gc)):
        v = src[...]
        hi = v.astype(BF16)
        lo = (v - hi.astype(F32)).astype(BF16)
        s = dot_nt(ones, hi) + dot_nt(ones, lo)
        for i in range(per):
            dst[chunk * per + i : chunk * per + i + 1, :] = s[0:1, i * 128 : (i + 1) * 128]


BACK_IN = (
    "back2", "gated", "low", "normed", "gz", "dt", "xt", "bb", "cb", "gt", "a2", "starts", "draw", "xs", "w0", "selt",
    "filt", "xin", "halo", "inx", "inz", "gain", "skipg", "tok", "cot",
)
BACK_LOAD = tuple(n for n in BACK_IN if n not in ("inx", "inz"))
BACK_OUT = ("tgrad", "gin", "gout", "gpack")
BACK_SCRATCH = BACK_LOAD[:-1] + (
    "wbuf", "keep", "decays", "pb", "pc", "rb", "rc", "ga", "gb", "gc", "proj", "xp", "gp", "rawlow", "gproj", "dw", "w0g",
    "selg", "edge", "gx", "gn", "gaing",
    "own", "other", "r1", "r2", "r3", "r4", "pown", "pother", "p1", "p2", "p3", "p4",
    "so", "final2",
    "load", "wsem", "send", "recv", "esend", "erecv", "rsend", "rrecv",
)
BLOCKS = 4


def back_body(*refs):
    hbm = dict(zip(BACK_IN, refs))
    refs = refs[len(BACK_IN) :]
    o = dict(zip(BACK_OUT, refs))
    v = dict(zip(BACK_SCRATCH, refs[len(BACK_OUT) :]))
    loads = {}
    for i, name in enumerate(BACK_LOAD):
        loads[name] = pltpu.make_async_copy(hbm[name], o["tgrad"] if name == "cot" else v[name], v["load"].at[i])
        loads[name].start()

    def need(*names):
        for name in names:
            loads[name].wait()

    y, c, z, x = place()
    b, s = lax.axis_index("batch"), lax.axis_index("seq")
    peers = lax.axis_size("seq")
    greet([(b, lax.rem(s + k, peers)) for k in range(1, peers)] + [device(1 - y, c, z, x), device(y, 1 - c, z, x)])
    need("back2")
    sent = carry_back(v["back2"], v["final2"], v["rsend"].at[0], v["rrecv"].at[0])

    rows, di = v["gz"].shape
    width = v["normed"].shape[1]
    tiles = di // 128
    cols = di // BLOCKS
    half = width // 2
    owned = v["own"].shape[4]
    jobs = []

    def job(out):
        i = len(jobs)
        at = i % (2 * BLOCKS)
        jobs.append(
            Share(
                v["own"].at[at], v["other"].at[at], v["r1"].at[i], v["r2"].at[i], v["r3"].at[i], v["r4"].at[i],
                out, v["send"].at[i], v["recv"].at[i],
            )
        )

    for i in range(4):
        job(o["gout"].at[i // 2 * owned : (i // 2 + 1) * owned, i % 2 * half : (i % 2 + 1) * half])
    for i in range(BLOCKS):
        job(o["gin"].at[:, di + i * cols : di + (i + 1) * cols])
    for i in range(BLOCKS):
        job(o["gin"].at[:, i * cols : (i + 1) * cols])
    last = len(jobs)
    jobs.append(
        Share(
            v["pown"], v["pother"], v["p1"], v["p2"], v["p3"], v["p4"], o["gpack"], v["send"].at[last], v["recv"].at[last]
        )
    )
    events, now, clock = [], [0], [0.0]
    first = [0]

    def enter(*blocks, steps=STEPS_BACK):
        for i in blocks:
            first[0] = max(first[0] + 1, now[0])
            events.extend((first[0] + steps[k], -k, i) for k in range(STAGES))
        events.sort()

    def advance():
        now[0], k, i = events.pop(0)
        jobs[i].stage(-k)

    def spend(time):
        clock[0] += time
        while clock[0] >= PACE_BACK:
            clock[0] -= PACE_BACK
            if events:
                advance()

    def finish(i):
        while any(e[2] == i for e in events):
            advance()
        jobs[i].drain()

    need("gated", "low")

    def out_blocks(core, dst):
        def block(i, _):
            first = pl.multiple_of(((i // 2) * 2 + core) * (di // 4) + (i % 2) * 256, 256)
            g = v["gated"][:, pl.ds(first, 256)]
            for q in range(2):
                r = dot_tn(g, v["low"][:, q * half : (q + 1) * half]).astype(BF16).reshape(2, 2, 2, owned, half)
                for p in range(2):
                    dst[p * 2 + q, i // 2, pl.ds((i % 2) * 2, 2)] = r[:, :, p]
            return 0

        lax.fori_loop(0, 4, block, 0)

    def in_blocks(core, dst, first, right):
        def block(i, _):
            n = v["normed"][:, pl.ds(pl.multiple_of((i * 2 + core) * (width // 4), 256), width // 4)]
            for q, g in enumerate(right):
                dst[first + q, i] = dot_tn(n, g()).astype(BF16).reshape(4, 2, owned, cols)
            return 0

        lax.fori_loop(0, 2, block, 0)

    out_blocks(1 - c, v["other"])
    enter(0, 1, 2, 3)
    advance()
    advance()
    out_blocks(c, v["own"])
    need("normed", "gz")
    z_right = [lambda q=q: v["gz"][:, q * cols : (q + 1) * cols] for q in range(BLOCKS)]
    in_blocks(1 - c, v["other"], BLOCKS, z_right)
    enter(4, 5, 6, 7)
    in_blocks(c, v["own"], BLOCKS, z_right)
    spend(3.0)
    arrived(sent)
    pair = DS // peers
    for j in range(peers):
        for i in range(pair):
            v["so"][j * pair + i] = v["final2"][j, i].astype(F32)

    need("dt", "xt", "bb", "cb", "gt", "a2", "starts")
    v["ga"][...] = jnp.zeros_like(v["ga"])
    chunks = v["starts"].shape[0]
    size = rows // chunks
    for chunk in reversed(range(chunks)):
        for h in range(2):
            adjoint_part(
                chunk, h, v["dt"], v["xt"], v["bb"], v["cb"], v["gt"], v["a2"], v["starts"], v["so"], v["keep"],
                v["decays"], v["pb"], v["pc"], v["rb"], v["rc"], v["ga"], size,
            )
            spend(2.0)
        collect_rows(chunk, size, v["rb"], v["rc"], v["gb"], v["gc"])
        spend(0.75)

    need("draw", "xs", "w0", "selt")
    v["proj"][:, 0:PACK0] = dot_nt(v["xs"][...], v["selt"][...])
    low = v["proj"][:, 0:DTR].astype(BF16)
    v["dw"][...] = v["w0"][DELTA0 : DELTA0 + DTR, :].astype(BF16)
    w0g = v["w0g"]

    def raw(k, _):
        at = lanes(k)
        g = v["dt"][pl.ds(k, rows, stride=tiles), :] * sigmoid(v["draw"][:, at])
        w0g[5:6, at] = jnp.sum(g, axis=0, keepdims=True)
        gl = g.astype(BF16)
        v["rawlow"][:, at] = gl
        w0g[DELTA0 : DELTA0 + DTR, at] = dot_tn(low, gl)
        return 0

    spend(0.5)
    for q in range(BLOCKS):
        lax.fori_loop(q * (tiles // BLOCKS), (q + 1) * (tiles // BLOCKS), raw, 0, unroll=2)
        spend(0.85)
    v["gproj"][:, 0:DTR] = dot_nt(v["rawlow"][...], v["dw"][...]).astype(BF16)
    per = 128 // DS
    for first_lane, src in ((DTR, v["gb"]), (DTR + DS, v["gc"])):
        for i in range(per):
            v["proj"][pl.ds(i, rows // per, stride=per), 0:DS] = src[:, i * DS : (i + 1) * DS]
        v["gproj"][:, first_lane : first_lane + DS] = v["proj"][:, 0:DS].astype(BF16)
    need("filt", "xin", "halo")
    not_first = jnp.where(s > 0, 1.0, 0.0)
    not_last = jnp.where(s < peers - 1, 1.0, 0.0)

    def point(k, _):
        at = lanes(k)
        gp = v["gproj"][...]
        v["selg"][:, at] = dot_tn(gp, v["xs"][:, at])
        into = dot(gp, v["selt"][:, at])
        here = pl.ds(k, rows, stride=tiles)
        g = v["gt"][here, :] * v["w0"][6:7, at] + v["xt"][here, :] + into
        f = v["filt"][:, at]
        sg = sigmoid(f)
        gf = g * (sg * (1.0 + f * (1.0 - sg)))
        v["filt"][:, at] = gf
        w0g[4:5, at] = jnp.sum(gf, axis=0, keepdims=True)
        v["xp"][0:16, :] = v["halo"][:, at].astype(F32) * not_first
        v["xp"][16 : 16 + rows, :] = v["xin"][:, at].astype(F32)
        for tap in range(KW):
            lo = 16 - (KW - 1) + tap
            w0g[tap : tap + 1, at] = jnp.sum(gf * v["xp"][lo : lo + rows, :], axis=0, keepdims=True)
        return 0

    edges = []

    def points(q):
        lax.fori_loop(q * (tiles // BLOCKS), (q + 1) * (tiles // BLOCKS), point, 0, unroll=2)
        at = pl.ds(q * cols, cols)
        copy = remote(
            v["filt"].at[pl.ds(0, 8), at], v["edge"].at[:, at], v["esend"].at[q], v["erecv"].at[q],
            (b, lax.rem(s + peers - 1, peers)),
        )
        copy.start()
        edges.append(copy)

    weights = {}

    def fetch(i):
        source = hbm["inx"].at[i] if i < WX else hbm["inz"].at[i - WX]
        weights[i] = pltpu.make_async_copy(source, v["wbuf"].at[i % 2], v["wsem"].at[i])
        weights[i].start()

    fetch(0)
    fetch(1)

    def blocks(q):
        edges[q].wait_recv()

        def conv(k, _):
            at = lanes(k)
            v["gp"][0:rows, :] = v["filt"][:, at]
            v["gp"][rows : rows + 8, :] = v["edge"][:, at] * not_last
            total = jnp.zeros((rows, 128), F32)
            for tap in range(KW):
                lo = KW - 1 - tap
                total = total + v["w0"][tap : tap + 1, at] * v["gp"][lo : lo + rows, :]
            v["gx"][:, at] = total.astype(BF16)
            return 0

        lax.fori_loop(q * (tiles // BLOCKS), (q + 1) * (tiles // BLOCKS), conv, 0)
        right = [lambda: v["gx"][:, q * cols : (q + 1) * cols]]
        finish(q)
        in_blocks(1 - c, v["other"], q, right)
        jobs[2 * BLOCKS + q].stage(0)
        enter(2 * BLOCKS + q, steps=STEPS_LAST)
        events.remove((first[0], 0, 2 * BLOCKS + q))
        in_blocks(c, v["own"], q, right)
        while events and events[0][0] <= first[0]:
            advance()

    def into_rows(i):
        weights[i].wait()
        g = v["gx"] if i < WX else v["gz"]
        q = i % WX
        for d in range(2):
            w = v["wbuf"][i % 2].reshape(width, cols)[d * half : (d + 1) * half]
            part = dot_nt(g[:, q * cols : (q + 1) * cols], w)
            at = slice(d * half, (d + 1) * half)
            v["gn"][:, at] = part if i == 0 else v["gn"][:, at] + part
        if i + 2 < 2 * WX:
            fetch(i + 2)
        spend(0.5)

    points(0)
    points(1)
    for q in range(2, BLOCKS):
        points(q)
        blocks(q - 2)
    blocks(BLOCKS - 2)
    blocks(BLOCKS - 1)
    for i in range(2 * WX):
        into_rows(i)
    need("tok", "cot", "gain")

    def rows_of(i, total):
        r = pl.ds(pl.multiple_of(i * 8, 8), 8)
        u = v["tok"][r, :]
        g = v["gn"][r, :]
        scale = lax.rsqrt(jnp.mean(u * u, axis=-1, keepdims=True) + EPS)
        w = g * v["gain"][0:1, :]
        mean = jnp.mean(w * u, axis=-1, keepdims=True)
        o["tgrad"][r, :] = o["tgrad"][r, :] + scale * w - u * (scale * scale * scale * mean)
        return total + g * u * scale

    total = lax.fori_loop(0, rows // 8, rows_of, jnp.zeros((8, width), F32), unroll=4)
    v["gaing"][...] = jnp.broadcast_to(jnp.sum(total, axis=0, keepdims=True), (8, width))
    need("skipg")
    w0g[6:7, :] = v["skipg"][0:1, :]
    w0g[7:8, :] = jnp.zeros((1, di), F32)
    w0g[DELTA0 + DTR : PACK0, :] = jnp.zeros((PACK0 - DELTA0 - DTR, di), F32)
    for k in range(tiles):
        w0g[ALOG0 : ALOG0 + DS, k * 128 : (k + 1) * 128] = v["ga"][:, k, :] * v["a2"][:, k, :] * LN2
    low_half = lax.broadcasted_iota(jnp.int32, (PACK0, 128), 1) < 64

    def pack(core, dst):
        def pair(i, _):
            j = i // 4 * 8 + core * 4 + i % 4
            at = lanes(j)
            l, r = w0g[:, at], v["selg"][:, at]
            dst[i // 4, i % 4, 0, 0:PACK0, :] = jnp.where(low_half, l, pltpu.roll(r, 64, 1)).astype(BF16)
            dst[i // 4, i % 4, 1, 0:PACK0, :] = jnp.where(low_half, pltpu.roll(l, 64, 1), r).astype(BF16)
            g = jnp.broadcast_to(v["gaing"][0:1, lanes(j // 2)], (PACK - PACK0, 128)).astype(BF16)
            for d in range(2):
                dst[i // 4, i % 4, d, PACK0:PACK, :] = g
            return 0

        lax.fori_loop(0, 8, pair, 0)

    spend(3.0)
    pack(1 - c, v["pother"])
    jobs[last].stage(0)
    pack(c, v["pown"])
    first[0] = now[0] - 1
    enter(last, steps=STEPS_PACK)
    events.remove((first[0], 0, last))
    while events:
        advance()
    for it in jobs:
        it.drain()
    for it in edges + sent:
        it.wait_send()


def back(f, tok, cot):
    rows, di = f["gz"].shape
    width = tok.shape[1]
    tiles = di // 128
    cols = di // BLOCKS
    chunks = f["starts"].shape[0]
    size = rows // chunks
    lead = (2, 4, 2)
    owned = width // 32
    inputs = dict(f, tok=tok, cot=cot)
    shapes = {n: (inputs[n].shape, inputs[n].dtype) for n in BACK_IN}
    peers = f["back2"].shape[0]
    pair = (DS // peers, tiles, 128)
    shapes.update(
        so=((DS, tiles, 128), F32), final2=((peers,) + pair, BF16),
    )

    def sums(prefix, n, rows, cols, held):
        names = ("own", "other", "r1", "r2", "r3", "r4") if not prefix else ("pown", "pother", "p1", "p2", "p3", "p4")
        dims = (
            lead + (rows, cols), lead + (rows, cols), lead + (rows, cols), (8, 2, rows // 2, cols),
            (2, 4, rows // 2, cols), (3, rows, cols),
        )
        for i, (name, d) in enumerate(zip(names, dims)):
            k = (held if i < 2 else n,) if not prefix else ()
            shapes[name] = (k + d, BF16)

    sums("", 3 * BLOCKS, owned, cols, 2 * BLOCKS)
    sums("p", 1, PACK, 128, 1)
    tall = ((size * DS, 128), F32)
    shapes.update(
        wbuf=((2, 2, 2, 4, 2, owned, cols), BF16), keep=(((size + 1) * 128, 128), F32), decays=((size * 128, 128), F32),
        pb=((256, 128), F32), pc=((256, 128), F32), rb=tall, rc=tall, ga=((DS, tiles, 128), F32), gb=((rows * DS // 128, 128), F32),
        gc=((rows * DS // 128, 128), F32), proj=((rows, 128), F32), xp=((rows + 16, 128), F32), gp=((rows + 8, 128), F32),
        rawlow=((rows, di), BF16), gproj=((rows, PACK0), BF16), dw=((DTR, di), BF16), w0g=((PACK0, di), F32),
        selg=((PACK0, di), F32), edge=((8, di), F32), gx=((rows, di), BF16), gn=((rows, width), F32), gaing=((8, width), F32),
    )
    dma = pltpu.SemaphoreType.DMA
    n_jobs = 3 * BLOCKS + 1
    sems = {
        "load": dma((len(BACK_LOAD),)), "wsem": dma((2 * WX,)), "send": dma((n_jobs, Share.COPIES)),
        "recv": dma((n_jobs, Share.COPIES)), "esend": dma((BLOCKS,)), "erecv": dma((BLOCKS,)),
        "rsend": dma((1, peers - 1)), "rrecv": dma((1, peers - 1)),
    }
    return pl.pallas_call(
        back_body,
        out_shape=(
            sds((rows, width), F32), sds((owned, 2 * di), F32), sds((di // 32, width), F32), sds((PACK, 128), F32),
        ),
        in_specs=[ANY] * len(BACK_IN),
        out_specs=(VM,) * 4,
        scratch_shapes=[sems[n] if n in sems else pltpu.VMEM(*shapes[n]) for n in BACK_SCRATCH],
        compiler_params=pltpu.CompilerParams(collective_id=1, has_side_effects=True, vmem_limit_bytes=GRANT),
    )(*(inputs[n] for n in BACK_IN))


def finish_body(*refs):
    big, pack = refs[:4], refs[4]
    outs, small, sem = refs[5:9], refs[9:17], refs[17]
    copies = [pltpu.make_async_copy(src, dst, sem.at[i]) for i, (src, dst) in enumerate(zip(big, outs))]
    for copy in copies:
        copy.start()
    gain, conv, conv_bias, select, delta, delta_bias, a_log, skip = small
    own = conv.shape[1]
    conv[...] = pack[0:KW, 0:own]
    for row, ref in ((4, conv_bias), (5, delta_bias), (6, skip)):
        ref[...] = pack[row : row + 1, 0:own]
    a_log[...] = pack[ALOG0 : ALOG0 + DS, 0:own]
    delta[...] = pack[DELTA0 : DELTA0 + DTR, 0:own]
    select[...] = pack[...].T[own : 2 * own, 0:PACK0]
    part = gain.shape[1]
    parts = 128 // part
    me = (lax.axis_index("batch") * lax.axis_size("seq") + lax.axis_index("seq")) % parts
    tile = pack[PACK0 : PACK0 + 1, :]
    total = jnp.zeros((1, part), F32)
    for i in range(parts):
        total = total + jnp.where(me == i, tile[:, i * part : (i + 1) * part], 0.0)
    gain[...] = total
    for copy in copies:
        copy.wait()


def finish(whole, small):
    block, tgrad, gin, gout, pack = whole
    big = (block, tgrad, gin, gout)
    return pl.pallas_call(
        finish_body,
        out_shape=tuple(sds(v.shape, F32) for v in big + small),
        in_specs=[VM] * 5,
        out_specs=(ANY,) * 4 + (VM,) * 8,
        scratch_shapes=[pltpu.SemaphoreType.DMA((4,))],
        compiler_params=pltpu.CompilerParams(vmem_limit_bytes=GRANT),
    )(*big, pack)


def on_slice(tokens, cotangent, norm_gain, in_weight, conv_weight, conv_bias, select_weight, delta_weight, delta_bias, a_log, skip_gain, out_weight):
    sizes = (lax.axis_size("batch"), lax.axis_size("seq"))
    tok, cot = tokens[0], cotangent[0]
    rows = tok.shape[0]
    small = (
        norm_gain[None], conv_weight, conv_bias[None], select_weight, delta_weight, delta_bias[None], a_log, skip_gain[None],
    )
    f = front(tok, cot, in_weight, out_weight, small, sizes[1], rows // 32)
    whole = (f["block"],) + back(f, tok, cot)
    block_out, tokens_grad, g_in, g_out, *grads = finish(whole, small)
    g_gain, g_conv, g_conv_bias, g_select, g_delta, g_delta_bias, g_a_log, g_skip = grads
    return (
        block_out[None], tokens_grad[None], g_gain[0], g_in, g_conv, g_conv_bias[0], g_select, g_delta, g_delta_bias[0],
        g_a_log, g_skip[0], g_out,
    )


def on_device(tokens, cotangent, norm_gain, in_weight, conv_weight, conv_bias, select_weight, delta_weight, delta_bias, a_log, skip_gain, out_weight):
    axes = ("batch", "seq")
    sizes = (lax.axis_size("batch"), lax.axis_size("seq"))
    if sizes == (4, 8):
        return on_slice(
            tokens, cotangent, norm_gain, in_weight, conv_weight, conv_bias, select_weight, delta_weight, delta_bias,
            a_log, skip_gain, out_weight,
        )
    tok, cot = tokens[0], cotangent[0]
    rows, width = tok.shape
    di = out_weight.shape[0] * sizes[0] * sizes[1]
    tiles = di // 128
    full = lambda v, axis: lax.all_gather(v, axes, axis=axis, tiled=True)
    in_full = full(in_weight, 0)
    in_x, in_z = in_full[:, :di], in_full[:, di:]
    out_full = full(out_weight, 0)
    sel_t = full(select_weight, 0).T
    gain = full(norm_gain, 0)[None].astype(F32)
    w0 = jnp.concatenate(
        [
            full(conv_weight, 1), full(conv_bias, 0)[None], full(delta_bias, 0)[None], full(skip_gain, 0)[None],
            jnp.zeros((1, di), BF16), full(a_log, 1), full(delta_weight, 1),
            jnp.zeros((PACK0 - DELTA0 - DTR, di), BF16),
        ],
        axis=0,
    ).astype(F32)

    flat = sds((rows * tiles, 128), F32)
    wide = sds((rows, di), F32)
    spread = sds((rows * DS, 128), F32)
    carry = sds((DS, tiles, 128), F32)

    normed, x_in = kernel_call(
        inproj_body, (sds((rows, width), BF16), sds((rows, di), BF16)), 3
    )(tok, gain, in_x)
    halo = shift(x_in[rows - 16 :], 1)
    filt, xs, xt, draw, dt, bb, cb = kernel_call(
        conv_body,
        (wide, sds((rows, di), BF16), flat, wide, flat, spread, spread),
        4,
        [pltpu.VMEM((rows, 128), F32), pltpu.VMEM((rows + 16, 128), F32)],
    )(x_in, halo, w0, sel_t)
    a2, total, end = kernel_call(lightf_body, (carry, carry, carry), 4)(dt, xt, bb, w0)
    gate, gzp, gt, low, adj = kernel_call(
        gate_body, (wide, wide, flat, sds((rows, width), BF16), carry), 7
    )(normed, in_z, cot, out_full, dt, cb, a2)
    state_in = carried_in(total, end, False)
    state_out = carried_in(total, adj, True)
    chunks = rows // 64
    starts, block_out, gz, out_grad, z_grad, skip_grad = kernel_call(
        forward_body,
        (
            sds((chunks, DS, tiles, 128), F32), sds((rows, width), F32), sds((rows, di), BF16),
            sds((di, width), BF16), sds((width, di), BF16), sds((1, di), F32),
        ),
        14,
        [pltpu.VMEM((rows * tiles, 128), F32), pltpu.VMEM((rows, di), BF16), pltpu.VMEM((8, 128), F32)],
    )(state_in, dt, xt, bb, cb, a2, w0, gate, gzp, gt, tok, low, normed, out_full)
    tall = pltpu.VMEM((rows * DS, 128), F32)
    gdt, gat, gb, gc, ga = kernel_call(
        backward_body,
        (flat, flat, sds((rows, 128), F32), sds((rows, 128), F32), carry),
        8,
        [
            pltpu.VMEM((65 * 128, 128), F32), pltpu.VMEM((64 * 128, 128), F32), pltpu.VMEM((256, 128), F32),
            pltpu.VMEM((256, 128), F32), tall, tall,
        ],
    )(state_out, starts, dt, xt, bb, cb, gt, a2)
    gf, w0g, selg = kernel_call(
        tail_body,
        (wide, sds((PACK0, di), F32), sds((PACK0, di), F32)),
        12,
        [
            pltpu.VMEM((rows, 128), F32), pltpu.VMEM((rows + 16, 128), F32), pltpu.VMEM((rows, di), BF16),
            pltpu.VMEM((rows, PACK0), BF16), pltpu.VMEM((DTR, di), BF16),
        ],
    )(gdt, gat, gb, gc, gt, draw, filt, x_in, halo, xs, w0, sel_t)
    edge = shift(gf[:8], -1)
    tokens_grad, x_grad, gain_grad = kernel_call(
        last_body,
        (sds((rows, width), F32), sds((width, di), BF16), sds((1, width), F32)),
        10,
        [pltpu.VMEM((rows + 8, 128), F32), pltpu.VMEM((rows, di), BF16), pltpu.VMEM((rows, width), F32)],
    )(gf, edge, w0, gz, normed, tok, cot, gain, in_x, in_z)

    share = lambda v, d: lax.psum_scatter(v.astype(F32), axes, scatter_dimension=d, tiled=True)
    ga_flat = ga.reshape(DS, di)
    grads = (
        share(gain_grad[0], 0), share(jnp.concatenate([x_grad, z_grad], axis=1), 0), share(w0g[0:KW], 1),
        share(w0g[4], 0), share(selg.T, 0), share(w0g[DELTA0 : DELTA0 + DTR], 1), share(w0g[5], 0),
        share(ga_flat, 1), share(skip_grad[0], 0), share(out_grad, 0),
    )
    return (block_out[None], tokens_grad[None]) + grads


def solution(mesh):
    both = ("batch", "seq")
    first, second = P(both), P(None, both)
    matrix = P(both, None)
    whole = P("batch", "seq", None)
    weights = (first, matrix, second, first, matrix, second, first, second, first, matrix)
    return jax.shard_map(
        on_device,
        mesh=mesh,
        in_specs=(whole, whole) + weights,
        out_specs=(whole, whole) + weights,
        check_vma=False,
    )
```

```python
import functools

import jax
import jax.numpy as jnp
from jax import lax
from jax.experimental import pallas as pl
from jax.experimental.pallas import tpu as pltpu
from jax.sharding import PartitionSpec as P

DS = 16
KW = 4
DTR = 64
EPS = 1e-05
LOG2E = 1.4426950408889634
LN2 = 0.6931471805599453
F32 = jnp.float32
BF16 = jnp.bfloat16
MESH = pl.DeviceIdType.MESH
VM = pl.BlockSpec(memory_space=pltpu.VMEM)
ANY = pl.BlockSpec(memory_space=pl.ANY)
GRANT = 60 << 20
ALOG0, DELTA0, PACK0, PACK = 8, 24, 96, 128


def sds(shape, dtype):
    return jax.ShapeDtypeStruct(shape, dtype)


def kernel_call(body, outs, n_in, scratch=(), flops=1e9, **params):
    return pl.pallas_call(
        body,
        out_shape=outs,
        in_specs=[VM] * n_in,
        out_specs=jax.tree.map(lambda _: VM, outs),
        scratch_shapes=list(scratch),
        cost_estimate=pl.CostEstimate(flops=int(flops), bytes_accessed=8 << 20, transcendentals=0),
        compiler_params=pltpu.CompilerParams(vmem_limit_bytes=GRANT, **params),
    )


def sigmoid(v):
    return 1.0 / (1.0 + jnp.exp(-v))


def dot(a, b):
    return jnp.dot(a, b, preferred_element_type=F32)


def dot_nt(a, b):
    return lax.dot_general(a, b, (((1,), (1,)), ((), ())), preferred_element_type=F32)


def dot_tn(a, b):
    return lax.dot_general(a, b, (((0,), (0,)), ((), ())), preferred_element_type=F32)


def lanes(k, width=128):
    return pl.ds(pl.multiple_of(k * width, width), width)


def inproj_body(tok_ref, gain_ref, inx_ref, normed_ref, xin_ref):
    rows = tok_ref.shape[0]

    def norm(i, _):
        r = pl.ds(pl.multiple_of(i * 16, 16), 16)
        u = tok_ref[r, :]
        scale = lax.rsqrt(jnp.mean(u * u, axis=-1, keepdims=True) + EPS)
        normed_ref[r, :] = (u * scale * gain_ref[...]).astype(BF16)
        return 0

    lax.fori_loop(0, rows // 16, norm, 0)
    width = 512

    def mm(j, _):
        c = lanes(j, width)
        xin_ref[:, c] = dot(normed_ref[...], inx_ref[:, c]).astype(BF16)
        return 0

    lax.fori_loop(0, inx_ref.shape[1] // width, mm, 0)


def conv_body(xin_ref, halo_ref, w0_ref, selt_ref, filt_ref, xs_ref, xt_ref, draw_ref, dt_ref, bb_ref, cb_ref, proj, xp):
    rows, di = xin_ref.shape
    tiles = di // 128
    xp_rows = 16 + rows

    def conv(k, _):
        c = lanes(k)
        xp[0:16, :] = halo_ref[:, c].astype(F32)
        xp[16:xp_rows, :] = xin_ref[:, c].astype(F32)
        for q in range(2):
            r0 = q * (rows // 2)
            f = w0_ref[4:5, c]
            for tap in range(KW):
                lo = 16 - (KW - 1) + tap + r0
                f = f + w0_ref[tap : tap + 1, c] * xp[lo : lo + rows // 2, :]
            s = (f * sigmoid(f)).astype(BF16)
            filt_ref[r0 : r0 + rows // 2, c] = f
            xs_ref[r0 : r0 + rows // 2, c] = s
            xt_ref[pl.ds(r0 * tiles + k, rows // 2, stride=tiles), :] = s.astype(F32)
        return 0

    lax.fori_loop(0, tiles, conv, 0)
    proj[:, 0:96] = dot_nt(xs_ref[...], selt_ref[...])
    low = proj[:, 0:DTR].astype(BF16)

    def delta(k, _):
        c = lanes(k)
        raw = dot(low, w0_ref[DELTA0 : DELTA0 + DTR, c].astype(BF16)) + w0_ref[5:6, c]
        draw_ref[:, c] = raw
        dt_ref[pl.ds(k, rows, stride=tiles), :] = jnp.maximum(raw, 0.0) + jnp.log1p(jnp.exp(-jnp.abs(raw)))
        return 0

    lax.fori_loop(0, tiles, delta, 0)
    row_ids = lax.broadcasted_iota(jnp.int32, (128, 128), 0) % DS
    lane_ids = lax.broadcasted_iota(jnp.int32, (128, 128), 1)
    ones = jnp.ones((128, 128), BF16)

    def spread(i, _):
        r = pl.ds(pl.multiple_of(i * 8, 8), 8)
        p = proj[r, :]
        tall = jnp.broadcast_to(p[:, None, :], (8, DS, 128)).reshape(128, 128)
        o = pl.ds(pl.multiple_of(i * 128, 128), 128)
        for first, ref in ((DTR, bb_ref), (DTR + DS, cb_ref)):
            v = jnp.where(lane_ids == row_ids + first, tall, 0.0)
            hi = v.astype(BF16)
            v = v - hi.astype(F32)
            mid = v.astype(BF16)
            lo = (v - mid.astype(F32)).astype(BF16)
            ref[o, :] = (dot(hi, ones) + dot(mid, ones)) + dot(lo, ones)
        return 0

    lax.fori_loop(0, rows // 8, spread, 0)


def row_of(ref, index):
    return ref[pl.ds(index, 8, stride=0), :]


def tile_at(ref, t, h):
    return ref[pl.ds(pl.multiple_of(t * 16 + h * 8, 8), 8), :]


def light_forward(dt_ref, xt_ref, bb_ref, a2_ref, total_ref, end_ref, rows):
    for h in range(2):
        hs = pl.ds(h * 8, 8)
        a = [a2_ref[n, hs, :] for n in range(DS)]

        def step(t, carry):
            state, run = carry
            d = tile_at(dt_ref, t, h)
            dx = d * tile_at(xt_ref, t, h)
            new = tuple(
                jnp.exp2(a[n] * d) * state[n] + dx * row_of(bb_ref, t * DS + n) for n in range(DS)
            )
            return (new, run + d)

        zero = jnp.zeros((8, 128), F32)
        state, run = lax.fori_loop(0, rows, step, ((zero,) * DS, zero), unroll=4)
        for n in range(DS):
            end_ref[n, hs, :] = state[n]
            total_ref[n, hs, :] = jnp.exp2(a[n] * run)


def light_backward(dt_ref, gt_ref, cb_ref, a2_ref, adj_ref, rows):
    for h in range(2):
        hs = pl.ds(h * 8, 8)
        a = [a2_ref[n, hs, :] for n in range(DS)]

        def step(i, carry):
            t = rows - 1 - i
            d = tile_at(dt_ref, t, h)
            g = tile_at(gt_ref, t, h)
            return tuple(
                jnp.exp2(a[n] * d) * (carry[n] + g * row_of(cb_ref, t * DS + n)) for n in range(DS)
            )

        out = lax.fori_loop(0, rows, step, (jnp.zeros((8, 128), F32),) * DS, unroll=4)
        for n in range(DS):
            adj_ref[n, hs, :] = out[n]


def lightf_body(dt_ref, xt_ref, bb_ref, w0_ref, a2_ref, total_ref, end_ref):
    rows = dt_ref.shape[0] // 16
    for k in range(16):
        a2_ref[:, k, :] = -jnp.exp(w0_ref[ALOG0 : ALOG0 + DS, k * 128 : (k + 1) * 128]) * LOG2E
    light_forward(dt_ref, xt_ref, bb_ref, a2_ref, total_ref, end_ref, rows)


def gate_body(normed_ref, inz_ref, cot_ref, out_ref, dt_ref, cb_ref, a2_ref, gate_ref, gzp_ref, gt_ref, low_ref, adj_ref):
    rows, di = gate_ref.shape
    tiles = di // 128
    low_ref[...] = cot_ref[...].astype(BF16)
    width = 512

    def block(j, _):
        c = lanes(j, width)
        gate_ref[:, c] = dot(normed_ref[...], inz_ref[:, c])
        gzp_ref[:, c] = dot_nt(low_ref[...], out_ref[c, :])
        return 0

    lax.fori_loop(0, di // width, block, 0)

    def point(k, _):
        c = lanes(k)
        for q in range(4):
            r = slice(q * (rows // 4), (q + 1) * (rows // 4))
            z = gate_ref[r, c]
            gg = gzp_ref[r, c]
            s = sigmoid(z)
            gate = z * s
            gate_ref[r, c] = gate
            gzp_ref[r, c] = gg * s * (1.0 + z * (1.0 - s))
            gt_ref[pl.ds(q * (rows // 4) * tiles + k, rows // 4, stride=tiles), :] = gg * gate
        return 0

    lax.fori_loop(0, tiles, point, 0)
    light_backward(dt_ref, gt_ref, cb_ref, a2_ref, adj_ref, rows)


def forward_body(
    si_ref, dt_ref, xt_ref, bb_ref, cb_ref, a2_ref, w0_ref, gate_ref, gzp_ref, gt_ref, tok_ref, low_ref, normed_ref, out_ref,
    starts_ref, block_ref, gz_ref, ograd_ref, zgrad_ref, skipg_ref, yt, gated, low_t,
):
    chunks = starts_ref.shape[0]
    rows, di = gate_ref.shape
    tiles = di // 128
    size = rows // chunks
    for h in range(2):
        hs = pl.ds(h * 8, 8)
        a = [a2_ref[n, hs, :] for n in range(DS)]
        state = tuple(si_ref[n, hs, :] for n in range(DS))
        for chunk in range(chunks):
            for n in range(DS):
                starts_ref[chunk, n, hs, :] = state[n]

            def step(i, carry):
                t = chunk * size + i
                d = tile_at(dt_ref, t, h)
                dx = d * tile_at(xt_ref, t, h)
                new, parts = [], []
                for n in range(DS):
                    s = jnp.exp2(a[n] * d) * carry[n] + dx * row_of(bb_ref, t * DS + n)
                    parts.append(s * row_of(cb_ref, t * DS + n))
                    new.append(s)
                while len(parts) > 1:
                    parts = [parts[i] + parts[i + 1] for i in range(0, len(parts), 2)]
                yt[pl.ds(pl.multiple_of(t * 16 + h * 8, 8), 8), :] = parts[0]
                return tuple(new)

            state = lax.fori_loop(0, size, step, state, unroll=4)

    def point(k, _):
        c = lanes(k)
        total = jnp.zeros((8, 128), F32)
        for q in range(4):
            r = slice(q * (rows // 4), (q + 1) * (rows // 4))
            here = pl.ds(q * (rows // 4) * tiles + k, rows // 4, stride=tiles)
            x = xt_ref[here, :]
            y = yt[here, :] + w0_ref[6:7, c] * x
            gated[r, c] = (y * gate_ref[r, c]).astype(BF16)
            gz_ref[r, c] = (gzp_ref[r, c] * y).astype(BF16)
            total = total + jnp.sum((gt_ref[here, :] * x).reshape(-1, 8, 128), axis=0)
        skipg_ref[:, c] = jnp.sum(total, axis=0, keepdims=True)
        return 0

    lax.fori_loop(0, tiles, point, 0)

    def project(j, _):
        c = lanes(j, 256)
        block_ref[:, c] = tok_ref[:, c] + dot(gated[...], out_ref[:, c])
        return 0

    lax.fori_loop(0, tok_ref.shape[1] // 256, project, 0)

    def wide(j, _):
        c = lanes(j, 256)
        ograd_ref[c, :] = dot_tn(gated[:, c], low_ref[...]).astype(BF16)
        return 0

    lax.fori_loop(0, di // 256, wide, 0)

    def wide_z(j, _):
        c = lanes(j, 256)
        zgrad_ref[:, c] = dot_tn(normed_ref[...], gz_ref[:, c]).astype(BF16)
        return 0

    lax.fori_loop(0, di // 256, wide_z, 0)


def backward_body(
    so_ref, starts_ref, dt_ref, xt_ref, bb_ref, cb_ref, gt_ref, a2_ref,
    gdt_ref, gat_ref, gb_ref, gc_ref, ga_ref, keep, decays, pb, pc, rb, rc,
):
    chunks = starts_ref.shape[0]
    rows = dt_ref.shape[0] // 16
    size = rows // chunks
    zero = jnp.zeros((8, 128), F32)
    for h in range(2):
        hs = pl.ds(h * 8, 8)
        a = [a2_ref[n, hs, :] for n in range(DS)]
        for n in range(DS):
            ga_ref[n, hs, :] = zero
        later = tuple(so_ref[n, hs, :] for n in range(DS))
        for chunk in reversed(range(chunks)):
            base = chunk * size
            first = tuple(starts_ref[chunk, n, hs, :] for n in range(DS))
            for n in range(DS):
                keep[n * 8 : n * 8 + 8, :] = first[n]

            def again(i, carry):
                t = base + i
                d = tile_at(dt_ref, t, h)
                dx = d * tile_at(xt_ref, t, h)
                new = []
                for n in range(DS):
                    w = jnp.exp2(a[n] * d)
                    s = w * carry[n] + dx * row_of(bb_ref, t * DS + n)
                    o = pl.multiple_of(i * 128 + n * 8, 8)
                    decays[pl.ds(o, 8), :] = w
                    keep[pl.ds(pl.multiple_of(o + 128, 8), 8), :] = s
                    new.append(s)
                return tuple(new)

            lax.fori_loop(0, size, again, first, unroll=4)

            def back(j, carry):
                i = size - 1 - j
                t = base + i
                d = tile_at(dt_ref, t, h)
                x = tile_at(xt_ref, t, h)
                gy = tile_at(gt_ref, t, h)
                dx = d * x
                slot = (j % 2) * 128
                new = []
                weighted, through_a = [], []
                for n in range(DS):
                    o = pl.multiple_of(i * 128 + n * 8, 8)
                    w = decays[pl.ds(o, 8), :]
                    before = keep[pl.ds(o, 8), :]
                    now = keep[pl.ds(pl.multiple_of(o + 128, 8), 8), :]
                    g = carry[n] + gy * row_of(cb_ref, t * DS + n)
                    at = pl.ds(pl.multiple_of(slot + n * 8, 8), 8)
                    pc[at, :] = now * gy
                    pb[at, :] = g * dx
                    weighted.append(g * row_of(bb_ref, t * DS + n))
                    g = g * w
                    through = g * before
                    through_a.append(through * a[n])
                    ga_ref[n, hs, :] += through * d
                    new.append(g)
                while len(weighted) > 1:
                    weighted = [weighted[i] + weighted[i + 1] for i in range(0, len(weighted), 2)]
                    through_a = [through_a[i] + through_a[i + 1] for i in range(0, len(through_a), 2)]
                o = pl.ds(pl.multiple_of(t * 16 + h * 8, 8), 8)
                gdt_ref[o, :] = through_a[0] * LN2 + weighted[0] * x
                gat_ref[o, :] = weighted[0] * d
                for src, dst in ((pb, rb), (pc, rc)):
                    for m in range(2):
                        parts = [src[pl.ds(slot + m * 64 + s, 8, stride=8), :] for s in range(8)]
                        while len(parts) > 1:
                            parts = [parts[i] + parts[i + 1] for i in range(0, len(parts), 2)]
                        q = pl.ds(pl.multiple_of(t * 16 + m * 8, 8), 8)
                        if h == 0:
                            dst[q, :] = parts[0]
                        else:
                            dst[q, :] += parts[0]
                return tuple(new)

            later = lax.fori_loop(0, size, back, later, unroll=2)
    for n in range(DS):
        ga_ref[n] = ga_ref[n] * a2_ref[n] * LN2
    ones = jnp.ones((128, 128), BF16)
    pick = lax.broadcasted_iota(jnp.int32, (128, 128), 0) % DS == lax.broadcasted_iota(jnp.int32, (128, 128), 1)

    def collect(i, _):
        o = pl.ds(pl.multiple_of(i * 128, 128), 128)
        for src, dst in ((rb, gb_ref), (rc, gc_ref)):
            v = src[o, :]
            hi = v.astype(BF16)
            lo = (v - hi.astype(F32)).astype(BF16)
            s = jnp.where(pick, dot(hi, ones) + dot(lo, ones), 0.0)
            dst[pl.ds(pl.multiple_of(i * 8, 8), 8), :] = jnp.sum(s.reshape(8, DS, 128), axis=1)
        return 0

    lax.fori_loop(0, rows // 8, collect, 0)


def tail_body(
    gdt_ref, gat_ref, gb_ref, gc_ref, gt_ref, draw_ref, filt_ref, xin_ref, halo_ref, xs_ref, w0_ref, selt_ref,
    gf_ref, w0g_ref, selg_ref, proj, xp, raw_low, gproj, dw,
):
    rows, di = draw_ref.shape
    tiles = di // 128
    proj[:, 0:96] = dot_nt(xs_ref[...], selt_ref[...])
    low = proj[:, 0:DTR].astype(BF16)
    dw[...] = w0_ref[DELTA0 : DELTA0 + DTR, :].astype(BF16)

    def raw(k, _):
        c = lanes(k)
        g = gdt_ref[pl.ds(k, rows, stride=tiles), :] * sigmoid(draw_ref[:, c])
        w0g_ref[5:6, c] = jnp.sum(g, axis=0, keepdims=True)
        gl = g.astype(BF16)
        raw_low[:, c] = gl
        w0g_ref[DELTA0 : DELTA0 + DTR, c] = dot_tn(low, gl)
        return 0

    lax.fori_loop(0, tiles, raw, 0)
    gproj[:, 0:DTR] = dot_nt(raw_low[...], dw[...]).astype(BF16)
    gproj[:, DTR : DTR + DS] = gb_ref[:, 0:DS].astype(BF16)
    gproj[:, DTR + DS : DTR + 2 * DS] = gc_ref[:, 0:DS].astype(BF16)

    def point(k, _):
        c = lanes(k)
        gp = gproj[...]
        selg_ref[:, c] = dot_tn(gp, xs_ref[:, c])
        back = dot(gp, selt_ref[:, c])
        here = pl.ds(k, rows, stride=tiles)
        ga = gt_ref[here, :] * w0_ref[6:7, c] + gat_ref[here, :] + back
        f = filt_ref[:, c]
        s = sigmoid(f)
        gf = ga * (s * (1.0 + f * (1.0 - s)))
        gf_ref[:, c] = gf
        w0g_ref[4:5, c] = jnp.sum(gf, axis=0, keepdims=True)
        xp[0:16, :] = halo_ref[:, c].astype(F32)
        xp[16 : 16 + rows, :] = xin_ref[:, c].astype(F32)
        for tap in range(KW):
            lo = 16 - (KW - 1) + tap
            w0g_ref[tap : tap + 1, c] = jnp.sum(gf * xp[lo : lo + rows, :], axis=0, keepdims=True)
        return 0

    lax.fori_loop(0, tiles, point, 0)


def last_body(gf_ref, edge_ref, w0_ref, gz_ref, normed_ref, tok_ref, cot_ref, gain_ref, inx_ref, inz_ref, tgrad_ref, xgrad_ref, gaing_ref, gp, gx, gn):
    rows, di = gf_ref.shape
    tiles = di // 128

    def conv(k, _):
        c = lanes(k)
        gp[0:rows, :] = gf_ref[:, c]
        gp[rows : rows + 8, :] = edge_ref[:, c]
        total = jnp.zeros((rows, 128), F32)
        for tap in range(KW):
            lo = KW - 1 - tap
            total = total + w0_ref[tap : tap + 1, c] * gp[lo : lo + rows, :]
        gx[:, c] = total.astype(BF16)
        return 0

    lax.fori_loop(0, tiles, conv, 0)

    def wide(j, _):
        c = lanes(j, 256)
        xgrad_ref[:, c] = dot_tn(normed_ref[...], gx[:, c]).astype(BF16)
        return 0

    lax.fori_loop(0, di // 256, wide, 0)

    def back(j, _):
        c = lanes(j, 256)
        gn[:, c] = dot_nt(gx[...], inx_ref[c, :]) + dot_nt(gz_ref[...], inz_ref[c, :])
        return 0

    lax.fori_loop(0, inx_ref.shape[0] // 256, back, 0)

    def rows_of(i, total):
        r = pl.ds(pl.multiple_of(i * 8, 8), 8)
        u = tok_ref[r, :]
        g = gn[r, :]
        scale = lax.rsqrt(jnp.mean(u * u, axis=-1, keepdims=True) + EPS)
        v = g * gain_ref[...]
        mean = jnp.mean(v * u, axis=-1, keepdims=True)
        tgrad_ref[r, :] = cot_ref[r, :] + scale * v - u * (scale * scale * scale * mean)
        return total + g * u * scale

    total = lax.fori_loop(0, rows // 8, rows_of, jnp.zeros((8, tok_ref.shape[1]), F32))
    gaing_ref[...] = jnp.sum(total, axis=0, keepdims=True)


def place():
    b, s = lax.axis_index("batch"), lax.axis_index("seq")
    return b // 2, b % 2, s // 2, s % 2


def device(y, c, z, x):
    return (y * 2 + c, z * 2 + x)


def greet(peers):
    barrier = pltpu.get_barrier_semaphore()
    for peer in peers:
        pl.semaphore_signal(barrier, inc=1, device_id=peer, device_id_type=MESH)
    pl.semaphore_wait(barrier, len(peers))


def remote(src, dst, send, recv, to):
    return pltpu.make_async_remote_copy(
        src_ref=src, dst_ref=dst, send_sem=send, recv_sem=recv, device_id=to, device_id_type=MESH
    )


def neighbours(y, c, z, x):
    return [device(y, c, z ^ k, x) for k in (1, 2, 3)] + [
        device(1 - y, c, z, x), device(y, c, z, 1 - x), device(y, 1 - c, z, x)
    ]


class Gather:
    COPIES = 14

    def __init__(self, src, out, send, recv, local):
        self.src, self.out, self.send, self.recv, self.local = src, out, send, recv, local
        self.at = place()
        self.count = 0
        self.copies = []

    def go(self, view, to):
        i = self.count
        self.count += 1
        source, target = view if isinstance(view, tuple) else (view, view)
        copy = remote(source, target, self.send.at[i], self.recv.at[i], to)
        copy.start()
        self.copies.append(copy)
        return copy

    def stage(self, k):
        y, c, z, x = self.at
        out = self.out
        half = out.shape[4] // 2
        top, bottom = pl.ds(0, half), pl.ds(half, half)
        to_y, to_x, to_c = device(1 - y, c, z, x), device(y, c, z, 1 - x), device(y, 1 - c, z, x)
        if k == 0:
            own = pltpu.make_async_copy(self.src, out.at[y, c, z, x], self.local)
            own.start()
            self.first = [self.go((self.src, out.at[y, c, z, x]), device(y, c, z ^ i, x)) for i in (1, 2, 3)]
            own.wait()
        elif k == 1:
            for copy in self.first:
                copy.wait_recv()
            self.a = self.go(out.at[y, c, :, x, top], to_y)
            self.b = self.go(out.at[y, c, :, x, bottom], to_x)
            self.go(out.at[y, c, :, x], to_c)
        elif k == 2:
            self.a.wait_recv()
            self.b.wait_recv()
            self.next = [self.go(out.at[i, c, :, x, top], to_x) for i in (0, 1)]
            self.next.append(self.go(out.at[y, c, :, :, bottom], to_y))
            self.go(out.at[1 - y, c, :, x, top], to_c)
            self.go(out.at[y, c, :, 1 - x, bottom], to_c)
        elif k == 3:
            for copy in self.next:
                copy.wait_recv()
            for i in (0, 1):
                self.go(out.at[i, c, :, 1 - x, top], to_c)
            self.go(out.at[1 - y, c, :, :, bottom], to_c)
        else:
            done = self.first + [self.a, self.b] + self.next
            for copy in self.copies:
                if not any(copy is other for other in done):
                    copy.wait_recv()

    def drain(self):
        for copy in self.copies:
            copy.wait_send()


STAGES = 5
STEPS = (0, 2, 4, 6, 7)
PACE = 1.4
DELAY = 0
STEPS_LATE = (0, 3, 6, 9, 11)
STEPS_BACK = (0, 3, 6, 9, 12)
STEPS_LAST = (0, 3, 6, 9, 12)
STEPS_PACK = (0, 1, 2, 3, 4)
PACE_BACK = 1.0


def shift(value, by):
    peers = lax.axis_size("seq")
    pairs = [(i, i + by) for i in range(peers) if 0 <= i + by < peers]
    return lax.ppermute(value, "seq", pairs)


def carried_in(total, value, reverse):
    peers, index = lax.axis_size("seq"), lax.axis_index("seq")
    totals = lax.all_gather(total.astype(BF16), "seq")
    values = lax.all_gather(value.astype(BF16), "seq")

    def turn(k, before):
        at = peers - 1 - k if reverse else k
        reached = at > index if reverse else at < index
        new = totals[at].astype(F32) * before + values[at].astype(F32)
        return jnp.where(reached, new, before)

    return lax.fori_loop(0, peers, turn, jnp.zeros(value.shape, F32))


def unpack_weights(pk, w0_ref, selt_ref, gain_ref):
    low_half = lax.broadcasted_iota(jnp.int32, (PACK0, 128), 1) < 64

    def pair(j, _):
        at = (j // 8, j // 4 % 2, j % 4)
        a = pk[at + (0, pl.ds(0, PACK0))].astype(F32)
        b = pk[at + (1, pl.ds(0, PACK0))].astype(F32)
        c = lanes(j)
        w0_ref[:, c] = jnp.where(low_half, a, pltpu.roll(b, 64, 1))
        selt_ref[:, c] = jnp.where(low_half, pltpu.roll(a, 64, 1), b).astype(BF16)
        return 0

    lax.fori_loop(0, 16, pair, 0)

    def gains(j, _):
        total = jnp.zeros((16, 128), F32)
        for i in range(4):
            v = pk[(j // 4, j // 2 % 2, j % 2 * 2 + i // 2, i % 2, pl.ds(PACK0, 16))]
            total = total + v.astype(F32)
        gain_ref[:, lanes(j)] = total[0:8, :]
        return 0

    lax.fori_loop(0, 8, gains, 0)


def normalise(tok, gain, normed):
    rows = tok.shape[0]

    def norm(i, _):
        r = pl.ds(pl.multiple_of(i * 16, 16), 16)
        u = tok[r, :]
        scale = lax.rsqrt(jnp.mean(u * u, axis=-1, keepdims=True) + EPS)
        normed[r, :] = (u * scale * gain[0:1, :]).astype(BF16)
        return 0

    lax.fori_loop(0, rows // 16, norm, 0, unroll=2)


def conv_tiles(first, count, xin, halo, live, w0, filt, xs, xt, xp):
    rows, di = xin.shape
    tiles = di // 128

    def conv(k, _):
        c = lanes(k)
        xp[0:16, :] = halo[:, c].astype(F32) * live
        xp[16 : 16 + rows, :] = xin[:, c].astype(F32)
        for q in range(2):
            r0 = q * (rows // 2)
            f = w0[4:5, c]
            for tap in range(KW):
                lo = 16 - (KW - 1) + tap + r0
                f = f + w0[tap : tap + 1, c] * xp[lo : lo + rows // 2, :]
            s = (f * sigmoid(f)).astype(BF16)
            filt[r0 : r0 + rows // 2, c] = f
            xs[r0 : r0 + rows // 2, c] = s
            xt[pl.ds(r0 * tiles + k, rows // 2, stride=tiles), :] = s.astype(F32)
        return 0

    lax.fori_loop(first, first + count, conv, 0)


def step_sizes(first, count, proj, w0, draw, dt):
    rows, di = draw.shape
    tiles = di // 128
    low = proj[:, 0:DTR].astype(BF16)

    def delta(k, _):
        c = lanes(k)
        raw = dot(low, w0[DELTA0 : DELTA0 + DTR, c].astype(BF16)) + w0[5:6, c]
        draw[:, c] = raw
        dt[pl.ds(k, rows, stride=tiles), :] = jnp.maximum(raw, 0.0) + jnp.log1p(jnp.exp(-jnp.abs(raw)))
        return 0

    lax.fori_loop(first, first + count, delta, 0, unroll=2)


def spread_rows(part, parts, proj, first, ref):
    row_ids = lax.broadcasted_iota(jnp.int32, (128, 128), 0) % DS
    lane_ids = lax.broadcasted_iota(jnp.int32, (128, 128), 1)
    ones = jnp.ones((128, 128), BF16)

    def spread(i, _):
        p = proj[pl.ds(pl.multiple_of(i * 8, 8), 8), :]
        tall = jnp.broadcast_to(p[:, None, :], (8, DS, 128)).reshape(128, 128)
        o = pl.ds(pl.multiple_of(i * 128, 128), 128)
        v = jnp.where(lane_ids == row_ids + first, tall, 0.0)
        hi = v.astype(BF16)
        v = v - hi.astype(F32)
        mid = v.astype(BF16)
        lo = (v - mid.astype(F32)).astype(BF16)
        ref[o, :] = (dot(hi, ones) + dot(mid, ones)) + dot(lo, ones)
        return 0

    count = proj.shape[0] // 8 // parts
    lax.fori_loop(part * count, (part + 1) * count, spread, 0, unroll=4)


def light_forward_part(h, part, parts, dt, xt, bb, a2, total, end, run):
    rows = dt.shape[0] // 16
    size = rows // parts
    hs = pl.ds(h * 8, 8)
    a = [a2[n, hs, :] for n in range(DS)]

    def step(i, carry):
        state, past = carry
        t = part * size + i
        d = tile_at(dt, t, h)
        dx = d * tile_at(xt, t, h)
        new = tuple(jnp.exp2(a[n] * d) * state[n] + dx * row_of(bb, t * DS + n) for n in range(DS))
        return (new, past + d)

    zero = jnp.zeros((8, 128), F32)
    start = ((zero,) * DS, zero) if part == 0 else (tuple(end[n, hs, :] for n in range(DS)), run[hs, :])
    state, past = lax.fori_loop(0, size, step, start, unroll=4)
    run[hs, :] = past
    for n in range(DS):
        end[n, hs, :] = state[n]
        if part == parts - 1:
            total[n, hs, :] = jnp.exp2(a[n] * past)


def light_backward_half(h, dt, gt, cb, a2, adj):
    rows = dt.shape[0] // 16
    hs = pl.ds(h * 8, 8)
    a = [a2[n, hs, :] for n in range(DS)]

    def step(i, carry):
        t = rows - 1 - i
        d = tile_at(dt, t, h)
        g = tile_at(gt, t, h)
        return tuple(jnp.exp2(a[n] * d) * (carry[n] + g * row_of(cb, t * DS + n)) for n in range(DS))

    out = lax.fori_loop(0, rows, step, (jnp.zeros((8, 128), F32),) * DS, unroll=4)
    for n in range(DS):
        adj[n, hs, :] = out[n]


def forward_part(h, q, si, dt, xt, bb, cb, a2, starts, yt):
    size = dt.shape[0] // 16 // starts.shape[0]
    hs = pl.ds(h * 8, 8)
    a = [a2[n, hs, :] for n in range(DS)]
    state = tuple(si[n, hs, :] for n in range(DS))
    for n in range(DS):
        starts[q, n, hs, :] = state[n]

    def step(i, carry):
        t = q * size + i
        d = tile_at(dt, t, h)
        dx = d * tile_at(xt, t, h)
        new, parts = [], []
        for n in range(DS):
            s = jnp.exp2(a[n] * d) * carry[n] + dx * row_of(bb, t * DS + n)
            parts.append(s * row_of(cb, t * DS + n))
            new.append(s)
        while len(parts) > 1:
            parts = [parts[i] + parts[i + 1] for i in range(0, len(parts), 2)]
        yt[pl.ds(pl.multiple_of(t * 16 + h * 8, 8), 8), :] = parts[0]
        return tuple(new)

    state = lax.fori_loop(0, size, step, state, unroll=4)
    for n in range(DS):
        si[n, hs, :] = state[n]


def carry_send(refs, mine, got, send, recv):
    peers = mine.shape[0]
    pair = DS // peers
    b, s = lax.axis_index("batch"), lax.axis_index("seq")
    for j in range(peers):
        for i in range(pair):
            for m, ref in enumerate(refs):
                mine[j, m, i] = ref[j * pair + i].astype(BF16)
    copies = []
    for k in range(1, peers):
        to = lax.rem(s + k, peers)
        copy = remote(mine.at[to], got.at[s], send.at[k - 1], recv.at[k - 1], (b, to))
        copy.start()
        copies.append(copy)
    got[s] = mine[s]
    return copies


def carry_back(back, final, send, recv):
    peers = back.shape[0]
    b, s = lax.axis_index("batch"), lax.axis_index("seq")
    copies = []
    for k in range(1, peers):
        to = lax.rem(s + k, peers)
        copy = remote(back.at[to], final.at[s], send.at[k - 1], recv.at[k - 1], (b, to))
        copy.start()
        copies.append(copy)
    final[s] = back[s]
    return copies


def arrived(copies):
    for copy in copies:
        copy.wait_recv()


WX, WZ, WO = 4, 4, 4


def pack_small(refs, out, me):
    gain, conv, conv_bias, select, delta, delta_bias, a_log, skip = (ref[...].astype(F32) for ref in refs)
    own = conv.shape[1]
    none = jnp.zeros((1, own), F32)
    left = jnp.concatenate([conv, conv_bias, delta_bias, skip, none, a_log, delta, jnp.zeros((PACK0 - DELTA0 - DTR, own), F32)], axis=0)
    right = jnp.concatenate([select, jnp.zeros((own, 128 - PACK0), F32)], axis=1).T[0:PACK0]
    out[0:PACK0, :] = jnp.concatenate([left, right], axis=1).astype(BF16)
    part = gain.shape[1]
    tile = jnp.concatenate([gain] * (128 // part), axis=1)
    mine = lax.broadcasted_iota(jnp.int32, tile.shape, 1) // part == me % (128 // part)
    out[PACK0:PACK, :] = jnp.broadcast_to(jnp.where(mine, tile, 0.0), (PACK - PACK0, 128)).astype(BF16)


def front_body(tok_in, cot_in, inw_in, outw_in, *refs):
    small, refs = refs[:8], refs[8:]
    names = FRONT_OUTS
    o = dict(zip(names, refs[: len(names)]))
    v = dict(zip(FRONT_SCRATCH, refs[len(names) :]))
    stash_sem, load_sem, job_send, job_recv, job_local, ring_send, ring_recv, halo_send, halo_recv = (
        v[n] for n in ("stash", "load", "jsend", "jrecv", "jlocal", "rsend", "rrecv", "hsend", "hrecv")
    )
    y, c, z, x = place()
    b, s = lax.axis_index("batch"), lax.axis_index("seq")
    peers = v["mine"].shape[0]
    stash = []

    def put(*keys):
        for key in keys:
            copy = pltpu.make_async_copy(v[key], o[key], stash_sem.at[len(stash)])
            copy.start()
            stash.append(copy)

    load_tok = pltpu.make_async_copy(tok_in, v["tok"], load_sem.at[0])
    load_cot = pltpu.make_async_copy(cot_in, v["cot"], load_sem.at[1])
    load_tok.start()
    load_cot.start()
    pack_small(small, v["packed"], b * peers + s)
    greet([(b, lax.rem(s + k, peers)) for k in range(1, peers)] + [device(1 - y, c, z, x), device(y, 1 - c, z, x)])

    jobs = []

    def job(src, out):
        i = len(jobs)
        jobs.append(Gather(src, out, job_send.at[i], job_recv.at[i], job_local.at[i]))

    width = inw_in.shape[1] // 2 // WX
    wide_z = inw_in.shape[1] // 2 // WZ
    wide_o = outw_in.shape[1] // WO
    job(v["packed"], v["pk"])
    for i in range(WX):
        job(inw_in.at[:, pl.ds(i * width, width)], v["inx"].at[i])
    for i in range(WZ):
        job(inw_in.at[:, pl.ds(inw_in.shape[1] // 2 + i * wide_z, wide_z)], v["inz"].at[i])
    for i in range(WO):
        job(outw_in.at[:, pl.ds(i * wide_o, wide_o)], v["wo"].at[i])
    events = sorted(
        (i + STEPS[k] if i <= WX else i + DELAY + STEPS_LATE[k], -k, i) for i in range(len(jobs)) for k in range(STAGES)
    )
    clock = [0.0]

    def advance():
        _, k, i = events.pop(0)
        jobs[i].stage(-k)

    def landed(i):
        while any(e[2] == i for e in events):
            advance()
            clock[0] = 0.0

    def spend(time):
        clock[0] += time
        while clock[0] >= PACE:
            clock[0] -= PACE
            if events:
                advance()

    di = v["xin"].shape[1]
    rows = v["xin"].shape[0]
    tiles = di // 128
    per = tiles // WX
    live = jnp.where(s > 0, 1.0, 0.0)
    halos = []

    def project_x(i):
        cols = pl.ds(i * width, width)
        v["xin"][:, cols] = dot(v["normed"][...], v["inx"][i].reshape(-1, width)).astype(BF16)
        copy = remote(
            v["xin"].at[pl.ds(rows - 16, 16), cols], v["halo"].at[:, cols],
            halo_send.at[i], halo_recv.at[i], (b, lax.rem(s + 1, peers)),
        )
        copy.start()
        halos.append(copy)

    def conv(i):
        halos[i].wait_recv()
        conv_tiles(i * per, per, v["xin"], v["halo"], live, v["w0"], v["filt"], v["xs"], v["xt"], v["xp"])

    landed(0)
    unpack_weights(v["pk"], v["w0"], v["selt"], v["gain"])
    load_tok.wait()
    normalise(v["tok"], v["gain"], v["normed"])
    put("w0", "selt", "gain", "normed")
    for k in range(16):
        v["a2"][:, k, :] = -jnp.exp(v["w0"][ALOG0 : ALOG0 + DS, k * 128 : (k + 1) * 128]) * LOG2E
    put("a2")
    for i in range(WX):
        landed(1 + i)
        project_x(i)
        if i > 0:
            conv(i - 1)
    put("inx")
    load_cot.wait()
    v["low"][...] = v["cot"][...].astype(BF16)
    put("low")
    conv(WX - 1)
    put("xin", "halo", "filt", "xs", "xt")
    v["proj"][:, 0:PACK0] = dot_nt(v["xs"][...], v["selt"][...])
    spend(1.5)
    for q in range(4):
        step_sizes(q * (tiles // 4), tiles // 4, v["proj"], v["w0"], v["draw"], v["dt"])
        spend(1.0)
    put("draw", "dt")
    for q in range(4):
        spread_rows(q, 4, v["proj"], DTR, v["bb"])
        spend(0.85)
    put("bb")
    for h in range(2):
        for q in range(4):
            light_forward_part(h, q, 4, v["dt"], v["xt"], v["bb"], v["a2"], v["total"], v["end"], v["run"])
            spend(0.8)

    sent = carry_send((v["total"], v["end"]), v["mine"], v["got"], ring_send.at[0], ring_recv.at[0])

    def project_z(i):
        landed(1 + WX + i)
        v["gate"][:, i * wide_z : (i + 1) * wide_z] = dot(v["normed"][...], v["inz"][i].reshape(-1, wide_z))

    for q in range(4):
        spread_rows(q, 4, v["proj"], DTR + DS, v["cb"])
        spend(0.85)
    put("cb")
    arrived(sent)
    state = jnp.zeros(v["back"].shape[1:], F32)
    for p in range(peers):
        v["back"][p] = state.astype(BF16)
        state = v["got"][p, 0].astype(F32) * state + v["got"][p, 1].astype(F32)
    more = carry_back(v["back"], v["final"], ring_send.at[1], ring_recv.at[1])
    sent += more
    for i in range(WZ - 1):
        project_z(i)
    arrived(more)
    pair = DS // peers
    for j in range(peers):
        for i in range(pair):
            v["si"][j * pair + i] = v["final"][j, i].astype(F32)
    clock[0] = 0.0
    for q in range(v["starts"].shape[0]):
        for h in range(2):
            forward_part(h, q, v["si"], v["dt"], v["xt"], v["bb"], v["cb"], v["a2"], v["starts"], v["yt"])
            spend(0.6)
    put("starts")
    project_z(3)
    put("inz")
    landed(len(jobs) - 1)

    block = 512
    per_b = block // (di // 32)

    def gated_grad(j, _):
        out = jnp.zeros((rows, block), F32)
        for i in range(WO):
            w = v["wo"][i, j // 2, j % 2].reshape(block, wide_o)
            out = out + dot_nt(v["low"][:, i * wide_o : (i + 1) * wide_o], w)
        v["gzp"][:, lanes(j, block)] = out
        return 0

    lax.fori_loop(0, di // block, gated_grad, 0)

    def point(k, _):
        cols = lanes(k)
        for q in range(4):
            r = slice(q * (rows // 4), (q + 1) * (rows // 4))
            zz = v["gate"][r, cols]
            gg = v["gzp"][r, cols]
            sg = sigmoid(zz)
            gate = zz * sg
            v["gate"][r, cols] = gate
            v["gzp"][r, cols] = gg * sg * (1.0 + zz * (1.0 - sg))
            v["gt"][pl.ds(q * (rows // 4) * tiles + k, rows // 4, stride=tiles), :] = gg * gate
        return 0

    lax.fori_loop(0, tiles, point, 0)
    put("gt")
    for h in range(2):
        light_backward_half(h, v["dt"], v["gt"], v["cb"], v["a2"], v["adj"])
    again = carry_send((v["adj"],), v["mine2"], v["got2"], ring_send.at[2], ring_recv.at[2])
    sent += again

    def emit(k, _):
        cols = lanes(k)
        total = jnp.zeros((8, 128), F32)
        for q in range(4):
            r = slice(q * (rows // 4), (q + 1) * (rows // 4))
            here = pl.ds(q * (rows // 4) * tiles + k, rows // 4, stride=tiles)
            xx = v["xt"][here, :]
            yy = v["yt"][here, :] + v["w0"][6:7, cols] * xx
            v["gated"][r, cols] = (yy * v["gate"][r, cols]).astype(BF16)
            v["gz"][r, cols] = (v["gzp"][r, cols] * yy).astype(BF16)
            total = total + jnp.sum((v["gt"][here, :] * xx).reshape(-1, 8, 128), axis=0)
        v["skipg"][:, cols] = jnp.broadcast_to(jnp.sum(total, axis=0, keepdims=True), (8, 128))
        return 0

    lax.fori_loop(0, tiles, emit, 0)
    put("gated", "gz", "skipg")
    for i in range(WO):
        cols = pl.ds(i * wide_o, wide_o)
        w = v["wo"][i].reshape(di, wide_o)
        v["tok"][:, cols] = v["tok"][:, cols] + dot(v["gated"][...], w)
    copy = pltpu.make_async_copy(v["tok"], o["block"], load_sem.at[0])
    copy.start()
    arrived(again)
    state = jnp.zeros(v["back2"].shape[1:], F32)
    for p in reversed(range(peers)):
        v["back2"][p] = state.astype(BF16)
        state = v["got"][p, 0].astype(F32) * state + v["got2"][p, 0].astype(F32)
    put("back2")
    copy.wait()
    for it in jobs:
        it.drain()
    for it in sent + halos:
        it.wait_send()
    for it in stash:
        it.wait()


FRONT_OUTS = (
    "block", "w0", "selt", "gain", "normed", "a2", "inx", "xin", "halo", "filt", "xs", "xt", "low", "draw", "dt",
    "bb", "cb", "inz", "starts", "gt", "gated", "gz", "skipg", "back2",
)
FRONT_SCRATCH = (
    "w0", "selt", "gain", "normed", "a2", "inx", "xin", "halo", "filt", "xs", "xt", "low", "draw", "dt",
    "bb", "cb", "inz", "starts", "gt", "gated", "gz", "skipg", "back2",
    "tok", "cot", "pk", "wo", "proj", "xp", "gate", "gzp", "yt", "total", "end", "adj", "si",
    "mine", "got", "back", "final", "mine2", "got2", "run", "packed",
    "stash", "load", "jsend", "jrecv", "jlocal", "rsend", "rrecv", "hsend", "hrecv",
)


def front(tok, cot, in_weight, out_weight, small, peers, chunks):
    rows, width = tok.shape
    di = in_weight.shape[1] // 2
    tiles = di // 128
    lead = (2, 2, 4, 2)
    flat, wide, carry = ((rows * tiles, 128), F32), ((rows, di), F32), ((DS, tiles, 128), F32)
    spread, half = ((rows * DS, 128), F32), ((rows, di), BF16)
    pair = (DS // peers, tiles, 128)
    shapes = {
        "block": ((rows, width), F32), "w0": ((PACK0, di), F32), "selt": ((PACK0, di), BF16), "gain": ((8, width), F32),
        "normed": ((rows, width), BF16), "a2": carry, "inx": ((WX,) + lead + (in_weight.shape[0], di // WX), BF16),
        "xin": half, "halo": ((16, di), BF16), "filt": wide, "xs": half, "xt": flat, "low": ((rows, width), BF16),
        "draw": wide, "dt": flat, "bb": spread, "cb": spread,
        "inz": ((WZ,) + lead + (in_weight.shape[0], di // WZ), BF16), "starts": ((chunks, DS, tiles, 128), F32),
        "gt": flat, "gated": half, "gz": half, "skipg": ((8, di), F32),
        "tok": ((rows, width), F32), "cot": ((rows, width), F32), "pk": (lead + (PACK, 128), BF16),
        "wo": ((WO,) + lead + (out_weight.shape[0], width // WO), BF16), "proj": ((rows, 128), F32),
        "xp": ((rows + 16, 128), F32), "gate": wide, "gzp": wide, "yt": flat, "total": carry, "end": carry, "adj": carry,
        "si": carry, "mine": ((peers, 2) + pair, BF16), "got": ((peers, 2) + pair, BF16), "back": ((peers,) + pair, BF16),
        "final": ((peers,) + pair, BF16), "mine2": ((peers, 1) + pair, BF16), "got2": ((peers, 1) + pair, BF16),
        "back2": ((peers,) + pair, BF16), "packed": ((PACK, 128), BF16), "run": ((tiles, 128), F32),
    }
    n_jobs = 1 + WX + WZ + WO
    dma = pltpu.SemaphoreType.DMA
    sems = {
        "stash": dma((len(FRONT_OUTS) - 1,)), "load": dma((2,)), "jsend": dma((n_jobs, Gather.COPIES)),
        "jrecv": dma((n_jobs, Gather.COPIES)), "jlocal": dma((n_jobs,)), "rsend": dma((3, peers - 1)),
        "rrecv": dma((3, peers - 1)), "hsend": dma((WX,)), "hrecv": dma((WX,)),
    }
    outs = pl.pallas_call(
        front_body,
        out_shape=tuple(sds(*shapes[n]) for n in FRONT_OUTS),
        in_specs=[ANY] * 4 + [VM] * len(small),
        out_specs=(ANY,) * len(FRONT_OUTS),
        scratch_shapes=[sems[n] if n in sems else pltpu.VMEM(*shapes[n]) for n in FRONT_SCRATCH],
        compiler_params=pltpu.CompilerParams(collective_id=0, has_side_effects=True, vmem_limit_bytes=GRANT),
    )(tok, cot, in_weight, out_weight, *small)
    return dict(zip(FRONT_OUTS, outs))


class Share:
    COPIES = 10

    def __init__(self, own, other, r1, r2, r3, r4, out, send, recv):
        self.own, self.other, self.r1, self.r2, self.r3, self.r4, self.out = own, other, r1, r2, r3, r4, out
        self.send, self.recv = send, recv
        self.at = place()
        self.copies = []

    def go(self, source, target, to):
        i = len(self.copies)
        copy = remote(source, target, self.send.at[i], self.recv.at[i], to)
        copy.start()
        self.copies.append(copy)
        return copy

    def stage(self, k):
        y, c, z, x = self.at
        own = self.own
        half = own.shape[3] // 2
        top, bottom = pl.ds(0, half), pl.ds(half, half)
        to_y, to_x, to_c = device(1 - y, c, z, x), device(y, c, z, 1 - x), device(y, 1 - c, z, x)
        if k > 0:
            arrived(self.wait)
        if k == 0:
            self.wait = [self.go(self.other.at[i], self.r1.at[i], to_c) for i in (0, 1)]
        elif k == 1:

            def piece(i, _):
                at = (i // 8, i // 2 % 4, i % 2)
                own[at] = own[at] + self.r1[at]
                return 0

            lax.fori_loop(0, 16, piece, 0)
            self.wait = [self.go(own.at[1 - y, :, :, top], self.r2.at[pl.ds(0, 4), :], to_y)]
            for i in (0, 1):
                self.wait.append(self.go(own.at[i, :, 1 - x, bottom], self.r2.at[pl.ds(4, 4), i], to_x))
        elif k == 2:

            def piece(i, _):
                b, d = i // 2, i % 2
                own[y, b, d, top] = own[y, b, d, top] + self.r2[b, d]
                own[d, b, x, bottom] = own[d, b, x, bottom] + self.r2[4 + b, d]
                return 0

            lax.fori_loop(0, 8, piece, 0)
            self.wait = [
                self.go(own.at[y, :, 1 - x, top], self.r3.at[0], to_x),
                self.go(own.at[1 - y, :, x, bottom], self.r3.at[1], to_y),
            ]
        elif k == 3:

            def piece(b, _):
                own[y, b, x, top] = own[y, b, x, top] + self.r3[0, b]
                own[y, b, x, bottom] = own[y, b, x, bottom] + self.r3[1, b]
                return 0

            lax.fori_loop(0, 4, piece, 0)
            self.wait = [
                self.go(own.at[y, z ^ i, x], self.r4.at[i - 1], device(y, c, z ^ i, x)) for i in (1, 2, 3)
            ]
        else:
            total = own[y, z, x].astype(F32)
            for i in range(3):
                total = total + self.r4[i].astype(F32)
            self.out[...] = total

    def drain(self):
        for copy in self.copies:
            copy.wait_send()
        self.copies = []


def adjoint_part(chunk, h, dt, xt, bb, cb, gt, a2, starts, later, keep, decays, pb, pc, rb, rc, ga, size):
    hs = pl.ds(h * 8, 8)
    base = chunk * size
    first = tuple(starts[chunk, n, hs, :] for n in range(DS))
    for n in range(DS):
        keep[n * 8 : n * 8 + 8, :] = first[n]

    def again(i, carry):
        t = base + i
        d = tile_at(dt, t, h)
        dx = d * tile_at(xt, t, h)
        new = []
        for n in range(DS):
            w = jnp.exp2(a2[n, hs, :] * d)
            s = w * carry[n] + dx * row_of(bb, t * DS + n)
            o = pl.multiple_of(i * 128 + n * 8, 8)
            decays[pl.ds(o, 8), :] = w
            keep[pl.ds(pl.multiple_of(o + 128, 8), 8), :] = s
            new.append(s)
        return tuple(new)

    lax.fori_loop(0, size, again, first, unroll=4)

    def back(j, carry):
        i = size - 1 - j
        t = base + i
        d = tile_at(dt, t, h)
        x = tile_at(xt, t, h)
        gy = tile_at(gt, t, h)
        dx = d * x
        slot = (j % 2) * 128
        new = []
        weighted, through_a = [], []
        for n in range(DS):
            o = pl.multiple_of(i * 128 + n * 8, 8)
            w = decays[pl.ds(o, 8), :]
            before = keep[pl.ds(o, 8), :]
            now = keep[pl.ds(pl.multiple_of(o + 128, 8), 8), :]
            g = carry[n] + gy * row_of(cb, t * DS + n)
            at = pl.ds(pl.multiple_of(slot + n * 8, 8), 8)
            pc[at, :] = now * gy
            pb[at, :] = g * dx
            weighted.append(g * row_of(bb, t * DS + n))
            g = g * w
            through = g * before
            through_a.append(through * a2[n, hs, :])
            ga[n, hs, :] += through * d
            new.append(g)
        while len(weighted) > 1:
            weighted = [weighted[i] + weighted[i + 1] for i in range(0, len(weighted), 2)]
            through_a = [through_a[i] + through_a[i + 1] for i in range(0, len(through_a), 2)]
        o = pl.ds(pl.multiple_of(t * 16 + h * 8, 8), 8)
        dt[o, :] = through_a[0] * LN2 + weighted[0] * x
        xt[o, :] = weighted[0] * d
        for src, dst in ((pb, rb), (pc, rc)):
            for m in range(2):
                parts = [src[pl.ds(slot + m * 64 + s, 8, stride=8), :] for s in range(8)]
                while len(parts) > 1:
                    parts = [parts[i] + parts[i + 1] for i in range(0, len(parts), 2)]
                q = pl.ds(pl.multiple_of(i * 16 + m * 8, 8), 8)
                if h == 0:
                    dst[q, :] = parts[0]
                else:
                    dst[q, :] += parts[0]
        return tuple(new)

    out = lax.fori_loop(0, size, back, tuple(later[n, hs, :] for n in range(DS)), unroll=2)
    for n in range(DS):
        later[n, hs, :] = out[n]


def collect_rows(chunk, size, rb, rc, gb, gc):
    ones = jnp.ones((8, 128), BF16)
    per = size * DS // 128
    for src, dst in ((rb, gb), (rc, gc)):
        v = src[...]
        hi = v.astype(BF16)
        lo = (v - hi.astype(F32)).astype(BF16)
        s = dot_nt(ones, hi) + dot_nt(ones, lo)
        for i in range(per):
            dst[chunk * per + i : chunk * per + i + 1, :] = s[0:1, i * 128 : (i + 1) * 128]


BACK_IN = (
    "back2", "gated", "low", "normed", "gz", "dt", "xt", "bb", "cb", "gt", "a2", "starts", "draw", "xs", "w0", "selt",
    "filt", "xin", "halo", "inx", "inz", "gain", "skipg", "tok", "cot",
)
BACK_LOAD = tuple(n for n in BACK_IN if n not in ("inx", "inz"))
BACK_OUT = ("tgrad", "gin", "gout", "gpack")
BACK_SCRATCH = BACK_LOAD[:-1] + (
    "wbuf", "keep", "decays", "pb", "pc", "rb", "rc", "ga", "gb", "gc", "proj", "xp", "gp", "rawlow", "gproj", "dw", "w0g",
    "selg", "edge", "gx", "gn", "gaing",
    "own", "other", "r1", "r2", "r3", "r4", "pown", "pother", "p1", "p2", "p3", "p4",
    "so", "final2",
    "load", "wsem", "send", "recv", "esend", "erecv", "rsend", "rrecv",
)
BLOCKS = 4


def back_body(*refs):
    hbm = dict(zip(BACK_IN, refs))
    refs = refs[len(BACK_IN) :]
    o = dict(zip(BACK_OUT, refs))
    v = dict(zip(BACK_SCRATCH, refs[len(BACK_OUT) :]))
    loads = {}
    for i, name in enumerate(BACK_LOAD):
        loads[name] = pltpu.make_async_copy(hbm[name], o["tgrad"] if name == "cot" else v[name], v["load"].at[i])
        loads[name].start()

    def need(*names):
        for name in names:
            loads[name].wait()

    y, c, z, x = place()
    b, s = lax.axis_index("batch"), lax.axis_index("seq")
    peers = lax.axis_size("seq")
    greet([(b, lax.rem(s + k, peers)) for k in range(1, peers)] + [device(1 - y, c, z, x), device(y, 1 - c, z, x)])
    need("back2")
    sent = carry_back(v["back2"], v["final2"], v["rsend"].at[0], v["rrecv"].at[0])

    rows, di = v["gz"].shape
    width = v["normed"].shape[1]
    tiles = di // 128
    cols = di // BLOCKS
    half = width // 2
    owned = v["own"].shape[4]
    jobs = []

    def job(out):
        i = len(jobs)
        at = i % (2 * BLOCKS)
        jobs.append(
            Share(
                v["own"].at[at], v["other"].at[at], v["r1"].at[i], v["r2"].at[i], v["r3"].at[i], v["r4"].at[i],
                out, v["send"].at[i], v["recv"].at[i],
            )
        )

    for i in range(4):
        job(o["gout"].at[i // 2 * owned : (i // 2 + 1) * owned, i % 2 * half : (i % 2 + 1) * half])
    for i in range(BLOCKS):
        job(o["gin"].at[:, di + i * cols : di + (i + 1) * cols])
    for i in range(BLOCKS):
        job(o["gin"].at[:, i * cols : (i + 1) * cols])
    last = len(jobs)
    jobs.append(
        Share(
            v["pown"], v["pother"], v["p1"], v["p2"], v["p3"], v["p4"], o["gpack"], v["send"].at[last], v["recv"].at[last]
        )
    )
    events, now, clock = [], [0], [0.0]
    first = [0]

    def enter(*blocks, steps=STEPS_BACK):
        for i in blocks:
            first[0] = max(first[0] + 1, now[0])
            events.extend((first[0] + steps[k], -k, i) for k in range(STAGES))
        events.sort()

    def advance():
        now[0], k, i = events.pop(0)
        jobs[i].stage(-k)

    def spend(time):
        clock[0] += time
        while clock[0] >= PACE_BACK:
            clock[0] -= PACE_BACK
            if events:
                advance()

    def finish(i):
        while any(e[2] == i for e in events):
            advance()
        jobs[i].drain()

    need("gated", "low")

    def out_blocks(core, dst):
        def block(i, _):
            first = pl.multiple_of(((i // 2) * 2 + core) * (di // 4) + (i % 2) * 256, 256)
            g = v["gated"][:, pl.ds(first, 256)]
            for q in range(2):
                r = dot_tn(g, v["low"][:, q * half : (q + 1) * half]).astype(BF16).reshape(2, 2, 2, owned, half)
                for p in range(2):
                    dst[p * 2 + q, i // 2, pl.ds((i % 2) * 2, 2)] = r[:, :, p]
            return 0

        lax.fori_loop(0, 4, block, 0)

    def in_blocks(core, dst, first, right):
        def block(i, _):
            n = v["normed"][:, pl.ds(pl.multiple_of((i * 2 + core) * (width // 4), 256), width // 4)]
            for q, g in enumerate(right):
                dst[first + q, i] = dot_tn(n, g()).astype(BF16).reshape(4, 2, owned, cols)
            return 0

        lax.fori_loop(0, 2, block, 0)

    out_blocks(1 - c, v["other"])
    enter(0, 1, 2, 3)
    advance()
    advance()
    out_blocks(c, v["own"])
    need("normed", "gz")
    z_right = [lambda q=q: v["gz"][:, q * cols : (q + 1) * cols] for q in range(BLOCKS)]
    in_blocks(1 - c, v["other"], BLOCKS, z_right)
    enter(4, 5, 6, 7)
    in_blocks(c, v["own"], BLOCKS, z_right)
    spend(3.0)
    arrived(sent)
    pair = DS // peers
    for j in range(peers):
        for i in range(pair):
            v["so"][j * pair + i] = v["final2"][j, i].astype(F32)

    need("dt", "xt", "bb", "cb", "gt", "a2", "starts")
    v["ga"][...] = jnp.zeros_like(v["ga"])
    chunks = v["starts"].shape[0]
    size = rows // chunks
    for chunk in reversed(range(chunks)):
        for h in range(2):
            adjoint_part(
                chunk, h, v["dt"], v["xt"], v["bb"], v["cb"], v["gt"], v["a2"], v["starts"], v["so"], v["keep"],
                v["decays"], v["pb"], v["pc"], v["rb"], v["rc"], v["ga"], size,
            )
            spend(2.0)
        collect_rows(chunk, size, v["rb"], v["rc"], v["gb"], v["gc"])
        spend(0.75)

    need("draw", "xs", "w0", "selt")
    v["proj"][:, 0:PACK0] = dot_nt(v["xs"][...], v["selt"][...])
    low = v["proj"][:, 0:DTR].astype(BF16)
    v["dw"][...] = v["w0"][DELTA0 : DELTA0 + DTR, :].astype(BF16)
    w0g = v["w0g"]

    def raw(k, _):
        at = lanes(k)
        g = v["dt"][pl.ds(k, rows, stride=tiles), :] * sigmoid(v["draw"][:, at])
        w0g[5:6, at] = jnp.sum(g, axis=0, keepdims=True)
        gl = g.astype(BF16)
        v["rawlow"][:, at] = gl
        w0g[DELTA0 : DELTA0 + DTR, at] = dot_tn(low, gl)
        return 0

    spend(0.5)
    for q in range(BLOCKS):
        lax.fori_loop(q * (tiles // BLOCKS), (q + 1) * (tiles // BLOCKS), raw, 0, unroll=2)
        spend(0.85)
    v["gproj"][:, 0:DTR] = dot_nt(v["rawlow"][...], v["dw"][...]).astype(BF16)
    per = 128 // DS
    for first_lane, src in ((DTR, v["gb"]), (DTR + DS, v["gc"])):
        for i in range(per):
            v["proj"][pl.ds(i, rows // per, stride=per), 0:DS] = src[:, i * DS : (i + 1) * DS]
        v["gproj"][:, first_lane : first_lane + DS] = v["proj"][:, 0:DS].astype(BF16)
    need("filt", "xin", "halo")
    not_first = jnp.where(s > 0, 1.0, 0.0)
    not_last = jnp.where(s < peers - 1, 1.0, 0.0)

    def point(k, _):
        at = lanes(k)
        gp = v["gproj"][...]
        v["selg"][:, at] = dot_tn(gp, v["xs"][:, at])
        into = dot(gp, v["selt"][:, at])
        here = pl.ds(k, rows, stride=tiles)
        g = v["gt"][here, :] * v["w0"][6:7, at] + v["xt"][here, :] + into
        f = v["filt"][:, at]
        sg = sigmoid(f)
        gf = g * (sg * (1.0 + f * (1.0 - sg)))
        v["filt"][:, at] = gf
        w0g[4:5, at] = jnp.sum(gf, axis=0, keepdims=True)
        v["xp"][0:16, :] = v["halo"][:, at].astype(F32) * not_first
        v["xp"][16 : 16 + rows, :] = v["xin"][:, at].astype(F32)
        for tap in range(KW):
            lo = 16 - (KW - 1) + tap
            w0g[tap : tap + 1, at] = jnp.sum(gf * v["xp"][lo : lo + rows, :], axis=0, keepdims=True)
        return 0

    edges = []

    def points(q):
        lax.fori_loop(q * (tiles // BLOCKS), (q + 1) * (tiles // BLOCKS), point, 0, unroll=2)
        at = pl.ds(q * cols, cols)
        copy = remote(
            v["filt"].at[pl.ds(0, 8), at], v["edge"].at[:, at], v["esend"].at[q], v["erecv"].at[q],
            (b, lax.rem(s + peers - 1, peers)),
        )
        copy.start()
        edges.append(copy)

    weights = {}

    def fetch(i):
        source = hbm["inx"].at[i] if i < WX else hbm["inz"].at[i - WX]
        weights[i] = pltpu.make_async_copy(source, v["wbuf"].at[i % 2], v["wsem"].at[i])
        weights[i].start()

    fetch(0)
    fetch(1)

    def blocks(q):
        edges[q].wait_recv()

        def conv(k, _):
            at = lanes(k)
            v["gp"][0:rows, :] = v["filt"][:, at]
            v["gp"][rows : rows + 8, :] = v["edge"][:, at] * not_last
            total = jnp.zeros((rows, 128), F32)
            for tap in range(KW):
                lo = KW - 1 - tap
                total = total + v["w0"][tap : tap + 1, at] * v["gp"][lo : lo + rows, :]
            v["gx"][:, at] = total.astype(BF16)
            return 0

        lax.fori_loop(q * (tiles // BLOCKS), (q + 1) * (tiles // BLOCKS), conv, 0)
        right = [lambda: v["gx"][:, q * cols : (q + 1) * cols]]
        finish(q)
        in_blocks(1 - c, v["other"], q, right)
        jobs[2 * BLOCKS + q].stage(0)
        enter(2 * BLOCKS + q, steps=STEPS_LAST)
        events.remove((first[0], 0, 2 * BLOCKS + q))
        in_blocks(c, v["own"], q, right)
        while events and events[0][0] <= first[0]:
            advance()

    def into_rows(i):
        weights[i].wait()
        g = v["gx"] if i < WX else v["gz"]
        q = i % WX
        for d in range(2):
            w = v["wbuf"][i % 2].reshape(width, cols)[d * half : (d + 1) * half]
            part = dot_nt(g[:, q * cols : (q + 1) * cols], w)
            at = slice(d * half, (d + 1) * half)
            v["gn"][:, at] = part if i == 0 else v["gn"][:, at] + part
        if i + 2 < 2 * WX:
            fetch(i + 2)
        spend(0.5)

    points(0)
    points(1)
    for q in range(2, BLOCKS):
        points(q)
        blocks(q - 2)
    blocks(BLOCKS - 2)
    blocks(BLOCKS - 1)
    for i in range(2 * WX):
        into_rows(i)
    need("tok", "cot", "gain")

    def rows_of(i, total):
        r = pl.ds(pl.multiple_of(i * 8, 8), 8)
        u = v["tok"][r, :]
        g = v["gn"][r, :]
        scale = lax.rsqrt(jnp.mean(u * u, axis=-1, keepdims=True) + EPS)
        w = g * v["gain"][0:1, :]
        mean = jnp.mean(w * u, axis=-1, keepdims=True)
        o["tgrad"][r, :] = o["tgrad"][r, :] + scale * w - u * (scale * scale * scale * mean)
        return total + g * u * scale

    total = lax.fori_loop(0, rows // 8, rows_of, jnp.zeros((8, width), F32), unroll=4)
    v["gaing"][...] = jnp.broadcast_to(jnp.sum(total, axis=0, keepdims=True), (8, width))
    need("skipg")
    w0g[6:7, :] = v["skipg"][0:1, :]
    w0g[7:8, :] = jnp.zeros((1, di), F32)
    w0g[DELTA0 + DTR : PACK0, :] = jnp.zeros((PACK0 - DELTA0 - DTR, di), F32)
    for k in range(tiles):
        w0g[ALOG0 : ALOG0 + DS, k * 128 : (k + 1) * 128] = v["ga"][:, k, :] * v["a2"][:, k, :] * LN2
    low_half = lax.broadcasted_iota(jnp.int32, (PACK0, 128), 1) < 64

    def pack(core, dst):
        def pair(i, _):
            j = i // 4 * 8 + core * 4 + i % 4
            at = lanes(j)
            l, r = w0g[:, at], v["selg"][:, at]
            dst[i // 4, i % 4, 0, 0:PACK0, :] = jnp.where(low_half, l, pltpu.roll(r, 64, 1)).astype(BF16)
            dst[i // 4, i % 4, 1, 0:PACK0, :] = jnp.where(low_half, pltpu.roll(l, 64, 1), r).astype(BF16)
            g = jnp.broadcast_to(v["gaing"][0:1, lanes(j // 2)], (PACK - PACK0, 128)).astype(BF16)
            for d in range(2):
                dst[i // 4, i % 4, d, PACK0:PACK, :] = g
            return 0

        lax.fori_loop(0, 8, pair, 0)

    spend(3.0)
    pack(1 - c, v["pother"])
    jobs[last].stage(0)
    pack(c, v["pown"])
    first[0] = now[0] - 1
    enter(last, steps=STEPS_PACK)
    events.remove((first[0], 0, last))
    while events:
        advance()
    for it in jobs:
        it.drain()
    for it in edges + sent:
        it.wait_send()


def back(f, tok, cot):
    rows, di = f["gz"].shape
    width = tok.shape[1]
    tiles = di // 128
    cols = di // BLOCKS
    chunks = f["starts"].shape[0]
    size = rows // chunks
    lead = (2, 4, 2)
    owned = width // 32
    inputs = dict(f, tok=tok, cot=cot)
    shapes = {n: (inputs[n].shape, inputs[n].dtype) for n in BACK_IN}
    peers = f["back2"].shape[0]
    pair = (DS // peers, tiles, 128)
    shapes.update(
        so=((DS, tiles, 128), F32), final2=((peers,) + pair, BF16),
    )

    def sums(prefix, n, rows, cols, held):
        names = ("own", "other", "r1", "r2", "r3", "r4") if not prefix else ("pown", "pother", "p1", "p2", "p3", "p4")
        dims = (
            lead + (rows, cols), lead + (rows, cols), lead + (rows, cols), (8, 2, rows // 2, cols),
            (2, 4, rows // 2, cols), (3, rows, cols),
        )
        for i, (name, d) in enumerate(zip(names, dims)):
            k = (held if i < 2 else n,) if not prefix else ()
            shapes[name] = (k + d, BF16)

    sums("", 3 * BLOCKS, owned, cols, 2 * BLOCKS)
    sums("p", 1, PACK, 128, 1)
    tall = ((size * DS, 128), F32)
    shapes.update(
        wbuf=((2, 2, 2, 4, 2, owned, cols), BF16), keep=(((size + 1) * 128, 128), F32), decays=((size * 128, 128), F32),
        pb=((256, 128), F32), pc=((256, 128), F32), rb=tall, rc=tall, ga=((DS, tiles, 128), F32), gb=((rows * DS // 128, 128), F32),
        gc=((rows * DS // 128, 128), F32), proj=((rows, 128), F32), xp=((rows + 16, 128), F32), gp=((rows + 8, 128), F32),
        rawlow=((rows, di), BF16), gproj=((rows, PACK0), BF16), dw=((DTR, di), BF16), w0g=((PACK0, di), F32),
        selg=((PACK0, di), F32), edge=((8, di), F32), gx=((rows, di), BF16), gn=((rows, width), F32), gaing=((8, width), F32),
    )
    dma = pltpu.SemaphoreType.DMA
    n_jobs = 3 * BLOCKS + 1
    sems = {
        "load": dma((len(BACK_LOAD),)), "wsem": dma((2 * WX,)), "send": dma((n_jobs, Share.COPIES)),
        "recv": dma((n_jobs, Share.COPIES)), "esend": dma((BLOCKS,)), "erecv": dma((BLOCKS,)),
        "rsend": dma((1, peers - 1)), "rrecv": dma((1, peers - 1)),
    }
    return pl.pallas_call(
        back_body,
        out_shape=(
            sds((rows, width), F32), sds((owned, 2 * di), F32), sds((di // 32, width), F32), sds((PACK, 128), F32),
        ),
        in_specs=[ANY] * len(BACK_IN),
        out_specs=(VM,) * 4,
        scratch_shapes=[sems[n] if n in sems else pltpu.VMEM(*shapes[n]) for n in BACK_SCRATCH],
        compiler_params=pltpu.CompilerParams(collective_id=1, has_side_effects=True, vmem_limit_bytes=GRANT),
    )(*(inputs[n] for n in BACK_IN))


def finish_body(*refs):
    big, pack = refs[:4], refs[4]
    outs, small, sem = refs[5:9], refs[9:17], refs[17]
    copies = [pltpu.make_async_copy(src, dst, sem.at[i]) for i, (src, dst) in enumerate(zip(big, outs))]
    for copy in copies:
        copy.start()
    gain, conv, conv_bias, select, delta, delta_bias, a_log, skip = small
    own = conv.shape[1]
    conv[...] = pack[0:KW, 0:own]
    for row, ref in ((4, conv_bias), (5, delta_bias), (6, skip)):
        ref[...] = pack[row : row + 1, 0:own]
    a_log[...] = pack[ALOG0 : ALOG0 + DS, 0:own]
    delta[...] = pack[DELTA0 : DELTA0 + DTR, 0:own]
    select[...] = pack[...].T[own : 2 * own, 0:PACK0]
    part = gain.shape[1]
    parts = 128 // part
    me = (lax.axis_index("batch") * lax.axis_size("seq") + lax.axis_index("seq")) % parts
    tile = pack[PACK0 : PACK0 + 1, :]
    total = jnp.zeros((1, part), F32)
    for i in range(parts):
        total = total + jnp.where(me == i, tile[:, i * part : (i + 1) * part], 0.0)
    gain[...] = total
    for copy in copies:
        copy.wait()


def finish(whole, small):
    block, tgrad, gin, gout, pack = whole
    big = (block, tgrad, gin, gout)
    return pl.pallas_call(
        finish_body,
        out_shape=tuple(sds(v.shape, F32) for v in big + small),
        in_specs=[VM] * 5,
        out_specs=(ANY,) * 4 + (VM,) * 8,
        scratch_shapes=[pltpu.SemaphoreType.DMA((4,))],
        compiler_params=pltpu.CompilerParams(vmem_limit_bytes=GRANT),
    )(*big, pack)


def on_slice(tokens, cotangent, norm_gain, in_weight, conv_weight, conv_bias, select_weight, delta_weight, delta_bias, a_log, skip_gain, out_weight):
    sizes = (lax.axis_size("batch"), lax.axis_size("seq"))
    tok, cot = tokens[0], cotangent[0]
    rows = tok.shape[0]
    small = (
        norm_gain[None], conv_weight, conv_bias[None], select_weight, delta_weight, delta_bias[None], a_log, skip_gain[None],
    )
    f = front(tok, cot, in_weight, out_weight, small, sizes[1], rows // 32)
    whole = (f["block"],) + back(f, tok, cot)
    block_out, tokens_grad, g_in, g_out, *grads = finish(whole, small)
    g_gain, g_conv, g_conv_bias, g_select, g_delta, g_delta_bias, g_a_log, g_skip = grads
    return (
        block_out[None], tokens_grad[None], g_gain[0], g_in, g_conv, g_conv_bias[0], g_select, g_delta, g_delta_bias[0],
        g_a_log, g_skip[0], g_out,
    )


def on_device(tokens, cotangent, norm_gain, in_weight, conv_weight, conv_bias, select_weight, delta_weight, delta_bias, a_log, skip_gain, out_weight):
    axes = ("batch", "seq")
    sizes = (lax.axis_size("batch"), lax.axis_size("seq"))
    if sizes == (4, 8):
        return on_slice(
            tokens, cotangent, norm_gain, in_weight, conv_weight, conv_bias, select_weight, delta_weight, delta_bias,
            a_log, skip_gain, out_weight,
        )
    tok, cot = tokens[0], cotangent[0]
    rows, width = tok.shape
    di = out_weight.shape[0] * sizes[0] * sizes[1]
    tiles = di // 128
    full = lambda v, axis: lax.all_gather(v, axes, axis=axis, tiled=True)
    in_full = full(in_weight, 0)
    in_x, in_z = in_full[:, :di], in_full[:, di:]
    out_full = full(out_weight, 0)
    sel_t = full(select_weight, 0).T
    gain = full(norm_gain, 0)[None].astype(F32)
    w0 = jnp.concatenate(
        [
            full(conv_weight, 1), full(conv_bias, 0)[None], full(delta_bias, 0)[None], full(skip_gain, 0)[None],
            jnp.zeros((1, di), BF16), full(a_log, 1), full(delta_weight, 1),
            jnp.zeros((PACK0 - DELTA0 - DTR, di), BF16),
        ],
        axis=0,
    ).astype(F32)

    flat = sds((rows * tiles, 128), F32)
    wide = sds((rows, di), F32)
    spread = sds((rows * DS, 128), F32)
    carry = sds((DS, tiles, 128), F32)

    normed, x_in = kernel_call(
        inproj_body, (sds((rows, width), BF16), sds((rows, di), BF16)), 3
    )(tok, gain, in_x)
    halo = shift(x_in[rows - 16 :], 1)
    filt, xs, xt, draw, dt, bb, cb = kernel_call(
        conv_body,
        (wide, sds((rows, di), BF16), flat, wide, flat, spread, spread),
        4,
        [pltpu.VMEM((rows, 128), F32), pltpu.VMEM((rows + 16, 128), F32)],
    )(x_in, halo, w0, sel_t)
    a2, total, end = kernel_call(lightf_body, (carry, carry, carry), 4)(dt, xt, bb, w0)
    gate, gzp, gt, low, adj = kernel_call(
        gate_body, (wide, wide, flat, sds((rows, width), BF16), carry), 7
    )(normed, in_z, cot, out_full, dt, cb, a2)
    state_in = carried_in(total, end, False)
    state_out = carried_in(total, adj, True)
    chunks = rows // 64
    starts, block_out, gz, out_grad, z_grad, skip_grad = kernel_call(
        forward_body,
        (
            sds((chunks, DS, tiles, 128), F32), sds((rows, width), F32), sds((rows, di), BF16),
            sds((di, width), BF16), sds((width, di), BF16), sds((1, di), F32),
        ),
        14,
        [pltpu.VMEM((rows * tiles, 128), F32), pltpu.VMEM((rows, di), BF16), pltpu.VMEM((8, 128), F32)],
    )(state_in, dt, xt, bb, cb, a2, w0, gate, gzp, gt, tok, low, normed, out_full)
    tall = pltpu.VMEM((rows * DS, 128), F32)
    gdt, gat, gb, gc, ga = kernel_call(
        backward_body,
        (flat, flat, sds((rows, 128), F32), sds((rows, 128), F32), carry),
        8,
        [
            pltpu.VMEM((65 * 128, 128), F32), pltpu.VMEM((64 * 128, 128), F32), pltpu.VMEM((256, 128), F32),
            pltpu.VMEM((256, 128), F32), tall, tall,
        ],
    )(state_out, starts, dt, xt, bb, cb, gt, a2)
    gf, w0g, selg = kernel_call(
        tail_body,
        (wide, sds((PACK0, di), F32), sds((PACK0, di), F32)),
        12,
        [
            pltpu.VMEM((rows, 128), F32), pltpu.VMEM((rows + 16, 128), F32), pltpu.VMEM((rows, di), BF16),
            pltpu.VMEM((rows, PACK0), BF16), pltpu.VMEM((DTR, di), BF16),
        ],
    )(gdt, gat, gb, gc, gt, draw, filt, x_in, halo, xs, w0, sel_t)
    edge = shift(gf[:8], -1)
    tokens_grad, x_grad, gain_grad = kernel_call(
        last_body,
        (sds((rows, width), F32), sds((width, di), BF16), sds((1, width), F32)),
        10,
        [pltpu.VMEM((rows + 8, 128), F32), pltpu.VMEM((rows, di), BF16), pltpu.VMEM((rows, width), F32)],
    )(gf, edge, w0, gz, normed, tok, cot, gain, in_x, in_z)

    share = lambda v, d: lax.psum_scatter(v.astype(F32), axes, scatter_dimension=d, tiled=True)
    ga_flat = ga.reshape(DS, di)
    grads = (
        share(gain_grad[0], 0), share(jnp.concatenate([x_grad, z_grad], axis=1), 0), share(w0g[0:KW], 1),
        share(w0g[4], 0), share(selg.T, 0), share(w0g[DELTA0 : DELTA0 + DTR], 1), share(w0g[5], 0),
        share(ga_flat, 1), share(skip_grad[0], 0), share(out_grad, 0),
    )
    return (block_out[None], tokens_grad[None]) + grads


def solution(mesh):
    both = ("batch", "seq")
    first, second = P(both), P(None, both)
    matrix = P(both, None)
    whole = P("batch", "seq", None)
    weights = (first, matrix, second, first, matrix, second, first, second, first, matrix)
    return jax.shard_map(
        on_device,
        mesh=mesh,
        in_specs=(whole, whole) + weights,
        out_specs=(whole, whole) + weights,
        check_vma=False,
    )
```
